32 devices in a mesh: dp: 4 (over y, x), seq: 8 (over z, core).
Axes of the slice: x: 2, y: 2, z: 4, core: 2. Of those that a mesh axis runs over, the one named last changes fastest.
Arguments:
- hidden_in: bfloat16 [8, 1024, 2048], P('dp', 'seq'), may hold values from -6 to 6
- segment_ids: int32 [8, 1024], P('dp', 'seq'), may hold values from 0 to 7, as said below
- positions: int32 [8, 1024], P('dp', 'seq'), may hold values from 0 to 1023, as said below
- attn_gain: bfloat16 [2048], P(('dp', 'seq')), may hold values from 0.099609375 to 1.8984375
- query_weight: bfloat16 [2048, 2048], P(('dp', 'seq')), may hold values from -0.125 to 0.125
- key_weight: bfloat16 [2048, 256], P(('dp', 'seq')), may hold values from -0.125 to 0.125
- value_weight: bfloat16 [2048, 256], P(('dp', 'seq')), may hold values from -0.125 to 0.125
- out_weight: bfloat16 [2048, 2048], P(('dp', 'seq')), may hold values from -1 to 1
- mlp_gain: bfloat16 [2048], P(('dp', 'seq')), may hold values from 0.099609375 to 1.8984375
- gate_weight: bfloat16 [2048, 5632], P(('dp', 'seq')), may hold values from -0.125 to 0.125
- up_weight: bfloat16 [2048, 5632], P(('dp', 'seq')), may hold values from -0.125 to 0.125
- down_weight: bfloat16 [5632, 2048], P(('dp', 'seq')), may hold values from -0.15625 to 0.15625
- cotangent: bfloat16 [8, 1024, 2048], P('dp', 'seq'), may hold values from -6 to 6
Outputs:
- out_hidden: bfloat16 [8, 1024, 2048], P('dp', 'seq')
- grad_hidden_in: float32 [8, 1024, 2048], P('dp', 'seq')
- grad_attn_gain: float32 [2048], P(('dp', 'seq'))
- grad_query_weight: float32 [2048, 2048], P(('dp', 'seq'))
- grad_key_weight: float32 [2048, 256], P(('dp', 'seq'))
- grad_value_weight: float32 [2048, 256], P(('dp', 'seq'))
- grad_out_weight: float32 [2048, 2048], P(('dp', 'seq'))
- grad_mlp_gain: float32 [2048], P(('dp', 'seq'))
- grad_gate_weight: float32 [2048, 5632], P(('dp', 'seq'))
- grad_up_weight: float32 [2048, 5632], P(('dp', 'seq'))
- grad_down_weight: float32 [5632, 2048], P(('dp', 'seq'))
The draws below stay inside these ranges and needn't reach their ends.
Inputs may be any that keep to these rules, and one draw needn't show every extreme that they name: `segment_ids`: in each row the ids start at 0 and never fall; a document is a run of equal ids; row 0 holds one document, every other row exactly 8. `positions`: each token's offset from the first token of its document in its row.
All inputs are finite; a program needn't handle non-finite values.
Results may differ from the reference program's by a relative error of at most 0.017.
Values may be sent and summed in bfloat16 or wider, within the bound.
A program may use at most 384 MiB of HBM per device.

```python
import jax
import jax.numpy as jnp
from jax import lax

D = 2048
HQ = 32
HD = 64
KVH = 4
FF = 5632
LENGTH = 1024
ROWS = 8


extra_starts = 7


def packed_documents(key):
    row_keys = jax.random.split(jax.random.fold_in(key, 7), ROWS)

    def pick_row(row_key):
        return (jax.random.permutation(row_key, LENGTH - 1)[:extra_starts] + 1).astype(jnp.int32)
    picks = jax.vmap(pick_row)(row_keys)
    row_index = jnp.arange(ROWS, dtype=jnp.int32)[:, None]
    marks = jnp.zeros((ROWS, LENGTH), jnp.int32).at[jnp.broadcast_to(row_index, picks.shape), picks].set(1)
    index = jnp.arange(LENGTH, dtype=jnp.int32)[None, :]
    starts = (marks > 0) & (row_index > 0) | (index == 0)
    segments = jnp.cumsum(starts.astype(jnp.int32), axis=1).astype(jnp.int32) - 1
    begin = lax.cummax(jnp.where(starts, index, 0), axis=1)
    return (segments.astype(jnp.int32), (index - begin).astype(jnp.int32))


def draw_segment_ids(key, part):
    return packed_documents(key)[0]


def draw_positions(key, part):
    return packed_documents(key)[1]


def steps_of(stream_key, extent, cuts, low, high):
    level = 1.0
    for axis_at, parts in cuts:
        steps = jax.random.uniform(jax.random.fold_in(jax.random.fold_in(stream_key, 6), axis_at), (parts,), jnp.float32, low / len(cuts), high / len(cuts))
        level = level * jnp.repeat(jnp.exp(steps), extent[axis_at] // parts).reshape((-1,) + (1,) * (len(extent) - 1 - axis_at))
    return level


def gaussian(rng, extent, spread, bound, cuts=(), kind=jnp.bfloat16):
    factor_of = steps_of(rng, extent, cuts, -0.22, 0.18) if cuts else 1.0
    values = jax.random.normal(rng, extent, jnp.float32) * spread * factor_of
    return jnp.minimum(jnp.maximum(values, -bound), bound).astype(kind)


def setup_inputs(seed: int = 0) -> dict:
    streams_of = jax.random.split(jax.random.key(seed), 14)
    hidden_in = gaussian(streams_of[0], (ROWS, LENGTH, D), 1.0, 6.0, ((0, 4), (1, 8)))
    segment_ids = draw_segment_ids(jax.random.fold_in(streams_of[13], 71), 0)
    positions = draw_positions(jax.random.fold_in(streams_of[13], 71), 0)
    attn_gain = jnp.clip(1.0 + 0.18 * jax.random.normal(streams_of[3], (D,), jnp.float32), 0.099609375, 1.8984375).astype(jnp.bfloat16)
    query_weight = gaussian(streams_of[4], (D, HQ * HD), D ** -0.5, 0.125, ((0, 32),))
    key_weight = gaussian(streams_of[5], (D, KVH * HD), D ** -0.5, 0.125, ((0, 32),))
    value_weight = gaussian(streams_of[6], (D, KVH * HD), D ** -0.5, 0.125, ((0, 32),))
    out_weight = gaussian(streams_of[7], (HQ * HD, D), (HQ * HD // 64) ** -0.5, 1.0, ((0, 32),))
    mlp_gain = jnp.clip(1.0 + 0.18 * jax.random.normal(streams_of[8], (D,), jnp.float32), 0.099609375, 1.8984375).astype(jnp.bfloat16)
    gate_weight = gaussian(streams_of[9], (D, FF), D ** -0.5, 0.125, ((0, 32),))
    up_weight = gaussian(streams_of[10], (D, FF), D ** -0.5, 0.125, ((0, 32),))
    down_weight = gaussian(streams_of[11], (FF, D), (FF // 4) ** -0.5, 0.15625, ((0, 32),))
    cotangent = gaussian(streams_of[12], (ROWS, LENGTH, D), 1.0, 6.0, ((0, 4), (1, 8)))
    return dict(hidden_in=hidden_in, segment_ids=segment_ids, positions=positions, attn_gain=attn_gain, query_weight=query_weight, key_weight=key_weight, value_weight=value_weight, out_weight=out_weight, mlp_gain=mlp_gain, gate_weight=gate_weight, up_weight=up_weight, down_weight=down_weight, cotangent=cotangent)


@jax.custom_vjp
def low(v):
    return lax.optimization_barrier(v.astype(jnp.bfloat16)).astype(jnp.float32)

@jax.custom_vjp
def low_back(v):
    return v

def low_keep(v):
    return (low(v), None)

def low_pass(kept, grad):
    return (grad,)

def back_keep(v):
    return (v, None)

def back_low(kept, grad):
    return (low(grad),)
low.defvjp(low_keep, low_pass)
low_back.defvjp(back_keep, back_low)
EPSILON = 1e-05
HIGHEST = lax.Precision.HIGHEST

def matmul(left, right):
    return jnp.dot(left, right, precision=HIGHEST, preferred_element_type=jnp.float32)

def rms_norm(values, gain):
    factor = lax.rsqrt(lax.optimization_barrier(jnp.mean(values * values, axis=-1, keepdims=True)) + EPSILON)
    return values * factor * gain

def angles_of(positions):
    freqs = 10000.0 ** (-jnp.arange(0, HD // 2, dtype=jnp.float32) * 2.0 / HD)
    return positions.astype(jnp.float32)[:, None] * freqs[None, :]

def rotate(vectors, angles):
    half = vectors.shape[-1] // 2
    cosine = jnp.cos(angles)[:, None, :]
    sine = jnp.sin(angles)[:, None, :]
    first = vectors[..., :half]
    second = vectors[..., half:]
    return jnp.concatenate([first * cosine - second * sine, second * cosine + first * sine], axis=-1)

def attend(queries, keys, values, segments):
    length = queries.shape[0]
    block_rows = min(512, length)
    blocks = length // block_rows
    order = jnp.arange(length)

    def block(args):
        query_block, seg_block, pos_block = args
        scores = jnp.einsum('cgjd,kgd->gjck', query_block, keys, precision=HIGHEST) * HD ** (-0.5)
        scores = low_back(scores)
        allowed = (order[None, :] <= pos_block[:, None]) & (segments[None, :] == seg_block[:, None])
        scores = jnp.where(allowed, scores, -1e+30)
        highest = lax.optimization_barrier(jnp.max(scores, axis=-1, keepdims=True))
        powers = jnp.exp(scores - highest)
        probs = low(powers / lax.optimization_barrier(jnp.sum(powers, axis=-1, keepdims=True)))
        return jnp.einsum('gjck,kgd->cgjd', probs, values, precision=HIGHEST)
    pieces = lax.map(jax.checkpoint(block), (queries.reshape(blocks, block_rows, KVH, HQ // KVH, HD), segments.reshape(blocks, block_rows), order.reshape(blocks, block_rows)))
    return pieces.reshape(length, HQ * HD)

def layer_row(rows_in, segments, positions, weights):
    attn_gain, query_weight, key_weight, value_weight, out_weight, mlp_gain, gate_weight, up_weight, down_weight = weights
    length = rows_in.shape[0]
    normed1 = low(rms_norm(rows_in, attn_gain))
    angles = angles_of(positions)
    queries = low_back(matmul(normed1, query_weight)).reshape(length, HQ, HD)
    keys = low_back(matmul(normed1, key_weight)).reshape(length, KVH, HD)
    values = low(low_back(matmul(normed1, value_weight))).reshape(length, KVH, HD)
    queries_rot = low(rotate(queries, angles)).reshape(length, KVH, HQ // KVH, HD)
    keys_rot = low(rotate(keys, angles))
    context = low(low_back(attend(queries_rot, keys_rot, values, segments)))
    middle = rows_in + low_back(matmul(context, out_weight))
    normed2 = low(rms_norm(middle, mlp_gain))
    gate = low_back(matmul(normed2, gate_weight))
    up = low_back(matmul(normed2, up_weight))
    hidden = low(jax.nn.silu(gate) * up)
    return middle + low_back(matmul(hidden, down_weight))

def reference(hidden_in, segment_ids, positions, attn_gain, query_weight, key_weight, value_weight, out_weight, mlp_gain, gate_weight, up_weight, down_weight, cotangent):
    weights = tuple((array.astype(jnp.float32) for array in (attn_gain, query_weight, key_weight, value_weight, out_weight, mlp_gain, gate_weight, up_weight, down_weight)))
    inputs = hidden_in.astype(jnp.float32)

    def forward(rows, params):

        def one_row(args):
            return layer_row(args[0], args[1], args[2], params)
        return lax.map(jax.checkpoint(one_row), (rows, segment_ids, positions))
    result, pull = jax.vjp(forward, inputs, weights)
    grad_rows, grads = pull(cotangent.astype(jnp.float32))
    return (result.astype(jnp.bfloat16), grad_rows, grads[0], grads[1], grads[2], grads[3], grads[4], grads[5], grads[6], grads[7], grads[8])
```

```python
import jax
import jax.numpy as jnp
from jax import lax
from jax.sharding import Mesh
from jax.sharding import PartitionSpec as P

HQ = 32
HD = 64
KVH = 4


EPSILON = 1e-05


def fetch_attention(attn_gain, query_weight, key_weight, value_weight, out_weight):
    return (
        lax.all_gather(attn_gain, ("dp", "seq"), axis=0, tiled=True),
        lax.all_gather(query_weight, ("dp", "seq"), axis=0, tiled=True),
        lax.all_gather(key_weight, ("dp", "seq"), axis=0, tiled=True),
        lax.all_gather(value_weight, ("dp", "seq"), axis=0, tiled=True),
        lax.all_gather(out_weight, ("dp", "seq"), axis=0, tiled=True),
    )


def fetch_mlp(mlp_gain, gate_weight, up_weight, down_weight):
    return (
        lax.all_gather(mlp_gain, ("dp", "seq"), axis=0, tiled=True),
        lax.all_gather(gate_weight, ("dp", "seq"), axis=0, tiled=True),
        lax.all_gather(up_weight, ("dp", "seq"), axis=0, tiled=True),
        lax.all_gather(down_weight, ("dp", "seq"), axis=0, tiled=True),
    )


def angles_of(positions):
    freqs = 10000.0 ** (-jnp.arange(0, HD // 2, dtype=jnp.float32) * 2.0 / HD)
    return positions.astype(jnp.float32)[:, None] * freqs[None, :]


def rotate(vectors, cosine, sine):
    half = vectors.shape[-1] // 2
    first = vectors[..., :half]
    second = vectors[..., half:]
    cosine = cosine[:, None, :]
    sine = sine[:, None, :]
    return jnp.concatenate(
        [first * cosine - second * sine, second * cosine + first * sine], axis=-1
    )


def norm_forward(values, gain):
    factor = lax.rsqrt(jnp.mean(values * values, axis=-1, keepdims=True) + EPSILON)
    return (values * factor * gain.astype(jnp.float32), factor)


def norm_backward(values, factor, gain, grad_normed):
    inner = grad_normed * gain.astype(jnp.float32)
    grad_gain = jnp.sum(grad_normed * values * factor, axis=0)
    grad_values = factor * inner - factor * factor * factor * values * jnp.mean(
        inner * values, axis=-1, keepdims=True
    )
    return (grad_values, grad_gain)


def masked_scores(queries_rot, keys_heads, query_pos, query_seg, seg_all):
    scores = jnp.einsum(
        "cgjd,kgd->gjck", queries_rot, keys_heads, preferred_element_type=jnp.float32
    ) * HD ** (-0.5)
    key_pos = jnp.arange(keys_heads.shape[0])
    allowed = (key_pos[None, :] <= query_pos[:, None]) & (seg_all[None, :] == query_seg[:, None])
    return jnp.where(allowed, scores, -1e30)


def add_up(total, extra):
    if total is None:
        return extra
    return jax.tree.map(jnp.add, total, extra)


def gathered_weights_layer(
    hidden_in,
    segment_ids,
    positions,
    attn_gain,
    query_weight,
    key_weight,
    value_weight,
    out_weight,
    mlp_gain,
    gate_weight,
    up_weight,
    down_weight,
    cotangent,
):
    batches, local_len, width = hidden_in.shape
    group = HQ // KVH
    query_pos = lax.axis_index("seq") * local_len + jnp.arange(local_len)
    outputs = []
    grads_in = []
    attn_total = None
    mlp_total = None
    for microbatch in range(batches):
        rows_in = hidden_in[microbatch].astype(jnp.float32)
        seg_own = segment_ids[microbatch]
        angles = angles_of(positions[microbatch])
        cosine = jnp.cos(angles)
        sine = jnp.sin(angles)
        attn_set = fetch_attention(attn_gain, query_weight, key_weight, value_weight, out_weight)
        gain_one, weight_query, weight_key, weight_value, weight_out = attn_set
        normed1, factor1 = norm_forward(rows_in, gain_one)
        normed1_low = normed1.astype(jnp.bfloat16)
        queries = jnp.dot(normed1_low, weight_query, preferred_element_type=jnp.float32).reshape(
            local_len, HQ, HD
        )
        keys_own = jnp.dot(normed1_low, weight_key, preferred_element_type=jnp.float32).reshape(
            local_len, KVH, HD
        )
        values_own = jnp.dot(normed1_low, weight_value, preferred_element_type=jnp.float32).astype(
            jnp.bfloat16
        )
        queries_rot = (
            rotate(queries, cosine, sine).astype(jnp.bfloat16).reshape(local_len, KVH, group, HD)
        )
        keys_rot = rotate(keys_own, cosine, sine).astype(jnp.bfloat16).reshape(local_len, KVH * HD)
        keys_all, values_all, seg_all = (
            lax.all_gather(keys_rot, "seq", axis=0, tiled=True),
            lax.all_gather(values_own, "seq", axis=0, tiled=True),
            lax.all_gather(seg_own, "seq", axis=0, tiled=True),
        )
        keys_heads = keys_all.reshape(-1, KVH, HD)
        values_heads = values_all.reshape(-1, KVH, HD)
        scores = masked_scores(queries_rot, keys_heads, query_pos, seg_own, seg_all)
        highest = jnp.max(scores, axis=-1, keepdims=True)
        powers = jnp.exp(scores - highest)
        totals = jnp.sum(powers, axis=-1, keepdims=True)
        logsum = highest + jnp.log(totals)
        probs_low = (powers / totals).astype(jnp.bfloat16)
        context = jnp.einsum(
            "gjck,kgd->cgjd", probs_low, values_heads, preferred_element_type=jnp.float32
        )
        context_low = context.reshape(local_len, HQ * HD).astype(jnp.bfloat16)
        middle = rows_in + jnp.dot(context_low, weight_out, preferred_element_type=jnp.float32)
        mlp_set = fetch_mlp(mlp_gain, gate_weight, up_weight, down_weight)
        gain_two, weight_gate, weight_up, weight_down = mlp_set
        normed2, factor2 = norm_forward(middle, gain_two)
        normed2_low = normed2.astype(jnp.bfloat16)
        gate = jnp.dot(normed2_low, weight_gate, preferred_element_type=jnp.float32)
        up = jnp.dot(normed2_low, weight_up, preferred_element_type=jnp.float32)
        sigma = jax.nn.sigmoid(gate)
        activation = gate * sigma
        hidden = (activation * up).astype(jnp.bfloat16)
        mlp_out = jnp.dot(hidden, weight_down, preferred_element_type=jnp.float32)
        outputs.append((middle + mlp_out).astype(jnp.bfloat16))
        grad_low = cotangent[microbatch]
        grad_out = grad_low.astype(jnp.float32)
        mlp_back = fetch_mlp(mlp_gain, gate_weight, up_weight, down_weight)
        gain_two, weight_gate, weight_up, weight_down = mlp_back
        grad_down = jnp.dot(hidden.T, grad_low, preferred_element_type=jnp.float32)
        grad_hid = jnp.dot(grad_low, weight_down.T, preferred_element_type=jnp.float32)
        grad_gate = (grad_hid * up * sigma * (1.0 + gate * (1.0 - sigma))).astype(jnp.bfloat16)
        grad_up = (grad_hid * activation).astype(jnp.bfloat16)
        grad_wgate = jnp.dot(normed2_low.T, grad_gate, preferred_element_type=jnp.float32)
        grad_wup = jnp.dot(normed2_low.T, grad_up, preferred_element_type=jnp.float32)
        grad_normed2 = jnp.dot(
            grad_gate, weight_gate.T, preferred_element_type=jnp.float32
        ) + jnp.dot(grad_up, weight_up.T, preferred_element_type=jnp.float32)
        grad_mid_norm, grad_gain_two = norm_backward(middle, factor2, gain_two, grad_normed2)
        grad_middle = grad_out + grad_mid_norm
        attn_back = fetch_attention(attn_gain, query_weight, key_weight, value_weight, out_weight)
        gain_one, weight_query, weight_key, weight_value, weight_out = attn_back
        grad_attn = grad_middle.astype(jnp.bfloat16)
        grad_wout = jnp.dot(context_low.T, grad_attn, preferred_element_type=jnp.float32)
        grad_context = (
            jnp.dot(grad_attn, weight_out.T, preferred_element_type=jnp.float32)
            .astype(jnp.bfloat16)
            .reshape(local_len, KVH, group, HD)
        )
        probs = jnp.exp(
            masked_scores(queries_rot, keys_heads, query_pos, seg_own, seg_all) - logsum
        )
        grad_probs = jnp.einsum(
            "cgjd,kgd->gjck", grad_context, values_heads, preferred_element_type=jnp.float32
        )
        inner = jnp.sum(probs * grad_probs, axis=-1, keepdims=True)
        grad_scores = (probs * (grad_probs - inner)).astype(jnp.bfloat16)
        grad_qrot = jnp.einsum(
            "gjck,kgd->cgjd", grad_scores, keys_heads, preferred_element_type=jnp.float32
        ) * HD ** (-0.5)
        grad_krot_all = jnp.einsum(
            "gjck,cgjd->kgd", grad_scores, queries_rot, preferred_element_type=jnp.float32
        ) * HD ** (-0.5)
        grad_vall = jnp.einsum(
            "gjck,cgjd->kgd", probs_low, grad_context, preferred_element_type=jnp.float32
        )
        row_len = keys_heads.shape[0]
        grad_key_own, grad_value_own = (
            lax.psum_scatter(
                grad_krot_all.reshape(row_len, KVH * HD).astype(jnp.bfloat16),
                "seq",
                scatter_dimension=0,
                tiled=True,
            ).astype(jnp.float32),
            lax.psum_scatter(
                grad_vall.reshape(row_len, KVH * HD).astype(jnp.bfloat16),
                "seq",
                scatter_dimension=0,
                tiled=True,
            ).astype(jnp.float32),
        )
        grad_keys = (
            rotate(grad_key_own.reshape(local_len, KVH, HD), cosine, -sine)
            .astype(jnp.bfloat16)
            .reshape(local_len, KVH * HD)
        )
        grad_values = grad_value_own.astype(jnp.bfloat16)
        grad_queries = (
            rotate(grad_qrot.reshape(local_len, HQ, HD), cosine, -sine)
            .astype(jnp.bfloat16)
            .reshape(local_len, HQ * HD)
        )
        grad_wquery = jnp.dot(normed1_low.T, grad_queries, preferred_element_type=jnp.float32)
        grad_wkey = jnp.dot(normed1_low.T, grad_keys, preferred_element_type=jnp.float32)
        grad_wvalue = jnp.dot(normed1_low.T, grad_values, preferred_element_type=jnp.float32)
        grad_normed1 = jnp.dot(grad_queries, weight_query.T, preferred_element_type=jnp.float32)
        grad_normed1 = grad_normed1 + jnp.dot(
            grad_keys, weight_key.T, preferred_element_type=jnp.float32
        )
        grad_normed1 = grad_normed1 + jnp.dot(
            grad_values, weight_value.T, preferred_element_type=jnp.float32
        )
        grad_rows_norm, grad_gain_one = norm_backward(rows_in, factor1, gain_one, grad_normed1)
        grads_in.append(grad_middle + grad_rows_norm)
        attn_terms = (grad_gain_one, grad_wquery, grad_wkey, grad_wvalue, grad_wout)
        mlp_terms = (grad_gain_two, grad_wgate, grad_wup, grad_down)
        attn_shares = (
            lax.psum_scatter(attn_terms[0], ("dp", "seq"), scatter_dimension=0, tiled=True),
            lax.psum_scatter(attn_terms[1], ("dp", "seq"), scatter_dimension=0, tiled=True),
            lax.psum_scatter(attn_terms[2], ("dp", "seq"), scatter_dimension=0, tiled=True),
            lax.psum_scatter(attn_terms[3], ("dp", "seq"), scatter_dimension=0, tiled=True),
            lax.psum_scatter(attn_terms[4], ("dp", "seq"), scatter_dimension=0, tiled=True),
        )
        mlp_shares = (
            lax.psum_scatter(mlp_terms[0], ("dp", "seq"), scatter_dimension=0, tiled=True),
            lax.psum_scatter(mlp_terms[1], ("dp", "seq"), scatter_dimension=0, tiled=True),
            lax.psum_scatter(mlp_terms[2], ("dp", "seq"), scatter_dimension=0, tiled=True),
            lax.psum_scatter(mlp_terms[3], ("dp", "seq"), scatter_dimension=0, tiled=True),
        )
        attn_total = add_up(attn_total, attn_shares)
        mlp_total = add_up(mlp_total, mlp_shares)
    return (
        jnp.stack(outputs),
        jnp.stack(grads_in),
        attn_total[0],
        attn_total[1],
        attn_total[2],
        attn_total[3],
        attn_total[4],
        mlp_total[0],
        mlp_total[1],
        mlp_total[2],
        mlp_total[3],
    )


def gathered_weights(mesh):
    return jax.shard_map(
        gathered_weights_layer,
        mesh=mesh,
        in_specs=(
            P("dp", "seq", None),
            P("dp", "seq"),
            P("dp", "seq"),
            P(("dp", "seq")),
            P(("dp", "seq"), None),
            P(("dp", "seq"), None),
            P(("dp", "seq"), None),
            P(("dp", "seq"), None),
            P(("dp", "seq")),
            P(("dp", "seq"), None),
            P(("dp", "seq"), None),
            P(("dp", "seq"), None),
            P("dp", "seq", None),
        ),
        out_specs=(
            P("dp", "seq", None),
            P("dp", "seq", None),
            P(("dp", "seq")),
            P(("dp", "seq"), None),
            P(("dp", "seq"), None),
            P(("dp", "seq"), None),
            P(("dp", "seq"), None),
            P(("dp", "seq")),
            P(("dp", "seq"), None),
            P(("dp", "seq"), None),
            P(("dp", "seq"), None),
        ),
        check_vma=False,
    )


def swap(values, axis_name, size, step):
    return lax.ppermute(values, axis_name, [(i, i ^ step) for i in range(size)])


def plane_gather(values, dp):
    near = jnp.stack([values] + [swap(values, "dp", dp, k) for k in range(1, dp)])
    return jnp.stack([near, swap(near, "core", 2, 1)], axis=1)


def plane_scatter(terms, dp):
    arrived = swap(terms[:, 1].astype(jnp.bfloat16), "core", 2, 1)
    halves = terms[:, 0] + arrived.astype(jnp.float32)
    total = halves[0]
    for k in range(1, dp):
        total = total + swap(halves[k].astype(jnp.bfloat16), "dp", dp, k).astype(jnp.float32)
    return total


def exchange(blocks):
    return lax.all_to_all(blocks, ("dp", "core"), split_axis=0, concat_axis=0, tiled=True)


def turn(vectors, cosine, sine):
    half = vectors.shape[-1] // 2
    first = vectors[..., :half]
    second = vectors[..., half:]
    return jnp.concatenate(
        [first * cosine - second * sine, second * cosine + first * sine], axis=-1
    )


def split_layer(dp, depth):
    def layer(
        hidden_in,
        segment_ids,
        positions,
        attn_gain,
        query_weight,
        key_weight,
        value_weight,
        out_weight,
        mlp_gain,
        gate_weight,
        up_weight,
        down_weight,
        cotangent,
    ):
        f32, bf16 = jnp.float32, jnp.bfloat16
        rows, length, width = hidden_in.shape
        own = rows * length
        team = 2 * dp
        tokens = team * own
        part = query_weight.shape[0]
        hidden_rows = down_weight.shape[0]
        inner = depth * hidden_rows
        heads = depth
        core = lax.axis_index("core")
        place = lax.axis_index("z")

        def dot(left, right):
            return jnp.dot(left, right, preferred_element_type=f32)

        def by_owner(columns, count):
            split = columns.reshape(part, dp, depth, 2, count)
            return split.transpose(1, 3, 0, 2, 4).reshape(team, part, depth * count)

        kv_pair = jnp.stack(
            [key_weight.reshape(part, dp, HD), value_weight.reshape(part, dp, HD)], axis=1
        )
        kv_blocks = kv_pair.transpose(2, 1, 0, 3).reshape(team, part, HD)
        attn_blocks = jnp.concatenate([by_owner(query_weight, HD), kv_blocks], axis=-1)
        gains = jnp.stack([attn_gain, mlp_gain])
        gain_rows = jnp.pad(gains, ((0, 6), (0, attn_blocks.shape[-1] - part)))
        attn_blocks = jnp.concatenate(
            [attn_blocks, jnp.broadcast_to(gain_rows, (team,) + gain_rows.shape)], axis=1
        )
        attn_got = lax.all_gather(exchange(attn_blocks), "z", axis=0)
        attn_got = attn_got.reshape(depth, dp, 2, part + 8, -1).transpose(1, 0, 2, 3, 4)
        weight_qkv = attn_got[:, :, :, :part].reshape(width, -1)
        gain_one = attn_got[:, :, :, part, :part].reshape(width)
        gain_two = attn_got[:, :, :, part + 1, :part].reshape(width)
        weight_out = lax.all_gather(out_weight, "z", axis=0, tiled=True)
        wide = jnp.stack(
            [by_owner(gate_weight, hidden_rows), by_owner(up_weight, hidden_rows)], axis=1
        )
        wide_got = lax.all_gather(exchange(wide), "z", axis=0)
        wide_got = wide_got.reshape(depth, dp, 2, 2, part, inner).transpose(3, 1, 0, 2, 4, 5)
        weight_gate = wide_got[0].reshape(width, inner)
        weight_up = wide_got[1].reshape(width, inner)
        weight_down = lax.all_gather(down_weight, "z", axis=0, tiled=True)

        x_own = hidden_in.reshape(own, width)
        cot_own = cotangent.reshape(own, width)
        x_all = plane_gather(x_own, dp).reshape(tokens, width)
        marks = plane_gather(jnp.stack([segment_ids, positions]), dp)
        seg_line = lax.all_gather(marks[:, :, 0], "z", axis=0)
        pos_here = marks[:, :, 1].reshape(tokens)
        seg_here = marks[:, :, 0]

        x_f32 = x_all.astype(f32)
        factor1 = lax.rsqrt(jnp.mean(x_f32 * x_f32, axis=-1, keepdims=True) + EPSILON)
        normed1 = (x_f32 * factor1 * gain_one.astype(f32)).astype(bf16)
        projected = dot(normed1, weight_qkv).reshape(tokens, heads + 1, HD)
        angles = angles_of(pos_here)
        head_turns = (jnp.arange(heads + 1) < heads) | (core == 0)
        cosine = jnp.where(head_turns[:, None], jnp.cos(angles)[:, None, :], 1.0)
        sine = jnp.where(head_turns[:, None], jnp.sin(angles)[:, None, :], 0.0)
        turned = turn(projected, cosine, sine).astype(bf16)
        queries = turned[:, :heads]

        def other_order(array):
            split = array.reshape(depth, dp, 2, rows * length, HD)
            return split[:, :, ::-1].reshape(depth, tokens, HD)

        line_one = lax.all_gather(turned[:, heads], "z", axis=0)
        line_two = other_order(swap(line_one, "core", 2, 1))
        keys = jnp.where(core == 0, line_one, line_two)
        values = jnp.where(core == 0, line_two, line_one)

        def row_queries(array):
            split = array.reshape(dp, 2, rows, length, heads, HD)
            return split.transpose(0, 2, 4, 1, 3, 5).reshape(dp * rows, heads, 2 * length, HD)

        def flat_queries(array):
            split = array.reshape(dp, rows, heads, 2, length, HD)
            return split.transpose(0, 3, 1, 4, 2, 5).reshape(tokens, heads * HD)

        def row_keys(array):
            split = array.reshape(depth, dp, 2, rows, length, HD)
            return split.transpose(1, 3, 0, 2, 4, 5).reshape(dp * rows, depth * 2 * length, HD)

        def line_keys(array):
            split = array.reshape(dp, rows, depth, 2, length, HD)
            return split.transpose(2, 0, 3, 1, 4, 5).reshape(depth, tokens, HD)

        queries_row = row_queries(queries)
        keys_row = row_keys(keys)
        values_row = row_keys(values)
        seg_q = seg_here.transpose(0, 2, 1, 3).reshape(dp * rows, 2 * length)
        seg_k = seg_line.transpose(1, 3, 0, 2, 4).reshape(dp * rows, depth * 2 * length)
        halves = jnp.where(jnp.arange(2) == 0, core, 1 - core)
        inside = (halves[:, None] * length + jnp.arange(length)).reshape(2 * length)
        order_q = place * 2 * length + inside
        order_k = (jnp.arange(depth)[:, None] * 2 * length + inside).reshape(-1)
        allowed = (order_k[None, None, :] <= order_q[None, :, None]) & (
            seg_k[:, None, :] == seg_q[:, :, None]
        )
        scores = jnp.einsum(
            "bhqd,bkd->bhqk", queries_row, keys_row, preferred_element_type=f32
        ) * HD ** (-0.5)
        scores = jnp.where(allowed[:, None], scores, -1e30)
        highest = jnp.max(scores, axis=-1, keepdims=True)
        powers = jnp.exp(scores - highest)
        totals = jnp.sum(powers, axis=-1, keepdims=True)
        probs = powers / totals
        probs_low = probs.astype(bf16)
        context = jnp.einsum("bhqk,bkd->bhqd", probs_low, values_row, preferred_element_type=f32)
        context = flat_queries(context.astype(bf16))
        attn_out = plane_scatter(dot(context, weight_out).reshape(dp, 2, own, width), dp)
        middle = x_own.astype(f32) + attn_out

        normed2, factor2 = norm_forward(middle, gain_two)
        normed2 = plane_gather(normed2.astype(bf16), dp).reshape(tokens, width)
        cot_all = plane_gather(cot_own, dp).reshape(tokens, width)
        gate = dot(normed2, weight_gate)
        up = dot(normed2, weight_up)
        sigma = jax.nn.sigmoid(gate)
        activation = gate * sigma
        hidden = (activation * up).astype(bf16)
        mlp_out = plane_scatter(dot(hidden, weight_down).reshape(dp, 2, own, width), dp)
        out_hidden = (middle + mlp_out).astype(bf16)
        grad_hid = dot(cot_all, weight_down.T)
        grad_gate = (grad_hid * up * sigma * (1.0 + gate * (1.0 - sigma))).astype(bf16)
        grad_up = (grad_hid * activation).astype(bf16)
        grad_normed2 = dot(grad_gate, weight_gate.T) + dot(grad_up, weight_up.T)
        grad_normed2 = plane_scatter(grad_normed2.reshape(dp, 2, own, width), dp)
        grad_down = dot(hidden.T, cot_all)
        grad_wide = jnp.stack([dot(normed2.T, grad_gate), dot(normed2.T, grad_up)])

        def line_sum(array):
            return lax.psum_scatter(array.astype(bf16), "z", scatter_dimension=0, tiled=True)

        def owner_rows(array, count):
            lead = array.shape[0]
            split = array.reshape(lead, dp, depth, 2, part, count).transpose(2, 1, 3, 0, 4, 5)
            summed = line_sum(split.reshape(depth * team, lead, part, count))
            return exchange(summed)

        def from_owner(blocks, count):
            split = blocks.reshape(dp, 2, part, depth, count).transpose(2, 0, 3, 1, 4)
            return split.reshape(part, dp * depth * 2 * count).astype(f32)

        grad_down = line_sum(grad_down).astype(f32)
        wide_back = owner_rows(grad_wide, inner)
        grad_wgate = from_owner(wide_back[:, 0], hidden_rows)
        grad_wup = from_owner(wide_back[:, 1], hidden_rows)

        inner2 = grad_normed2 * gain_two.astype(f32)
        grad_middle = (
            cot_own.astype(f32)
            + factor2 * inner2
            - factor2 * factor2 * factor2 * middle * jnp.mean(inner2 * middle, axis=-1, keepdims=True)
        )
        grad_attn = plane_gather(grad_middle.astype(bf16), dp).reshape(tokens, width)
        grad_wout = line_sum(dot(context.T, grad_attn)).astype(f32)
        grad_context = dot(grad_attn, weight_out.T).astype(bf16)
        grad_context = row_queries(grad_context)
        grad_probs = jnp.einsum(
            "bhqd,bkd->bhqk", grad_context, values_row, preferred_element_type=f32
        )
        inner = jnp.sum(probs * grad_probs, axis=-1, keepdims=True)
        grad_scores = (probs * (grad_probs - inner)).astype(bf16)
        grad_queries = jnp.einsum(
            "bhqk,bkd->bhqd", grad_scores, keys_row, preferred_element_type=f32
        ) * HD ** (-0.5)
        grad_keys = jnp.einsum(
            "bhqk,bhqd->bkd", grad_scores, queries_row, preferred_element_type=f32
        ) * HD ** (-0.5)
        grad_values = jnp.einsum(
            "bhqk,bhqd->bkd", probs_low, grad_context, preferred_element_type=f32
        )
        grad_keys = line_keys(grad_keys)
        grad_values = line_keys(grad_values)
        kept = jnp.where(core == 0, grad_keys, grad_values)
        given = jnp.where(core == 0, grad_values, grad_keys)
        kept = kept + other_order(swap(given.astype(bf16), "core", 2, 1)).astype(f32)
        grad_pair = line_sum(kept.reshape(depth * tokens, HD)).astype(f32)
        grad_turned = jnp.concatenate(
            [flat_queries(grad_queries).reshape(tokens, heads, HD), grad_pair[:, None]], axis=1
        )
        grad_projected = turn(grad_turned, cosine, -sine).astype(bf16).reshape(tokens, -1)
        grad_normed1 = plane_scatter(
            dot(grad_projected, weight_qkv.T).reshape(dp, 2, own, width), dp
        )
        attn_back = owner_rows(dot(normed1.T, grad_projected)[None], (heads + 1) * HD)[:, 0]
        grad_wquery = from_owner(attn_back[:, :, : heads * HD], HD)
        pair_back = attn_back[:, :, heads * HD :].reshape(dp, 2, part, HD).transpose(1, 2, 0, 3)
        grad_wkey = pair_back[0].reshape(part, dp * HD).astype(f32)
        grad_wvalue = pair_back[1].reshape(part, dp * HD).astype(f32)

        own_f32 = x_own.astype(f32)
        factor = lax.rsqrt(jnp.mean(own_f32 * own_f32, axis=-1, keepdims=True) + EPSILON)
        inner1 = grad_normed1 * gain_one.astype(f32)
        grad_in = (
            grad_middle
            + factor * inner1
            - factor * factor * factor * own_f32 * jnp.mean(inner1 * own_f32, axis=-1, keepdims=True)
        )

        def rows_of(weight, grad):
            return jnp.sum(weight.astype(f32) * grad, axis=-1)

        grad_gain_one = (
            rows_of(query_weight, grad_wquery)
            + rows_of(key_weight, grad_wkey)
            + rows_of(value_weight, grad_wvalue)
        ) / attn_gain.astype(f32)
        grad_gain_two = (
            rows_of(gate_weight, grad_wgate) + rows_of(up_weight, grad_wup)
        ) / mlp_gain.astype(f32)
        return (
            out_hidden.reshape(rows, length, width),
            grad_in.reshape(rows, length, width),
            grad_gain_one,
            grad_wquery,
            grad_wkey,
            grad_wvalue,
            grad_wout,
            grad_gain_two,
            grad_wgate,
            grad_wup,
            grad_down,
        )

    return layer


def solution(mesh):
    dp, seq = mesh.shape["dp"], mesh.shape["seq"]
    if dp != KVH or seq % 2 or HQ != dp * seq:
        return gathered_weights(mesh)
    depth = seq // 2
    mesh = Mesh(mesh.devices.reshape(dp, depth, 2), ("dp", "z", "core"))
    every = ("dp", "z", "core")
    tokens = P("dp", ("z", "core"), None)
    matrix = P(every, None)
    return jax.shard_map(
        split_layer(dp, depth),
        mesh=mesh,
        in_specs=(
            tokens,
            P("dp", ("z", "core")),
            P("dp", ("z", "core")),
            P(every),
            matrix,
            matrix,
            matrix,
            matrix,
            P(every),
            matrix,
            matrix,
            matrix,
            tokens,
        ),
        out_specs=(
            tokens,
            tokens,
            P(every),
            matrix,
            matrix,
            matrix,
            matrix,
            P(every),
            matrix,
            matrix,
            matrix,
        ),
        check_vma=False,
    )
```

```python
import functools

import jax
import jax.numpy as jnp
from jax import lax
from jax.experimental import pallas as pl
from jax.experimental.pallas import tpu as pltpu
from jax.sharding import Mesh
from jax.sharding import PartitionSpec as P

HQ = 32
HD = 64
KVH = 4


EPSILON = 1e-05


def fetch_attention(attn_gain, query_weight, key_weight, value_weight, out_weight):
    return (
        lax.all_gather(attn_gain, ("dp", "seq"), axis=0, tiled=True),
        lax.all_gather(query_weight, ("dp", "seq"), axis=0, tiled=True),
        lax.all_gather(key_weight, ("dp", "seq"), axis=0, tiled=True),
        lax.all_gather(value_weight, ("dp", "seq"), axis=0, tiled=True),
        lax.all_gather(out_weight, ("dp", "seq"), axis=0, tiled=True),
    )


def fetch_mlp(mlp_gain, gate_weight, up_weight, down_weight):
    return (
        lax.all_gather(mlp_gain, ("dp", "seq"), axis=0, tiled=True),
        lax.all_gather(gate_weight, ("dp", "seq"), axis=0, tiled=True),
        lax.all_gather(up_weight, ("dp", "seq"), axis=0, tiled=True),
        lax.all_gather(down_weight, ("dp", "seq"), axis=0, tiled=True),
    )


def angles_of(positions):
    freqs = 10000.0 ** (-jnp.arange(0, HD // 2, dtype=jnp.float32) * 2.0 / HD)
    return positions.astype(jnp.float32)[:, None] * freqs[None, :]


def rotate(vectors, cosine, sine):
    half = vectors.shape[-1] // 2
    first = vectors[..., :half]
    second = vectors[..., half:]
    cosine = cosine[:, None, :]
    sine = sine[:, None, :]
    return jnp.concatenate(
        [first * cosine - second * sine, second * cosine + first * sine], axis=-1
    )


def norm_forward(values, gain):
    factor = lax.rsqrt(jnp.mean(values * values, axis=-1, keepdims=True) + EPSILON)
    return (values * factor * gain.astype(jnp.float32), factor)


def norm_backward(values, factor, gain, grad_normed):
    inner = grad_normed * gain.astype(jnp.float32)
    grad_gain = jnp.sum(grad_normed * values * factor, axis=0)
    grad_values = factor * inner - factor * factor * factor * values * jnp.mean(
        inner * values, axis=-1, keepdims=True
    )
    return (grad_values, grad_gain)


def masked_scores(queries_rot, keys_heads, query_pos, query_seg, seg_all):
    scores = jnp.einsum(
        "cgjd,kgd->gjck", queries_rot, keys_heads, preferred_element_type=jnp.float32
    ) * HD ** (-0.5)
    key_pos = jnp.arange(keys_heads.shape[0])
    allowed = (key_pos[None, :] <= query_pos[:, None]) & (seg_all[None, :] == query_seg[:, None])
    return jnp.where(allowed, scores, -1e30)


def add_up(total, extra):
    if total is None:
        return extra
    return jax.tree.map(jnp.add, total, extra)


def gathered_weights_layer(
    hidden_in,
    segment_ids,
    positions,
    attn_gain,
    query_weight,
    key_weight,
    value_weight,
    out_weight,
    mlp_gain,
    gate_weight,
    up_weight,
    down_weight,
    cotangent,
):
    batches, local_len, width = hidden_in.shape
    group = HQ // KVH
    query_pos = lax.axis_index("seq") * local_len + jnp.arange(local_len)
    outputs = []
    grads_in = []
    attn_total = None
    mlp_total = None
    for microbatch in range(batches):
        rows_in = hidden_in[microbatch].astype(jnp.float32)
        seg_own = segment_ids[microbatch]
        angles = angles_of(positions[microbatch])
        cosine = jnp.cos(angles)
        sine = jnp.sin(angles)
        attn_set = fetch_attention(attn_gain, query_weight, key_weight, value_weight, out_weight)
        gain_one, weight_query, weight_key, weight_value, weight_out = attn_set
        normed1, factor1 = norm_forward(rows_in, gain_one)
        normed1_low = normed1.astype(jnp.bfloat16)
        queries = jnp.dot(normed1_low, weight_query, preferred_element_type=jnp.float32).reshape(
            local_len, HQ, HD
        )
        keys_own = jnp.dot(normed1_low, weight_key, preferred_element_type=jnp.float32).reshape(
            local_len, KVH, HD
        )
        values_own = jnp.dot(normed1_low, weight_value, preferred_element_type=jnp.float32).astype(
            jnp.bfloat16
        )
        queries_rot = (
            rotate(queries, cosine, sine).astype(jnp.bfloat16).reshape(local_len, KVH, group, HD)
        )
        keys_rot = rotate(keys_own, cosine, sine).astype(jnp.bfloat16).reshape(local_len, KVH * HD)
        keys_all, values_all, seg_all = (
            lax.all_gather(keys_rot, "seq", axis=0, tiled=True),
            lax.all_gather(values_own, "seq", axis=0, tiled=True),
            lax.all_gather(seg_own, "seq", axis=0, tiled=True),
        )
        keys_heads = keys_all.reshape(-1, KVH, HD)
        values_heads = values_all.reshape(-1, KVH, HD)
        scores = masked_scores(queries_rot, keys_heads, query_pos, seg_own, seg_all)
        highest = jnp.max(scores, axis=-1, keepdims=True)
        powers = jnp.exp(scores - highest)
        totals = jnp.sum(powers, axis=-1, keepdims=True)
        logsum = highest + jnp.log(totals)
        probs_low = (powers / totals).astype(jnp.bfloat16)
        context = jnp.einsum(
            "gjck,kgd->cgjd", probs_low, values_heads, preferred_element_type=jnp.float32
        )
        context_low = context.reshape(local_len, HQ * HD).astype(jnp.bfloat16)
        middle = rows_in + jnp.dot(context_low, weight_out, preferred_element_type=jnp.float32)
        mlp_set = fetch_mlp(mlp_gain, gate_weight, up_weight, down_weight)
        gain_two, weight_gate, weight_up, weight_down = mlp_set
        normed2, factor2 = norm_forward(middle, gain_two)
        normed2_low = normed2.astype(jnp.bfloat16)
        gate = jnp.dot(normed2_low, weight_gate, preferred_element_type=jnp.float32)
        up = jnp.dot(normed2_low, weight_up, preferred_element_type=jnp.float32)
        sigma = jax.nn.sigmoid(gate)
        activation = gate * sigma
        hidden = (activation * up).astype(jnp.bfloat16)
        mlp_out = jnp.dot(hidden, weight_down, preferred_element_type=jnp.float32)
        outputs.append((middle + mlp_out).astype(jnp.bfloat16))
        grad_low = cotangent[microbatch]
        grad_out = grad_low.astype(jnp.float32)
        mlp_back = fetch_mlp(mlp_gain, gate_weight, up_weight, down_weight)
        gain_two, weight_gate, weight_up, weight_down = mlp_back
        grad_down = jnp.dot(hidden.T, grad_low, preferred_element_type=jnp.float32)
        grad_hid = jnp.dot(grad_low, weight_down.T, preferred_element_type=jnp.float32)
        grad_gate = (grad_hid * up * sigma * (1.0 + gate * (1.0 - sigma))).astype(jnp.bfloat16)
        grad_up = (grad_hid * activation).astype(jnp.bfloat16)
        grad_wgate = jnp.dot(normed2_low.T, grad_gate, preferred_element_type=jnp.float32)
        grad_wup = jnp.dot(normed2_low.T, grad_up, preferred_element_type=jnp.float32)
        grad_normed2 = jnp.dot(
            grad_gate, weight_gate.T, preferred_element_type=jnp.float32
        ) + jnp.dot(grad_up, weight_up.T, preferred_element_type=jnp.float32)
        grad_mid_norm, grad_gain_two = norm_backward(middle, factor2, gain_two, grad_normed2)
        grad_middle = grad_out + grad_mid_norm
        attn_back = fetch_attention(attn_gain, query_weight, key_weight, value_weight, out_weight)
        gain_one, weight_query, weight_key, weight_value, weight_out = attn_back
        grad_attn = grad_middle.astype(jnp.bfloat16)
        grad_wout = jnp.dot(context_low.T, grad_attn, preferred_element_type=jnp.float32)
        grad_context = (
            jnp.dot(grad_attn, weight_out.T, preferred_element_type=jnp.float32)
            .astype(jnp.bfloat16)
            .reshape(local_len, KVH, group, HD)
        )
        probs = jnp.exp(
            masked_scores(queries_rot, keys_heads, query_pos, seg_own, seg_all) - logsum
        )
        grad_probs = jnp.einsum(
            "cgjd,kgd->gjck", grad_context, values_heads, preferred_element_type=jnp.float32
        )
        inner = jnp.sum(probs * grad_probs, axis=-1, keepdims=True)
        grad_scores = (probs * (grad_probs - inner)).astype(jnp.bfloat16)
        grad_qrot = jnp.einsum(
            "gjck,kgd->cgjd", grad_scores, keys_heads, preferred_element_type=jnp.float32
        ) * HD ** (-0.5)
        grad_krot_all = jnp.einsum(
            "gjck,cgjd->kgd", grad_scores, queries_rot, preferred_element_type=jnp.float32
        ) * HD ** (-0.5)
        grad_vall = jnp.einsum(
            "gjck,cgjd->kgd", probs_low, grad_context, preferred_element_type=jnp.float32
        )
        row_len = keys_heads.shape[0]
        grad_key_own, grad_value_own = (
            lax.psum_scatter(
                grad_krot_all.reshape(row_len, KVH * HD).astype(jnp.bfloat16),
                "seq",
                scatter_dimension=0,
                tiled=True,
            ).astype(jnp.float32),
            lax.psum_scatter(
                grad_vall.reshape(row_len, KVH * HD).astype(jnp.bfloat16),
                "seq",
                scatter_dimension=0,
                tiled=True,
            ).astype(jnp.float32),
        )
        grad_keys = (
            rotate(grad_key_own.reshape(local_len, KVH, HD), cosine, -sine)
            .astype(jnp.bfloat16)
            .reshape(local_len, KVH * HD)
        )
        grad_values = grad_value_own.astype(jnp.bfloat16)
        grad_queries = (
            rotate(grad_qrot.reshape(local_len, HQ, HD), cosine, -sine)
            .astype(jnp.bfloat16)
            .reshape(local_len, HQ * HD)
        )
        grad_wquery = jnp.dot(normed1_low.T, grad_queries, preferred_element_type=jnp.float32)
        grad_wkey = jnp.dot(normed1_low.T, grad_keys, preferred_element_type=jnp.float32)
        grad_wvalue = jnp.dot(normed1_low.T, grad_values, preferred_element_type=jnp.float32)
        grad_normed1 = jnp.dot(grad_queries, weight_query.T, preferred_element_type=jnp.float32)
        grad_normed1 = grad_normed1 + jnp.dot(
            grad_keys, weight_key.T, preferred_element_type=jnp.float32
        )
        grad_normed1 = grad_normed1 + jnp.dot(
            grad_values, weight_value.T, preferred_element_type=jnp.float32
        )
        grad_rows_norm, grad_gain_one = norm_backward(rows_in, factor1, gain_one, grad_normed1)
        grads_in.append(grad_middle + grad_rows_norm)
        attn_terms = (grad_gain_one, grad_wquery, grad_wkey, grad_wvalue, grad_wout)
        mlp_terms = (grad_gain_two, grad_wgate, grad_wup, grad_down)
        attn_shares = (
            lax.psum_scatter(attn_terms[0], ("dp", "seq"), scatter_dimension=0, tiled=True),
            lax.psum_scatter(attn_terms[1], ("dp", "seq"), scatter_dimension=0, tiled=True),
            lax.psum_scatter(attn_terms[2], ("dp", "seq"), scatter_dimension=0, tiled=True),
            lax.psum_scatter(attn_terms[3], ("dp", "seq"), scatter_dimension=0, tiled=True),
            lax.psum_scatter(attn_terms[4], ("dp", "seq"), scatter_dimension=0, tiled=True),
        )
        mlp_shares = (
            lax.psum_scatter(mlp_terms[0], ("dp", "seq"), scatter_dimension=0, tiled=True),
            lax.psum_scatter(mlp_terms[1], ("dp", "seq"), scatter_dimension=0, tiled=True),
            lax.psum_scatter(mlp_terms[2], ("dp", "seq"), scatter_dimension=0, tiled=True),
            lax.psum_scatter(mlp_terms[3], ("dp", "seq"), scatter_dimension=0, tiled=True),
        )
        attn_total = add_up(attn_total, attn_shares)
        mlp_total = add_up(mlp_total, mlp_shares)
    return (
        jnp.stack(outputs),
        jnp.stack(grads_in),
        attn_total[0],
        attn_total[1],
        attn_total[2],
        attn_total[3],
        attn_total[4],
        mlp_total[0],
        mlp_total[1],
        mlp_total[2],
        mlp_total[3],
    )


def gathered_weights(mesh):
    return jax.shard_map(
        gathered_weights_layer,
        mesh=mesh,
        in_specs=(
            P("dp", "seq", None),
            P("dp", "seq"),
            P("dp", "seq"),
            P(("dp", "seq")),
            P(("dp", "seq"), None),
            P(("dp", "seq"), None),
            P(("dp", "seq"), None),
            P(("dp", "seq"), None),
            P(("dp", "seq")),
            P(("dp", "seq"), None),
            P(("dp", "seq"), None),
            P(("dp", "seq"), None),
            P("dp", "seq", None),
        ),
        out_specs=(
            P("dp", "seq", None),
            P("dp", "seq", None),
            P(("dp", "seq")),
            P(("dp", "seq"), None),
            P(("dp", "seq"), None),
            P(("dp", "seq"), None),
            P(("dp", "seq"), None),
            P(("dp", "seq")),
            P(("dp", "seq"), None),
            P(("dp", "seq"), None),
            P(("dp", "seq"), None),
        ),
        check_vma=False,
    )


def swap(values, axis_name, size, step):
    return lax.ppermute(values, axis_name, [(i, i ^ step) for i in range(size)])


def plane_gather(values, dp, core):
    near = jnp.stack([values] + [swap(values, "dp", dp, k) for k in range(1, dp)])
    far = swap(near, "core", 2, 1)
    first = jnp.where(core == 0, near, far)
    second = jnp.where(core == 0, far, near)
    return jnp.stack([first, second], axis=2)


def plane_scatter(terms, dp, core):
    mine = lax.dynamic_index_in_dim(terms, core, 2, keepdims=False)
    other = lax.dynamic_index_in_dim(terms, 1 - core, 2, keepdims=False)
    halves = mine + swap(other.astype(jnp.bfloat16), "core", 2, 1).astype(jnp.float32)
    total = halves[0]
    for k in range(1, dp):
        total = total + swap(halves[k].astype(jnp.bfloat16), "dp", dp, k).astype(jnp.float32)
    return total


def exchange(blocks):
    return lax.all_to_all(blocks, ("dp", "core"), split_axis=0, concat_axis=0, tiled=True)


NEGATIVE = -1e30
VMEM_LIMIT = 56 * 1024 * 1024
MESH = pl.DeviceIdType.MESH


def contract_last(left, right):
    return lax.dot_general(
        left, right, (((1,), (1,)), ((), ())), preferred_element_type=jnp.float32
    )


def multiply(left, right):
    return jnp.dot(left, right, preferred_element_type=jnp.float32)


def spread_keys(block, heads):
    half = block.shape[0] // 2
    return jnp.concatenate([block[:half]] * heads + [block[half:]] * heads, axis=0)


def fold_keys(block, heads):
    half = block.shape[0] // (2 * heads)
    first = sum(block[h * half : (h + 1) * half] for h in range(heads))
    rest = range(heads, 2 * heads)
    return jnp.concatenate([first, sum(block[h * half : (h + 1) * half] for h in rest)], axis=0)


def fold_values(block, heads):
    size = block.shape[0] // heads
    return sum(block[h * size : (h + 1) * size] for h in range(heads))


def turned_head(shape, dim, heads):
    index = lax.broadcasted_iota(jnp.int32, shape, dim)
    return lax.rem(index, shape[dim] // 2) // (shape[dim] // 2 // heads)


def plain_head(shape, dim, heads):
    index = lax.broadcasted_iota(jnp.int32, shape, dim)
    return index // (shape[dim] // heads)


def per_head(values, owner, heads, axis):
    zero = jnp.zeros_like(values)
    return jnp.concatenate([jnp.where(owner == h, values, zero) for h in range(heads)], axis=axis)


def join_heads(stacked, owner, heads):
    size = stacked.shape[0] // heads
    return sum(
        jnp.where(owner == h, stacked[h * size : (h + 1) * size], 0.0) for h in range(heads)
    )


def masked(scores, block, start, order_q, heads):
    size = order_q.shape[0]
    order_k = block * size + lax.broadcasted_iota(jnp.int32, (size, size), 1)
    allowed = (order_k >= start) & (order_k <= order_q)
    split = scores.reshape(heads, size, size)
    return jnp.where(allowed[None], split, NEGATIVE).reshape(scores.shape)


def attend_kernel(heads, low_ref, place_ref, offset_ref, q_ref, k_ref, v_ref, out_ref, log_ref, held):
    row = pl.program_id(0)
    place = place_ref[0]
    queries = q_ref[0]
    size = queries.shape[0]
    stacked = per_head(queries, turned_head(queries.shape, 1, heads), heads, 0)
    order_q = place * size + lax.broadcasted_iota(jnp.int32, (size, 1), 0)
    start = order_q - offset_ref[0]

    def score(block, highest):
        scores = multiply(stacked, spread_keys(k_ref[block, 0], heads))
        scores = masked(scores, block, start, order_q, heads)
        held[block] = scores
        return jnp.maximum(highest, jnp.max(scores, axis=1, keepdims=True))

    highest = lax.fori_loop(
        low_ref[row], place + 1, score, jnp.full((heads * size, 1), NEGATIVE, jnp.float32)
    )

    def mix(block, carry):
        total, context = carry
        powers = jnp.exp(held[block] - highest)
        total = total + jnp.sum(powers, axis=1, keepdims=True)
        spread = jnp.concatenate([v_ref[block, 0]] * heads, axis=0)
        return total, context + contract_last(powers.astype(jnp.bfloat16), spread)

    total, context = lax.fori_loop(
        low_ref[row],
        place + 1,
        mix,
        (
            jnp.zeros((heads * size, 1), jnp.float32),
            jnp.zeros((heads * size, queries.shape[1]), jnp.float32),
        ),
    )
    owner = plain_head(queries.shape, 1, heads)
    out_ref[0] = join_heads(context / total, owner, heads).astype(jnp.bfloat16)
    log_ref[0] = highest + jnp.log(total)


def attend_back_kernel(
    heads,
    low_ref,
    place_ref,
    offset_ref,
    q_ref,
    k_ref,
    v_ref,
    context_ref,
    log_ref,
    grad_ref,
    cosine_ref,
    sine_ref,
    grad_q_ref,
    grad_k_ref,
    grad_v_ref,
):
    row = pl.program_id(0)
    place = place_ref[0]
    queries = q_ref[0]
    grads = grad_ref[0]
    size = queries.shape[0]
    turned = turned_head(queries.shape, 1, heads)
    plain = plain_head(queries.shape, 1, heads)
    stacked = per_head(queries, turned, heads, 0)
    stacked_grad = per_head(grads, plain, heads, 0)
    flipped = per_head(queries.T, turned_head(queries.shape, 0, heads), heads, 1)
    flipped_grad = per_head(grads.T, plain_head(queries.shape, 0, heads), heads, 1)
    product = grads.astype(jnp.float32) * context_ref[0].astype(jnp.float32)
    inner = jnp.sum(per_head(product, plain, heads, 0), axis=1, keepdims=True)
    logs = log_ref[0]
    order_q = place * size + lax.broadcasted_iota(jnp.int32, (size, 1), 0)
    start = order_q - offset_ref[0]
    grad_k_ref[...] = jnp.zeros_like(grad_k_ref)
    grad_v_ref[...] = jnp.zeros_like(grad_v_ref)

    def step(block, grad_q):
        keys = spread_keys(k_ref[block, 0], heads)
        spread = jnp.concatenate([v_ref[block, 0]] * heads, axis=0)
        scores = masked(multiply(stacked, keys), block, start, order_q, heads)
        probs = jnp.exp(scores - logs)
        grad_probs = multiply(stacked_grad, spread)
        grad_scores = (probs * (grad_probs - inner)).astype(jnp.bfloat16)
        grad_k = fold_keys(multiply(flipped, grad_scores), heads)
        grad_v = fold_values(multiply(flipped_grad, probs.astype(jnp.bfloat16)), heads)
        grad_k_ref[block, 0] = grad_k.astype(jnp.bfloat16)
        grad_v_ref[block, 0] = grad_v.astype(jnp.bfloat16)
        return grad_q + contract_last(grad_scores, keys)

    grad_q = lax.fori_loop(
        low_ref[row],
        place + 1,
        step,
        jnp.zeros((heads * size, queries.shape[1]), jnp.float32),
    )
    grad_q = join_heads(grad_q, turned, heads) * HD ** (-0.5)
    half = grad_q.shape[1] // 2
    first, second = grad_q[:, :half], grad_q[:, half:]
    cosine, sine = cosine_ref[0], sine_ref[0]
    grad_q_ref[0, :, :half] = (first * cosine + second * sine).astype(jnp.bfloat16)
    grad_q_ref[0, :, half:] = (second * cosine - first * sine).astype(jnp.bfloat16)


def row_spec(*shape):
    return pl.BlockSpec((1,) + shape, lambda row, low, place: (row,) + (0,) * len(shape))


def line_spec(depth, *shape):
    return pl.BlockSpec((depth, 1) + shape, lambda row, low, place: (0, row) + (0,) * len(shape))


def attend(low, place, offsets, queries, keys, values):
    rows, size, width = queries.shape
    depth, features = keys.shape[0], keys.shape[2]
    heads = width // features
    line = line_spec(depth, features, size)
    return pl.pallas_call(
        functools.partial(attend_kernel, heads),
        out_shape=(
            jax.ShapeDtypeStruct((rows, size, width), jnp.bfloat16),
            jax.ShapeDtypeStruct((rows, heads * size, 1), jnp.float32),
        ),
        grid_spec=pltpu.PrefetchScalarGridSpec(
            num_scalar_prefetch=2,
            grid=(rows,),
            in_specs=[row_spec(size, 1), row_spec(size, width), line, line],
            out_specs=[row_spec(size, width), row_spec(heads * size, 1)],
            scratch_shapes=[pltpu.VMEM((depth, heads * size, size), jnp.float32)],
        ),
        compiler_params=pltpu.CompilerParams(vmem_limit_bytes=VMEM_LIMIT),
        name="attend",
    )(low, place, offsets, queries, keys, values)


def attend_back(low, place, offsets, queries, keys, values, context, logs, grads, cosine, sine):
    rows, size, width = queries.shape
    depth, features = keys.shape[0], keys.shape[2]
    heads = width // features
    line = line_spec(depth, features, size)
    whole = row_spec(size, width)
    half = row_spec(size, width // 2)
    return pl.pallas_call(
        functools.partial(attend_back_kernel, heads),
        out_shape=(
            jax.ShapeDtypeStruct((rows, size, width), jnp.bfloat16),
            jax.ShapeDtypeStruct(keys.shape, jnp.bfloat16),
            jax.ShapeDtypeStruct(keys.shape, jnp.bfloat16),
        ),
        grid_spec=pltpu.PrefetchScalarGridSpec(
            num_scalar_prefetch=2,
            grid=(rows,),
            in_specs=[
                row_spec(size, 1),
                whole,
                line,
                line,
                whole,
                row_spec(heads * size, 1),
                whole,
                half,
                half,
            ],
            out_specs=[whole, line, line],
        ),
        compiler_params=pltpu.CompilerParams(vmem_limit_bytes=VMEM_LIMIT),
        name="attend_back",
    )(low, place, offsets, queries, keys, values, context, logs, grads, cosine, sine)


def mlp_kernel(
    dp,
    depth,
    x_hbm,
    cot_hbm,
    wide_hbm,
    down_hbm,
    grad_ref,
    part_hbm,
    wide_grad_hbm,
    down_grad_hbm,
    tokens,
    cots,
    gates,
    ups,
    downs,
    hidden_t,
    gate_t,
    up_t,
    held,
    side_send,
    side_got,
    far_got,
    part_out,
    tile_out,
    load_sem,
    near_send_sem,
    near_got_sem,
    side_send_sem,
    side_got_sem,
    pass_send_sem,
    pass_got_sem,
    sum_send_sem,
    sum_got_sem,
    far_send_sem,
    far_got_sem,
    part_sem,
    tile_sem,
):
    f32, bf16 = jnp.float32, jnp.bfloat16
    data = lax.axis_index("dp")
    place = lax.axis_index("z")
    core = lax.axis_index("core")
    size = x_hbm.shape[0]
    half = size // 2
    width = x_hbm.shape[1]

    def peer(k):
        high = lax.rem(data // 2 + k // 2, 2)
        low = lax.rem(lax.rem(data, 2) + lax.rem(k, 2), 2)
        return (high * 2 + low, place, core)

    twin = (data, place, 1 - core)

    loads = [pltpu.make_async_copy(x_hbm, tokens.at[0, core], load_sem.at[0])]
    for z in range(depth):
        loads.append(
            pltpu.make_async_copy(wide_hbm.at[z, :, :, 0], gates.at[:, z], load_sem.at[1 + 2 * z])
        )
        loads.append(
            pltpu.make_async_copy(wide_hbm.at[z, :, :, 1], ups.at[:, z], load_sem.at[2 + 2 * z])
        )
    loads.append(pltpu.make_async_copy(down_hbm, downs, load_sem.at[2 * depth + 1]))
    loads.append(pltpu.make_async_copy(cot_hbm, cots, load_sem.at[2 * depth + 2]))
    for load in loads:
        load.start()

    barrier = pltpu.get_barrier_semaphore()
    for target in [peer(k) for k in range(1, dp)] + [twin]:
        pl.semaphore_signal(barrier, inc=1, device_id=target, device_id_type=MESH)
    pl.semaphore_wait(barrier, dp)
    loads[0].wait()

    def near_copy(k):
        return pltpu.make_async_remote_copy(
            src_ref=tokens.at[0, core],
            dst_ref=tokens.at[k, core],
            send_sem=near_send_sem.at[k],
            recv_sem=near_got_sem.at[k],
            device_id=peer(k),
            device_id_type=MESH,
        )

    def pass_copy(part):
        return pltpu.make_async_remote_copy(
            src_ref=tokens.at[1 + part, core, pl.ds(part * half, half)],
            dst_ref=tokens.at[3, core, pl.ds(part * half, half)],
            send_sem=pass_send_sem.at[part],
            recv_sem=pass_got_sem.at[part],
            device_id=peer(2 - part),
            device_id_type=MESH,
        )

    def side_copy(k):
        return pltpu.make_async_remote_copy(
            src_ref=tokens.at[k, core],
            dst_ref=tokens.at[k, core],
            send_sem=side_send_sem.at[k],
            recv_sem=side_got_sem.at[k],
            device_id=twin,
            device_id_type=MESH,
        )

    def side_arrival(k):
        return pltpu.make_async_remote_copy(
            src_ref=tokens.at[k, 1 - core],
            dst_ref=tokens.at[k, 1 - core],
            send_sem=side_send_sem.at[k],
            recv_sem=side_got_sem.at[k],
            device_id=twin,
            device_id_type=MESH,
        )

    def sum_copy(k):
        return pltpu.make_async_remote_copy(
            src_ref=side_send.at[lax.rem(k, 2)],
            dst_ref=side_got.at[k],
            send_sem=sum_send_sem.at[lax.rem(k, 2)],
            recv_sem=sum_got_sem.at[k],
            device_id=twin,
            device_id_type=MESH,
        )

    def far_copy(k):
        return pltpu.make_async_remote_copy(
            src_ref=side_got.at[k],
            dst_ref=far_got.at[k],
            send_sem=far_send_sem.at[k],
            recv_sem=far_got_sem.at[k],
            device_id=peer(k),
            device_id_type=MESH,
        )

    def part_copy(k, e, slot):
        return pltpu.make_async_copy(part_out.at[slot], part_hbm.at[k, e], part_sem.at[slot])

    near_copy(1).start()
    near_copy(2).start()
    side_copy(0).start()
    for load in loads[1:]:
        load.wait()

    def process(k, e, slot):
        row = tokens[k, e]
        gate = multiply(row, gates[...].reshape(width, -1))
        up = multiply(row, ups[...].reshape(width, -1))
        sigma = 1.0 / (1.0 + jnp.exp(-gate))
        active = gate * sigma
        hidden = (active * up).astype(bf16)
        grad_hid = contract_last(cots[k, e], downs[...])
        grad_gate = (grad_hid * up * sigma * (1.0 + gate * (1.0 - sigma))).astype(bf16)
        grad_up = (grad_hid * active).astype(bf16)
        spot = pl.ds(pl.multiple_of((k * 2 + e) * size, size), size)
        hidden_t[:, spot] = hidden.T
        gate_t[:, spot] = grad_gate.T
        up_t[:, spot] = grad_up.T

        @pl.when(k > 0)
        def _():
            part_copy(k, e, slot).wait()

        part_out[slot] = multiply(hidden, downs[...]).astype(bf16)
        part_copy(k, e, slot).start()
        return contract_last(grad_gate, gates[...].reshape(width, -1)) + contract_last(
            grad_up, ups[...].reshape(width, -1)
        )

    def finish(k):
        sum_copy(k).wait_recv()
        total = held[lax.rem(k, 2)] + side_got[k].astype(f32)

        @pl.when(k == 0)
        def _():
            grad_ref[...] = total

        @pl.when(k > 0)
        def _():
            side_got[k] = total.astype(bf16)
            far_copy(k).start()

    def step(k, carry):
        @pl.when(k == 1)
        def _():
            near_copy(1).wait_recv()
            pass_copy(0).start()
            side_copy(1).start()
            near_copy(2).wait_recv()
            pass_copy(1).start()
            side_copy(2).start()

        @pl.when(k == 3)
        def _():
            pass_copy(0).wait_recv()
            pass_copy(1).wait_recv()
            side_copy(3).start()

        held[lax.rem(k, 2)] = process(k, core, 0)

        @pl.when(k > 0)
        def _():
            finish(k - 1)

        side_arrival(k).wait_recv()
        other = process(k, 1 - core, 1)

        @pl.when(k > 1)
        def _():
            sum_copy(k - 2).wait_send()

        side_send[lax.rem(k, 2)] = other.astype(bf16)
        sum_copy(k).start()
        return carry

    lax.fori_loop(0, dp, step, 0)
    finish(dp - 1)

    block = 256
    count = width // block

    def tile_copies(which, j, slot):
        if which == 2:
            spot = pl.ds(pl.multiple_of(j * block, block), block)
            return [
                pltpu.make_async_copy(
                    tile_out.at[slot], down_grad_hbm.at[:, spot], tile_sem.at[slot, 0]
                )
            ]
        per = depth * 128 // block
        return [
            pltpu.make_async_copy(
                tile_out.at[slot, :, pl.ds(i * 128, 128)],
                wide_grad_hbm.at[lax.rem(j, per) * (block // 128) + i, which, j // per],
                tile_sem.at[slot, i],
            )
            for i in range(block // 128)
        ]

    for which, left, right in ((2, hidden_t, cots), (0, gate_t, tokens), (1, up_t, tokens)):

        def tile(j, carry, which=which, left=left, right=right):
            slot = lax.rem(j, 2)

            @pl.when(j > 1)
            def _():
                for copy in tile_copies(which, j - 2, slot):
                    copy.wait()

            spot = pl.ds(pl.multiple_of(j * block, block), block)
            columns = right[:, :, :, spot].reshape(-1, block)
            tile_out[slot] = multiply(left[...], columns).astype(bf16)
            for copy in tile_copies(which, j, slot):
                copy.start()
            return carry

        lax.fori_loop(0, count, tile, 0)
        for j in (count - 2, count - 1):
            for copy in tile_copies(which, j, j % 2):
                copy.wait()

    for k in range(1, dp):
        far_copy(k).wait_recv()
        grad_ref[...] += far_got[k].astype(f32)
    for k in range(1, 3):
        near_copy(k).wait_send()
    for k in range(2):
        pass_copy(k).wait_send()
        sum_copy(dp - 2 + k).wait_send()
        part_copy(dp - 1, core, 0).wait() if k == 0 else part_copy(dp - 1, 1 - core, 1).wait()
    for k in range(dp):
        side_copy(k).wait_send()
    for k in range(1, dp):
        far_copy(k).wait_send()


def mlp(x_own, cot_all, wide, down):
    depth, dp = wide.shape[:2]
    size, width = x_own.shape
    inner = wide.shape[-1]
    f32, bf16 = jnp.float32, jnp.bfloat16
    hbm = pl.BlockSpec(memory_space=pl.ANY)
    dma = pltpu.SemaphoreType.DMA
    weight = pltpu.VMEM((dp, depth) + wide.shape[2:3] + wide.shape[4:], bf16)
    turned = pltpu.VMEM((inner, 2 * dp * size), bf16)
    flops = 2 * 2 * dp * size * width * inner * 9
    return pl.pallas_call(
        functools.partial(mlp_kernel, dp, depth),
        out_shape=(
            jax.ShapeDtypeStruct((size, width), f32),
            jax.ShapeDtypeStruct((dp, 2, size, width), bf16),
            jax.ShapeDtypeStruct((depth, 2, dp, inner, width // (depth * dp)), bf16),
            jax.ShapeDtypeStruct((inner, width), bf16),
        ),
        in_specs=[hbm] * 4,
        out_specs=(pl.BlockSpec(memory_space=pltpu.VMEM), hbm, hbm, hbm),
        scratch_shapes=[
            pltpu.VMEM((dp, 2, size, width), bf16),
            pltpu.VMEM((dp, 2, size, width), bf16),
            weight,
            weight,
            pltpu.VMEM((inner, width), bf16),
            turned,
            turned,
            turned,
            pltpu.VMEM((2, size, width), f32),
            pltpu.VMEM((2, size, width), bf16),
            pltpu.VMEM((dp, size, width), bf16),
            pltpu.VMEM((dp, size, width), bf16),
            pltpu.VMEM((2, size, width), bf16),
            pltpu.VMEM((2, inner, 256), bf16),
            dma((2 * depth + 3,)),
            dma((dp,)),
            dma((dp,)),
            dma((dp,)),
            dma((dp,)),
            dma((2,)),
            dma((2,)),
            dma((2,)),
            dma((dp,)),
            dma((dp,)),
            dma((dp,)),
            dma((2,)),
            dma((2, 2)),
        ],
        compiler_params=pltpu.CompilerParams(
            collective_id=1, has_side_effects=True, vmem_limit_bytes=62 * 1024 * 1024
        ),
        cost_estimate=pl.CostEstimate(flops=flops, bytes_accessed=0, transcendentals=0),
        name="mlp",
    )(x_own, cot_all, wide, down)


def split_layer(dp, depth):
    def layer(
        hidden_in,
        segment_ids,
        positions,
        attn_gain,
        query_weight,
        key_weight,
        value_weight,
        out_weight,
        mlp_gain,
        gate_weight,
        up_weight,
        down_weight,
        cotangent,
    ):
        f32, bf16 = jnp.float32, jnp.bfloat16
        rows, length, width = hidden_in.shape
        own = rows * length
        team = 2 * dp
        tokens = team * own
        part = query_weight.shape[0]
        hidden_rows = down_weight.shape[0]
        inner = depth * hidden_rows
        heads = depth
        row_count, size = dp * rows, 2 * length
        core = lax.axis_index("core")
        place = lax.axis_index("z")

        def dot(left, right):
            return jnp.dot(left, right, preferred_element_type=f32)

        def by_owner(columns, count):
            split = columns.reshape(part, dp, depth, 2, count)
            return split.transpose(1, 3, 0, 2, 4).reshape(team, part, depth * count)

        kv_pair = jnp.stack(
            [key_weight.reshape(part, dp, HD), value_weight.reshape(part, dp, HD)], axis=1
        )
        kv_blocks = kv_pair.transpose(2, 1, 0, 3).reshape(team, part, HD)
        query_blocks = query_weight.reshape(part, dp, depth, 2, 2, HD // 2)
        query_blocks = query_blocks.transpose(1, 3, 0, 4, 2, 5).reshape(team, part, heads * HD)
        attn_blocks = jnp.concatenate([query_blocks, kv_blocks], axis=-1)
        gains = jnp.stack([attn_gain, mlp_gain])
        gain_rows = jnp.pad(gains, ((0, 6), (0, attn_blocks.shape[-1] - part)))
        attn_blocks = jnp.concatenate(
            [attn_blocks, jnp.broadcast_to(gain_rows, (team,) + gain_rows.shape)], axis=1
        )
        attn_got = lax.all_gather(exchange(attn_blocks), "z", axis=0)
        attn_got = attn_got.reshape(depth, dp, 2, part + 8, -1).transpose(1, 0, 2, 3, 4)
        weight_q = attn_got[:, :, :, :part, : heads * HD].reshape(width, heads * HD)
        weight_pair = attn_got[:, :, :, :part, heads * HD :].reshape(width, HD)
        gain_one = attn_got[:, :, :, part, :part].reshape(width)
        gain_two = attn_got[:, :, :, part + 1, :part].reshape(width)
        weight_out = lax.all_gather(out_weight, "z", axis=0, tiled=True)
        wide = jnp.stack(
            [by_owner(gate_weight, hidden_rows), by_owner(up_weight, hidden_rows)], axis=1
        )
        wide_got = lax.all_gather(exchange(wide), "z", axis=0)
        wide_got = wide_got.reshape(depth, dp, 2, 2, part, inner)
        weight_down = lax.all_gather(down_weight, "z", axis=0, tiled=True)

        x_own = hidden_in.reshape(own, width)
        cot_own = cotangent.reshape(own, width)
        x_all = plane_gather(hidden_in, dp, core).reshape(tokens, width)
        offsets = plane_gather(positions, dp, core).reshape(row_count, size)

        x_f32 = x_all.astype(f32)
        factor1 = lax.rsqrt(jnp.mean(x_f32 * x_f32, axis=-1, keepdims=True) + EPSILON)
        normed1 = (x_f32 * factor1 * gain_one.astype(f32)).astype(bf16)
        freqs = 10000.0 ** (-jnp.arange(0, HD // 2, dtype=f32) * 2.0 / HD)
        offsets_f32 = offsets.astype(f32)
        angles = offsets_f32[:, :, None] * jnp.tile(freqs, heads)
        cosine, sine = jnp.cos(angles), jnp.sin(angles)
        angles_pair = jnp.where(core == 0, offsets_f32[:, None, :] * freqs[:, None], 0.0)
        cosine_pair, sine_pair = jnp.cos(angles_pair), jnp.sin(angles_pair)
        queries = dot(normed1, weight_q).reshape(row_count, size, heads * HD)
        first, second = queries[..., : heads * HD // 2], queries[..., heads * HD // 2 :]
        queries = jnp.concatenate(
            [first * cosine - second * sine, second * cosine + first * sine], axis=-1
        ).astype(bf16)
        queries = queries * jnp.bfloat16(HD ** (-0.5))
        pair = jnp.einsum(
            "wf,rsw->rfs", weight_pair, normed1.reshape(row_count, size, width),
            preferred_element_type=f32,
        )
        first, second = pair[:, : HD // 2], pair[:, HD // 2 :]
        pair = jnp.concatenate(
            [
                first * cosine_pair - second * sine_pair,
                second * cosine_pair + first * sine_pair,
            ],
            axis=1,
        ).astype(bf16)
        line_one = lax.all_gather(pair, "z", axis=0)
        line_two = swap(line_one, "core", 2, 1)
        keys = jnp.where(core == 0, line_one, line_two)
        values = jnp.where(core == 0, line_two, line_one)
        low_block = (place * size - offsets[:, 0]) // size
        low_block = jnp.maximum(low_block, 0).astype(jnp.int32)
        place_one = place.astype(jnp.int32).reshape(1)
        context, logs = attend(
            low_block, place_one, offsets[:, :, None], queries, keys, values
        )
        context_flat = context.reshape(tokens, heads * HD)

        def scatter(terms):
            split = terms.reshape(dp, rows, 2, length, width)
            return plane_scatter(split, dp, core).reshape(own, width)

        def gather(array):
            return plane_gather(array.reshape(rows, length, width), dp, core).reshape(tokens, width)

        attn_out = scatter(dot(context_flat, weight_out))
        middle = x_own.astype(f32) + attn_out

        normed2, factor2 = norm_forward(middle, gain_two)
        cot_all = plane_gather(cotangent, dp, core)
        cot_all = cot_all.transpose(0, 2, 1, 3, 4).reshape(dp, 2, own, width)
        grad_normed2, mlp_parts, grad_wide, grad_down = mlp(
            normed2.astype(bf16), cot_all, wide_got, weight_down
        )
        mlp_parts = mlp_parts.reshape(dp, 2, rows, length, width).transpose(0, 2, 1, 3, 4)
        mlp_out = plane_scatter(mlp_parts.astype(f32), dp, core).reshape(own, width)
        out_hidden = (middle + mlp_out).astype(bf16)

        def line_sum(array):
            return lax.psum_scatter(array.astype(bf16), "z", scatter_dimension=0, tiled=True)

        def owner_rows(array, count):
            lead = array.shape[0]
            split = array.reshape(lead, dp, depth, 2, part, count).transpose(2, 1, 3, 0, 4, 5)
            summed = line_sum(split.reshape(depth * team, lead, part, count))
            return exchange(summed)

        def from_owner(blocks, count):
            split = blocks.reshape(dp, 2, part, depth, count).transpose(2, 0, 3, 1, 4)
            return split.reshape(part, dp * depth * 2 * count).astype(f32)

        grad_down = line_sum(grad_down).astype(f32)
        wide_sum = line_sum(grad_wide)[0]

        inner2 = grad_normed2 * gain_two.astype(f32)
        grad_middle = (
            cot_own.astype(f32)
            + factor2 * inner2
            - factor2 * factor2 * factor2 * middle * jnp.mean(inner2 * middle, axis=-1, keepdims=True)
        )
        grad_attn = gather(grad_middle.astype(bf16))
        grad_wout = line_sum(dot(context_flat.T, grad_attn)).astype(f32)
        grad_context = dot(grad_attn, weight_out.T).astype(bf16)
        grad_queries, grad_keys, grad_values = attend_back(
            low_block,
            place_one,
            offsets[:, :, None],
            queries,
            keys,
            values,
            context,
            logs,
            grad_context.reshape(row_count, size, heads * HD),
            cosine,
            sine,
        )
        kept = jnp.where(core == 0, grad_keys, grad_values)
        given = jnp.where(core == 0, grad_values, grad_keys)
        kept, given, wide_sum = lax.optimization_barrier((kept, given, wide_sum))
        wide_back = wide_sum.reshape(2, dp, inner, 2, part)
        wide_back = exchange(wide_back.transpose(1, 3, 0, 4, 2).reshape(team, 2, part, inner))
        grad_wgate = from_owner(wide_back[:, 0], hidden_rows)
        grad_wup = from_owner(wide_back[:, 1], hidden_rows)
        kept = kept.astype(f32) + swap(given, "core", 2, 1).astype(f32)
        grad_pair = line_sum(kept)[0].astype(f32)
        first, second = grad_pair[:, : HD // 2], grad_pair[:, HD // 2 :]
        grad_pair = jnp.concatenate(
            [
                first * cosine_pair + second * sine_pair,
                second * cosine_pair - first * sine_pair,
            ],
            axis=1,
        ).astype(bf16)
        grad_queries = grad_queries.reshape(tokens, heads * HD)
        grad_pair = grad_pair.transpose(0, 2, 1).reshape(tokens, HD)
        grad_normed1 = dot(grad_queries, weight_q.T) + dot(grad_pair, weight_pair.T)
        grad_normed1 = scatter(grad_normed1)
        grad_wattn = jnp.concatenate(
            [dot(normed1.T, grad_queries), dot(normed1.T, grad_pair)], axis=-1
        )
        attn_back = owner_rows(grad_wattn[None], (heads + 1) * HD)[:, 0]
        grad_wquery = attn_back[:, :, : heads * HD].reshape(dp, 2, part, 2, depth, HD // 2)
        grad_wquery = grad_wquery.transpose(2, 0, 4, 1, 3, 5).reshape(part, -1).astype(f32)
        pair_back = attn_back[:, :, heads * HD :].reshape(dp, 2, part, HD).transpose(1, 2, 0, 3)
        grad_wkey = pair_back[0].reshape(part, dp * HD).astype(f32)
        grad_wvalue = pair_back[1].reshape(part, dp * HD).astype(f32)

        own_f32 = x_own.astype(f32)
        factor = lax.rsqrt(jnp.mean(own_f32 * own_f32, axis=-1, keepdims=True) + EPSILON)
        inner1 = grad_normed1 * gain_one.astype(f32)
        grad_in = (
            grad_middle
            + factor * inner1
            - factor * factor * factor * own_f32 * jnp.mean(inner1 * own_f32, axis=-1, keepdims=True)
        )

        def rows_of(weight, grad):
            return jnp.sum(weight.astype(f32) * grad, axis=-1)

        grad_gain_one = (
            rows_of(query_weight, grad_wquery)
            + rows_of(key_weight, grad_wkey)
            + rows_of(value_weight, grad_wvalue)
        ) / attn_gain.astype(f32)
        grad_gain_two = (
            rows_of(gate_weight, grad_wgate) + rows_of(up_weight, grad_wup)
        ) / mlp_gain.astype(f32)
        return (
            out_hidden.reshape(rows, length, width),
            grad_in.reshape(rows, length, width),
            grad_gain_one,
            grad_wquery,
            grad_wkey,
            grad_wvalue,
            grad_wout,
            grad_gain_two,
            grad_wgate,
            grad_wup,
            grad_down,
        )

    return layer


def solution(mesh):
    dp, seq = mesh.shape["dp"], mesh.shape["seq"]
    if dp != KVH or seq % 2 or HQ != dp * seq:
        return gathered_weights(mesh)
    depth = seq // 2
    mesh = Mesh(mesh.devices.reshape(dp, depth, 2), ("dp", "z", "core"))
    every = ("dp", "z", "core")
    tokens = P("dp", ("z", "core"), None)
    matrix = P(every, None)
    return jax.shard_map(
        split_layer(dp, depth),
        mesh=mesh,
        in_specs=(
            tokens,
            P("dp", ("z", "core")),
            P("dp", ("z", "core")),
            P(every),
            matrix,
            matrix,
            matrix,
            matrix,
            P(every),
            matrix,
            matrix,
            matrix,
            tokens,
        ),
        out_specs=(
            tokens,
            tokens,
            P(every),
            matrix,
            matrix,
            matrix,
            matrix,
            P(every),
            matrix,
            matrix,
            matrix,
        ),
        check_vma=False,
    )
```

```python
import functools

import jax
import jax.numpy as jnp
from jax import lax
from jax.experimental import pallas as pl
from jax.experimental.pallas import tpu as pltpu
from jax.sharding import Mesh
from jax.sharding import PartitionSpec as P

HQ = 32
HD = 64
KVH = 4


EPSILON = 1e-05


def fetch_attention(attn_gain, query_weight, key_weight, value_weight, out_weight):
    return (
        lax.all_gather(attn_gain, ("dp", "seq"), axis=0, tiled=True),
        lax.all_gather(query_weight, ("dp", "seq"), axis=0, tiled=True),
        lax.all_gather(key_weight, ("dp", "seq"), axis=0, tiled=True),
        lax.all_gather(value_weight, ("dp", "seq"), axis=0, tiled=True),
        lax.all_gather(out_weight, ("dp", "seq"), axis=0, tiled=True),
    )


def fetch_mlp(mlp_gain, gate_weight, up_weight, down_weight):
    return (
        lax.all_gather(mlp_gain, ("dp", "seq"), axis=0, tiled=True),
        lax.all_gather(gate_weight, ("dp", "seq"), axis=0, tiled=True),
        lax.all_gather(up_weight, ("dp", "seq"), axis=0, tiled=True),
        lax.all_gather(down_weight, ("dp", "seq"), axis=0, tiled=True),
    )


def angles_of(positions):
    freqs = 10000.0 ** (-jnp.arange(0, HD // 2, dtype=jnp.float32) * 2.0 / HD)
    return positions.astype(jnp.float32)[:, None] * freqs[None, :]


def rotate(vectors, cosine, sine):
    half = vectors.shape[-1] // 2
    first = vectors[..., :half]
    second = vectors[..., half:]
    cosine = cosine[:, None, :]
    sine = sine[:, None, :]
    return jnp.concatenate(
        [first * cosine - second * sine, second * cosine + first * sine], axis=-1
    )


def norm_forward(values, gain):
    factor = lax.rsqrt(jnp.mean(values * values, axis=-1, keepdims=True) + EPSILON)
    return (values * factor * gain.astype(jnp.float32), factor)


def norm_backward(values, factor, gain, grad_normed):
    inner = grad_normed * gain.astype(jnp.float32)
    grad_gain = jnp.sum(grad_normed * values * factor, axis=0)
    grad_values = factor * inner - factor * factor * factor * values * jnp.mean(
        inner * values, axis=-1, keepdims=True
    )
    return (grad_values, grad_gain)


def masked_scores(queries_rot, keys_heads, query_pos, query_seg, seg_all):
    scores = jnp.einsum(
        "cgjd,kgd->gjck", queries_rot, keys_heads, preferred_element_type=jnp.float32
    ) * HD ** (-0.5)
    key_pos = jnp.arange(keys_heads.shape[0])
    allowed = (key_pos[None, :] <= query_pos[:, None]) & (seg_all[None, :] == query_seg[:, None])
    return jnp.where(allowed, scores, -1e30)


def add_up(total, extra):
    if total is None:
        return extra
    return jax.tree.map(jnp.add, total, extra)


def gathered_weights_layer(
    hidden_in,
    segment_ids,
    positions,
    attn_gain,
    query_weight,
    key_weight,
    value_weight,
    out_weight,
    mlp_gain,
    gate_weight,
    up_weight,
    down_weight,
    cotangent,
):
    batches, local_len, width = hidden_in.shape
    group = HQ // KVH
    query_pos = lax.axis_index("seq") * local_len + jnp.arange(local_len)
    outputs = []
    grads_in = []
    attn_total = None
    mlp_total = None
    for microbatch in range(batches):
        rows_in = hidden_in[microbatch].astype(jnp.float32)
        seg_own = segment_ids[microbatch]
        angles = angles_of(positions[microbatch])
        cosine = jnp.cos(angles)
        sine = jnp.sin(angles)
        attn_set = fetch_attention(attn_gain, query_weight, key_weight, value_weight, out_weight)
        gain_one, weight_query, weight_key, weight_value, weight_out = attn_set
        normed1, factor1 = norm_forward(rows_in, gain_one)
        normed1_low = normed1.astype(jnp.bfloat16)
        queries = jnp.dot(normed1_low, weight_query, preferred_element_type=jnp.float32).reshape(
            local_len, HQ, HD
        )
        keys_own = jnp.dot(normed1_low, weight_key, preferred_element_type=jnp.float32).reshape(
            local_len, KVH, HD
        )
        values_own = jnp.dot(normed1_low, weight_value, preferred_element_type=jnp.float32).astype(
            jnp.bfloat16
        )
        queries_rot = (
            rotate(queries, cosine, sine).astype(jnp.bfloat16).reshape(local_len, KVH, group, HD)
        )
        keys_rot = rotate(keys_own, cosine, sine).astype(jnp.bfloat16).reshape(local_len, KVH * HD)
        keys_all, values_all, seg_all = (
            lax.all_gather(keys_rot, "seq", axis=0, tiled=True),
            lax.all_gather(values_own, "seq", axis=0, tiled=True),
            lax.all_gather(seg_own, "seq", axis=0, tiled=True),
        )
        keys_heads = keys_all.reshape(-1, KVH, HD)
        values_heads = values_all.reshape(-1, KVH, HD)
        scores = masked_scores(queries_rot, keys_heads, query_pos, seg_own, seg_all)
        highest = jnp.max(scores, axis=-1, keepdims=True)
        powers = jnp.exp(scores - highest)
        totals = jnp.sum(powers, axis=-1, keepdims=True)
        logsum = highest + jnp.log(totals)
        probs_low = (powers / totals).astype(jnp.bfloat16)
        context = jnp.einsum(
            "gjck,kgd->cgjd", probs_low, values_heads, preferred_element_type=jnp.float32
        )
        context_low = context.reshape(local_len, HQ * HD).astype(jnp.bfloat16)
        middle = rows_in + jnp.dot(context_low, weight_out, preferred_element_type=jnp.float32)
        mlp_set = fetch_mlp(mlp_gain, gate_weight, up_weight, down_weight)
        gain_two, weight_gate, weight_up, weight_down = mlp_set
        normed2, factor2 = norm_forward(middle, gain_two)
        normed2_low = normed2.astype(jnp.bfloat16)
        gate = jnp.dot(normed2_low, weight_gate, preferred_element_type=jnp.float32)
        up = jnp.dot(normed2_low, weight_up, preferred_element_type=jnp.float32)
        sigma = jax.nn.sigmoid(gate)
        activation = gate * sigma
        hidden = (activation * up).astype(jnp.bfloat16)
        mlp_out = jnp.dot(hidden, weight_down, preferred_element_type=jnp.float32)
        outputs.append((middle + mlp_out).astype(jnp.bfloat16))
        grad_low = cotangent[microbatch]
        grad_out = grad_low.astype(jnp.float32)
        mlp_back = fetch_mlp(mlp_gain, gate_weight, up_weight, down_weight)
        gain_two, weight_gate, weight_up, weight_down = mlp_back
        grad_down = jnp.dot(hidden.T, grad_low, preferred_element_type=jnp.float32)
        grad_hid = jnp.dot(grad_low, weight_down.T, preferred_element_type=jnp.float32)
        grad_gate = (grad_hid * up * sigma * (1.0 + gate * (1.0 - sigma))).astype(jnp.bfloat16)
        grad_up = (grad_hid * activation).astype(jnp.bfloat16)
        grad_wgate = jnp.dot(normed2_low.T, grad_gate, preferred_element_type=jnp.float32)
        grad_wup = jnp.dot(normed2_low.T, grad_up, preferred_element_type=jnp.float32)
        grad_normed2 = jnp.dot(
            grad_gate, weight_gate.T, preferred_element_type=jnp.float32
        ) + jnp.dot(grad_up, weight_up.T, preferred_element_type=jnp.float32)
        grad_mid_norm, grad_gain_two = norm_backward(middle, factor2, gain_two, grad_normed2)
        grad_middle = grad_out + grad_mid_norm
        attn_back = fetch_attention(attn_gain, query_weight, key_weight, value_weight, out_weight)
        gain_one, weight_query, weight_key, weight_value, weight_out = attn_back
        grad_attn = grad_middle.astype(jnp.bfloat16)
        grad_wout = jnp.dot(context_low.T, grad_attn, preferred_element_type=jnp.float32)
        grad_context = (
            jnp.dot(grad_attn, weight_out.T, preferred_element_type=jnp.float32)
            .astype(jnp.bfloat16)
            .reshape(local_len, KVH, group, HD)
        )
        probs = jnp.exp(
            masked_scores(queries_rot, keys_heads, query_pos, seg_own, seg_all) - logsum
        )
        grad_probs = jnp.einsum(
            "cgjd,kgd->gjck", grad_context, values_heads, preferred_element_type=jnp.float32
        )
        inner = jnp.sum(probs * grad_probs, axis=-1, keepdims=True)
        grad_scores = (probs * (grad_probs - inner)).astype(jnp.bfloat16)
        grad_qrot = jnp.einsum(
            "gjck,kgd->cgjd", grad_scores, keys_heads, preferred_element_type=jnp.float32
        ) * HD ** (-0.5)
        grad_krot_all = jnp.einsum(
            "gjck,cgjd->kgd", grad_scores, queries_rot, preferred_element_type=jnp.float32
        ) * HD ** (-0.5)
        grad_vall = jnp.einsum(
            "gjck,cgjd->kgd", probs_low, grad_context, preferred_element_type=jnp.float32
        )
        row_len = keys_heads.shape[0]
        grad_key_own, grad_value_own = (
            lax.psum_scatter(
                grad_krot_all.reshape(row_len, KVH * HD).astype(jnp.bfloat16),
                "seq",
                scatter_dimension=0,
                tiled=True,
            ).astype(jnp.float32),
            lax.psum_scatter(
                grad_vall.reshape(row_len, KVH * HD).astype(jnp.bfloat16),
                "seq",
                scatter_dimension=0,
                tiled=True,
            ).astype(jnp.float32),
        )
        grad_keys = (
            rotate(grad_key_own.reshape(local_len, KVH, HD), cosine, -sine)
            .astype(jnp.bfloat16)
            .reshape(local_len, KVH * HD)
        )
        grad_values = grad_value_own.astype(jnp.bfloat16)
        grad_queries = (
            rotate(grad_qrot.reshape(local_len, HQ, HD), cosine, -sine)
            .astype(jnp.bfloat16)
            .reshape(local_len, HQ * HD)
        )
        grad_wquery = jnp.dot(normed1_low.T, grad_queries, preferred_element_type=jnp.float32)
        grad_wkey = jnp.dot(normed1_low.T, grad_keys, preferred_element_type=jnp.float32)
        grad_wvalue = jnp.dot(normed1_low.T, grad_values, preferred_element_type=jnp.float32)
        grad_normed1 = jnp.dot(grad_queries, weight_query.T, preferred_element_type=jnp.float32)
        grad_normed1 = grad_normed1 + jnp.dot(
            grad_keys, weight_key.T, preferred_element_type=jnp.float32
        )
        grad_normed1 = grad_normed1 + jnp.dot(
            grad_values, weight_value.T, preferred_element_type=jnp.float32
        )
        grad_rows_norm, grad_gain_one = norm_backward(rows_in, factor1, gain_one, grad_normed1)
        grads_in.append(grad_middle + grad_rows_norm)
        attn_terms = (grad_gain_one, grad_wquery, grad_wkey, grad_wvalue, grad_wout)
        mlp_terms = (grad_gain_two, grad_wgate, grad_wup, grad_down)
        attn_shares = (
            lax.psum_scatter(attn_terms[0], ("dp", "seq"), scatter_dimension=0, tiled=True),
            lax.psum_scatter(attn_terms[1], ("dp", "seq"), scatter_dimension=0, tiled=True),
            lax.psum_scatter(attn_terms[2], ("dp", "seq"), scatter_dimension=0, tiled=True),
            lax.psum_scatter(attn_terms[3], ("dp", "seq"), scatter_dimension=0, tiled=True),
            lax.psum_scatter(attn_terms[4], ("dp", "seq"), scatter_dimension=0, tiled=True),
        )
        mlp_shares = (
            lax.psum_scatter(mlp_terms[0], ("dp", "seq"), scatter_dimension=0, tiled=True),
            lax.psum_scatter(mlp_terms[1], ("dp", "seq"), scatter_dimension=0, tiled=True),
            lax.psum_scatter(mlp_terms[2], ("dp", "seq"), scatter_dimension=0, tiled=True),
            lax.psum_scatter(mlp_terms[3], ("dp", "seq"), scatter_dimension=0, tiled=True),
        )
        attn_total = add_up(attn_total, attn_shares)
        mlp_total = add_up(mlp_total, mlp_shares)
    return (
        jnp.stack(outputs),
        jnp.stack(grads_in),
        attn_total[0],
        attn_total[1],
        attn_total[2],
        attn_total[3],
        attn_total[4],
        mlp_total[0],
        mlp_total[1],
        mlp_total[2],
        mlp_total[3],
    )


def gathered_weights(mesh):
    return jax.shard_map(
        gathered_weights_layer,
        mesh=mesh,
        in_specs=(
            P("dp", "seq", None),
            P("dp", "seq"),
            P("dp", "seq"),
            P(("dp", "seq")),
            P(("dp", "seq"), None),
            P(("dp", "seq"), None),
            P(("dp", "seq"), None),
            P(("dp", "seq"), None),
            P(("dp", "seq")),
            P(("dp", "seq"), None),
            P(("dp", "seq"), None),
            P(("dp", "seq"), None),
            P("dp", "seq", None),
        ),
        out_specs=(
            P("dp", "seq", None),
            P("dp", "seq", None),
            P(("dp", "seq")),
            P(("dp", "seq"), None),
            P(("dp", "seq"), None),
            P(("dp", "seq"), None),
            P(("dp", "seq"), None),
            P(("dp", "seq")),
            P(("dp", "seq"), None),
            P(("dp", "seq"), None),
            P(("dp", "seq"), None),
        ),
        check_vma=False,
    )


def swap(values, axis_name, size, step):
    return lax.ppermute(values, axis_name, [(i, i ^ step) for i in range(size)])


def plane_pieces(values, dp):
    return [values] + [swap(values, "dp", dp, k) for k in range(1, dp)]


def plane_scatter(terms, dp, core):
    mine = lax.dynamic_index_in_dim(terms, core, 2, keepdims=False)
    other = lax.dynamic_index_in_dim(terms, 1 - core, 2, keepdims=False)
    arrived = swap(other, "core", 2, 1)
    total = mine[0].astype(jnp.float32) + arrived[0].astype(jnp.float32)
    for k in range(1, dp):
        term = mine[k].astype(jnp.float32) + arrived[k].astype(jnp.float32)
        total = total + swap(term.astype(jnp.bfloat16), "dp", dp, k).astype(jnp.float32)
    return total


def exchange(blocks):
    return lax.all_to_all(blocks, ("dp", "core"), split_axis=0, concat_axis=0, tiled=True)


NEGATIVE = -1e30
VMEM_LIMIT = 56 * 1024 * 1024
MESH = pl.DeviceIdType.MESH
LIGHT = pl.CostEstimate(flops=0, bytes_accessed=1024, transcendentals=0)


def contract_last(left, right):
    return lax.dot_general(
        left, right, (((1,), (1,)), ((), ())), preferred_element_type=jnp.float32
    )


def multiply(left, right):
    return jnp.dot(left, right, preferred_element_type=jnp.float32)


def spread_keys(block, heads):
    half = block.shape[0] // 2
    return jnp.concatenate([block[:half]] * heads + [block[half:]] * heads, axis=0)


def fold_keys(block, heads):
    half = block.shape[0] // (2 * heads)
    first = sum(block[h * half : (h + 1) * half] for h in range(heads))
    rest = range(heads, 2 * heads)
    return jnp.concatenate([first, sum(block[h * half : (h + 1) * half] for h in rest)], axis=0)


def fold_values(block, heads):
    size = block.shape[0] // heads
    return sum(block[h * size : (h + 1) * size] for h in range(heads))


def turned_head(shape, dim, heads):
    index = lax.broadcasted_iota(jnp.int32, shape, dim)
    return lax.rem(index, shape[dim] // 2) // (shape[dim] // 2 // heads)


def plain_head(shape, dim, heads):
    index = lax.broadcasted_iota(jnp.int32, shape, dim)
    return index // (shape[dim] // heads)


def per_head(values, owner, heads, axis):
    zero = jnp.zeros_like(values)
    return jnp.concatenate([jnp.where(owner == h, values, zero) for h in range(heads)], axis=axis)


def join_heads(stacked, owner, heads):
    size = stacked.shape[0] // heads
    return sum(
        jnp.where(owner == h, stacked[h * size : (h + 1) * size], 0.0) for h in range(heads)
    )


def masked(scores, block, start, order_q, heads):
    size = order_q.shape[0]
    order_k = block * size + lax.broadcasted_iota(jnp.int32, (size, size), 1)
    allowed = (order_k >= start) & (order_k <= order_q)
    split = scores.reshape(heads, size, size)
    return jnp.where(allowed[None], split, NEGATIVE).reshape(scores.shape)


def attend_kernel(heads, low_ref, place_ref, offset_ref, q_ref, k_ref, v_ref, out_ref, log_ref, held):
    row = pl.program_id(0)
    place = place_ref[0]
    queries = q_ref[0]
    size = queries.shape[0]
    stacked = per_head(queries, turned_head(queries.shape, 1, heads), heads, 0)
    order_q = place * size + lax.broadcasted_iota(jnp.int32, (size, 1), 0)
    start = order_q - offset_ref[0]

    def score(block, highest):
        scores = multiply(stacked, spread_keys(k_ref[block, 0], heads))
        scores = masked(scores, block, start, order_q, heads)
        held[block] = scores
        return jnp.maximum(highest, jnp.max(scores, axis=1, keepdims=True))

    highest = lax.fori_loop(
        low_ref[row], place + 1, score, jnp.full((heads * size, 1), NEGATIVE, jnp.float32)
    )

    def mix(block, carry):
        total, context = carry
        powers = jnp.exp(held[block] - highest)
        total = total + jnp.sum(powers, axis=1, keepdims=True)
        spread = jnp.concatenate([v_ref[block, 0]] * heads, axis=0)
        return total, context + contract_last(powers.astype(jnp.bfloat16), spread)

    total, context = lax.fori_loop(
        low_ref[row],
        place + 1,
        mix,
        (
            jnp.zeros((heads * size, 1), jnp.float32),
            jnp.zeros((heads * size, queries.shape[1]), jnp.float32),
        ),
    )
    owner = plain_head(queries.shape, 1, heads)
    out_ref[0] = join_heads(context / total, owner, heads).astype(jnp.bfloat16)
    log_ref[0] = highest + jnp.log(total)


def attend_back_kernel(
    heads,
    low_ref,
    place_ref,
    offset_ref,
    q_ref,
    k_ref,
    v_ref,
    context_ref,
    log_ref,
    grad_ref,
    cosine_ref,
    sine_ref,
    grad_q_ref,
    grad_k_ref,
    grad_v_ref,
):
    row = pl.program_id(0)
    place = place_ref[0]
    queries = q_ref[0]
    grads = grad_ref[0]
    size = queries.shape[0]
    turned = turned_head(queries.shape, 1, heads)
    plain = plain_head(queries.shape, 1, heads)
    stacked = per_head(queries, turned, heads, 0)
    stacked_grad = per_head(grads, plain, heads, 0)
    flipped = per_head(queries.T, turned_head(queries.shape, 0, heads), heads, 1)
    flipped_grad = per_head(grads.T, plain_head(queries.shape, 0, heads), heads, 1)
    product = grads.astype(jnp.float32) * context_ref[0].astype(jnp.float32)
    inner = jnp.sum(per_head(product, plain, heads, 0), axis=1, keepdims=True)
    logs = log_ref[0]
    order_q = place * size + lax.broadcasted_iota(jnp.int32, (size, 1), 0)
    start = order_q - offset_ref[0]
    grad_k_ref[...] = jnp.zeros_like(grad_k_ref)
    grad_v_ref[...] = jnp.zeros_like(grad_v_ref)

    def step(block, grad_q):
        keys = spread_keys(k_ref[block, 0], heads)
        spread = jnp.concatenate([v_ref[block, 0]] * heads, axis=0)
        scores = masked(multiply(stacked, keys), block, start, order_q, heads)
        probs = jnp.exp(scores - logs)
        grad_probs = multiply(stacked_grad, spread)
        grad_scores = (probs * (grad_probs - inner)).astype(jnp.bfloat16)
        grad_k = fold_keys(multiply(flipped, grad_scores), heads)
        grad_v = fold_values(multiply(flipped_grad, probs.astype(jnp.bfloat16)), heads)
        grad_k_ref[block, 0] = grad_k.astype(jnp.bfloat16)
        grad_v_ref[block, 0] = grad_v.astype(jnp.bfloat16)
        return grad_q + contract_last(grad_scores, keys)

    grad_q = lax.fori_loop(
        low_ref[row],
        place + 1,
        step,
        jnp.zeros((heads * size, queries.shape[1]), jnp.float32),
    )
    grad_q = join_heads(grad_q, turned, heads) * HD ** (-0.5)
    half = grad_q.shape[1] // 2
    first, second = grad_q[:, :half], grad_q[:, half:]
    cosine, sine = cosine_ref[0], sine_ref[0]
    grad_q_ref[0, :, :half] = (first * cosine + second * sine).astype(jnp.bfloat16)
    grad_q_ref[0, :, half:] = (second * cosine - first * sine).astype(jnp.bfloat16)


def row_spec(*shape):
    return pl.BlockSpec((1,) + shape, lambda row, low, place: (row,) + (0,) * len(shape))


def line_spec(depth, *shape):
    return pl.BlockSpec((depth, 1) + shape, lambda row, low, place: (0, row) + (0,) * len(shape))


def pair_spec(which, depth, *shape):
    return pl.BlockSpec(
        (None, depth, 1) + shape, lambda row, low, place: (which, 0, row) + (0,) * len(shape)
    )


def attend(low, place, offsets, queries, lines):
    rows, size, width = queries.shape
    depth, features = lines.shape[1], lines.shape[3]
    heads = width // features
    return pl.pallas_call(
        functools.partial(attend_kernel, heads),
        out_shape=(
            jax.ShapeDtypeStruct((rows, size, width), jnp.bfloat16),
            jax.ShapeDtypeStruct((rows, heads * size, 1), jnp.float32),
        ),
        grid_spec=pltpu.PrefetchScalarGridSpec(
            num_scalar_prefetch=2,
            grid=(rows,),
            in_specs=[
                row_spec(size, 1),
                row_spec(size, width),
                pair_spec(0, depth, features, size),
                pair_spec(1, depth, features, size),
            ],
            out_specs=[row_spec(size, width), row_spec(heads * size, 1)],
            scratch_shapes=[pltpu.VMEM((depth, heads * size, size), jnp.float32)],
        ),
        compiler_params=pltpu.CompilerParams(vmem_limit_bytes=VMEM_LIMIT),
        cost_estimate=LIGHT,
        name="attend",
    )(low, place, offsets, queries, lines, lines)


def attend_back(low, place, offsets, queries, lines, context, logs, grads, cosine, sine):
    rows, size, width = queries.shape
    depth, features = lines.shape[1], lines.shape[3]
    heads = width // features
    line = line_spec(depth, features, size)
    whole = row_spec(size, width)
    half = row_spec(size, width // 2)
    return pl.pallas_call(
        functools.partial(attend_back_kernel, heads),
        out_shape=(
            jax.ShapeDtypeStruct((rows, size, width), jnp.bfloat16),
            jax.ShapeDtypeStruct(lines.shape[1:], jnp.bfloat16),
            jax.ShapeDtypeStruct(lines.shape[1:], jnp.bfloat16),
        ),
        grid_spec=pltpu.PrefetchScalarGridSpec(
            num_scalar_prefetch=2,
            grid=(rows,),
            in_specs=[
                row_spec(size, 1),
                whole,
                pair_spec(0, depth, features, size),
                pair_spec(1, depth, features, size),
                whole,
                row_spec(heads * size, 1),
                whole,
                half,
                half,
            ],
            out_specs=[whole, line, line],
        ),
        compiler_params=pltpu.CompilerParams(vmem_limit_bytes=VMEM_LIMIT),
        cost_estimate=LIGHT,
        name="attend_back",
    )(low, place, offsets, queries, lines, lines, context, logs, grads, cosine, sine)


def team_places():
    data = lax.axis_index("dp")
    place = lax.axis_index("z")
    core = lax.axis_index("core")

    def peer(k):
        high = lax.rem(data // 2 + k // 2, 2)
        low = lax.rem(lax.rem(data, 2) + lax.rem(k, 2), 2)
        return (high * 2 + low, place, core)

    return data, place, core, peer, (data, place, 1 - core)


def greet(targets):
    barrier = pltpu.get_barrier_semaphore()
    for target in targets:
        pl.semaphore_signal(barrier, inc=1, device_id=target, device_id_type=MESH)
    pl.semaphore_wait(barrier, len(targets))


def send(source, target, send_sem, got_sem, device):
    return pltpu.make_async_remote_copy(
        src_ref=source,
        dst_ref=target,
        send_sem=send_sem,
        recv_sem=got_sem,
        device_id=device,
        device_id_type=MESH,
    )


def sum_scratch(dp, size, width):
    dma = pltpu.SemaphoreType.DMA
    block = pltpu.VMEM((dp, size, width), jnp.bfloat16)
    return [
        block,
        block,
        pltpu.VMEM((2, size // 2, width), jnp.bfloat16),
        pltpu.VMEM((2, size, width), jnp.bfloat16),
        dma((dp,)),
        dma((dp,)),
        dma((2,)),
        dma((2,)),
        dma((2, 2)),
        dma((2, 2)),
    ]


def plane_sum(dp, product, total_ref, scratch):
    side, got, relay, far, side_send, side_got, relay_send, relay_got, far_send, far_got = scratch
    f32, bf16 = jnp.float32, jnp.bfloat16
    _, _, core, peer, twin = team_places()
    size = side.shape[1]
    half = size // 2

    def rows(part):
        return pl.ds(part * half, half)

    def side_copy(k):
        return send(side.at[k], got.at[k], side_send.at[k], side_got.at[k], twin)

    def relay_copy(part):
        return send(
            got.at[3, rows(part)],
            relay.at[part],
            relay_send.at[part],
            relay_got.at[part],
            peer(1 + part),
        )

    def far_copy(which, part):
        return send(
            got.at[1 + which, rows(part)],
            far.at[which, rows(part)],
            far_send.at[which, part],
            far_got.at[which, part],
            peer(1 + which),
        )

    def first(step, carry):
        k = dp - 1 - step
        side[k] = product(k, 1 - core, 0).astype(bf16)
        side_copy(k).start()
        return carry

    lax.fori_loop(0, dp, first, 0)

    def second(step, carry):
        k = dp - 1 - step
        total = product(k, core, 1)
        side_copy(k).wait_recv()
        total = total + got[k].astype(f32)

        @pl.when(k == 0)
        def _():
            total_ref[...] = total

        @pl.when(k > 0)
        def _():
            got[k] = total.astype(bf16)

        @pl.when(k == 3)
        def _():
            relay_copy(0).start()
            relay_copy(1).start()

        @pl.when(k == 2)
        def _():
            far_copy(1, 1).start()

        @pl.when(k == 1)
        def _():
            far_copy(0, 0).start()

        return carry

    lax.fori_loop(0, dp, second, 0)
    for part in range(2):
        which = 1 - part
        relay_copy(part).wait_recv()
        total = got[1 + which, rows(part)].astype(f32) + relay[part].astype(f32)
        got[1 + which, rows(part)] = total.astype(bf16)
        far_copy(which, part).start()

    def complete():
        for which, part in ((0, 0), (1, 1), (0, 1), (1, 0)):
            far_copy(which, part).wait_recv()
            total_ref[rows(part)] += far[which, rows(part)].astype(f32)
        for part in range(2):
            relay_copy(part).wait_send()
            for which in range(2):
                far_copy(which, part).wait_send()
        for k in range(dp):
            side_copy(k).wait_send()

    return complete


def mlp_forward_kernel(dp, depth, x_hbm, wide_hbm, *refs):
    cot_hbms = refs[:dp]
    tokens_hbm, cots_hbm, hidden_hbm, slope_hbm, active_hbm, down_grad_hbm = refs[dp : dp + 6]
    (
        tokens,
        cots,
        gates,
        ups,
        hidden_t,
        chunk,
        tile_out,
        load_sem,
        cots_sem,
        near_send,
        near_got,
        side_send,
        side_got,
        pass_send,
        pass_got,
        tokens_sem,
        chunk_sem,
        tile_sem,
        twin_send,
        twin_got,
    ) = refs[dp + 6 :]
    bf16 = jnp.bfloat16
    _, _, core, peer, twin = team_places()
    size, width = x_hbm.shape
    half = size // 2
    loads = [pltpu.make_async_copy(x_hbm, tokens.at[0, core], load_sem.at[0])]
    for z in range(depth):
        for which, target in ((0, gates), (1, ups)):
            sem = load_sem.at[1 + 2 * z + which]
            loads.append(pltpu.make_async_copy(wide_hbm.at[z, :, :, which], target.at[:, z], sem))
    cot_loads = []
    for k in range(dp):
        sem = load_sem.at[2 * depth + 1 + k]
        cot_loads.append(pltpu.make_async_copy(cot_hbms[k], cots.at[k, core], sem))
    for load in loads + cot_loads:
        load.start()
    greet([peer(k) for k in range(1, 3)] + [twin])
    loads[0].wait()

    def near_copy(k):
        return send(
            tokens.at[0, core], tokens.at[k, core], near_send.at[k], near_got.at[k], peer(k)
        )

    def pass_copy(part):
        spot = pl.ds(part * half, half)
        return send(
            tokens.at[1 + part, core, spot],
            tokens.at[3, core, spot],
            pass_send.at[part],
            pass_got.at[part],
            peer(2 - part),
        )

    def side_copy(k):
        block = tokens.at[k, core]
        return send(block, block, side_send.at[k], side_got.at[k], twin)

    def side_arrival(k):
        block = tokens.at[k, 1 - core]
        return send(block, block, side_send.at[k], side_got.at[k], twin)

    def twin_copy(k):
        block = cots.at[k, core]
        return send(block, block, twin_send.at[k], twin_got.at[k], twin)

    def twin_arrival(k):
        block = cots.at[k, 1 - core]
        return send(block, block, twin_send.at[k], twin_got.at[k], twin)

    def tokens_out(k, e):
        return pltpu.make_async_copy(tokens.at[k, e], tokens_hbm.at[k, e], tokens_sem.at[k, e])

    def chunk_out(k, e, slot):
        return [
            pltpu.make_async_copy(chunk.at[slot, i], target.at[k, e], chunk_sem.at[slot, i])
            for i, target in enumerate((hidden_hbm, slope_hbm, active_hbm))
        ]

    near_copy(1).start()
    near_copy(2).start()
    side_copy(0).start()
    for load in loads[1:]:
        load.wait()

    def process(k, e, slot, reuse):
        row = tokens[k, e]
        tokens_out(k, e).start()
        gate = multiply(row, gates[...].reshape(width, -1))
        up = multiply(row, ups[...].reshape(width, -1))
        sigma = 1.0 / (1.0 + jnp.exp(-gate))
        active = gate * sigma
        hidden = (active * up).astype(bf16)
        if reuse:
            for copy in chunk_out(k, e, slot):
                copy.wait()
        chunk[slot, 0] = hidden
        chunk[slot, 1] = (up * sigma * (1.0 + gate * (1.0 - sigma))).astype(bf16)
        chunk[slot, 2] = active.astype(bf16)
        for copy in chunk_out(k, e, slot):
            copy.start()
        spot = pl.ds(pl.multiple_of((k * 2 + e) * size, size), size)
        hidden_t[:, spot] = hidden.T

    process(0, core, 0, False)
    side_arrival(0).wait_recv()
    process(0, 1 - core, 1, False)
    for k in range(dp):
        cot_loads[k].wait()
        twin_copy(k).start()
    for k in range(1, 3):
        near_copy(k).wait_recv()
        pass_copy(k - 1).start()
        side_copy(k).start()
    for k in range(dp):
        twin_arrival(k).wait_recv()
    cots_out = pltpu.make_async_copy(cots, cots_hbm, cots_sem)
    cots_out.start()

    def step(k, carry):
        @pl.when(k == 3)
        def _():
            pass_copy(0).wait_recv()
            pass_copy(1).wait_recv()
            side_copy(3).start()

        process(k, core, 0, True)
        side_arrival(k).wait_recv()
        process(k, 1 - core, 1, True)
        return carry

    lax.fori_loop(1, dp, step, 0)

    def tile_copy(j, slot):
        spot = pl.ds(pl.multiple_of(j * 256, 256), 256)
        return pltpu.make_async_copy(tile_out.at[slot], down_grad_hbm.at[:, spot], tile_sem.at[slot])

    count = width // 256

    def tile(j, carry):
        slot = lax.rem(j, 2)

        @pl.when(j > 1)
        def _():
            tile_copy(j - 2, slot).wait()

        spot = pl.ds(pl.multiple_of(j * 256, 256), 256)
        columns = cots[:, :, :, spot].reshape(-1, 256)
        tile_out[slot] = multiply(hidden_t[...], columns).astype(bf16)
        tile_copy(j, slot).start()
        return carry

    lax.fori_loop(0, count, tile, 0)
    for j in (count - 2, count - 1):
        tile_copy(j, j % 2).wait()
    cots_out.wait()
    for slot, e in ((0, core), (1, 1 - core)):
        for copy in chunk_out(dp - 1, e, slot):
            copy.wait()
    for k in range(dp):
        for e in range(2):
            tokens_out(k, e).wait()
        side_copy(k).wait_send()
        twin_copy(k).wait_send()
    for k in range(1, 3):
        near_copy(k).wait_send()
        pass_copy(k - 1).wait_send()


def mlp_forward(x_own, wide, cots):
    depth, dp = wide.shape[:2]
    size, width = x_own.shape
    inner = wide.shape[-1]
    bf16 = jnp.bfloat16
    hbm = pl.BlockSpec(memory_space=pl.ANY)
    dma = pltpu.SemaphoreType.DMA
    weight = pltpu.VMEM((dp, depth) + wide.shape[2:3] + wide.shape[4:], bf16)
    whole = jax.ShapeDtypeStruct((dp, 2, size, width), bf16)
    thin = jax.ShapeDtypeStruct((dp, 2, size, inner), bf16)
    return pl.pallas_call(
        functools.partial(mlp_forward_kernel, dp, depth),
        out_shape=(whole, whole, thin, thin, thin, jax.ShapeDtypeStruct((inner, width), bf16)),
        in_specs=[hbm] * (2 + dp),
        out_specs=(hbm,) * 6,
        scratch_shapes=[
            pltpu.VMEM((dp, 2, size, width), bf16),
            pltpu.VMEM((dp, 2, size, width), bf16),
            weight,
            weight,
            pltpu.VMEM((inner, 2 * dp * size), bf16),
            pltpu.VMEM((2, 3, size, inner), bf16),
            pltpu.VMEM((2, inner, 256), bf16),
            dma((2 * depth + 1 + dp,)),
            dma,
            dma((dp,)),
            dma((dp,)),
            dma((dp,)),
            dma((dp,)),
            dma((2,)),
            dma((2,)),
            dma((dp, 2)),
            dma((2, 3)),
            dma((2,)),
            dma((dp,)),
            dma((dp,)),
        ],
        compiler_params=pltpu.CompilerParams(
            collective_id=1, has_side_effects=True, vmem_limit_bytes=VMEM_LIMIT
        ),
        cost_estimate=LIGHT,
        name="mlp_forward",
    )(x_own, wide, *cots)


def mlp_backward_kernel(
    dp,
    depth,
    tokens_hbm,
    cots_hbm,
    hidden_hbm,
    slope_hbm,
    active_hbm,
    wide_hbm,
    down_hbm,
    grad_ref,
    part_hbm,
    wide_grad_hbm,
    tokens,
    gates,
    ups,
    downs,
    gate_t,
    up_t,
    cot_slots,
    chunk,
    part_out,
    tile_out,
    load_sem,
    slot_sem,
    part_sem,
    tile_sem,
    *sum_refs,
):
    bf16 = jnp.bfloat16
    _, _, core, peer, twin = team_places()
    size, width = grad_ref.shape
    loads = [pltpu.make_async_copy(down_hbm, downs, load_sem.at[0])]
    for z in range(depth):
        for which, target in ((0, gates), (1, ups)):
            sem = load_sem.at[1 + 2 * z + which]
            loads.append(pltpu.make_async_copy(wide_hbm.at[z, :, :, which], target.at[:, z], sem))
    tokens_load = pltpu.make_async_copy(tokens_hbm, tokens, load_sem.at[2 * depth + 1])

    def slot_loads(k, e, slot):
        copies = [pltpu.make_async_copy(cots_hbm.at[k, e], cot_slots.at[slot], slot_sem.at[slot, 3])]
        for i, source in enumerate((hidden_hbm, slope_hbm, active_hbm)):
            copies.append(
                pltpu.make_async_copy(source.at[k, e], chunk.at[slot, i], slot_sem.at[slot, i])
            )
        return copies

    for copy in slot_loads(dp - 1, 1 - core, (dp - 1) % 2):
        copy.start()
    for load in loads:
        load.start()
    greet([peer(k) for k in range(1, 3)] + [twin])
    for load in loads:
        load.wait()
    tokens_load.start()

    def part_copy(k, e, slot):
        return pltpu.make_async_copy(part_out.at[slot], part_hbm.at[k, e], part_sem.at[slot])

    def product(k, e, turn):
        slot = lax.rem(k, 2)
        for copy in slot_loads(k, e, slot):
            copy.wait()

        @pl.when(k > 0)
        def _():
            for copy in slot_loads(k - 1, e, 1 - slot):
                copy.start()

        if turn == 0:

            @pl.when(k == 0)
            def _():
                for copy in slot_loads(dp - 1, core, 1 - slot):
                    copy.start()

        grad_hid = contract_last(cot_slots[slot], downs[...])
        grad_gate = (grad_hid * chunk[slot, 1].astype(jnp.float32)).astype(bf16)
        grad_up = (grad_hid * chunk[slot, 2].astype(jnp.float32)).astype(bf16)
        spot = pl.ds(pl.multiple_of((k * 2 + e) * size, size), size)
        gate_t[:, spot] = grad_gate.T
        up_t[:, spot] = grad_up.T
        if turn == 0:

            @pl.when(k < dp - 2)
            def _():
                part_copy(k, e, slot).wait()
        else:
            part_copy(k, e, slot).wait()
        part_out[slot] = multiply(chunk[slot, 0], downs[...]).astype(bf16)
        part_copy(k, e, slot).start()
        return contract_last(grad_gate, gates[...].reshape(width, -1)) + contract_last(
            grad_up, ups[...].reshape(width, -1)
        )

    complete = plane_sum(dp, product, grad_ref, sum_refs)
    tokens_load.wait()
    block = 256
    count = width // block

    def tile_copies(which, j, slot):
        per = depth * 128 // block
        return [
            pltpu.make_async_copy(
                tile_out.at[slot, :, pl.ds(i * 128, 128)],
                wide_grad_hbm.at[lax.rem(j, per) * (block // 128) + i, which, j // per],
                tile_sem.at[slot, i],
            )
            for i in range(block // 128)
        ]

    for which, left in ((0, gate_t), (1, up_t)):

        def tile(j, carry, which=which, left=left):
            slot = lax.rem(j, 2)

            @pl.when(j > 1)
            def _():
                for copy in tile_copies(which, j - 2, slot):
                    copy.wait()

            spot = pl.ds(pl.multiple_of(j * block, block), block)
            columns = tokens[:, :, :, spot].reshape(-1, block)
            tile_out[slot] = multiply(left[...], columns).astype(bf16)
            for copy in tile_copies(which, j, slot):
                copy.start()
            return carry

        lax.fori_loop(0, count, tile, 0)
        for j in (count - 2, count - 1):
            for copy in tile_copies(which, j, j % 2):
                copy.wait()
    complete()
    for slot in range(2):
        part_copy(slot, core, slot).wait()


def mlp_backward(tokens, cots, hidden, slope, active, wide, down):
    depth, dp = wide.shape[:2]
    size, width = tokens.shape[2:]
    inner = wide.shape[-1]
    f32, bf16 = jnp.float32, jnp.bfloat16
    hbm = pl.BlockSpec(memory_space=pl.ANY)
    dma = pltpu.SemaphoreType.DMA
    weight = pltpu.VMEM((dp, depth) + wide.shape[2:3] + wide.shape[4:], bf16)
    turned = pltpu.VMEM((inner, 2 * dp * size), bf16)
    return pl.pallas_call(
        functools.partial(mlp_backward_kernel, dp, depth),
        out_shape=(
            jax.ShapeDtypeStruct((size, width), f32),
            jax.ShapeDtypeStruct((dp, 2, size, width), bf16),
            jax.ShapeDtypeStruct((depth, 2, dp, inner, width // (depth * dp)), bf16),
        ),
        in_specs=[hbm] * 7,
        out_specs=(pl.BlockSpec(memory_space=pltpu.VMEM), hbm, hbm),
        scratch_shapes=[
            pltpu.VMEM((dp, 2, size, width), bf16),
            weight,
            weight,
            pltpu.VMEM((inner, width), bf16),
            turned,
            turned,
            pltpu.VMEM((2, size, width), bf16),
            pltpu.VMEM((2, 3, size, inner), bf16),
            pltpu.VMEM((2, size, width), bf16),
            pltpu.VMEM((2, inner, 256), bf16),
            dma((2 * depth + 2,)),
            dma((2, 4)),
            dma((2,)),
            dma((2, 2)),
        ]
        + sum_scratch(dp, size, width),
        compiler_params=pltpu.CompilerParams(
            collective_id=6, has_side_effects=True, vmem_limit_bytes=60 * 1024 * 1024
        ),
        cost_estimate=LIGHT,
        name="mlp_backward",
    )(tokens, cots, hidden, slope, active, wide, down)


def attend_sum_kernel(
    dp, rows, context_ref, weight_ref, own_ref, gain_ref, middle_ref, normed_ref, *scratch
):
    _, _, _, peer, twin = team_places()
    length = own_ref.shape[1]
    size, width = middle_ref.shape
    greet([peer(k) for k in range(1, 3)] + [twin])

    def product(k, e, turn):
        spot = pl.ds(pl.multiple_of(e * length, length), length)
        block = context_ref[pl.ds(k * rows, rows), spot].reshape(size, -1)
        return multiply(block, weight_ref[...])

    plane_sum(dp, product, middle_ref, scratch)()
    middle = middle_ref[...] + own_ref[...].reshape(size, width).astype(jnp.float32)
    middle_ref[...] = middle
    factor = lax.rsqrt(jnp.mean(middle * middle, axis=-1, keepdims=True) + EPSILON)
    normed_ref[...] = (middle * factor * gain_ref[...].astype(jnp.float32)).astype(jnp.bfloat16)


def attend_sum(dp, context, weight, own, gain):
    rows, length, width = own.shape
    size = rows * length
    vmem = pl.BlockSpec(memory_space=pltpu.VMEM)
    return pl.pallas_call(
        functools.partial(attend_sum_kernel, dp, rows),
        out_shape=(
            jax.ShapeDtypeStruct((size, width), jnp.float32),
            jax.ShapeDtypeStruct((size, width), jnp.bfloat16),
        ),
        in_specs=[vmem] * 4,
        out_specs=(vmem, vmem),
        scratch_shapes=sum_scratch(dp, size, width),
        compiler_params=pltpu.CompilerParams(
            collective_id=4, has_side_effects=True, vmem_limit_bytes=VMEM_LIMIT
        ),
        cost_estimate=LIGHT,
        name="attend_sum",
    )(context, weight, own, gain)


def middle_back_kernel(
    dp,
    rows,
    grad_ref,
    middle_ref,
    cot_ref,
    gain_ref,
    context_ref,
    weight_ref,
    grad_middle_ref,
    grad_context_ref,
    weight_grad_ref,
    tokens,
    context_t,
    near_send,
    near_got,
    side_send,
    side_got,
    pass_send,
    pass_got,
):
    f32, bf16 = jnp.float32, jnp.bfloat16
    _, _, core, peer, twin = team_places()
    size, width = grad_ref.shape
    length = size // rows
    half = size // 2
    greet([peer(k) for k in range(1, 3)] + [twin])
    middle = middle_ref[...]
    factor = lax.rsqrt(jnp.mean(middle * middle, axis=-1, keepdims=True) + EPSILON)
    inner = grad_ref[...] * gain_ref[...].astype(f32)
    mean = jnp.mean(inner * middle, axis=-1, keepdims=True)
    total = cot_ref[...].astype(f32) + factor * inner - factor * factor * factor * middle * mean
    grad_middle_ref[...] = total
    tokens[0, core] = total.astype(bf16)

    def near_copy(k):
        return send(
            tokens.at[0, core], tokens.at[k, core], near_send.at[k], near_got.at[k], peer(k)
        )

    def pass_copy(part):
        spot = pl.ds(part * half, half)
        return send(
            tokens.at[1 + part, core, spot],
            tokens.at[3, core, spot],
            pass_send.at[part],
            pass_got.at[part],
            peer(2 - part),
        )

    def side_copy(k):
        block = tokens.at[k, core]
        return send(block, block, side_send.at[k], side_got.at[k], twin)

    def side_arrival(k):
        block = tokens.at[k, 1 - core]
        return send(block, block, side_send.at[k], side_got.at[k], twin)

    near_copy(1).start()
    near_copy(2).start()
    side_copy(0).start()
    for k in range(dp):
        for e in range(2):
            for r in range(rows):
                block = context_ref[k * rows + r, e * length : (e + 1) * length]
                spot = pl.ds(((k * 2 + e) * rows + r) * length, length)
                context_t[:, spot] = block.T

    def process(k, e):
        block = contract_last(tokens[k, e], weight_ref[...]).astype(bf16)
        spot = pl.ds(pl.multiple_of(e * length, length), length)
        grad_context_ref[pl.ds(k * rows, rows), spot] = block.reshape(rows, length, -1)

    process(0, core)
    side_arrival(0).wait_recv()
    process(0, 1 - core)
    for k in range(1, 3):
        near_copy(k).wait_recv()
        pass_copy(k - 1).start()
        side_copy(k).start()

    def step(k, carry):
        @pl.when(k == 3)
        def _():
            pass_copy(0).wait_recv()
            pass_copy(1).wait_recv()
            side_copy(3).start()

        process(k, core)
        side_arrival(k).wait_recv()
        process(k, 1 - core)
        return carry

    lax.fori_loop(1, dp, step, 0)

    def tile(j, carry):
        spot = pl.ds(pl.multiple_of(j * 256, 256), 256)
        columns = tokens[:, :, :, spot].reshape(-1, 256)
        weight_grad_ref[:, spot] = multiply(context_t[...], columns).astype(bf16)
        return carry

    lax.fori_loop(0, width // 256, tile, 0)
    for k in range(1, 3):
        near_copy(k).wait_send()
        pass_copy(k - 1).wait_send()
    for k in range(dp):
        side_copy(k).wait_send()


def middle_back(dp, rows, grad, middle, cot, gain, context, weight):
    f32, bf16 = jnp.float32, jnp.bfloat16
    size, width = grad.shape
    vmem = pl.BlockSpec(memory_space=pltpu.VMEM)
    dma = pltpu.SemaphoreType.DMA
    return pl.pallas_call(
        functools.partial(middle_back_kernel, dp, rows),
        out_shape=(
            jax.ShapeDtypeStruct((size, width), f32),
            jax.ShapeDtypeStruct(context.shape, bf16),
            jax.ShapeDtypeStruct(weight.shape, bf16),
        ),
        in_specs=[vmem] * 6,
        out_specs=(vmem, vmem, vmem),
        scratch_shapes=[
            pltpu.VMEM((dp, 2, size, width), bf16),
            pltpu.VMEM((weight.shape[0], 2 * dp * size), bf16),
            dma((dp,)),
            dma((dp,)),
            dma((dp,)),
            dma((dp,)),
            dma((2,)),
            dma((2,)),
        ],
        compiler_params=pltpu.CompilerParams(
            collective_id=5, has_side_effects=True, vmem_limit_bytes=VMEM_LIMIT
        ),
        cost_estimate=LIGHT,
        name="middle_back",
    )(grad, middle, cot, gain, context, weight)


def open_kernel(
    dp,
    depth,
    query_ref,
    key_ref,
    value_ref,
    attn_gain_ref,
    mlp_gain_ref,
    gate_ref,
    up_ref,
    places_ref,
    own_ref,
    attn_hbm,
    wide_hbm,
    places_hbm,
    near_hbm,
    attn_blocks,
    wide_blocks,
    local_sem,
    attn_send,
    attn_got,
    wide_send,
    wide_got,
    places_send,
    places_got,
    line_send,
    line_got,
    near_send,
    near_got,
    pass_send,
    pass_got,
):
    data, place, core, peer, twin = team_places()
    part = query_ref.shape[0]
    half = HD // 2
    count = wide_blocks.shape[3] // depth
    side = depth * half
    middle = own_ref.shape[0] // 2
    attn_blocks[...] = jnp.zeros_like(attn_blocks)
    for d in range(dp):
        for c in range(2):
            team = 2 * d + c
            for z in range(depth):
                owner = (d * depth + z) * 2 + c
                for h in range(2):
                    spot = owner * HD + h * half
                    attn_blocks[team, :part, h * side + z * half : h * side + (z + 1) * half] = (
                        query_ref[:, spot : spot + half]
                    )
            pair = key_ref if c == 0 else value_ref
            attn_blocks[team, :part, 2 * side :] = pair[:, d * HD : (d + 1) * HD]
            attn_blocks[team, part : part + 1, :part] = attn_gain_ref[...]
            attn_blocks[team, part + 1 : part + 2, :part] = mlp_gain_ref[...]

    def device(k, other):
        return (peer(k)[0], place, 1 - core if other else core)

    def number(k, other):
        return 2 * peer(k)[0] + (1 - core if other else core)

    pairs = [(k, other) for k in range(dp) for other in range(2) if k or other]
    others = [(data, lax.rem(place + step, depth), core) for step in range(1, depth)]
    greet([device(k, other) for k, other in pairs] + others)

    def attn_copy(k, other):
        return send(
            attn_blocks.at[number(k, other)],
            attn_hbm.at[place, data, core],
            attn_send.at[k, other],
            attn_got.at[k, other],
            device(k, other),
        )

    def wide_copy(k, other):
        return send(
            wide_blocks.at[number(k, other)],
            wide_hbm.at[data, core],
            wide_send.at[k, other],
            wide_got.at[k, other],
            device(k, other),
        )

    def places_copy(k, other):
        return send(
            places_ref,
            places_hbm.at[k, core],
            places_send.at[k, other],
            places_got.at[k, other],
            device(k, other),
        )

    def arrival(target, send_sem, got_sem):
        return send(target, target, send_sem, got_sem, twin)

    def near_copy(k):
        return send(own_ref, near_hbm.at[k], near_send.at[k], near_got.at[k], peer(k))

    def pass_copy(which):
        spot = pl.ds(which * middle, middle)
        return send(
            near_hbm.at[1 + which, spot],
            near_hbm.at[3, spot],
            pass_send.at[which],
            pass_got.at[which],
            peer(2 - which),
        )

    def line_copy(z):
        return send(
            attn_hbm.at[place],
            attn_hbm.at[place],
            line_send.at[z],
            line_got.at[place],
            (data, z, core),
        )

    for k, other in pairs:
        attn_copy(k, other).start()
    for k, other in pairs:
        places_copy(k, other).start()
    near_copy(1).start()
    near_copy(2).start()
    locals_ = [
        pltpu.make_async_copy(
            attn_blocks.at[2 * data + core], attn_hbm.at[place, data, core], local_sem.at[0]
        ),
        pltpu.make_async_copy(places_ref, places_hbm.at[0, core], local_sem.at[1]),
        pltpu.make_async_copy(own_ref, near_hbm.at[0], local_sem.at[2]),
    ]
    for copy in locals_:
        copy.start()
    for d in range(dp):
        for c in range(2):
            for z in range(depth):
                owner = (d * depth + z) * 2 + c
                for which, source in ((0, gate_ref), (1, up_ref)):
                    wide_blocks[2 * d + c, which, :, z * count : (z + 1) * count] = source[
                        :, owner * count : (owner + 1) * count
                    ]
    wide_local = pltpu.make_async_copy(
        wide_blocks.at[2 * data + core], wide_hbm.at[data, core], local_sem.at[3]
    )
    wide_local.start()
    locals_[0].wait()
    for k, other in pairs:
        target = attn_hbm.at[place, peer(k)[0], 1 - core if other else core]
        arrival(target, attn_send.at[k, other], attn_got.at[k, other]).wait_recv()
    for z in range(depth):

        @pl.when(z != place)
        def _(z=z):
            line_copy(z).start()

    for k, other in pairs:
        wide_copy(k, other).start()
    for which in range(2):
        near_copy(1 + which).wait_recv()
        pass_copy(which).start()
    for copy in locals_[1:] + [wide_local]:
        copy.wait()
    for k, other in pairs:
        spot = (peer(k)[0], 1 - core if other else core)
        arrival(wide_hbm.at[spot], wide_send.at[k, other], wide_got.at[k, other]).wait_recv()
        target = places_hbm.at[k, 1 - core if other else core]
        arrival(target, places_send.at[k, other], places_got.at[k, other]).wait_recv()
    for which in range(2):
        pass_copy(which).wait_recv()
        pass_copy(which).wait_send()
        near_copy(1 + which).wait_send()
    for z in range(depth):

        @pl.when(z != place)
        def _(z=z):
            arrival(attn_hbm.at[z], line_send.at[z], line_got.at[z]).wait_recv()
            line_copy(z).wait_send()

    for k, other in pairs:
        attn_copy(k, other).wait_send()
        wide_copy(k, other).wait_send()
        places_copy(k, other).wait_send()


def open_layer(dp, depth, query, key, value, attn_gain, mlp_gain, gate, up, places, own):
    part = query.shape[0]
    inner = gate.shape[1] // (2 * dp)
    columns = depth * HD + HD
    bf16 = jnp.bfloat16
    hbm = pl.BlockSpec(memory_space=pl.ANY)
    vmem = pl.BlockSpec(memory_space=pltpu.VMEM)
    dma = pltpu.SemaphoreType.DMA
    return pl.pallas_call(
        functools.partial(open_kernel, dp, depth),
        out_shape=(
            jax.ShapeDtypeStruct((depth, dp, 2, part + 8, columns), bf16),
            jax.ShapeDtypeStruct((dp, 2, 2, part, inner), bf16),
            jax.ShapeDtypeStruct((dp, 2) + places.shape, places.dtype),
            jax.ShapeDtypeStruct((dp,) + own.shape, bf16),
        ),
        in_specs=[vmem] * 9,
        out_specs=(hbm,) * 4,
        scratch_shapes=[
            pltpu.VMEM((2 * dp, part + 8, columns), bf16),
            pltpu.VMEM((2 * dp, 2, part, inner), bf16),
            dma((4,)),
            dma((dp, 2)),
            dma((dp, 2)),
            dma((dp, 2)),
            dma((dp, 2)),
            dma((dp, 2)),
            dma((dp, 2)),
            dma((depth,)),
            dma((depth,)),
            dma((dp,)),
            dma((dp,)),
            dma((2,)),
            dma((2,)),
        ],
        compiler_params=pltpu.CompilerParams(
            collective_id=7, has_side_effects=True, vmem_limit_bytes=VMEM_LIMIT
        ),
        cost_estimate=LIGHT,
        name="open_layer",
    )(query, key, value, attn_gain[None], mlp_gain[None], gate, up, places, own)


def unpack_kernel(dp, depth, blocks_ref, gate_ref, up_ref, gate_grad_ref, up_grad_ref, gain_ref):
    f32 = jnp.float32
    count = blocks_ref.shape[3] // depth
    for which, grad_ref in ((0, gate_grad_ref), (1, up_grad_ref)):
        for d in range(dp):
            for c in range(2):
                block = blocks_ref[2 * d + c, which].astype(f32)
                for z in range(depth):
                    spot = ((d * depth + z) * 2 + c) * count
                    grad_ref[:, spot : spot + count] = block[:, z * count : (z + 1) * count]
    products = gate_ref[...].astype(f32) * gate_grad_ref[...]
    products = products + up_ref[...].astype(f32) * up_grad_ref[...]
    gain_ref[...] = jnp.sum(products, axis=-1, keepdims=True)


def unpack(dp, depth, blocks, gate, up):
    f32 = jnp.float32
    vmem = pl.BlockSpec(memory_space=pltpu.VMEM)
    return pl.pallas_call(
        functools.partial(unpack_kernel, dp, depth),
        out_shape=(
            jax.ShapeDtypeStruct(gate.shape, f32),
            jax.ShapeDtypeStruct(gate.shape, f32),
            jax.ShapeDtypeStruct((gate.shape[0], 1), f32),
        ),
        in_specs=[vmem] * 3,
        out_specs=(vmem, vmem, vmem),
        compiler_params=pltpu.CompilerParams(vmem_limit_bytes=VMEM_LIMIT),
        cost_estimate=LIGHT,
        name="unpack",
    )(blocks, gate, up)


def project_kernel(
    dp,
    depth,
    rows,
    *refs,
):
    pieces, gain_ref, cosine_ref, sine_ref, cosine_pair_ref, sine_pair_ref, weight_hbm = refs[:7]
    query_ref, normed_ref, line_hbm = refs[7:10]
    (
        weight,
        pair,
        far_pieces,
        load_sem,
        own_sem,
        line_send,
        line_got,
        side_send,
        side_got,
        twin_send,
        twin_got,
    ) = refs[10:]
    f32, bf16 = jnp.float32, jnp.bfloat16
    data, place, core, peer, twin = team_places()
    length, width = pieces.shape[2:]
    part = weight.shape[3]
    columns = query_ref.shape[2]
    loads = [
        pltpu.make_async_copy(
            weight_hbm.at[z, :, :, pl.ds(0, part)], weight.at[:, z], load_sem.at[z]
        )
        for z in range(depth)
    ]
    for load in loads:
        load.start()
    others = [(data, lax.rem(place + step, depth), core) for step in range(1, depth)]
    greet(others + [twin])

    def twin_copy(k):
        return send(pieces.at[k], far_pieces.at[k], twin_send.at[k], twin_got.at[k], twin)

    for k in range(dp):
        twin_copy(k).start()
    for load in loads:
        load.wait()
    gain = gain_ref[...].astype(f32)

    def block_of(which, z, k):
        return line_hbm.at[which, z, pl.ds(k * rows, rows)]

    def pair_of(k):
        return pair.at[pl.ds(k * rows, rows)]

    def own_copy(k):
        return pltpu.make_async_copy(pair_of(k), block_of(core, place, k), own_sem.at[k])

    def own_side_copy(k):
        return send(
            pair_of(k),
            block_of(core, place, k),
            side_send.at[place, k],
            side_got.at[place, k],
            twin,
        )

    def line_copy(z, k):
        return send(
            pair_of(k),
            block_of(core, place, k),
            line_send.at[z, k],
            line_got.at[place, k],
            (data, z, core),
        )

    def line_arrival(z, k):
        block = block_of(core, z, k)
        return send(block, block, line_send.at[z, k], line_got.at[z, k], twin)

    def side_copy(z, k):
        block = block_of(core, z, k)
        return send(block, block, side_send.at[z, k], side_got.at[z, k], twin)

    def side_arrival(z, k):
        block = block_of(1 - core, z, k)
        return send(block, block, side_send.at[z, k], side_got.at[z, k], twin)

    for k in range(dp):
        for far in range(2):
            e = core if far == 0 else 1 - core
            if far:
                twin_copy(k).wait_recv()
            source = far_pieces.at[k] if far else pieces.at[k]
            values = source[...].reshape(rows * length, width).astype(f32)
            factor = lax.rsqrt(jnp.mean(values * values, axis=-1, keepdims=True) + EPSILON)
            normed = (values * factor * gain).astype(bf16)
            normed_ref[k, e] = normed
            result = multiply(normed, weight[...].reshape(width, -1))
            spot = pl.ds(pl.multiple_of(e * length, length), length)
            for r in range(rows):
                row = k * rows + r
                block = result[r * length : (r + 1) * length]
                cosine, sine = cosine_ref[row, spot], sine_ref[row, spot]
                first, second = block[:, : columns // 2], block[:, columns // 2 : columns]
                turned = (first * cosine - second * sine).astype(bf16)
                query_ref[row, spot, : columns // 2] = turned * bf16(HD ** (-0.5))
                turned = (second * cosine + first * sine).astype(bf16)
                query_ref[row, spot, columns // 2 :] = turned * bf16(HD ** (-0.5))
                keys = block[:, columns:].T
                cosine, sine = cosine_pair_ref[row, :, spot], sine_pair_ref[row, :, spot]
                first, second = keys[: HD // 2], keys[HD // 2 :]
                pair[row, : HD // 2, spot] = (first * cosine - second * sine).astype(bf16)
                pair[row, HD // 2 :, spot] = (second * cosine + first * sine).astype(bf16)
        own_copy(k).start()
        own_side_copy(k).start()
        for z in range(depth):

            @pl.when(z > place)
            def _(z=z, k=k):
                line_copy(z, k).start()

    for k in range(dp):
        for z in reversed(range(depth)):

            @pl.when(z < place)
            def _(z=z, k=k):
                line_arrival(z, k).wait_recv()
                side_copy(z, k).start()

    for k in range(dp):
        twin_copy(k).wait_send()
        own_copy(k).wait()
        own_side_copy(k).wait_send()
        for z in range(depth):

            @pl.when(z <= place)
            def _(z=z, k=k):
                side_arrival(z, k).wait_recv()

            @pl.when(z < place)
            def _(z=z, k=k):
                side_copy(z, k).wait_send()

            @pl.when(z > place)
            def _(z=z, k=k):
                line_copy(z, k).wait_send()


def project(near, gain, cosine, sine, cosine_pair, sine_pair, weight):
    f32, bf16 = jnp.float32, jnp.bfloat16
    dp, rows, length, width = near.shape
    depth = weight.shape[0]
    row_count, size = cosine.shape[:2]
    columns = 2 * cosine.shape[2]
    part = width // (2 * dp * depth)
    hbm = pl.BlockSpec(memory_space=pl.ANY)
    vmem = pl.BlockSpec(memory_space=pltpu.VMEM)
    dma = pltpu.SemaphoreType.DMA
    return pl.pallas_call(
        functools.partial(project_kernel, dp, depth, rows),
        out_shape=(
            jax.ShapeDtypeStruct((row_count, size, columns), bf16),
            jax.ShapeDtypeStruct((dp, 2, rows * length, width), bf16),
            jax.ShapeDtypeStruct((2, depth, row_count, HD, size), bf16),
        ),
        in_specs=[vmem] * 6 + [hbm],
        out_specs=(vmem, vmem, hbm),
        scratch_shapes=[
            pltpu.VMEM((dp, depth, 2, part, columns + HD), bf16),
            pltpu.VMEM((row_count, HD, size), bf16),
            pltpu.VMEM((dp, rows, length, width), bf16),
            dma((depth,)),
            dma((dp,)),
            dma((depth, dp)),
            dma((depth, dp)),
            dma((depth, dp)),
            dma((depth, dp)),
            dma((dp,)),
            dma((dp,)),
        ],
        compiler_params=pltpu.CompilerParams(
            collective_id=2, has_side_effects=True, vmem_limit_bytes=VMEM_LIMIT
        ),
        cost_estimate=LIGHT,
        name="project",
    )(near, gain, cosine, sine, cosine_pair, sine_pair, weight)


def finish_kernel(
    dp,
    depth,
    rows,
    query_ref,
    cosine_ref,
    sine_ref,
    out_grad_ref,
    grad_k_hbm,
    grad_v_hbm,
    normed_hbm,
    weight_hbm,
    grad_ref,
    out_sum_ref,
    weight_grad_hbm,
    out_got_block,
    normed,
    weight,
    kept,
    given,
    arrived,
    line_block,
    line_got_block,
    terms,
    terms_t,
    held,
    line_grads,
    line_grads_got,
    summed,
    load_sem,
    swap_send,
    swap_got,
    line_send,
    line_got,
    grads_send,
    grads_got,
    team_send,
    team_got,
    own_sem,
    out_send,
    out_got,
    *sum_refs,
):
    f32, bf16 = jnp.float32, jnp.bfloat16
    data, place, core, peer, twin = team_places()
    columns = query_ref.shape[2]
    size = query_ref.shape[1]
    length = size // 2
    width = grad_ref.shape[1]
    part = weight.shape[3]
    features = columns + HD
    loads = [
        pltpu.make_async_copy(
            weight_hbm.at[z, :, :, pl.ds(0, part)], weight.at[:, z], load_sem.at[z]
        )
        for z in range(depth)
    ]
    loads.append(pltpu.make_async_copy(normed_hbm, normed, load_sem.at[depth]))
    for load in loads:
        load.start()

    @pl.when(core == 0)
    def _():
        pltpu.make_async_copy(grad_k_hbm, kept, load_sem.at[depth + 1]).start()
        pltpu.make_async_copy(grad_v_hbm, given, load_sem.at[depth + 2]).start()

    @pl.when(core == 1)
    def _():
        pltpu.make_async_copy(grad_v_hbm, kept, load_sem.at[depth + 1]).start()
        pltpu.make_async_copy(grad_k_hbm, given, load_sem.at[depth + 2]).start()

    others = [(data, lax.rem(place + step, depth), core) for step in range(1, depth)]
    team = [peer(k) for k in range(1, dp)]
    cross = [(target[0], place, 1 - core) for target in team]
    greet(others + [twin] + team + cross)
    pltpu.make_async_copy(grad_v_hbm, given, load_sem.at[depth + 2]).wait()
    swap_copy = send(given, arrived, swap_send, swap_got, twin)
    swap_copy.start()
    pltpu.make_async_copy(grad_k_hbm, kept, load_sem.at[depth + 1]).wait()
    swap_copy.wait_recv()

    def line_copy(z):
        return send(
            line_block.at[z],
            line_got_block.at[place],
            line_send.at[z],
            line_got.at[place],
            (data, z, core),
        )

    def line_arrival(z):
        return send(
            line_block.at[z], line_got_block.at[z], line_send.at[z], line_got.at[z], twin
        )

    for z in range(depth):

        @pl.when(z < place)
        def _(z=z):
            total = kept[z].astype(f32) + arrived[z].astype(f32)
            line_block[z] = total.astype(bf16)
            line_copy(z).start()

    for load in loads:
        load.wait()
    for k in range(dp):
        for e in range(2):
            for r in range(rows):
                block = query_ref[k * rows + r, e * length : (e + 1) * length]
                terms[k, e, r * length : (r + 1) * length, :columns] = block
                spot = pl.ds(((k * 2 + e) * rows + r) * length, length)
                terms_t[:columns, spot] = block.T

    def tile_rows(first, count):
        def tile(j, carry):
            spot = pl.ds(pl.multiple_of(j * 256, 256), 256)
            block = multiply(
                terms_t[first : first + count], normed[:, :, :, spot].reshape(-1, 256)
            ).astype(bf16)
            for i in range(2):
                group = 2 * j + i
                line_grads[lax.rem(group, depth), group // depth, first : first + count] = block[
                    :, i * 128 : (i + 1) * 128
                ]
            return carry

        lax.fori_loop(0, width // 256, tile, 0)

    tile_rows(0, columns)
    for z in range(depth):

        @pl.when(z == place)
        def _(z=z):
            held[...] = kept[z].astype(f32) + arrived[z].astype(f32)

    for z in range(depth):

        @pl.when(z > place)
        def _(z=z):
            line_arrival(z).wait_recv()
            held[...] += line_got_block[z].astype(f32)

    for k in range(dp):
        for r in range(rows):
            row = k * rows + r
            first, second = held[row, : HD // 2], held[row, HD // 2 :]
            cosine, sine = cosine_ref[row], sine_ref[row]
            turned = jnp.concatenate(
                [first * cosine + second * sine, second * cosine - first * sine], axis=0
            ).astype(bf16)
            for e in range(2):
                block = turned[:, e * length : (e + 1) * length]
                spot = pl.ds(((k * 2 + e) * rows + r) * length, length)
                terms_t[columns:, spot] = block
                terms[k, e, r * length : (r + 1) * length, columns:] = block.T

    def product(k, e, turn):
        return contract_last(terms[k, e], weight[...].reshape(width, features))

    out_rows = out_sum_ref.shape[0]

    def out_copy(z):
        return send(
            out_grad_ref.at[pl.ds(z * out_rows, out_rows)],
            out_got_block.at[place],
            out_send.at[z],
            out_got.at[place],
            (data, z, core),
        )

    def out_arrival(z):
        block = out_got_block.at[z]
        return send(block, block, out_send.at[z], out_got.at[z], twin)

    for z in range(depth):

        @pl.when(z != place)
        def _(z=z):
            out_copy(z).start()

    complete = plane_sum(dp, product, grad_ref, sum_refs)
    tile_rows(columns, HD)

    def grads_copy(z):
        return send(
            line_grads.at[z],
            line_grads_got.at[place],
            grads_send.at[z],
            grads_got.at[place],
            (data, z, core),
        )

    def grads_arrival(z):
        return send(
            line_grads.at[z], line_grads_got.at[z], grads_send.at[z], grads_got.at[z], twin
        )

    for z in range(depth):

        @pl.when(z != place)
        def _(z=z):
            grads_copy(z).start()

    total = line_grads[place].astype(f32)
    line_grads_got[place] = jnp.zeros(line_grads.shape[1:], bf16)
    for z in range(depth):

        @pl.when(z != place)
        def _(z=z):
            grads_arrival(z).wait_recv()

    for z in range(depth):
        total = total + line_grads_got[z].astype(f32)
    summed[...] = total.astype(bf16)
    own = pltpu.make_async_copy(summed.at[data], weight_grad_hbm.at[data, core], own_sem)
    own.start()

    def team_copy(k, other):
        target = peer(k)
        device = (target[0], place, 1 - core if other else core)
        return send(
            summed.at[target[0]],
            weight_grad_hbm.at[data, core],
            team_send.at[k, other],
            team_got.at[k, other],
            device,
        )

    def team_arrival(k, other):
        block = weight_grad_hbm.at[peer(k)[0], 1 - core if other else core]
        return send(block, block, team_send.at[k, other], team_got.at[k, other], twin)

    pairs = [(k, other) for k in range(dp) for other in range(2) if k or other]
    for k, other in pairs:
        team_copy(k, other).start()
    complete()
    for k, other in pairs:
        team_arrival(k, other).wait_recv()
        team_copy(k, other).wait_send()
    own.wait()
    spot = pl.ds(pl.multiple_of(place * out_rows, out_rows), out_rows)
    out_sum_ref[...] = out_grad_ref[spot].astype(f32)
    for z in range(depth):

        @pl.when(z != place)
        def _(z=z):
            out_arrival(z).wait_recv()
            out_sum_ref[...] += out_got_block[z].astype(f32)
            out_copy(z).wait_send()

    swap_copy.wait_send()
    for z in range(depth):

        @pl.when(z < place)
        def _(z=z):
            line_copy(z).wait_send()

        @pl.when(z != place)
        def _(z=z):
            grads_copy(z).wait_send()


def finish(
    grad_queries, cosine_pair, sine_pair, out_grad, grad_keys, grad_values, normed, weight, rows
):
    f32, bf16 = jnp.float32, jnp.bfloat16
    dp, _, own, width = normed.shape
    depth, row_count, features, size = grad_keys.shape
    columns = grad_queries.shape[2]
    part = width // (2 * dp * depth)
    total = columns + features
    hbm = pl.BlockSpec(memory_space=pl.ANY)
    vmem = pl.BlockSpec(memory_space=pltpu.VMEM)
    dma = pltpu.SemaphoreType.DMA
    line = pltpu.VMEM((depth, row_count, features, size), bf16)
    grads = pltpu.VMEM((depth, dp, total, 2 * part), bf16)
    return pl.pallas_call(
        functools.partial(finish_kernel, dp, depth, rows),
        out_shape=(
            jax.ShapeDtypeStruct((own, width), f32),
            jax.ShapeDtypeStruct((out_grad.shape[0] // depth, width), f32),
            jax.ShapeDtypeStruct((dp, 2, total, 2 * part), bf16),
        ),
        in_specs=[vmem] * 4 + [hbm] * 4,
        out_specs=(vmem, vmem, hbm),
        scratch_shapes=[
            pltpu.VMEM((depth, out_grad.shape[0] // depth, width), bf16),
            pltpu.VMEM((dp, 2, own, width), bf16),
            pltpu.VMEM((dp, depth, 2, part, total), bf16),
            line,
            line,
            line,
            line,
            line,
            pltpu.VMEM((dp, 2, own, total), bf16),
            pltpu.VMEM((total, 2 * dp * own), bf16),
            pltpu.VMEM((row_count, features, size), f32),
            grads,
            grads,
            pltpu.VMEM((dp, total, 2 * part), bf16),
            dma((depth + 3,)),
            dma,
            dma,
            dma((depth,)),
            dma((depth,)),
            dma((depth,)),
            dma((depth,)),
            dma((dp, 2)),
            dma((dp, 2)),
            dma,
            dma((depth,)),
            dma((depth,)),
        ]
        + sum_scratch(dp, own, width),
        compiler_params=pltpu.CompilerParams(
            collective_id=3, has_side_effects=True, vmem_limit_bytes=60 * 1024 * 1024
        ),
        cost_estimate=LIGHT,
        name="finish",
    )(grad_queries, cosine_pair, sine_pair, out_grad, grad_keys, grad_values, normed, weight)


def split_layer(dp, depth):
    def layer(
        hidden_in,
        segment_ids,
        positions,
        attn_gain,
        query_weight,
        key_weight,
        value_weight,
        out_weight,
        mlp_gain,
        gate_weight,
        up_weight,
        down_weight,
        cotangent,
    ):
        f32, bf16 = jnp.float32, jnp.bfloat16
        rows, length, width = hidden_in.shape
        own = rows * length
        team = 2 * dp
        tokens = team * own
        part = query_weight.shape[0]
        hidden_rows = down_weight.shape[0]
        inner = depth * hidden_rows
        heads = depth
        row_count, size = dp * rows, 2 * length
        core = lax.axis_index("core")
        place = lax.axis_index("z")

        def dot(left, right):
            return jnp.dot(left, right, preferred_element_type=f32)

        weight_out = lax.all_gather(out_weight, "z", axis=0, tiled=True)
        weight_attn, wide_mine, offsets, near = open_layer(
            dp, depth, query_weight, key_weight, value_weight, attn_gain, mlp_gain, gate_weight,
            up_weight, positions, hidden_in,
        )
        offsets = offsets.transpose(0, 2, 1, 3).reshape(row_count, size)
        gain_rows = weight_attn[:, :, :, part : part + 2, :part].transpose(3, 1, 0, 2, 4)
        gain_one, gain_two = gain_rows.reshape(2, 1, width)
        wide_got = lax.all_gather(wide_mine, "z", axis=0)
        wide_got = wide_got.reshape(depth, dp, 2, 2, part, inner)
        weight_down = lax.all_gather(down_weight, "z", axis=0, tiled=True)

        x_own = hidden_in.reshape(own, width)
        cot_own = cotangent.reshape(own, width)
        freqs = 10000.0 ** (-jnp.arange(0, HD // 2, dtype=f32) * 2.0 / HD)
        offsets_f32 = offsets.astype(f32)
        angles = offsets_f32[:, :, None] * jnp.tile(freqs, heads)
        cosine, sine = jnp.cos(angles), jnp.sin(angles)
        angles_pair = jnp.where(core == 0, offsets_f32[:, None, :] * freqs[:, None], 0.0)
        cosine_pair, sine_pair = jnp.cos(angles_pair), jnp.sin(angles_pair)
        cotangent, near, wide_mine = lax.optimization_barrier((cotangent, near, wide_mine))
        cots = plane_pieces(cotangent, dp)
        cots = [piece.reshape(own, width) for piece in cots]
        queries, normed1, lines = project(
            near, gain_one, cosine, sine, cosine_pair, sine_pair, weight_attn
        )
        low_block = (place * size - offsets[:, 0]) // size
        low_block = jnp.maximum(low_block, 0).astype(jnp.int32)
        place_one = place.astype(jnp.int32).reshape(1)
        queries, cots = lax.optimization_barrier((queries, cots))
        context, logs = attend(
            low_block, place_one, offsets[:, :, None], queries, lines
        )

        middle, normed2 = attend_sum(dp, context, weight_out, hidden_in, gain_two)
        all_normed2, all_cots, hidden, slope, active, grad_down = mlp_forward(
            normed2, wide_got, cots
        )
        grad_normed2, mlp_parts, grad_wide = mlp_backward(
            all_normed2, all_cots, hidden, slope, active, wide_got, weight_down
        )
        def line_sum(array):
            return lax.psum_scatter(array.astype(bf16), "z", scatter_dimension=0, tiled=True)

        down_sum = line_sum(grad_down)
        grad_wide, down_sum = lax.optimization_barrier((grad_wide, down_sum))
        wide_sum = line_sum(grad_wide)[0]
        grad_normed2, down_sum = lax.optimization_barrier((grad_normed2, down_sum))
        grad_middle, grad_context, grad_wout = middle_back(
            dp, rows, grad_normed2, middle, cot_own, gain_two, context, weight_out
        )
        grad_down = down_sum.astype(f32)
        mlp_parts, grad_context = lax.optimization_barrier((mlp_parts, grad_context))
        mlp_parts = mlp_parts.reshape(dp, 2, rows, length, width).transpose(0, 2, 1, 3, 4)
        mlp_out = plane_scatter(mlp_parts, dp, core).reshape(own, width)
        out_hidden = (middle + mlp_out).astype(bf16)

        grad_queries, grad_keys, grad_values = attend_back(
            low_block,
            place_one,
            offsets[:, :, None],
            queries,
            lines,
            context,
            logs,
            grad_context,
            cosine,
            sine,
        )
        grad_queries, out_hidden, wide_sum = lax.optimization_barrier(
            (grad_queries, out_hidden, wide_sum)
        )
        grad_normed1, grad_wout, attn_back = finish(
            grad_queries,
            cosine_pair,
            sine_pair,
            grad_wout,
            grad_keys,
            grad_values,
            normed1,
            weight_attn,
            rows,
        )
        wide_back = wide_sum.reshape(2, dp, inner, 2, part)
        wide_back = exchange(wide_back.transpose(1, 3, 0, 4, 2).reshape(team, 2, part, inner))
        grad_wgate, grad_wup, gain_rows = unpack(dp, depth, wide_back, gate_weight, up_weight)
        attn_back = attn_back.reshape(team, (heads + 1) * HD, 2, part)
        attn_back = lax.dynamic_index_in_dim(attn_back, core, 2, keepdims=False)
        attn_back = attn_back.transpose(0, 2, 1)
        grad_wquery = attn_back[:, :, : heads * HD].reshape(dp, 2, part, 2, depth, HD // 2)
        grad_wquery = grad_wquery.transpose(2, 0, 4, 1, 3, 5).reshape(part, -1).astype(f32)
        pair_back = attn_back[:, :, heads * HD :].reshape(dp, 2, part, HD).transpose(1, 2, 0, 3)
        grad_wkey = pair_back[0].reshape(part, dp * HD).astype(f32)
        grad_wvalue = pair_back[1].reshape(part, dp * HD).astype(f32)

        own_f32 = x_own.astype(f32)
        factor = lax.rsqrt(jnp.mean(own_f32 * own_f32, axis=-1, keepdims=True) + EPSILON)
        inner1 = grad_normed1 * gain_one.astype(f32)
        grad_in = (
            grad_middle
            + factor * inner1
            - factor * factor * factor * own_f32 * jnp.mean(inner1 * own_f32, axis=-1, keepdims=True)
        )

        def rows_of(weight, grad):
            return jnp.sum(weight.astype(f32) * grad, axis=-1)

        grad_gain_one = (
            rows_of(query_weight, grad_wquery)
            + rows_of(key_weight, grad_wkey)
            + rows_of(value_weight, grad_wvalue)
        ) / attn_gain.astype(f32)
        grad_gain_two = gain_rows[:, 0] / mlp_gain.astype(f32)
        return (
            out_hidden.reshape(rows, length, width),
            grad_in.reshape(rows, length, width),
            grad_gain_one,
            grad_wquery,
            grad_wkey,
            grad_wvalue,
            grad_wout,
            grad_gain_two,
            grad_wgate,
            grad_wup,
            grad_down,
        )

    return layer


def solution(mesh):
    dp, seq = mesh.shape["dp"], mesh.shape["seq"]
    if dp != KVH or seq % 2 or HQ != dp * seq:
        return gathered_weights(mesh)
    depth = seq // 2
    mesh = Mesh(mesh.devices.reshape(dp, depth, 2), ("dp", "z", "core"))
    every = ("dp", "z", "core")
    tokens = P("dp", ("z", "core"), None)
    matrix = P(every, None)
    return jax.shard_map(
        split_layer(dp, depth),
        mesh=mesh,
        in_specs=(
            tokens,
            P("dp", ("z", "core")),
            P("dp", ("z", "core")),
            P(every),
            matrix,
            matrix,
            matrix,
            matrix,
            P(every),
            matrix,
            matrix,
            matrix,
            tokens,
        ),
        out_specs=(
            tokens,
            tokens,
            P(every),
            matrix,
            matrix,
            matrix,
            matrix,
            P(every),
            matrix,
            matrix,
            matrix,
        ),
        check_vma=False,
    )
```

```python
import functools

import jax
import jax.numpy as jnp
from jax import lax
from jax.experimental import pallas as pl
from jax.experimental.pallas import tpu as pltpu
from jax.sharding import Mesh
from jax.sharding import PartitionSpec as P

HQ = 32
HD = 64
KVH = 4


EPSILON = 1e-05


def fetch_attention(attn_gain, query_weight, key_weight, value_weight, out_weight):
    return (
        lax.all_gather(attn_gain, ("dp", "seq"), axis=0, tiled=True),
        lax.all_gather(query_weight, ("dp", "seq"), axis=0, tiled=True),
        lax.all_gather(key_weight, ("dp", "seq"), axis=0, tiled=True),
        lax.all_gather(value_weight, ("dp", "seq"), axis=0, tiled=True),
        lax.all_gather(out_weight, ("dp", "seq"), axis=0, tiled=True),
    )


def fetch_mlp(mlp_gain, gate_weight, up_weight, down_weight):
    return (
        lax.all_gather(mlp_gain, ("dp", "seq"), axis=0, tiled=True),
        lax.all_gather(gate_weight, ("dp", "seq"), axis=0, tiled=True),
        lax.all_gather(up_weight, ("dp", "seq"), axis=0, tiled=True),
        lax.all_gather(down_weight, ("dp", "seq"), axis=0, tiled=True),
    )


def angles_of(positions):
    freqs = 10000.0 ** (-jnp.arange(0, HD // 2, dtype=jnp.float32) * 2.0 / HD)
    return positions.astype(jnp.float32)[:, None] * freqs[None, :]


def rotate(vectors, cosine, sine):
    half = vectors.shape[-1] // 2
    first = vectors[..., :half]
    second = vectors[..., half:]
    cosine = cosine[:, None, :]
    sine = sine[:, None, :]
    return jnp.concatenate(
        [first * cosine - second * sine, second * cosine + first * sine], axis=-1
    )


def norm_forward(values, gain):
    factor = lax.rsqrt(jnp.mean(values * values, axis=-1, keepdims=True) + EPSILON)
    return (values * factor * gain.astype(jnp.float32), factor)


def norm_backward(values, factor, gain, grad_normed):
    inner = grad_normed * gain.astype(jnp.float32)
    grad_gain = jnp.sum(grad_normed * values * factor, axis=0)
    grad_values = factor * inner - factor * factor * factor * values * jnp.mean(
        inner * values, axis=-1, keepdims=True
    )
    return (grad_values, grad_gain)


def masked_scores(queries_rot, keys_heads, query_pos, query_seg, seg_all):
    scores = jnp.einsum(
        "cgjd,kgd->gjck", queries_rot, keys_heads, preferred_element_type=jnp.float32
    ) * HD ** (-0.5)
    key_pos = jnp.arange(keys_heads.shape[0])
    allowed = (key_pos[None, :] <= query_pos[:, None]) & (seg_all[None, :] == query_seg[:, None])
    return jnp.where(allowed, scores, -1e30)


def add_up(total, extra):
    if total is None:
        return extra
    return jax.tree.map(jnp.add, total, extra)


def gathered_weights_layer(
    hidden_in,
    segment_ids,
    positions,
    attn_gain,
    query_weight,
    key_weight,
    value_weight,
    out_weight,
    mlp_gain,
    gate_weight,
    up_weight,
    down_weight,
    cotangent,
):
    batches, local_len, width = hidden_in.shape
    group = HQ // KVH
    query_pos = lax.axis_index("seq") * local_len + jnp.arange(local_len)
    outputs = []
    grads_in = []
    attn_total = None
    mlp_total = None
    for microbatch in range(batches):
        rows_in = hidden_in[microbatch].astype(jnp.float32)
        seg_own = segment_ids[microbatch]
        angles = angles_of(positions[microbatch])
        cosine = jnp.cos(angles)
        sine = jnp.sin(angles)
        attn_set = fetch_attention(attn_gain, query_weight, key_weight, value_weight, out_weight)
        gain_one, weight_query, weight_key, weight_value, weight_out = attn_set
        normed1, factor1 = norm_forward(rows_in, gain_one)
        normed1_low = normed1.astype(jnp.bfloat16)
        queries = jnp.dot(normed1_low, weight_query, preferred_element_type=jnp.float32).reshape(
            local_len, HQ, HD
        )
        keys_own = jnp.dot(normed1_low, weight_key, preferred_element_type=jnp.float32).reshape(
            local_len, KVH, HD
        )
        values_own = jnp.dot(normed1_low, weight_value, preferred_element_type=jnp.float32).astype(
            jnp.bfloat16
        )
        queries_rot = (
            rotate(queries, cosine, sine).astype(jnp.bfloat16).reshape(local_len, KVH, group, HD)
        )
        keys_rot = rotate(keys_own, cosine, sine).astype(jnp.bfloat16).reshape(local_len, KVH * HD)
        keys_all, values_all, seg_all = (
            lax.all_gather(keys_rot, "seq", axis=0, tiled=True),
            lax.all_gather(values_own, "seq", axis=0, tiled=True),
            lax.all_gather(seg_own, "seq", axis=0, tiled=True),
        )
        keys_heads = keys_all.reshape(-1, KVH, HD)
        values_heads = values_all.reshape(-1, KVH, HD)
        scores = masked_scores(queries_rot, keys_heads, query_pos, seg_own, seg_all)
        highest = jnp.max(scores, axis=-1, keepdims=True)
        powers = jnp.exp(scores - highest)
        totals = jnp.sum(powers, axis=-1, keepdims=True)
        logsum = highest + jnp.log(totals)
        probs_low = (powers / totals).astype(jnp.bfloat16)
        context = jnp.einsum(
            "gjck,kgd->cgjd", probs_low, values_heads, preferred_element_type=jnp.float32
        )
        context_low = context.reshape(local_len, HQ * HD).astype(jnp.bfloat16)
        middle = rows_in + jnp.dot(context_low, weight_out, preferred_element_type=jnp.float32)
        mlp_set = fetch_mlp(mlp_gain, gate_weight, up_weight, down_weight)
        gain_two, weight_gate, weight_up, weight_down = mlp_set
        normed2, factor2 = norm_forward(middle, gain_two)
        normed2_low = normed2.astype(jnp.bfloat16)
        gate = jnp.dot(normed2_low, weight_gate, preferred_element_type=jnp.float32)
        up = jnp.dot(normed2_low, weight_up, preferred_element_type=jnp.float32)
        sigma = jax.nn.sigmoid(gate)
        activation = gate * sigma
        hidden = (activation * up).astype(jnp.bfloat16)
        mlp_out = jnp.dot(hidden, weight_down, preferred_element_type=jnp.float32)
        outputs.append((middle + mlp_out).astype(jnp.bfloat16))
        grad_low = cotangent[microbatch]
        grad_out = grad_low.astype(jnp.float32)
        mlp_back = fetch_mlp(mlp_gain, gate_weight, up_weight, down_weight)
        gain_two, weight_gate, weight_up, weight_down = mlp_back
        grad_down = jnp.dot(hidden.T, grad_low, preferred_element_type=jnp.float32)
        grad_hid = jnp.dot(grad_low, weight_down.T, preferred_element_type=jnp.float32)
        grad_gate = (grad_hid * up * sigma * (1.0 + gate * (1.0 - sigma))).astype(jnp.bfloat16)
        grad_up = (grad_hid * activation).astype(jnp.bfloat16)
        grad_wgate = jnp.dot(normed2_low.T, grad_gate, preferred_element_type=jnp.float32)
        grad_wup = jnp.dot(normed2_low.T, grad_up, preferred_element_type=jnp.float32)
        grad_normed2 = jnp.dot(
            grad_gate, weight_gate.T, preferred_element_type=jnp.float32
        ) + jnp.dot(grad_up, weight_up.T, preferred_element_type=jnp.float32)
        grad_mid_norm, grad_gain_two = norm_backward(middle, factor2, gain_two, grad_normed2)
        grad_middle = grad_out + grad_mid_norm
        attn_back = fetch_attention(attn_gain, query_weight, key_weight, value_weight, out_weight)
        gain_one, weight_query, weight_key, weight_value, weight_out = attn_back
        grad_attn = grad_middle.astype(jnp.bfloat16)
        grad_wout = jnp.dot(context_low.T, grad_attn, preferred_element_type=jnp.float32)
        grad_context = (
            jnp.dot(grad_attn, weight_out.T, preferred_element_type=jnp.float32)
            .astype(jnp.bfloat16)
            .reshape(local_len, KVH, group, HD)
        )
        probs = jnp.exp(
            masked_scores(queries_rot, keys_heads, query_pos, seg_own, seg_all) - logsum
        )
        grad_probs = jnp.einsum(
            "cgjd,kgd->gjck", grad_context, values_heads, preferred_element_type=jnp.float32
        )
        inner = jnp.sum(probs * grad_probs, axis=-1, keepdims=True)
        grad_scores = (probs * (grad_probs - inner)).astype(jnp.bfloat16)
        grad_qrot = jnp.einsum(
            "gjck,kgd->cgjd", grad_scores, keys_heads, preferred_element_type=jnp.float32
        ) * HD ** (-0.5)
        grad_krot_all = jnp.einsum(
            "gjck,cgjd->kgd", grad_scores, queries_rot, preferred_element_type=jnp.float32
        ) * HD ** (-0.5)
        grad_vall = jnp.einsum(
            "gjck,cgjd->kgd", probs_low, grad_context, preferred_element_type=jnp.float32
        )
        row_len = keys_heads.shape[0]
        grad_key_own, grad_value_own = (
            lax.psum_scatter(
                grad_krot_all.reshape(row_len, KVH * HD).astype(jnp.bfloat16),
                "seq",
                scatter_dimension=0,
                tiled=True,
            ).astype(jnp.float32),
            lax.psum_scatter(
                grad_vall.reshape(row_len, KVH * HD).astype(jnp.bfloat16),
                "seq",
                scatter_dimension=0,
                tiled=True,
            ).astype(jnp.float32),
        )
        grad_keys = (
            rotate(grad_key_own.reshape(local_len, KVH, HD), cosine, -sine)
            .astype(jnp.bfloat16)
            .reshape(local_len, KVH * HD)
        )
        grad_values = grad_value_own.astype(jnp.bfloat16)
        grad_queries = (
            rotate(grad_qrot.reshape(local_len, HQ, HD), cosine, -sine)
            .astype(jnp.bfloat16)
            .reshape(local_len, HQ * HD)
        )
        grad_wquery = jnp.dot(normed1_low.T, grad_queries, preferred_element_type=jnp.float32)
        grad_wkey = jnp.dot(normed1_low.T, grad_keys, preferred_element_type=jnp.float32)
        grad_wvalue = jnp.dot(normed1_low.T, grad_values, preferred_element_type=jnp.float32)
        grad_normed1 = jnp.dot(grad_queries, weight_query.T, preferred_element_type=jnp.float32)
        grad_normed1 = grad_normed1 + jnp.dot(
            grad_keys, weight_key.T, preferred_element_type=jnp.float32
        )
        grad_normed1 = grad_normed1 + jnp.dot(
            grad_values, weight_value.T, preferred_element_type=jnp.float32
        )
        grad_rows_norm, grad_gain_one = norm_backward(rows_in, factor1, gain_one, grad_normed1)
        grads_in.append(grad_middle + grad_rows_norm)
        attn_terms = (grad_gain_one, grad_wquery, grad_wkey, grad_wvalue, grad_wout)
        mlp_terms = (grad_gain_two, grad_wgate, grad_wup, grad_down)
        attn_shares = (
            lax.psum_scatter(attn_terms[0], ("dp", "seq"), scatter_dimension=0, tiled=True),
            lax.psum_scatter(attn_terms[1], ("dp", "seq"), scatter_dimension=0, tiled=True),
            lax.psum_scatter(attn_terms[2], ("dp", "seq"), scatter_dimension=0, tiled=True),
            lax.psum_scatter(attn_terms[3], ("dp", "seq"), scatter_dimension=0, tiled=True),
            lax.psum_scatter(attn_terms[4], ("dp", "seq"), scatter_dimension=0, tiled=True),
        )
        mlp_shares = (
            lax.psum_scatter(mlp_terms[0], ("dp", "seq"), scatter_dimension=0, tiled=True),
            lax.psum_scatter(mlp_terms[1], ("dp", "seq"), scatter_dimension=0, tiled=True),
            lax.psum_scatter(mlp_terms[2], ("dp", "seq"), scatter_dimension=0, tiled=True),
            lax.psum_scatter(mlp_terms[3], ("dp", "seq"), scatter_dimension=0, tiled=True),
        )
        attn_total = add_up(attn_total, attn_shares)
        mlp_total = add_up(mlp_total, mlp_shares)
    return (
        jnp.stack(outputs),
        jnp.stack(grads_in),
        attn_total[0],
        attn_total[1],
        attn_total[2],
        attn_total[3],
        attn_total[4],
        mlp_total[0],
        mlp_total[1],
        mlp_total[2],
        mlp_total[3],
    )


def gathered_weights(mesh):
    return jax.shard_map(
        gathered_weights_layer,
        mesh=mesh,
        in_specs=(
            P("dp", "seq", None),
            P("dp", "seq"),
            P("dp", "seq"),
            P(("dp", "seq")),
            P(("dp", "seq"), None),
            P(("dp", "seq"), None),
            P(("dp", "seq"), None),
            P(("dp", "seq"), None),
            P(("dp", "seq")),
            P(("dp", "seq"), None),
            P(("dp", "seq"), None),
            P(("dp", "seq"), None),
            P("dp", "seq", None),
        ),
        out_specs=(
            P("dp", "seq", None),
            P("dp", "seq", None),
            P(("dp", "seq")),
            P(("dp", "seq"), None),
            P(("dp", "seq"), None),
            P(("dp", "seq"), None),
            P(("dp", "seq"), None),
            P(("dp", "seq")),
            P(("dp", "seq"), None),
            P(("dp", "seq"), None),
            P(("dp", "seq"), None),
        ),
        check_vma=False,
    )


def swap(values, axis_name, size, step):
    return lax.ppermute(values, axis_name, [(i, i ^ step) for i in range(size)])


def plane_pieces(values, dp):
    return [values] + [swap(values, "dp", dp, k) for k in range(1, dp)]


NEGATIVE = -1e30
VMEM_LIMIT = 56 * 1024 * 1024
MESH = pl.DeviceIdType.MESH
LIGHT = pl.CostEstimate(flops=0, bytes_accessed=1024, transcendentals=0)


def contract_last(left, right):
    return lax.dot_general(
        left, right, (((1,), (1,)), ((), ())), preferred_element_type=jnp.float32
    )


def multiply(left, right):
    return jnp.dot(left, right, preferred_element_type=jnp.float32)


def spread_keys(block, heads):
    half = block.shape[0] // 2
    return jnp.concatenate([block[:half]] * heads + [block[half:]] * heads, axis=0)


def fold_keys(block, heads):
    half = block.shape[0] // (2 * heads)
    first = sum(block[h * half : (h + 1) * half] for h in range(heads))
    rest = range(heads, 2 * heads)
    return jnp.concatenate([first, sum(block[h * half : (h + 1) * half] for h in rest)], axis=0)


def fold_values(block, heads):
    size = block.shape[0] // heads
    return sum(block[h * size : (h + 1) * size] for h in range(heads))


def turned_head(shape, dim, heads):
    index = lax.broadcasted_iota(jnp.int32, shape, dim)
    return lax.rem(index, shape[dim] // 2) // (shape[dim] // 2 // heads)


def plain_head(shape, dim, heads):
    index = lax.broadcasted_iota(jnp.int32, shape, dim)
    return index // (shape[dim] // heads)


def per_head(values, owner, heads, axis):
    zero = jnp.zeros_like(values)
    return jnp.concatenate([jnp.where(owner == h, values, zero) for h in range(heads)], axis=axis)


def join_heads(stacked, owner, heads):
    size = stacked.shape[0] // heads
    return sum(
        jnp.where(owner == h, stacked[h * size : (h + 1) * size], 0.0) for h in range(heads)
    )


def masked(scores, block, start, order_q, heads):
    size = order_q.shape[0]
    order_k = block * size + lax.broadcasted_iota(jnp.int32, (size, size), 1)
    allowed = (order_k >= start) & (order_k <= order_q)
    split = scores.reshape(heads, size, size)
    return jnp.where(allowed[None], split, NEGATIVE).reshape(scores.shape)


def attend_kernel(heads, low_ref, place_ref, offset_ref, q_ref, k_ref, v_ref, out_ref, log_ref, held):
    row = pl.program_id(0)
    place = place_ref[0]
    queries = q_ref[0]
    size = queries.shape[0]
    stacked = per_head(queries, turned_head(queries.shape, 1, heads), heads, 0)
    order_q = place * size + lax.broadcasted_iota(jnp.int32, (size, 1), 0)
    start = order_q - offset_ref[0][:, :1]

    def score(block, highest):
        scores = multiply(stacked, spread_keys(k_ref[block, 0], heads))
        scores = masked(scores, block, start, order_q, heads)
        held[block] = scores
        return jnp.maximum(highest, jnp.max(scores, axis=1, keepdims=True))

    highest = lax.fori_loop(
        low_ref[row], place + 1, score, jnp.full((heads * size, 1), NEGATIVE, jnp.float32)
    )

    def mix(block, carry):
        total, context = carry
        powers = jnp.exp(held[block] - highest)
        total = total + jnp.sum(powers, axis=1, keepdims=True)
        spread = jnp.concatenate([v_ref[block, 0]] * heads, axis=0)
        return total, context + contract_last(powers.astype(jnp.bfloat16), spread)

    total, context = lax.fori_loop(
        low_ref[row],
        place + 1,
        mix,
        (
            jnp.zeros((heads * size, 1), jnp.float32),
            jnp.zeros((heads * size, queries.shape[1]), jnp.float32),
        ),
    )
    owner = plain_head(queries.shape, 1, heads)
    out_ref[0] = join_heads(context / total, owner, heads).astype(jnp.bfloat16)
    log_ref[0] = highest + jnp.log(total)


def attend_back_kernel(
    heads,
    low_ref,
    place_ref,
    offset_ref,
    q_ref,
    k_ref,
    v_ref,
    context_ref,
    log_ref,
    grad_ref,
    cosine_ref,
    sine_ref,
    grad_q_ref,
    grad_k_ref,
    grad_v_ref,
):
    row = pl.program_id(0)
    place = place_ref[0]
    queries = q_ref[0]
    grads = grad_ref[0]
    size = queries.shape[0]
    turned = turned_head(queries.shape, 1, heads)
    plain = plain_head(queries.shape, 1, heads)
    stacked = per_head(queries, turned, heads, 0)
    stacked_grad = per_head(grads, plain, heads, 0)
    flipped = per_head(queries.T, turned_head(queries.shape, 0, heads), heads, 1)
    flipped_grad = per_head(grads.T, plain_head(queries.shape, 0, heads), heads, 1)
    product = grads.astype(jnp.float32) * context_ref[0].astype(jnp.float32)
    inner = jnp.sum(per_head(product, plain, heads, 0), axis=1, keepdims=True)
    logs = log_ref[0]
    order_q = place * size + lax.broadcasted_iota(jnp.int32, (size, 1), 0)
    start = order_q - offset_ref[0][:, :1]
    grad_k_ref[...] = jnp.zeros_like(grad_k_ref)
    grad_v_ref[...] = jnp.zeros_like(grad_v_ref)

    def step(block, grad_q):
        keys = spread_keys(k_ref[block, 0], heads)
        spread = jnp.concatenate([v_ref[block, 0]] * heads, axis=0)
        scores = masked(multiply(stacked, keys), block, start, order_q, heads)
        probs = jnp.exp(scores - logs)
        grad_probs = multiply(stacked_grad, spread)
        grad_scores = (probs * (grad_probs - inner)).astype(jnp.bfloat16)
        grad_k = fold_keys(multiply(flipped, grad_scores), heads)
        grad_v = fold_values(multiply(flipped_grad, probs.astype(jnp.bfloat16)), heads)
        grad_k_ref[block, 0] = grad_k.astype(jnp.bfloat16)
        grad_v_ref[block, 0] = grad_v.astype(jnp.bfloat16)
        return grad_q + contract_last(grad_scores, keys)

    grad_q = lax.fori_loop(
        low_ref[row],
        place + 1,
        step,
        jnp.zeros((heads * size, queries.shape[1]), jnp.float32),
    )
    grad_q = join_heads(grad_q, turned, heads) * HD ** (-0.5)
    half = grad_q.shape[1] // 2
    first, second = grad_q[:, :half], grad_q[:, half:]
    cosine, sine = cosine_ref[0], sine_ref[0]
    grad_q_ref[0, :, :half] = (first * cosine + second * sine).astype(jnp.bfloat16)
    grad_q_ref[0, :, half:] = (second * cosine - first * sine).astype(jnp.bfloat16)


def row_spec(*shape):
    return pl.BlockSpec((1,) + shape, lambda row, low, place: (row,) + (0,) * len(shape))


def line_spec(depth, *shape):
    return pl.BlockSpec((depth, 1) + shape, lambda row, low, place: (0, row) + (0,) * len(shape))


def pair_spec(which, depth, *shape):
    return pl.BlockSpec(
        (None, depth, 1) + shape, lambda row, low, place: (which, 0, row) + (0,) * len(shape)
    )


def attend(low, place, offsets, queries, lines):
    rows, size, width = queries.shape
    depth, features = lines.shape[1], lines.shape[3]
    heads = width // features
    return pl.pallas_call(
        functools.partial(attend_kernel, heads),
        out_shape=(
            jax.ShapeDtypeStruct((rows, size, width), jnp.bfloat16),
            jax.ShapeDtypeStruct((rows, heads * size, 1), jnp.float32),
        ),
        grid_spec=pltpu.PrefetchScalarGridSpec(
            num_scalar_prefetch=2,
            grid=(rows,),
            in_specs=[
                row_spec(size, offsets.shape[2]),
                row_spec(size, width),
                pair_spec(0, depth, features, size),
                pair_spec(1, depth, features, size),
            ],
            out_specs=[row_spec(size, width), row_spec(heads * size, 1)],
            scratch_shapes=[pltpu.VMEM((depth, heads * size, size), jnp.float32)],
        ),
        compiler_params=pltpu.CompilerParams(vmem_limit_bytes=VMEM_LIMIT),
        cost_estimate=LIGHT,
        name="attend",
    )(low, place, offsets, queries, lines, lines)


def attend_back(low, place, offsets, queries, lines, context, logs, grads, cosine, sine):
    rows, size, width = queries.shape
    depth, features = lines.shape[1], lines.shape[3]
    heads = width // features
    line = line_spec(depth, features, size)
    whole = row_spec(size, width)
    half = row_spec(size, width // 2)
    return pl.pallas_call(
        functools.partial(attend_back_kernel, heads),
        out_shape=(
            jax.ShapeDtypeStruct((rows, size, width), jnp.bfloat16),
            jax.ShapeDtypeStruct(lines.shape[1:], jnp.bfloat16),
            jax.ShapeDtypeStruct(lines.shape[1:], jnp.bfloat16),
        ),
        grid_spec=pltpu.PrefetchScalarGridSpec(
            num_scalar_prefetch=2,
            grid=(rows,),
            in_specs=[
                row_spec(size, offsets.shape[2]),
                whole,
                pair_spec(0, depth, features, size),
                pair_spec(1, depth, features, size),
                whole,
                row_spec(heads * size, 1),
                whole,
                half,
                half,
            ],
            out_specs=[whole, line, line],
        ),
        compiler_params=pltpu.CompilerParams(vmem_limit_bytes=VMEM_LIMIT),
        cost_estimate=LIGHT,
        name="attend_back",
    )(low, place, offsets, queries, lines, lines, context, logs, grads, cosine, sine)


def team_places():
    data = lax.axis_index("dp")
    place = lax.axis_index("z")
    core = lax.axis_index("core")

    def peer(k):
        high = lax.rem(data // 2 + k // 2, 2)
        low = lax.rem(lax.rem(data, 2) + lax.rem(k, 2), 2)
        return (high * 2 + low, place, core)

    return data, place, core, peer, (data, place, 1 - core)


def greet(targets):
    barrier = pltpu.get_barrier_semaphore()
    for target in targets:
        pl.semaphore_signal(barrier, inc=1, device_id=target, device_id_type=MESH)
    pl.semaphore_wait(barrier, len(targets))


def send(source, target, send_sem, got_sem, device):
    return pltpu.make_async_remote_copy(
        src_ref=source,
        dst_ref=target,
        send_sem=send_sem,
        recv_sem=got_sem,
        device_id=device,
        device_id_type=MESH,
    )


def sum_scratch(dp, size, width):
    dma = pltpu.SemaphoreType.DMA
    block = pltpu.VMEM((dp, size, width), jnp.bfloat16)
    return [
        block,
        block,
        pltpu.VMEM((2, size // 2, width), jnp.bfloat16),
        pltpu.VMEM((2, size, width), jnp.bfloat16),
        dma((dp,)),
        dma((dp,)),
        dma((2,)),
        dma((2,)),
        dma((2, 2)),
        dma((2, 2)),
    ]


def plane_sum(dp, product, total_ref, scratch):
    side, got, relay, far, side_send, side_got, relay_send, relay_got, far_send, far_got = scratch
    f32, bf16 = jnp.float32, jnp.bfloat16
    _, _, core, peer, twin = team_places()
    size = side.shape[1]
    half = size // 2

    def rows(part):
        return pl.ds(part * half, half)

    def side_copy(k):
        return send(side.at[k], got.at[k], side_send.at[k], side_got.at[k], twin)

    def relay_copy(part):
        return send(
            got.at[3, rows(part)],
            relay.at[part],
            relay_send.at[part],
            relay_got.at[part],
            peer(1 + part),
        )

    def far_copy(which, part):
        return send(
            got.at[1 + which, rows(part)],
            far.at[which, rows(part)],
            far_send.at[which, part],
            far_got.at[which, part],
            peer(1 + which),
        )

    def one(step, carry):
        k = dp - 1 - step
        side[k] = product(k, 1 - core, 0).astype(bf16)
        side_copy(k).start()
        total = product(k, core, 1)
        side_copy(k).wait_recv()
        total = total + got[k].astype(f32)

        @pl.when(k == 0)
        def _():
            total_ref[...] = total

        @pl.when(k > 0)
        def _():
            got[k] = total.astype(bf16)

        @pl.when(k == 3)
        def _():
            relay_copy(0).start()
            relay_copy(1).start()

        @pl.when(k == 2)
        def _():
            far_copy(1, 1).start()

        @pl.when(k == 1)
        def _():
            far_copy(0, 0).start()

        return carry

    lax.fori_loop(0, dp, one, 0)
    for part in range(2):
        which = 1 - part
        relay_copy(part).wait_recv()
        total = got[1 + which, rows(part)].astype(f32) + relay[part].astype(f32)
        got[1 + which, rows(part)] = total.astype(bf16)
        far_copy(which, part).start()

    def complete():
        for which, part in ((0, 0), (1, 1), (0, 1), (1, 0)):
            far_copy(which, part).wait_recv()
            total_ref[rows(part)] += far[which, rows(part)].astype(f32)
        for part in range(2):
            relay_copy(part).wait_send()
            for which in range(2):
                far_copy(which, part).wait_send()
        for k in range(dp):
            side_copy(k).wait_send()

    return complete


def mlp_forward_kernel(dp, depth, x_hbm, wide_hbm, *refs):
    cot_hbms = refs[:dp]
    tokens_hbm, cots_hbm, hidden_hbm, slope_hbm, active_hbm, down_grad_hbm = refs[dp : dp + 6]
    (
        tokens,
        cots,
        gates,
        ups,
        hidden_t,
        chunk,
        tile_out,
        load_sem,
        cots_sem,
        near_send,
        near_got,
        side_send,
        side_got,
        pass_send,
        pass_got,
        tokens_sem,
        chunk_sem,
        tile_sem,
        twin_send,
        twin_got,
    ) = refs[dp + 6 :]
    bf16 = jnp.bfloat16
    _, _, core, peer, twin = team_places()
    size, width = x_hbm.shape
    half = size // 2
    loads = [pltpu.make_async_copy(x_hbm, tokens.at[0, core], load_sem.at[0])]
    for z in range(depth):
        for which, target in ((0, gates), (1, ups)):
            sem = load_sem.at[1 + 2 * z + which]
            loads.append(pltpu.make_async_copy(wide_hbm.at[z, :, :, which], target.at[:, z], sem))
    cot_loads = []
    for k in range(dp):
        sem = load_sem.at[2 * depth + 1 + k]
        cot_loads.append(pltpu.make_async_copy(cot_hbms[k], cots.at[k, core], sem))
    for load in loads + cot_loads:
        load.start()
    greet([peer(k) for k in range(1, 3)] + [twin])
    loads[0].wait()

    def near_copy(k):
        return send(
            tokens.at[0, core], tokens.at[k, core], near_send.at[k], near_got.at[k], peer(k)
        )

    def pass_copy(part):
        spot = pl.ds(part * half, half)
        return send(
            tokens.at[1 + part, core, spot],
            tokens.at[3, core, spot],
            pass_send.at[part],
            pass_got.at[part],
            peer(2 - part),
        )

    def side_copy(k):
        block = tokens.at[k, core]
        return send(block, block, side_send.at[k], side_got.at[k], twin)

    def side_arrival(k):
        block = tokens.at[k, 1 - core]
        return send(block, block, side_send.at[k], side_got.at[k], twin)

    def twin_copy(k):
        block = cots.at[k, core]
        return send(block, block, twin_send.at[k], twin_got.at[k], twin)

    def twin_arrival(k):
        block = cots.at[k, 1 - core]
        return send(block, block, twin_send.at[k], twin_got.at[k], twin)

    def tokens_out(k, e):
        return pltpu.make_async_copy(tokens.at[k, e], tokens_hbm.at[k, e], tokens_sem.at[k, e])

    def chunk_out(k, e, slot):
        return [
            pltpu.make_async_copy(chunk.at[slot, i], target.at[k, e], chunk_sem.at[slot, i])
            for i, target in enumerate((hidden_hbm, slope_hbm, active_hbm))
        ]

    near_copy(1).start()
    near_copy(2).start()
    side_copy(0).start()
    for load in loads[1:]:
        load.wait()

    def process(k, e, slot, reuse):
        row = tokens[k, e]
        tokens_out(k, e).start()
        gate = multiply(row, gates[...].reshape(width, -1))
        up = multiply(row, ups[...].reshape(width, -1))
        sigma = 1.0 / (1.0 + jnp.exp(-gate))
        active = gate * sigma
        hidden = (active * up).astype(bf16)
        if reuse:
            for copy in chunk_out(k, e, slot):
                copy.wait()
        chunk[slot, 0] = hidden
        chunk[slot, 1] = (up * sigma * (1.0 + gate * (1.0 - sigma))).astype(bf16)
        chunk[slot, 2] = active.astype(bf16)
        for copy in chunk_out(k, e, slot):
            copy.start()
        spot = pl.ds(pl.multiple_of((k * 2 + e) * size, size), size)
        hidden_t[:, spot] = hidden.T

    process(0, core, 0, False)
    side_arrival(0).wait_recv()
    process(0, 1 - core, 1, False)
    for k in range(dp):
        cot_loads[k].wait()
        twin_copy(k).start()
    for k in range(1, 3):
        near_copy(k).wait_recv()
        pass_copy(k - 1).start()
        side_copy(k).start()
    for k in range(dp):
        twin_arrival(k).wait_recv()
    cots_out = pltpu.make_async_copy(cots, cots_hbm, cots_sem)
    cots_out.start()

    def step(k, carry):
        @pl.when(k == 3)
        def _():
            pass_copy(0).wait_recv()
            pass_copy(1).wait_recv()
            side_copy(3).start()

        process(k, core, 0, True)
        side_arrival(k).wait_recv()
        process(k, 1 - core, 1, True)
        return carry

    lax.fori_loop(1, dp, step, 0)

    def tile_copy(j, slot):
        spot = pl.ds(pl.multiple_of(j * 256, 256), 256)
        return pltpu.make_async_copy(tile_out.at[slot], down_grad_hbm.at[:, spot], tile_sem.at[slot])

    count = width // 256

    def tile(j, carry):
        slot = lax.rem(j, 2)

        @pl.when(j > 1)
        def _():
            tile_copy(j - 2, slot).wait()

        spot = pl.ds(pl.multiple_of(j * 256, 256), 256)
        columns = cots[:, :, :, spot].reshape(-1, 256)
        tile_out[slot] = multiply(hidden_t[...], columns).astype(bf16)
        tile_copy(j, slot).start()
        return carry

    lax.fori_loop(0, count, tile, 0)
    for j in (count - 2, count - 1):
        tile_copy(j, j % 2).wait()
    cots_out.wait()
    for slot, e in ((0, core), (1, 1 - core)):
        for copy in chunk_out(dp - 1, e, slot):
            copy.wait()
    for k in range(dp):
        for e in range(2):
            tokens_out(k, e).wait()
        side_copy(k).wait_send()
        twin_copy(k).wait_send()
    for k in range(1, 3):
        near_copy(k).wait_send()
        pass_copy(k - 1).wait_send()


def mlp_forward(x_own, wide, cots):
    depth, dp = wide.shape[:2]
    size, width = x_own.shape
    inner = wide.shape[-1]
    bf16 = jnp.bfloat16
    hbm = pl.BlockSpec(memory_space=pl.ANY)
    dma = pltpu.SemaphoreType.DMA
    weight = pltpu.VMEM((dp, depth) + wide.shape[2:3] + wide.shape[4:], bf16)
    whole = jax.ShapeDtypeStruct((dp, 2, size, width), bf16)
    thin = jax.ShapeDtypeStruct((dp, 2, size, inner), bf16)
    return pl.pallas_call(
        functools.partial(mlp_forward_kernel, dp, depth),
        out_shape=(whole, whole, thin, thin, thin, jax.ShapeDtypeStruct((inner, width), bf16)),
        in_specs=[hbm] * (2 + dp),
        out_specs=(hbm,) * 6,
        scratch_shapes=[
            pltpu.VMEM((dp, 2, size, width), bf16),
            pltpu.VMEM((dp, 2, size, width), bf16),
            weight,
            weight,
            pltpu.VMEM((inner, 2 * dp * size), bf16),
            pltpu.VMEM((2, 3, size, inner), bf16),
            pltpu.VMEM((2, inner, 256), bf16),
            dma((2 * depth + 1 + dp,)),
            dma,
            dma((dp,)),
            dma((dp,)),
            dma((dp,)),
            dma((dp,)),
            dma((2,)),
            dma((2,)),
            dma((dp, 2)),
            dma((2, 3)),
            dma((2,)),
            dma((dp,)),
            dma((dp,)),
        ],
        compiler_params=pltpu.CompilerParams(
            collective_id=1, has_side_effects=True, vmem_limit_bytes=VMEM_LIMIT
        ),
        cost_estimate=LIGHT,
        name="mlp_forward",
    )(x_own, wide, *cots)


def mlp_backward_kernel(
    dp,
    depth,
    tokens_hbm,
    cots_hbm,
    hidden_hbm,
    slope_hbm,
    active_hbm,
    wide_hbm,
    down_hbm,
    grad_ref,
    part_hbm,
    wide_grad_hbm,
    tokens,
    gates,
    ups,
    downs,
    gate_t,
    up_t,
    cot_slots,
    chunk,
    part_out,
    part_side,
    tile_out,
    load_sem,
    slot_sem,
    part_sem,
    part_send,
    part_got,
    tile_sem,
    *sum_refs,
):
    bf16 = jnp.bfloat16
    _, _, core, peer, twin = team_places()
    size, width = grad_ref.shape
    loads = [pltpu.make_async_copy(down_hbm, downs, load_sem.at[0])]
    for z in range(depth):
        for which, target in ((0, gates), (1, ups)):
            sem = load_sem.at[1 + 2 * z + which]
            loads.append(pltpu.make_async_copy(wide_hbm.at[z, :, :, which], target.at[:, z], sem))
    tokens_load = pltpu.make_async_copy(tokens_hbm, tokens, load_sem.at[2 * depth + 1])

    def slot_loads(k, e, slot):
        copies = [pltpu.make_async_copy(cots_hbm.at[k, e], cot_slots.at[slot], slot_sem.at[slot, 3])]
        for i, source in enumerate((hidden_hbm, slope_hbm, active_hbm)):
            copies.append(
                pltpu.make_async_copy(source.at[k, e], chunk.at[slot, i], slot_sem.at[slot, i])
            )
        return copies

    for copy in slot_loads(dp - 1, 1 - core, 0):
        copy.start()
    for load in loads:
        load.start()
    greet([peer(k) for k in range(1, 3)] + [twin])
    for load in loads:
        load.wait()
    tokens_load.start()

    def part_copy(k):
        return pltpu.make_async_copy(part_out.at[1], part_hbm.at[k], part_sem)

    def part_side_copy(k):
        return send(part_out.at[0], part_side.at[k], part_send.at[k], part_got.at[k], twin)

    def product(k, e, turn):
        slot = turn
        for copy in slot_loads(k, e, slot):
            copy.wait()
        if turn == 0:
            for copy in slot_loads(k, core, 1):
                copy.start()
        else:

            @pl.when(k > 0)
            def _():
                for copy in slot_loads(k - 1, 1 - core, 0):
                    copy.start()

        grad_hid = contract_last(cot_slots[slot], downs[...])
        grad_gate = (grad_hid * chunk[slot, 1].astype(jnp.float32)).astype(bf16)
        grad_up = (grad_hid * chunk[slot, 2].astype(jnp.float32)).astype(bf16)
        spot = pl.ds(pl.multiple_of((k * 2 + e) * size, size), size)
        gate_t[:, spot] = grad_gate.T
        up_t[:, spot] = grad_up.T
        terms = multiply(chunk[slot, 0], downs[...])
        if turn == 0:

            @pl.when(k < dp - 1)
            def _():
                part_side_copy(k + 1).wait_send()

            part_out[0] = terms.astype(bf16)
            part_side_copy(k).start()
        else:

            @pl.when(k < dp - 1)
            def _():
                part_copy(k + 1).wait()

            part_side_copy(k).wait_recv()
            part_out[1] = (terms + part_side[k].astype(jnp.float32)).astype(bf16)
            part_copy(k).start()
        return contract_last(grad_gate, gates[...].reshape(width, -1)) + contract_last(
            grad_up, ups[...].reshape(width, -1)
        )

    complete = plane_sum(dp, product, grad_ref, sum_refs)
    tokens_load.wait()
    block = 256
    count = width // block

    def tile_copies(which, j, slot):
        per = depth * 128 // block
        return [
            pltpu.make_async_copy(
                tile_out.at[slot, :, pl.ds(i * 128, 128)],
                wide_grad_hbm.at[lax.rem(j, per) * (block // 128) + i, which, j // per],
                tile_sem.at[slot, i],
            )
            for i in range(block // 128)
        ]

    for which, left in ((0, gate_t), (1, up_t)):

        def tile(j, carry, which=which, left=left):
            slot = lax.rem(j, 2)

            @pl.when(j > 1)
            def _():
                for copy in tile_copies(which, j - 2, slot):
                    copy.wait()

            spot = pl.ds(pl.multiple_of(j * block, block), block)
            columns = tokens[:, :, :, spot].reshape(-1, block)
            tile_out[slot] = multiply(left[...], columns).astype(bf16)
            for copy in tile_copies(which, j, slot):
                copy.start()
            return carry

        lax.fori_loop(0, count, tile, 0)
        for j in (count - 2, count - 1):
            for copy in tile_copies(which, j, j % 2):
                copy.wait()
    complete()
    part_side_copy(0).wait_send()
    part_copy(0).wait()


def mlp_backward(tokens, cots, hidden, slope, active, wide, down):
    depth, dp = wide.shape[:2]
    size, width = tokens.shape[2:]
    inner = wide.shape[-1]
    f32, bf16 = jnp.float32, jnp.bfloat16
    hbm = pl.BlockSpec(memory_space=pl.ANY)
    dma = pltpu.SemaphoreType.DMA
    weight = pltpu.VMEM((dp, depth) + wide.shape[2:3] + wide.shape[4:], bf16)
    turned = pltpu.VMEM((inner, 2 * dp * size), bf16)
    return pl.pallas_call(
        functools.partial(mlp_backward_kernel, dp, depth),
        out_shape=(
            jax.ShapeDtypeStruct((size, width), f32),
            jax.ShapeDtypeStruct((dp, size, width), bf16),
            jax.ShapeDtypeStruct((depth, 2, dp, inner, width // (depth * dp)), bf16),
        ),
        in_specs=[hbm] * 7,
        out_specs=(pl.BlockSpec(memory_space=pltpu.VMEM), hbm, hbm),
        scratch_shapes=[
            pltpu.VMEM((dp, 2, size, width), bf16),
            weight,
            weight,
            pltpu.VMEM((inner, width), bf16),
            turned,
            turned,
            pltpu.VMEM((2, size, width), bf16),
            pltpu.VMEM((2, 3, size, inner), bf16),
            pltpu.VMEM((2, size, width), bf16),
            pltpu.VMEM((dp, size, width), bf16),
            pltpu.VMEM((2, inner, 256), bf16),
            dma((2 * depth + 2,)),
            dma((2, 4)),
            dma,
            dma((dp,)),
            dma((dp,)),
            dma((2, 2)),
        ]
        + sum_scratch(dp, size, width),
        compiler_params=pltpu.CompilerParams(
            collective_id=6, has_side_effects=True, vmem_limit_bytes=60 * 1024 * 1024
        ),
        cost_estimate=LIGHT,
        name="mlp_backward",
    )(tokens, cots, hidden, slope, active, wide, down)


def attend_sum_kernel(
    dp, rows, context_ref, weight_ref, own_ref, gain_ref, middle_ref, normed_ref, *scratch
):
    _, _, _, peer, twin = team_places()
    length = own_ref.shape[1]
    size, width = middle_ref.shape
    greet([peer(k) for k in range(1, 3)] + [twin])

    def product(k, e, turn):
        spot = pl.ds(pl.multiple_of(e * length, length), length)
        block = context_ref[pl.ds(k * rows, rows), spot].reshape(size, -1)
        return multiply(block, weight_ref[...])

    plane_sum(dp, product, middle_ref, scratch)()
    middle = middle_ref[...] + own_ref[...].reshape(size, width).astype(jnp.float32)
    middle_ref[...] = middle
    factor = lax.rsqrt(jnp.mean(middle * middle, axis=-1, keepdims=True) + EPSILON)
    normed_ref[...] = (middle * factor * gain_ref[1:2].astype(jnp.float32)).astype(jnp.bfloat16)


def attend_sum(dp, context, weight, own, gain):
    rows, length, width = own.shape
    size = rows * length
    vmem = pl.BlockSpec(memory_space=pltpu.VMEM)
    return pl.pallas_call(
        functools.partial(attend_sum_kernel, dp, rows),
        out_shape=(
            jax.ShapeDtypeStruct((size, width), jnp.float32),
            jax.ShapeDtypeStruct((size, width), jnp.bfloat16),
        ),
        in_specs=[vmem] * 4,
        out_specs=(vmem, vmem),
        scratch_shapes=sum_scratch(dp, size, width),
        compiler_params=pltpu.CompilerParams(
            collective_id=4, has_side_effects=True, vmem_limit_bytes=VMEM_LIMIT
        ),
        cost_estimate=LIGHT,
        name="attend_sum",
    )(context, weight, own, gain)


def middle_back_kernel(
    dp,
    rows,
    grad_ref,
    middle_ref,
    cot_ref,
    gain_ref,
    context_ref,
    weight_ref,
    grad_middle_ref,
    grad_context_ref,
    weight_grad_ref,
    tokens,
    context_t,
    near_send,
    near_got,
    side_send,
    side_got,
    pass_send,
    pass_got,
):
    f32, bf16 = jnp.float32, jnp.bfloat16
    _, _, core, peer, twin = team_places()
    size, width = grad_ref.shape
    length = size // rows
    half = size // 2
    greet([peer(k) for k in range(1, 3)] + [twin])
    middle = middle_ref[...]
    factor = lax.rsqrt(jnp.mean(middle * middle, axis=-1, keepdims=True) + EPSILON)
    inner = grad_ref[...] * gain_ref[1:2].astype(f32)
    mean = jnp.mean(inner * middle, axis=-1, keepdims=True)
    total = cot_ref[...].astype(f32) + factor * inner - factor * factor * factor * middle * mean
    grad_middle_ref[...] = total
    tokens[0, core] = total.astype(bf16)

    def near_copy(k):
        return send(
            tokens.at[0, core], tokens.at[k, core], near_send.at[k], near_got.at[k], peer(k)
        )

    def pass_copy(part):
        spot = pl.ds(part * half, half)
        return send(
            tokens.at[1 + part, core, spot],
            tokens.at[3, core, spot],
            pass_send.at[part],
            pass_got.at[part],
            peer(2 - part),
        )

    def side_copy(k):
        block = tokens.at[k, core]
        return send(block, block, side_send.at[k], side_got.at[k], twin)

    def side_arrival(k):
        block = tokens.at[k, 1 - core]
        return send(block, block, side_send.at[k], side_got.at[k], twin)

    near_copy(1).start()
    near_copy(2).start()
    side_copy(0).start()
    for k in range(dp):
        for e in range(2):
            for r in range(rows):
                block = context_ref[k * rows + r, e * length : (e + 1) * length]
                spot = pl.ds(((k * 2 + e) * rows + r) * length, length)
                context_t[:, spot] = block.T

    def process(k, e):
        block = contract_last(tokens[k, e], weight_ref[...]).astype(bf16)
        spot = pl.ds(pl.multiple_of(e * length, length), length)
        grad_context_ref[pl.ds(k * rows, rows), spot] = block.reshape(rows, length, -1)

    process(0, core)
    side_arrival(0).wait_recv()
    process(0, 1 - core)
    for k in range(1, 3):
        near_copy(k).wait_recv()
        pass_copy(k - 1).start()
        side_copy(k).start()

    def step(k, carry):
        @pl.when(k == 3)
        def _():
            pass_copy(0).wait_recv()
            pass_copy(1).wait_recv()
            side_copy(3).start()

        process(k, core)
        side_arrival(k).wait_recv()
        process(k, 1 - core)
        return carry

    lax.fori_loop(1, dp, step, 0)

    def tile(j, carry):
        spot = pl.ds(pl.multiple_of(j * 256, 256), 256)
        columns = tokens[:, :, :, spot].reshape(-1, 256)
        weight_grad_ref[:, spot] = multiply(context_t[...], columns).astype(bf16)
        return carry

    lax.fori_loop(0, width // 256, tile, 0)
    for k in range(1, 3):
        near_copy(k).wait_send()
        pass_copy(k - 1).wait_send()
    for k in range(dp):
        side_copy(k).wait_send()


def middle_back(dp, rows, grad, middle, cot, gain, context, weight):
    f32, bf16 = jnp.float32, jnp.bfloat16
    size, width = grad.shape
    vmem = pl.BlockSpec(memory_space=pltpu.VMEM)
    dma = pltpu.SemaphoreType.DMA
    return pl.pallas_call(
        functools.partial(middle_back_kernel, dp, rows),
        out_shape=(
            jax.ShapeDtypeStruct((size, width), f32),
            jax.ShapeDtypeStruct(context.shape, bf16),
            jax.ShapeDtypeStruct(weight.shape, bf16),
        ),
        in_specs=[vmem] * 6,
        out_specs=(vmem, vmem, vmem),
        scratch_shapes=[
            pltpu.VMEM((dp, 2, size, width), bf16),
            pltpu.VMEM((weight.shape[0], 2 * dp * size), bf16),
            dma((dp,)),
            dma((dp,)),
            dma((dp,)),
            dma((dp,)),
            dma((2,)),
            dma((2,)),
        ],
        compiler_params=pltpu.CompilerParams(
            collective_id=5, has_side_effects=True, vmem_limit_bytes=VMEM_LIMIT
        ),
        cost_estimate=LIGHT,
        name="middle_back",
    )(grad, middle, cot, gain, context, weight)


def open_kernel(
    dp,
    depth,
    query_ref,
    key_ref,
    value_ref,
    attn_gain_ref,
    mlp_gain_ref,
    gate_ref,
    up_ref,
    places_ref,
    own_ref,
    attn_hbm,
    wide_hbm,
    places_hbm,
    near_hbm,
    attn_blocks,
    wide_blocks,
    local_sem,
    attn_send,
    attn_got,
    wide_send,
    wide_got,
    places_send,
    places_got,
    line_send,
    line_got,
    near_send,
    near_got,
    pass_send,
    pass_got,
):
    data, place, core, peer, twin = team_places()
    part = query_ref.shape[0]
    half = HD // 2
    count = wide_blocks.shape[3] // depth
    side = depth * half
    middle = own_ref.shape[0] // 2
    attn_blocks[...] = jnp.zeros_like(attn_blocks)
    for d in range(dp):
        for c in range(2):
            team = 2 * d + c
            for z in range(depth):
                owner = (d * depth + z) * 2 + c
                for h in range(2):
                    spot = owner * HD + h * half
                    attn_blocks[team, :part, h * side + z * half : h * side + (z + 1) * half] = (
                        query_ref[:, spot : spot + half]
                    )
            pair = key_ref if c == 0 else value_ref
            attn_blocks[team, :part, 2 * side :] = pair[:, d * HD : (d + 1) * HD]
            attn_blocks[team, part : part + 1, :part] = attn_gain_ref[...]
            attn_blocks[team, part + 1 : part + 2, :part] = mlp_gain_ref[...]

    def device(k, other):
        return (peer(k)[0], place, 1 - core if other else core)

    def number(k, other):
        return 2 * peer(k)[0] + (1 - core if other else core)

    pairs = [(k, other) for k in range(dp) for other in range(2) if k or other]
    others = [(data, lax.rem(place + step, depth), core) for step in range(1, depth)]
    greet([device(k, other) for k, other in pairs] + others)

    def attn_copy(k, other):
        return send(
            attn_blocks.at[number(k, other)],
            attn_hbm.at[place, data, core],
            attn_send.at[k, other],
            attn_got.at[k, other],
            device(k, other),
        )

    def wide_copy(k, other):
        return send(
            wide_blocks.at[number(k, other)],
            wide_hbm.at[data, core],
            wide_send.at[k, other],
            wide_got.at[k, other],
            device(k, other),
        )

    def places_copy(k, other):
        return send(
            places_ref,
            places_hbm.at[k, core],
            places_send.at[k, other],
            places_got.at[k, other],
            device(k, other),
        )

    def arrival(target, send_sem, got_sem):
        return send(target, target, send_sem, got_sem, twin)

    def near_copy(k):
        return send(own_ref, near_hbm.at[k], near_send.at[k], near_got.at[k], peer(k))

    def pass_copy(which):
        spot = pl.ds(which * middle, middle)
        return send(
            near_hbm.at[1 + which, spot],
            near_hbm.at[3, spot],
            pass_send.at[which],
            pass_got.at[which],
            peer(2 - which),
        )

    def line_copy(z):
        return send(
            attn_hbm.at[place],
            attn_hbm.at[place],
            line_send.at[z],
            line_got.at[place],
            (data, z, core),
        )

    for k, other in pairs:
        attn_copy(k, other).start()
    for k, other in pairs:
        places_copy(k, other).start()
    near_copy(1).start()
    near_copy(2).start()
    locals_ = [
        pltpu.make_async_copy(
            attn_blocks.at[2 * data + core], attn_hbm.at[place, data, core], local_sem.at[0]
        ),
        pltpu.make_async_copy(places_ref, places_hbm.at[0, core], local_sem.at[1]),
        pltpu.make_async_copy(own_ref, near_hbm.at[0], local_sem.at[2]),
    ]
    for copy in locals_:
        copy.start()
    for d in range(dp):
        for c in range(2):
            for z in range(depth):
                owner = (d * depth + z) * 2 + c
                for which, source in ((0, gate_ref), (1, up_ref)):
                    wide_blocks[2 * d + c, which, :, z * count : (z + 1) * count] = source[
                        :, owner * count : (owner + 1) * count
                    ]
    wide_local = pltpu.make_async_copy(
        wide_blocks.at[2 * data + core], wide_hbm.at[data, core], local_sem.at[3]
    )
    wide_local.start()
    locals_[0].wait()
    for k, other in pairs:
        target = attn_hbm.at[place, peer(k)[0], 1 - core if other else core]
        arrival(target, attn_send.at[k, other], attn_got.at[k, other]).wait_recv()
    for z in range(depth):

        @pl.when(z != place)
        def _(z=z):
            line_copy(z).start()

    for k, other in pairs:
        wide_copy(k, other).start()
    for which in range(2):
        near_copy(1 + which).wait_recv()
        pass_copy(which).start()
    for copy in locals_[1:] + [wide_local]:
        copy.wait()
    for k, other in pairs:
        spot = (peer(k)[0], 1 - core if other else core)
        arrival(wide_hbm.at[spot], wide_send.at[k, other], wide_got.at[k, other]).wait_recv()
        target = places_hbm.at[k, 1 - core if other else core]
        arrival(target, places_send.at[k, other], places_got.at[k, other]).wait_recv()
    for which in range(2):
        pass_copy(which).wait_recv()
        pass_copy(which).wait_send()
        near_copy(1 + which).wait_send()
    for z in range(depth):

        @pl.when(z != place)
        def _(z=z):
            arrival(attn_hbm.at[z], line_send.at[z], line_got.at[z]).wait_recv()
            line_copy(z).wait_send()

    for k, other in pairs:
        attn_copy(k, other).wait_send()
        wide_copy(k, other).wait_send()
        places_copy(k, other).wait_send()


def open_layer(dp, depth, query, key, value, attn_gain, mlp_gain, gate, up, places, own):
    part = query.shape[0]
    inner = gate.shape[1] // (2 * dp)
    columns = depth * HD + HD
    bf16 = jnp.bfloat16
    hbm = pl.BlockSpec(memory_space=pl.ANY)
    vmem = pl.BlockSpec(memory_space=pltpu.VMEM)
    dma = pltpu.SemaphoreType.DMA
    return pl.pallas_call(
        functools.partial(open_kernel, dp, depth),
        out_shape=(
            jax.ShapeDtypeStruct((depth, dp, 2, part + 8, columns), bf16),
            jax.ShapeDtypeStruct((dp, 2, 2, part, inner), bf16),
            jax.ShapeDtypeStruct((dp, 2) + places.shape, places.dtype),
            jax.ShapeDtypeStruct((dp,) + own.shape, bf16),
        ),
        in_specs=[vmem] * 9,
        out_specs=(hbm,) * 4,
        scratch_shapes=[
            pltpu.VMEM((2 * dp, part + 8, columns), bf16),
            pltpu.VMEM((2 * dp, 2, part, inner), bf16),
            dma((4,)),
            dma((dp, 2)),
            dma((dp, 2)),
            dma((dp, 2)),
            dma((dp, 2)),
            dma((dp, 2)),
            dma((dp, 2)),
            dma((depth,)),
            dma((depth,)),
            dma((dp,)),
            dma((dp,)),
            dma((2,)),
            dma((2,)),
        ],
        compiler_params=pltpu.CompilerParams(
            collective_id=7, has_side_effects=True, vmem_limit_bytes=VMEM_LIMIT
        ),
        cost_estimate=LIGHT,
        name="open_layer",
    )(query, key, value, attn_gain[None], mlp_gain[None], gate, up, places, own)


def project_kernel(
    dp,
    depth,
    rows,
    *refs,
):
    pieces, places_ref, freq_ref, freq_pair_ref, weight_hbm = refs[:5]
    query_ref, normed_ref, cosine_ref, sine_ref, cosine_pair_ref, sine_pair_ref = refs[5:11]
    offset_ref, gain_ref, pair_weight_ref, line_hbm = refs[11:15]
    (
        weight,
        gain_blocks,
        pair,
        far_pieces,
        load_sem,
        own_sem,
        line_send,
        line_got,
        side_send,
        side_got,
        twin_send,
        twin_got,
    ) = refs[15:]
    f32, bf16 = jnp.float32, jnp.bfloat16
    data, place, core, peer, twin = team_places()
    length, width = pieces.shape[2:]
    part = weight.shape[3]
    columns = query_ref.shape[2]
    loads = [
        pltpu.make_async_copy(
            weight_hbm.at[z, :, :, pl.ds(0, part)], weight.at[:, z], load_sem.at[z]
        )
        for z in range(depth)
    ]
    for z in range(depth):
        source = weight_hbm.at[z, :, :, pl.ds(part, 8)]
        sem = load_sem.at[depth + z]
        loads.append(pltpu.make_async_copy(source, gain_blocks.at[:, z], sem))
    for load in loads:
        load.start()
    others = [(data, lax.rem(place + step, depth), core) for step in range(1, depth)]
    greet(others + [twin])

    def twin_copy(k):
        return send(pieces.at[k], far_pieces.at[k], twin_send.at[k], twin_got.at[k], twin)

    for k in range(dp):
        twin_copy(k).start()
    for load in loads:
        load.wait()
    for d in range(dp):
        for z in range(depth):
            for c in range(2):
                spot = ((d * depth + z) * 2 + c) * part
                gain_ref[:, spot : spot + part] = gain_blocks[d, z, c, 0:2, :part]
    pair_weight_ref[...] = weight[...].reshape(width, -1)[:, columns:].T
    gain = gain_ref[0:1].astype(f32)
    turning = (1 - core).astype(f32)

    def block_of(which, z, k):
        return line_hbm.at[which, z, pl.ds(k * rows, rows)]

    def pair_of(k):
        return pair.at[pl.ds(k * rows, rows)]

    def own_copy(k):
        return pltpu.make_async_copy(pair_of(k), block_of(core, place, k), own_sem.at[k])

    def own_side_copy(k):
        return send(
            pair_of(k),
            block_of(core, place, k),
            side_send.at[place, k],
            side_got.at[place, k],
            twin,
        )

    def line_copy(z, k):
        block = block_of(core, place if z is None else z, k)
        return send(
            pair_of(k) if z is None else block,
            block,
            line_send.at[place if z is None else z, k],
            line_got.at[place if z is None else z, k],
            (data, lax.rem(place + 1, depth), core),
        )

    def line_arrival(z, k):
        block = block_of(core, z, k)
        return send(block, block, line_send.at[z, k], line_got.at[z, k], twin)

    def side_copy(z, k):
        block = block_of(core, z, k)
        return send(block, block, side_send.at[z, k], side_got.at[z, k], twin)

    def side_arrival(z, k):
        block = block_of(1 - core, z, k)
        return send(block, block, side_send.at[z, k], side_got.at[z, k], twin)

    for k in range(dp):
        for far in range(2):
            e = core if far == 0 else 1 - core
            if far:
                twin_copy(k).wait_recv()
            source = far_pieces.at[k] if far else pieces.at[k]
            values = source[...].reshape(rows * length, width).astype(f32)
            factor = lax.rsqrt(jnp.mean(values * values, axis=-1, keepdims=True) + EPSILON)
            normed = (values * factor * gain).astype(bf16)
            normed_ref[k, e] = normed
            result = multiply(normed, weight[...].reshape(width, -1))
            spot = pl.ds(pl.multiple_of(e * length, length), length)
            for r in range(rows):
                row = k * rows + r
                block = result[r * length : (r + 1) * length]
                offsets = places_ref[k, e][r : r + 1].astype(f32)
                column = jnp.broadcast_to(offsets, (length, length)).T
                offset_ref[row, spot] = column.astype(jnp.int32)
                angles = column * freq_ref[...]
                cosine, sine = jnp.cos(angles), jnp.sin(angles)
                cosine_ref[row, spot] = cosine
                sine_ref[row, spot] = sine
                first, second = block[:, : columns // 2], block[:, columns // 2 : columns]
                turned = (first * cosine - second * sine).astype(bf16)
                query_ref[row, spot, : columns // 2] = turned * bf16(HD ** (-0.5))
                turned = (second * cosine + first * sine).astype(bf16)
                query_ref[row, spot, columns // 2 :] = turned * bf16(HD ** (-0.5))
                keys = block[:, columns:].T
                angles = offsets * freq_pair_ref[...] * turning
                cosine, sine = jnp.cos(angles), jnp.sin(angles)
                cosine_pair_ref[row, :, spot] = cosine
                sine_pair_ref[row, :, spot] = sine
                first, second = keys[: HD // 2], keys[HD // 2 :]
                pair[row, : HD // 2, spot] = (first * cosine - second * sine).astype(bf16)
                pair[row, HD // 2 :, spot] = (second * cosine + first * sine).astype(bf16)
        own_copy(k).start()
        own_side_copy(k).start()

        @pl.when(place < depth - 1)
        def _(k=k):
            line_copy(None, k).start()

    for z in reversed(range(depth)):
        for k in range(dp):

            @pl.when(z < place)
            def _(z=z, k=k):
                line_arrival(z, k).wait_recv()
                side_copy(z, k).start()

            @pl.when((z < place) & (place < depth - 1))
            def _(z=z, k=k):
                line_copy(z, k).start()

    for k in range(dp):
        twin_copy(k).wait_send()
        own_copy(k).wait()
        own_side_copy(k).wait_send()
        for z in range(depth):

            @pl.when(z <= place)
            def _(z=z, k=k):
                side_arrival(z, k).wait_recv()

            @pl.when(z < place)
            def _(z=z, k=k):
                side_copy(z, k).wait_send()

            @pl.when((z <= place) & (place < depth - 1))
            def _(z=z, k=k):
                line_copy(z, k).wait_send()


def project(near, places, freqs, weight):
    f32, bf16 = jnp.float32, jnp.bfloat16
    dp, rows, length, width = near.shape
    depth = weight.shape[0]
    heads = depth
    row_count, size = dp * rows, 2 * length
    columns = heads * HD
    part = width // (2 * dp * depth)
    hbm = pl.BlockSpec(memory_space=pl.ANY)
    vmem = pl.BlockSpec(memory_space=pltpu.VMEM)
    dma = pltpu.SemaphoreType.DMA
    turned = jax.ShapeDtypeStruct((row_count, size, columns // 2), f32)
    turned_pair = jax.ShapeDtypeStruct((row_count, HD // 2, size), f32)
    return pl.pallas_call(
        functools.partial(project_kernel, dp, depth, rows),
        out_shape=(
            jax.ShapeDtypeStruct((row_count, size, columns), bf16),
            jax.ShapeDtypeStruct((dp, 2, rows * length, width), bf16),
            turned,
            turned,
            turned_pair,
            turned_pair,
            jax.ShapeDtypeStruct((row_count, size, length), jnp.int32),
            jax.ShapeDtypeStruct((2, width), bf16),
            jax.ShapeDtypeStruct((HD, width), bf16),
            jax.ShapeDtypeStruct((2, depth, row_count, HD, size), bf16),
        ),
        in_specs=[vmem] * 4 + [hbm],
        out_specs=(vmem,) * 9 + (hbm,),
        scratch_shapes=[
            pltpu.VMEM((dp, depth, 2, part, columns + HD), bf16),
            pltpu.VMEM((dp, depth, 2, 8, columns + HD), bf16),
            pltpu.VMEM((row_count, HD, size), bf16),
            pltpu.VMEM((dp, rows, length, width), bf16),
            dma((2 * depth,)),
            dma((dp,)),
            dma((depth, dp)),
            dma((depth, dp)),
            dma((depth, dp)),
            dma((depth, dp)),
            dma((dp,)),
            dma((dp,)),
        ],
        compiler_params=pltpu.CompilerParams(
            collective_id=2, has_side_effects=True, vmem_limit_bytes=VMEM_LIMIT
        ),
        cost_estimate=LIGHT,
        name="project",
    )(near, places, jnp.tile(freqs, heads)[None], freqs[:, None], weight)


def finish_kernel(
    dp,
    depth,
    rows,
    query_ref,
    cosine_ref,
    sine_ref,
    wide_ref,
    own_ref,
    grad_middle_ref,
    gain_ref,
    query_weight_ref,
    key_weight_ref,
    value_weight_ref,
    gate_weight_ref,
    up_weight_ref,
    grad_k_hbm,
    grad_v_hbm,
    normed_hbm,
    weight_hbm,
    *refs,
):
    pair_hbms, refs = refs[:dp], refs[dp:]
    finish_body(
        dp, depth, rows, query_ref, cosine_ref, sine_ref, wide_ref, own_ref,
        grad_middle_ref, gain_ref, query_weight_ref, key_weight_ref, value_weight_ref,
        gate_weight_ref, up_weight_ref, grad_k_hbm, grad_v_hbm, normed_hbm, weight_hbm, pair_hbms,
        *refs,
    )


def finish_body(
    dp,
    depth,
    rows,
    query_ref,
    cosine_ref,
    sine_ref,
    wide_ref,
    own_ref,
    grad_middle_ref,
    gain_ref,
    query_weight_ref,
    key_weight_ref,
    value_weight_ref,
    gate_weight_ref,
    up_weight_ref,
    grad_k_hbm,
    grad_v_hbm,
    normed_hbm,
    weight_hbm,
    pair_hbms,
    grad_ref,
    query_grad_ref,
    key_grad_ref,
    value_grad_ref,
    gate_grad_ref,
    up_grad_ref,
    attn_gain_ref,
    mlp_gain_ref,
    normed,
    weight,
    kept,
    given,
    arrived,
    line_block,
    line_got_block,
    terms,
    terms_t,
    held,
    line_grads,
    line_grads_got,
    team_block,
    team_got_block,
    wide_block,
    wide_got_block,
    load_sem,
    swap_send,
    swap_got,
    line_send,
    line_got,
    grads_send,
    grads_got,
    team_send,
    team_got,
    wide_send,
    wide_got,
    pair_weight,
    pair_out,
    pair_in,
    pair_load_sem,
    pair_twin_send,
    pair_twin_got,
    pair_send,
    pair_got,
    *sum_refs,
):
    f32, bf16 = jnp.float32, jnp.bfloat16
    data, place, core, peer, twin = team_places()
    columns = query_ref.shape[2]
    size = query_ref.shape[1]
    length = size // 2
    width = grad_ref.shape[1]
    part = weight.shape[3]
    features = columns + HD
    half = HD // 2
    loads = [
        pltpu.make_async_copy(
            weight_hbm.at[z, :, :, pl.ds(0, part), pl.ds(0, columns)],
            weight.at[:, z],
            load_sem.at[z],
        )
        for z in range(depth)
    ]
    pair_loads = [
        pltpu.make_async_copy(pair_hbms[k], pair_weight.at[k, core], pair_load_sem.at[k])
        for k in range(dp)
    ]
    loads.append(pltpu.make_async_copy(normed_hbm, normed, load_sem.at[depth]))

    @pl.when(core == 0)
    def _():
        pltpu.make_async_copy(grad_k_hbm, kept, load_sem.at[depth + 1]).start()
        pltpu.make_async_copy(grad_v_hbm, given, load_sem.at[depth + 2]).start()

    @pl.when(core == 1)
    def _():
        pltpu.make_async_copy(grad_v_hbm, kept, load_sem.at[depth + 1]).start()
        pltpu.make_async_copy(grad_k_hbm, given, load_sem.at[depth + 2]).start()

    for load in loads + pair_loads:
        load.start()
    others = [(data, lax.rem(place + step, depth), core) for step in range(1, depth)]

    def device(k, other):
        return (peer(k)[0], place, 1 - core if other else core)

    pairs = [(k, other) for k in range(dp) for other in range(2) if k or other]
    greet(others + [device(k, other) for k, other in pairs])
    pltpu.make_async_copy(grad_v_hbm, given, load_sem.at[depth + 2]).wait()
    swap_copy = send(given, arrived, swap_send, swap_got, twin)
    swap_copy.start()

    def pair_twin(k):
        block = pair_weight.at[k, core]
        return send(block, block, pair_twin_send.at[k], pair_twin_got.at[k], twin)

    def pair_twin_arrival(k):
        block = pair_weight.at[k, 1 - core]
        return send(block, block, pair_twin_send.at[k], pair_twin_got.at[k], twin)

    def pair_copy(k, other):
        e = 1 - core if other else core
        return send(
            pair_out.at[k, e],
            pair_in.at[k, core],
            pair_send.at[k, other],
            pair_got.at[k, other],
            device(k, other),
        )

    def pair_arrival(k, other):
        block = pair_in.at[k, 1 - core if other else core]
        return send(block, block, pair_send.at[k, other], pair_got.at[k, other], twin)

    def wide_copy(k, other):
        spot = (peer(k)[0], 1 - core if other else core)
        return send(
            wide_block.at[spot],
            wide_got_block.at[data, core],
            wide_send.at[k, other],
            wide_got.at[k, other],
            device(k, other),
        )

    def wide_arrival(k, other):
        block = wide_got_block.at[peer(k)[0], 1 - core if other else core]
        return send(block, block, wide_send.at[k, other], wide_got.at[k, other], twin)

    def line_copy(z):
        return send(
            line_block.at[z],
            line_got_block.at[place],
            line_send.at[z],
            line_got.at[place],
            (data, z, core),
        )

    def line_arrival(z):
        block = line_got_block.at[z]
        return send(block, block, line_send.at[z], line_got.at[z], twin)

    pltpu.make_async_copy(grad_k_hbm, kept, load_sem.at[depth + 1]).wait()
    swap_copy.wait_recv()
    for z in range(depth):

        @pl.when(z < place)
        def _(z=z):
            total = kept[z].astype(f32) + arrived[z].astype(f32)
            line_block[z] = total.astype(bf16)
            line_copy(z).start()

    for load in loads:
        load.wait()
    for k in range(dp):
        for e in range(2):
            for r in range(rows):
                block = query_ref[k * rows + r, e * length : (e + 1) * length]
                terms[k, e, r * length : (r + 1) * length] = block
                spot = pl.ds(((k * 2 + e) * rows + r) * length, length)
                terms_t[:columns, spot] = block.T

    def tile_rows(first, count):
        def tile(j, carry):
            spot = pl.ds(pl.multiple_of(j * 256, 256), 256)
            block = multiply(
                terms_t[first : first + count], normed[:, :, :, spot].reshape(-1, 256)
            ).astype(bf16)
            for i in range(2):
                group = 2 * j + i
                line_grads[lax.rem(group, depth), group // depth, first : first + count] = block[
                    :, i * 128 : (i + 1) * 128
                ]
            return carry

        lax.fori_loop(0, width // 256, tile, 0)

    def grads_copy(z, piece):
        spot = pl.ds(piece * columns, HD if piece else columns)
        return send(
            line_grads.at[z, :, spot],
            line_grads_got.at[place, :, spot],
            grads_send.at[z, piece],
            grads_got.at[place, piece],
            (data, z, core),
        )

    def grads_arrival(z, piece):
        spot = pl.ds(piece * columns, HD if piece else columns)
        block = line_grads_got.at[z, :, spot]
        return send(block, block, grads_send.at[z, piece], grads_got.at[z, piece], twin)

    def product(k, e, turn):
        return contract_last(terms[k, e], weight[...].reshape(width, columns))

    complete = plane_sum(dp, product, grad_ref, sum_refs)
    for k in range(dp):
        pair_loads[k].wait()
        pair_twin(k).start()
    for which in range(2):
        for d in range(dp):
            block = wide_ref[which, d].T
            wide_block[d, 0, which] = block[:part]
            wide_block[d, 1, which] = block[part:]
    for k, other in pairs:
        wide_copy(k, other).start()
    wide_got_block[data, core] = wide_block[data, core]
    tile_rows(0, columns)
    for z in range(depth):

        @pl.when(z > place)
        def _(z=z):
            grads_copy(z, 0).start()

    for z in range(depth):

        @pl.when(z == place)
        def _(z=z):
            held[...] = kept[z].astype(f32) + arrived[z].astype(f32)

    for z in range(depth):

        @pl.when(z > place)
        def _(z=z):
            line_arrival(z).wait_recv()
            held[...] += line_got_block[z].astype(f32)

    for z in range(depth):

        @pl.when(z < place)
        def _(z=z):
            grads_copy(z, 0).start()

    for k in range(dp):
        for r in range(rows):
            row = k * rows + r
            first, second = held[row, :half], held[row, half:]
            cosine, sine = cosine_ref[row], sine_ref[row]
            turned = jnp.concatenate(
                [first * cosine + second * sine, second * cosine - first * sine], axis=0
            ).astype(bf16)
            for e in range(2):
                block = turned[:, e * length : (e + 1) * length]
                spot = pl.ds(((k * 2 + e) * rows + r) * length, length)
                terms_t[columns:, spot] = block
                pair_out[k, e, :, r * length : (r + 1) * length] = block
    for k, other in pairs:
        pair_copy(k, other).start()
    pair_in[0, core] = pair_out[0, core]

    tile_rows(columns, HD)
    for z in range(depth):

        @pl.when(z != place)
        def _(z=z):
            grads_copy(z, 1).start()

    for k, other in pairs:
        wide_arrival(k, other).wait_recv()
    count = wide_block.shape[4] // depth
    for d in range(dp):
        for c in range(2):
            for which, target in ((0, gate_grad_ref), (1, up_grad_ref)):
                block = wide_got_block[d, c, which].astype(f32)
                for z in range(depth):
                    spot = ((d * depth + z) * 2 + c) * count
                    target[:, spot : spot + count] = block[:, z * count : (z + 1) * count]
    products = gate_weight_ref[...].astype(f32) * gate_grad_ref[...]
    products = products + up_weight_ref[...].astype(f32) * up_grad_ref[...]
    mlp_gain_ref[...] = jnp.sum(products, axis=-1, keepdims=True)

    def team_copy(k, other, piece):
        spot = (peer(k)[0], 1 - core if other else core)
        return send(
            team_block.at[spot + (piece,)],
            team_got_block.at[data, core, piece],
            team_send.at[k, other, piece],
            team_got.at[k, other, piece],
            device(k, other),
        )

    def team_arrival(k, other, piece):
        block = team_got_block.at[peer(k)[0], 1 - core if other else core, piece]
        send_sem, got_sem = team_send.at[k, other, piece], team_got.at[k, other, piece]
        return send(block, block, send_sem, got_sem, twin)

    line_grads_got[place] = line_grads[place]

    def team_piece(piece, first, last):
        for z in range(depth):

            @pl.when(z != place)
            def _(z=z):
                grads_arrival(z, piece).wait_recv()

        for d in range(dp):
            total = line_grads_got[0, d, first:last].astype(f32)
            for z in range(1, depth):
                total = total + line_grads_got[z, d, first:last].astype(f32)
            total = total.T.astype(bf16)
            team_block[d, 0, piece, :, : last - first] = total[:part]
            team_block[d, 1, piece, :, : last - first] = total[part:]
        for k, other in pairs:
            team_copy(k, other, piece).start()
        team_got_block[data, core, piece] = team_block[data, core, piece]

    team_block[...] = jnp.zeros_like(team_block)
    team_piece(0, 0, columns)
    complete()
    for k, other in pairs:
        pair_arrival(k, other).wait_recv()
    for k in range(dp):
        pair_twin_arrival(k).wait_recv()
    grad_ref[...] += multiply(
        pair_in[...].reshape(2 * dp * HD, -1).T, pair_weight[...].reshape(2 * dp * HD, width)
    )
    own = own_ref[...].reshape(grad_ref.shape).astype(f32)
    factor = lax.rsqrt(jnp.mean(own * own, axis=-1, keepdims=True) + EPSILON)
    inner = grad_ref[...] * gain_ref[0:1].astype(f32)
    mean = jnp.mean(inner * own, axis=-1, keepdims=True)
    grad_ref[...] = grad_middle_ref[...] + factor * inner - factor * factor * factor * own * mean
    team_piece(1, columns, features)
    for k, other in pairs:
        team_arrival(k, other, 0).wait_recv()
    side = depth * half
    for d in range(dp):
        for c in range(2):
            block = team_got_block[d, c, 0].astype(f32)
            for z in range(depth):
                for h in range(2):
                    spot = ((d * depth + z) * 2 + c) * HD + h * half
                    start = h * side + z * half
                    query_grad_ref[:, spot : spot + half] = block[:, start : start + half]
    for k, other in pairs:
        team_arrival(k, other, 1).wait_recv()
    for d in range(dp):
        for c in range(2):
            target = key_grad_ref if c == 0 else value_grad_ref
            target[:, d * HD : (d + 1) * HD] = team_got_block[d, c, 1, :, :HD].astype(f32)
    attn_gain_ref[...] = sum(
        jnp.sum(before[...].astype(f32) * after[...], axis=-1, keepdims=True)
        for before, after in (
            (query_weight_ref, query_grad_ref),
            (key_weight_ref, key_grad_ref),
            (value_weight_ref, value_grad_ref),
        )
    )
    swap_copy.wait_send()
    for k in range(dp):
        pair_twin(k).wait_send()
    for k, other in pairs:
        team_copy(k, other, 0).wait_send()
        team_copy(k, other, 1).wait_send()
        pair_copy(k, other).wait_send()
        wide_copy(k, other).wait_send()
    for z in range(depth):

        @pl.when(z < place)
        def _(z=z):
            line_copy(z).wait_send()

        @pl.when(z != place)
        def _(z=z):
            grads_copy(z, 0).wait_send()
            grads_copy(z, 1).wait_send()


def finish(grad_queries, cosine_pair, sine_pair, wide_sum, own, grad_middle, gain, weights, grad_keys, grad_values, normed, weight, pair_weights):
    f32, bf16 = jnp.float32, jnp.bfloat16
    dp, _, size, width = normed.shape
    rows = own.shape[0]
    depth, row_count, features, line_size = grad_keys.shape
    columns = grad_queries.shape[2]
    part = width // (2 * dp * depth)
    inner = wide_sum.shape[2]
    total = columns + features
    hbm = pl.BlockSpec(memory_space=pl.ANY)
    vmem = pl.BlockSpec(memory_space=pltpu.VMEM)
    dma = pltpu.SemaphoreType.DMA
    line = pltpu.VMEM((depth, row_count, features, line_size), bf16)
    grads = pltpu.VMEM((depth, dp, total, 2 * part), bf16)
    team = pltpu.VMEM((dp, 2, 2, part, columns), bf16)
    wide = pltpu.VMEM((dp, 2, 2, part, inner), bf16)
    query_weight, key_weight, value_weight, gate_weight, up_weight = weights
    return pl.pallas_call(
        functools.partial(finish_kernel, dp, depth, rows),
        out_shape=(
            jax.ShapeDtypeStruct((size, width), f32),
            jax.ShapeDtypeStruct(query_weight.shape, f32),
            jax.ShapeDtypeStruct(key_weight.shape, f32),
            jax.ShapeDtypeStruct(value_weight.shape, f32),
            jax.ShapeDtypeStruct(gate_weight.shape, f32),
            jax.ShapeDtypeStruct(up_weight.shape, f32),
            jax.ShapeDtypeStruct((part, 1), f32),
            jax.ShapeDtypeStruct((part, 1), f32),
        ),
        in_specs=[vmem] * 12 + [hbm] * (4 + dp),
        out_specs=(vmem,) * 8,
        scratch_shapes=[
            pltpu.VMEM((dp, 2, size, width), bf16),
            pltpu.VMEM((dp, depth, 2, part, columns), bf16),
            line,
            line,
            line,
            line,
            line,
            pltpu.VMEM((dp, 2, size, columns), bf16),
            pltpu.VMEM((total, 2 * dp * size), bf16),
            pltpu.VMEM((row_count, features, line_size), f32),
            grads,
            grads,
            team,
            team,
            wide,
            wide,
            dma((depth + 3,)),
            dma,
            dma,
            dma((depth,)),
            dma((depth,)),
            dma((depth, 2)),
            dma((depth, 2)),
            dma((dp, 2, 2)),
            dma((dp, 2, 2)),
            dma((dp, 2)),
            dma((dp, 2)),
            pltpu.VMEM((dp, 2, features, width), bf16),
            pltpu.VMEM((dp, 2, features, size), bf16),
            pltpu.VMEM((dp, 2, features, size), bf16),
            dma((dp,)),
            dma((dp,)),
            dma((dp,)),
            dma((dp, 2)),
            dma((dp, 2)),
        ]
        + sum_scratch(dp, size, width),
        compiler_params=pltpu.CompilerParams(
            collective_id=3, has_side_effects=True, vmem_limit_bytes=60 * 1024 * 1024
        ),
        cost_estimate=pl.CostEstimate(flops=10**11, bytes_accessed=1024, transcendentals=0),
        name="finish",
    )(
        grad_queries,
        cosine_pair,
        sine_pair,
        wide_sum,
        own,
        grad_middle,
        gain,
        *weights,
        grad_keys,
        grad_values,
        normed,
        weight,
        *pair_weights,
    )


def split_layer(dp, depth):
    def layer(
        hidden_in,
        segment_ids,
        positions,
        attn_gain,
        query_weight,
        key_weight,
        value_weight,
        out_weight,
        mlp_gain,
        gate_weight,
        up_weight,
        down_weight,
        cotangent,
    ):
        f32, bf16 = jnp.float32, jnp.bfloat16
        rows, length, width = hidden_in.shape
        own = rows * length
        team = 2 * dp
        tokens = team * own
        part = query_weight.shape[0]
        hidden_rows = down_weight.shape[0]
        inner = depth * hidden_rows
        heads = depth
        row_count, size = dp * rows, 2 * length
        core = lax.axis_index("core")
        place = lax.axis_index("z")

        def dot(left, right):
            return jnp.dot(left, right, preferred_element_type=f32)

        weight_out = lax.all_gather(out_weight, "z", axis=0, tiled=True)
        weight_attn, wide_mine, places, near = open_layer(
            dp, depth, query_weight, key_weight, value_weight, attn_gain, mlp_gain, gate_weight,
            up_weight, positions, hidden_in,
        )
        wide_got = lax.all_gather(wide_mine, "z", axis=0)
        wide_got = wide_got.reshape(depth, dp, 2, 2, part, inner)
        weight_down = lax.all_gather(down_weight, "z", axis=0, tiled=True)

        x_own = hidden_in.reshape(own, width)
        cot_own = cotangent.reshape(own, width)
        freqs = 10000.0 ** (-jnp.arange(0, HD // 2, dtype=f32) * 2.0 / HD)
        cotangent, near, wide_mine = lax.optimization_barrier((cotangent, near, wide_mine))
        cots = plane_pieces(cotangent, dp)
        cots = [piece.reshape(own, width) for piece in cots]
        queries, normed1, cosine, sine, cosine_pair, sine_pair, offsets, gains, pair_weight, lines = project(
            near, places, freqs, weight_attn
        )
        pair_weights = plane_pieces(pair_weight, dp)
        low_block = (place * size - places[:, 0, :, 0].reshape(row_count)) // size
        low_block = jnp.maximum(low_block, 0).astype(jnp.int32)
        place_one = place.astype(jnp.int32).reshape(1)
        queries, cots = lax.optimization_barrier((queries, cots))
        context, logs = attend(
            low_block, place_one, offsets, queries, lines
        )

        context, pair_weights = lax.optimization_barrier((context, pair_weights))
        middle, normed2 = attend_sum(dp, context, weight_out, hidden_in, gains)
        all_normed2, all_cots, hidden, slope, active, grad_down = mlp_forward(
            normed2, wide_got, cots
        )
        grad_normed2, mlp_parts, grad_wide = mlp_backward(
            all_normed2, all_cots, hidden, slope, active, wide_got, weight_down
        )
        def line_sum(array):
            return lax.psum_scatter(array.astype(bf16), "z", scatter_dimension=0, tiled=True)

        down_sum = line_sum(grad_down)
        grad_wide, down_sum = lax.optimization_barrier((grad_wide, down_sum))
        wide_sum = line_sum(grad_wide)[0]
        grad_normed2, down_sum = lax.optimization_barrier((grad_normed2, down_sum))
        grad_middle, grad_context, grad_wout = middle_back(
            dp, rows, grad_normed2, middle, cot_own, gains, context, weight_out
        )
        grad_down = down_sum.astype(f32)
        mlp_parts, grad_context = lax.optimization_barrier((mlp_parts, grad_context))
        mlp_got = [swap(mlp_parts[k], "dp", dp, k) for k in range(1, dp)]
        grad_queries, grad_keys, grad_values = attend_back(
            low_block,
            place_one,
            offsets,
            queries,
            lines,
            context,
            logs,
            grad_context,
            cosine,
            sine,
        )
        out_hidden = middle + mlp_parts[0].astype(f32)
        for got in mlp_got:
            out_hidden = out_hidden + got.astype(f32)
        out_hidden = out_hidden.astype(bf16)
        grad_queries, out_hidden, grad_wout = lax.optimization_barrier(
            (grad_queries, out_hidden, grad_wout)
        )
        out_sum = line_sum(grad_wout)
        (
            grad_in,
            grad_wquery,
            grad_wkey,
            grad_wvalue,
            grad_wgate,
            grad_wup,
            attn_rows,
            mlp_rows,
        ) = finish(
            grad_queries,
            cosine_pair,
            sine_pair,
            wide_sum,
            hidden_in,
            grad_middle,
            gains,
            (query_weight, key_weight, value_weight, gate_weight, up_weight),
            grad_keys,
            grad_values,
            normed1,
            weight_attn,
            pair_weights,
        )
        out_sum, grad_in = lax.optimization_barrier((out_sum, grad_in))
        grad_wout = out_sum.astype(f32)
        grad_gain_one = attn_rows[:, 0] / attn_gain.astype(f32)
        grad_gain_two = mlp_rows[:, 0] / mlp_gain.astype(f32)
        return (
            out_hidden.reshape(rows, length, width),
            grad_in.reshape(rows, length, width),
            grad_gain_one,
            grad_wquery,
            grad_wkey,
            grad_wvalue,
            grad_wout,
            grad_gain_two,
            grad_wgate,
            grad_wup,
            grad_down,
        )

    return layer


def solution(mesh):
    dp, seq = mesh.shape["dp"], mesh.shape["seq"]
    if dp != KVH or seq % 2 or HQ != dp * seq:
        return gathered_weights(mesh)
    depth = seq // 2
    mesh = Mesh(mesh.devices.reshape(dp, depth, 2), ("dp", "z", "core"))
    every = ("dp", "z", "core")
    tokens = P("dp", ("z", "core"), None)
    matrix = P(every, None)
    return jax.shard_map(
        split_layer(dp, depth),
        mesh=mesh,
        in_specs=(
            tokens,
            P("dp", ("z", "core")),
            P("dp", ("z", "core")),
            P(every),
            matrix,
            matrix,
            matrix,
            matrix,
            P(every),
            matrix,
            matrix,
            matrix,
            tokens,
        ),
        out_specs=(
            tokens,
            tokens,
            P(every),
            matrix,
            matrix,
            matrix,
            matrix,
            P(every),
            matrix,
            matrix,
            matrix,
        ),
        check_vma=False,
    )
```

```python
import functools

import jax
import jax.numpy as jnp
from jax import lax
from jax.experimental import pallas as pl
from jax.experimental.pallas import tpu as pltpu
from jax.sharding import Mesh
from jax.sharding import PartitionSpec as P

HQ = 32
HD = 64
KVH = 4


EPSILON = 1e-05


def fetch_attention(attn_gain, query_weight, key_weight, value_weight, out_weight):
    return (
        lax.all_gather(attn_gain, ("dp", "seq"), axis=0, tiled=True),
        lax.all_gather(query_weight, ("dp", "seq"), axis=0, tiled=True),
        lax.all_gather(key_weight, ("dp", "seq"), axis=0, tiled=True),
        lax.all_gather(value_weight, ("dp", "seq"), axis=0, tiled=True),
        lax.all_gather(out_weight, ("dp", "seq"), axis=0, tiled=True),
    )


def fetch_mlp(mlp_gain, gate_weight, up_weight, down_weight):
    return (
        lax.all_gather(mlp_gain, ("dp", "seq"), axis=0, tiled=True),
        lax.all_gather(gate_weight, ("dp", "seq"), axis=0, tiled=True),
        lax.all_gather(up_weight, ("dp", "seq"), axis=0, tiled=True),
        lax.all_gather(down_weight, ("dp", "seq"), axis=0, tiled=True),
    )


def angles_of(positions):
    freqs = 10000.0 ** (-jnp.arange(0, HD // 2, dtype=jnp.float32) * 2.0 / HD)
    return positions.astype(jnp.float32)[:, None] * freqs[None, :]


def rotate(vectors, cosine, sine):
    half = vectors.shape[-1] // 2
    first = vectors[..., :half]
    second = vectors[..., half:]
    cosine = cosine[:, None, :]
    sine = sine[:, None, :]
    return jnp.concatenate(
        [first * cosine - second * sine, second * cosine + first * sine], axis=-1
    )


def norm_forward(values, gain):
    factor = lax.rsqrt(jnp.mean(values * values, axis=-1, keepdims=True) + EPSILON)
    return (values * factor * gain.astype(jnp.float32), factor)


def norm_backward(values, factor, gain, grad_normed):
    inner = grad_normed * gain.astype(jnp.float32)
    grad_gain = jnp.sum(grad_normed * values * factor, axis=0)
    grad_values = factor * inner - factor * factor * factor * values * jnp.mean(
        inner * values, axis=-1, keepdims=True
    )
    return (grad_values, grad_gain)


def masked_scores(queries_rot, keys_heads, query_pos, query_seg, seg_all):
    scores = jnp.einsum(
        "cgjd,kgd->gjck", queries_rot, keys_heads, preferred_element_type=jnp.float32
    ) * HD ** (-0.5)
    key_pos = jnp.arange(keys_heads.shape[0])
    allowed = (key_pos[None, :] <= query_pos[:, None]) & (seg_all[None, :] == query_seg[:, None])
    return jnp.where(allowed, scores, -1e30)


def add_up(total, extra):
    if total is None:
        return extra
    return jax.tree.map(jnp.add, total, extra)


def gathered_weights_layer(
    hidden_in,
    segment_ids,
    positions,
    attn_gain,
    query_weight,
    key_weight,
    value_weight,
    out_weight,
    mlp_gain,
    gate_weight,
    up_weight,
    down_weight,
    cotangent,
):
    batches, local_len, width = hidden_in.shape
    group = HQ // KVH
    query_pos = lax.axis_index("seq") * local_len + jnp.arange(local_len)
    outputs = []
    grads_in = []
    attn_total = None
    mlp_total = None
    for microbatch in range(batches):
        rows_in = hidden_in[microbatch].astype(jnp.float32)
        seg_own = segment_ids[microbatch]
        angles = angles_of(positions[microbatch])
        cosine = jnp.cos(angles)
        sine = jnp.sin(angles)
        attn_set = fetch_attention(attn_gain, query_weight, key_weight, value_weight, out_weight)
        gain_one, weight_query, weight_key, weight_value, weight_out = attn_set
        normed1, factor1 = norm_forward(rows_in, gain_one)
        normed1_low = normed1.astype(jnp.bfloat16)
        queries = jnp.dot(normed1_low, weight_query, preferred_element_type=jnp.float32).reshape(
            local_len, HQ, HD
        )
        keys_own = jnp.dot(normed1_low, weight_key, preferred_element_type=jnp.float32).reshape(
            local_len, KVH, HD
        )
        values_own = jnp.dot(normed1_low, weight_value, preferred_element_type=jnp.float32).astype(
            jnp.bfloat16
        )
        queries_rot = (
            rotate(queries, cosine, sine).astype(jnp.bfloat16).reshape(local_len, KVH, group, HD)
        )
        keys_rot = rotate(keys_own, cosine, sine).astype(jnp.bfloat16).reshape(local_len, KVH * HD)
        keys_all, values_all, seg_all = (
            lax.all_gather(keys_rot, "seq", axis=0, tiled=True),
            lax.all_gather(values_own, "seq", axis=0, tiled=True),
            lax.all_gather(seg_own, "seq", axis=0, tiled=True),
        )
        keys_heads = keys_all.reshape(-1, KVH, HD)
        values_heads = values_all.reshape(-1, KVH, HD)
        scores = masked_scores(queries_rot, keys_heads, query_pos, seg_own, seg_all)
        highest = jnp.max(scores, axis=-1, keepdims=True)
        powers = jnp.exp(scores - highest)
        totals = jnp.sum(powers, axis=-1, keepdims=True)
        logsum = highest + jnp.log(totals)
        probs_low = (powers / totals).astype(jnp.bfloat16)
        context = jnp.einsum(
            "gjck,kgd->cgjd", probs_low, values_heads, preferred_element_type=jnp.float32
        )
        context_low = context.reshape(local_len, HQ * HD).astype(jnp.bfloat16)
        middle = rows_in + jnp.dot(context_low, weight_out, preferred_element_type=jnp.float32)
        mlp_set = fetch_mlp(mlp_gain, gate_weight, up_weight, down_weight)
        gain_two, weight_gate, weight_up, weight_down = mlp_set
        normed2, factor2 = norm_forward(middle, gain_two)
        normed2_low = normed2.astype(jnp.bfloat16)
        gate = jnp.dot(normed2_low, weight_gate, preferred_element_type=jnp.float32)
        up = jnp.dot(normed2_low, weight_up, preferred_element_type=jnp.float32)
        sigma = jax.nn.sigmoid(gate)
        activation = gate * sigma
        hidden = (activation * up).astype(jnp.bfloat16)
        mlp_out = jnp.dot(hidden, weight_down, preferred_element_type=jnp.float32)
        outputs.append((middle + mlp_out).astype(jnp.bfloat16))
        grad_low = cotangent[microbatch]
        grad_out = grad_low.astype(jnp.float32)
        mlp_back = fetch_mlp(mlp_gain, gate_weight, up_weight, down_weight)
        gain_two, weight_gate, weight_up, weight_down = mlp_back
        grad_down = jnp.dot(hidden.T, grad_low, preferred_element_type=jnp.float32)
        grad_hid = jnp.dot(grad_low, weight_down.T, preferred_element_type=jnp.float32)
        grad_gate = (grad_hid * up * sigma * (1.0 + gate * (1.0 - sigma))).astype(jnp.bfloat16)
        grad_up = (grad_hid * activation).astype(jnp.bfloat16)
        grad_wgate = jnp.dot(normed2_low.T, grad_gate, preferred_element_type=jnp.float32)
        grad_wup = jnp.dot(normed2_low.T, grad_up, preferred_element_type=jnp.float32)
        grad_normed2 = jnp.dot(
            grad_gate, weight_gate.T, preferred_element_type=jnp.float32
        ) + jnp.dot(grad_up, weight_up.T, preferred_element_type=jnp.float32)
        grad_mid_norm, grad_gain_two = norm_backward(middle, factor2, gain_two, grad_normed2)
        grad_middle = grad_out + grad_mid_norm
        attn_back = fetch_attention(attn_gain, query_weight, key_weight, value_weight, out_weight)
        gain_one, weight_query, weight_key, weight_value, weight_out = attn_back
        grad_attn = grad_middle.astype(jnp.bfloat16)
        grad_wout = jnp.dot(context_low.T, grad_attn, preferred_element_type=jnp.float32)
        grad_context = (
            jnp.dot(grad_attn, weight_out.T, preferred_element_type=jnp.float32)
            .astype(jnp.bfloat16)
            .reshape(local_len, KVH, group, HD)
        )
        probs = jnp.exp(
            masked_scores(queries_rot, keys_heads, query_pos, seg_own, seg_all) - logsum
        )
        grad_probs = jnp.einsum(
            "cgjd,kgd->gjck", grad_context, values_heads, preferred_element_type=jnp.float32
        )
        inner = jnp.sum(probs * grad_probs, axis=-1, keepdims=True)
        grad_scores = (probs * (grad_probs - inner)).astype(jnp.bfloat16)
        grad_qrot = jnp.einsum(
            "gjck,kgd->cgjd", grad_scores, keys_heads, preferred_element_type=jnp.float32
        ) * HD ** (-0.5)
        grad_krot_all = jnp.einsum(
            "gjck,cgjd->kgd", grad_scores, queries_rot, preferred_element_type=jnp.float32
        ) * HD ** (-0.5)
        grad_vall = jnp.einsum(
            "gjck,cgjd->kgd", probs_low, grad_context, preferred_element_type=jnp.float32
        )
        row_len = keys_heads.shape[0]
        grad_key_own, grad_value_own = (
            lax.psum_scatter(
                grad_krot_all.reshape(row_len, KVH * HD).astype(jnp.bfloat16),
                "seq",
                scatter_dimension=0,
                tiled=True,
            ).astype(jnp.float32),
            lax.psum_scatter(
                grad_vall.reshape(row_len, KVH * HD).astype(jnp.bfloat16),
                "seq",
                scatter_dimension=0,
                tiled=True,
            ).astype(jnp.float32),
        )
        grad_keys = (
            rotate(grad_key_own.reshape(local_len, KVH, HD), cosine, -sine)
            .astype(jnp.bfloat16)
            .reshape(local_len, KVH * HD)
        )
        grad_values = grad_value_own.astype(jnp.bfloat16)
        grad_queries = (
            rotate(grad_qrot.reshape(local_len, HQ, HD), cosine, -sine)
            .astype(jnp.bfloat16)
            .reshape(local_len, HQ * HD)
        )
        grad_wquery = jnp.dot(normed1_low.T, grad_queries, preferred_element_type=jnp.float32)
        grad_wkey = jnp.dot(normed1_low.T, grad_keys, preferred_element_type=jnp.float32)
        grad_wvalue = jnp.dot(normed1_low.T, grad_values, preferred_element_type=jnp.float32)
        grad_normed1 = jnp.dot(grad_queries, weight_query.T, preferred_element_type=jnp.float32)
        grad_normed1 = grad_normed1 + jnp.dot(
            grad_keys, weight_key.T, preferred_element_type=jnp.float32
        )
        grad_normed1 = grad_normed1 + jnp.dot(
            grad_values, weight_value.T, preferred_element_type=jnp.float32
        )
        grad_rows_norm, grad_gain_one = norm_backward(rows_in, factor1, gain_one, grad_normed1)
        grads_in.append(grad_middle + grad_rows_norm)
        attn_terms = (grad_gain_one, grad_wquery, grad_wkey, grad_wvalue, grad_wout)
        mlp_terms = (grad_gain_two, grad_wgate, grad_wup, grad_down)
        attn_shares = (
            lax.psum_scatter(attn_terms[0], ("dp", "seq"), scatter_dimension=0, tiled=True),
            lax.psum_scatter(attn_terms[1], ("dp", "seq"), scatter_dimension=0, tiled=True),
            lax.psum_scatter(attn_terms[2], ("dp", "seq"), scatter_dimension=0, tiled=True),
            lax.psum_scatter(attn_terms[3], ("dp", "seq"), scatter_dimension=0, tiled=True),
            lax.psum_scatter(attn_terms[4], ("dp", "seq"), scatter_dimension=0, tiled=True),
        )
        mlp_shares = (
            lax.psum_scatter(mlp_terms[0], ("dp", "seq"), scatter_dimension=0, tiled=True),
            lax.psum_scatter(mlp_terms[1], ("dp", "seq"), scatter_dimension=0, tiled=True),
            lax.psum_scatter(mlp_terms[2], ("dp", "seq"), scatter_dimension=0, tiled=True),
            lax.psum_scatter(mlp_terms[3], ("dp", "seq"), scatter_dimension=0, tiled=True),
        )
        attn_total = add_up(attn_total, attn_shares)
        mlp_total = add_up(mlp_total, mlp_shares)
    return (
        jnp.stack(outputs),
        jnp.stack(grads_in),
        attn_total[0],
        attn_total[1],
        attn_total[2],
        attn_total[3],
        attn_total[4],
        mlp_total[0],
        mlp_total[1],
        mlp_total[2],
        mlp_total[3],
    )


def gathered_weights(mesh):
    return jax.shard_map(
        gathered_weights_layer,
        mesh=mesh,
        in_specs=(
            P("dp", "seq", None),
            P("dp", "seq"),
            P("dp", "seq"),
            P(("dp", "seq")),
            P(("dp", "seq"), None),
            P(("dp", "seq"), None),
            P(("dp", "seq"), None),
            P(("dp", "seq"), None),
            P(("dp", "seq")),
            P(("dp", "seq"), None),
            P(("dp", "seq"), None),
            P(("dp", "seq"), None),
            P("dp", "seq", None),
        ),
        out_specs=(
            P("dp", "seq", None),
            P("dp", "seq", None),
            P(("dp", "seq")),
            P(("dp", "seq"), None),
            P(("dp", "seq"), None),
            P(("dp", "seq"), None),
            P(("dp", "seq"), None),
            P(("dp", "seq")),
            P(("dp", "seq"), None),
            P(("dp", "seq"), None),
            P(("dp", "seq"), None),
        ),
        check_vma=False,
    )


def swap(values, axis_name, size, step):
    return lax.ppermute(values, axis_name, [(i, i ^ step) for i in range(size)])


def plane_pieces(values, dp):
    return [values] + [swap(values, "dp", dp, k) for k in range(1, dp)]


NEGATIVE = -1e30
VMEM_LIMIT = 56 * 1024 * 1024
MESH = pl.DeviceIdType.MESH
LIGHT = pl.CostEstimate(flops=0, bytes_accessed=1024, transcendentals=0)


def contract_last(left, right):
    return lax.dot_general(
        left, right, (((1,), (1,)), ((), ())), preferred_element_type=jnp.float32
    )


def multiply(left, right):
    return jnp.dot(left, right, preferred_element_type=jnp.float32)


def spread_keys(block, heads):
    half = block.shape[0] // 2
    return jnp.concatenate([block[:half]] * heads + [block[half:]] * heads, axis=0)


def fold_keys(block, heads):
    half = block.shape[0] // (2 * heads)
    first = sum(block[h * half : (h + 1) * half] for h in range(heads))
    rest = range(heads, 2 * heads)
    return jnp.concatenate([first, sum(block[h * half : (h + 1) * half] for h in rest)], axis=0)


def fold_values(block, heads):
    size = block.shape[0] // heads
    return sum(block[h * size : (h + 1) * size] for h in range(heads))


def turned_head(shape, dim, heads):
    index = lax.broadcasted_iota(jnp.int32, shape, dim)
    return lax.rem(index, shape[dim] // 2) // (shape[dim] // 2 // heads)


def plain_head(shape, dim, heads):
    index = lax.broadcasted_iota(jnp.int32, shape, dim)
    return index // (shape[dim] // heads)


def per_head(values, owner, heads, axis):
    zero = jnp.zeros_like(values)
    return jnp.concatenate([jnp.where(owner == h, values, zero) for h in range(heads)], axis=axis)


def join_heads(stacked, owner, heads):
    size = stacked.shape[0] // heads
    return sum(
        jnp.where(owner == h, stacked[h * size : (h + 1) * size], 0.0) for h in range(heads)
    )


def masked(scores, block, start, order_q, heads):
    size = order_q.shape[0]
    order_k = block * size + lax.broadcasted_iota(jnp.int32, (size, size), 1)
    allowed = (order_k >= start) & (order_k <= order_q)
    split = scores.reshape(heads, size, size)
    return jnp.where(allowed[None], split, NEGATIVE).reshape(scores.shape)


def attend_kernel(heads, low_ref, place_ref, offset_ref, q_ref, k_ref, v_ref, out_ref, log_ref, held):
    row = pl.program_id(0)
    place = place_ref[0]
    queries = q_ref[0]
    size = queries.shape[0]
    stacked = per_head(queries, turned_head(queries.shape, 1, heads), heads, 0)
    order_q = place * size + lax.broadcasted_iota(jnp.int32, (size, 1), 0)
    start = order_q - offset_ref[0][:, :1]

    def score(block, highest):
        scores = multiply(stacked, spread_keys(k_ref[block, 0], heads))
        scores = masked(scores, block, start, order_q, heads)
        held[block] = scores
        return jnp.maximum(highest, jnp.max(scores, axis=1, keepdims=True))

    highest = lax.fori_loop(
        low_ref[row], place + 1, score, jnp.full((heads * size, 1), NEGATIVE, jnp.float32)
    )

    def mix(block, carry):
        total, context = carry
        powers = jnp.exp(held[block] - highest)
        total = total + jnp.sum(powers, axis=1, keepdims=True)
        spread = jnp.concatenate([v_ref[block, 0]] * heads, axis=0)
        return total, context + contract_last(powers.astype(jnp.bfloat16), spread)

    total, context = lax.fori_loop(
        low_ref[row],
        place + 1,
        mix,
        (
            jnp.zeros((heads * size, 1), jnp.float32),
            jnp.zeros((heads * size, queries.shape[1]), jnp.float32),
        ),
    )
    owner = plain_head(queries.shape, 1, heads)
    out_ref[0] = join_heads(context / total, owner, heads).astype(jnp.bfloat16)
    log_ref[0] = highest + jnp.log(total)


def attend_back_kernel(
    heads,
    low_ref,
    place_ref,
    offset_ref,
    q_ref,
    k_ref,
    v_ref,
    context_ref,
    log_ref,
    grad_ref,
    cosine_ref,
    sine_ref,
    grad_q_ref,
    grad_k_ref,
    grad_v_ref,
):
    row = pl.program_id(0)
    place = place_ref[0]
    queries = q_ref[0]
    grads = grad_ref[0]
    size = queries.shape[0]
    turned = turned_head(queries.shape, 1, heads)
    plain = plain_head(queries.shape, 1, heads)
    stacked = per_head(queries, turned, heads, 0)
    stacked_grad = per_head(grads, plain, heads, 0)
    flipped = per_head(queries.T, turned_head(queries.shape, 0, heads), heads, 1)
    flipped_grad = per_head(grads.T, plain_head(queries.shape, 0, heads), heads, 1)
    product = grads.astype(jnp.float32) * context_ref[0].astype(jnp.float32)
    inner = jnp.sum(per_head(product, plain, heads, 0), axis=1, keepdims=True)
    logs = log_ref[0]
    order_q = place * size + lax.broadcasted_iota(jnp.int32, (size, 1), 0)
    start = order_q - offset_ref[0][:, :1]
    grad_k_ref[...] = jnp.zeros_like(grad_k_ref)
    grad_v_ref[...] = jnp.zeros_like(grad_v_ref)

    def step(block, grad_q):
        keys = spread_keys(k_ref[block, 0], heads)
        spread = jnp.concatenate([v_ref[block, 0]] * heads, axis=0)
        scores = masked(multiply(stacked, keys), block, start, order_q, heads)
        probs = jnp.exp(scores - logs)
        grad_probs = multiply(stacked_grad, spread)
        grad_scores = (probs * (grad_probs - inner)).astype(jnp.bfloat16)
        grad_k = fold_keys(multiply(flipped, grad_scores), heads)
        grad_v = fold_values(multiply(flipped_grad, probs.astype(jnp.bfloat16)), heads)
        grad_k_ref[block, 0] = grad_k.astype(jnp.bfloat16)
        grad_v_ref[block, 0] = grad_v.astype(jnp.bfloat16)
        return grad_q + contract_last(grad_scores, keys)

    grad_q = lax.fori_loop(
        low_ref[row],
        place + 1,
        step,
        jnp.zeros((heads * size, queries.shape[1]), jnp.float32),
    )
    grad_q = join_heads(grad_q, turned, heads) * HD ** (-0.5)
    half = grad_q.shape[1] // 2
    first, second = grad_q[:, :half], grad_q[:, half:]
    cosine, sine = cosine_ref[0], sine_ref[0]
    grad_q_ref[0, :, :half] = (first * cosine + second * sine).astype(jnp.bfloat16)
    grad_q_ref[0, :, half:] = (second * cosine - first * sine).astype(jnp.bfloat16)


def row_spec(*shape):
    return pl.BlockSpec((1,) + shape, lambda row, low, place: (row,) + (0,) * len(shape))


def line_spec(depth, *shape):
    return pl.BlockSpec((depth, 1) + shape, lambda row, low, place: (0, row) + (0,) * len(shape))


def pair_spec(which, depth, *shape):
    return pl.BlockSpec(
        (None, depth, 1) + shape, lambda row, low, place: (which, 0, row) + (0,) * len(shape)
    )


def attend(low, place, offsets, queries, lines):
    rows, size, width = queries.shape
    depth, features = lines.shape[1], lines.shape[3]
    heads = width // features
    return pl.pallas_call(
        functools.partial(attend_kernel, heads),
        out_shape=(
            jax.ShapeDtypeStruct((rows, size, width), jnp.bfloat16),
            jax.ShapeDtypeStruct((rows, heads * size, 1), jnp.float32),
        ),
        grid_spec=pltpu.PrefetchScalarGridSpec(
            num_scalar_prefetch=2,
            grid=(rows,),
            in_specs=[
                row_spec(size, offsets.shape[2]),
                row_spec(size, width),
                pair_spec(0, depth, features, size),
                pair_spec(1, depth, features, size),
            ],
            out_specs=[row_spec(size, width), row_spec(heads * size, 1)],
            scratch_shapes=[pltpu.VMEM((depth, heads * size, size), jnp.float32)],
        ),
        compiler_params=pltpu.CompilerParams(vmem_limit_bytes=VMEM_LIMIT),
        cost_estimate=LIGHT,
        name="attend",
    )(low, place, offsets, queries, lines, lines)


def attend_back(low, place, offsets, queries, lines, context, logs, grads, cosine, sine):
    rows, size, width = queries.shape
    depth, features = lines.shape[1], lines.shape[3]
    heads = width // features
    line = line_spec(depth, features, size)
    whole = row_spec(size, width)
    half = row_spec(size, width // 2)
    return pl.pallas_call(
        functools.partial(attend_back_kernel, heads),
        out_shape=(
            jax.ShapeDtypeStruct((rows, size, width), jnp.bfloat16),
            jax.ShapeDtypeStruct(lines.shape[1:], jnp.bfloat16),
            jax.ShapeDtypeStruct(lines.shape[1:], jnp.bfloat16),
        ),
        grid_spec=pltpu.PrefetchScalarGridSpec(
            num_scalar_prefetch=2,
            grid=(rows,),
            in_specs=[
                row_spec(size, offsets.shape[2]),
                whole,
                pair_spec(0, depth, features, size),
                pair_spec(1, depth, features, size),
                whole,
                row_spec(heads * size, 1),
                whole,
                half,
                half,
            ],
            out_specs=[whole, line, line],
        ),
        compiler_params=pltpu.CompilerParams(vmem_limit_bytes=VMEM_LIMIT),
        cost_estimate=LIGHT,
        name="attend_back",
    )(low, place, offsets, queries, lines, lines, context, logs, grads, cosine, sine)


def team_places():
    data = lax.axis_index("dp")
    place = lax.axis_index("z")
    core = lax.axis_index("core")

    def peer(k):
        high = lax.rem(data // 2 + k // 2, 2)
        low = lax.rem(lax.rem(data, 2) + lax.rem(k, 2), 2)
        return (high * 2 + low, place, core)

    return data, place, core, peer, (data, place, 1 - core)


def line_neighbours(depth):
    data, place, core, _, _ = team_places()
    return [(data, lax.rem(place + step, depth), core) for step in (1, depth - 1)]


def greet(targets):
    barrier = pltpu.get_barrier_semaphore()
    for target in targets:
        pl.semaphore_signal(barrier, inc=1, device_id=target, device_id_type=MESH)
    pl.semaphore_wait(barrier, len(targets))


def send(source, target, send_sem, got_sem, device):
    return pltpu.make_async_remote_copy(
        src_ref=source,
        dst_ref=target,
        send_sem=send_sem,
        recv_sem=got_sem,
        device_id=device,
        device_id_type=MESH,
    )


def line_gather(depth, block_of, send_sem, got_sem):
    data, place, core, _, twin = team_places()

    def copy(z, step):
        device = (data, lax.rem(place + depth + step, depth), core)
        block = block_of(z)
        return send(block, block, send_sem.at[z, (1 - step) // 2], got_sem.at[z], device)

    def arrival(z):
        block = block_of(z)
        return send(block, block, send_sem.at[z, 0], got_sem.at[z], twin)

    def start():
        @pl.when(place < depth - 1)
        def _():
            copy(place, 1).start()

        @pl.when(place > 0)
        def _():
            copy(place, -1).start()

    def relay(distance):
        @pl.when(place >= distance)
        def _():
            arrival(place - distance).wait_recv()

            @pl.when(place < depth - 1)
            def _():
                copy(place - distance, 1).start()

        @pl.when(place + distance < depth)
        def _():
            arrival(place + distance).wait_recv()

            @pl.when(place > 0)
            def _():
                copy(place + distance, -1).start()

    def finish():
        for z in range(depth):

            @pl.when((z <= place) & (place < depth - 1))
            def _(z=z):
                copy(z, 1).wait_send()

            @pl.when((z >= place) & (place > 0))
            def _(z=z):
                copy(z, -1).wait_send()

    return start, relay, finish


def sum_scratch(dp, size, width):
    dma = pltpu.SemaphoreType.DMA
    block = pltpu.VMEM((dp, size, width), jnp.bfloat16)
    return [
        block,
        block,
        pltpu.VMEM((2, size // 2, width), jnp.bfloat16),
        pltpu.VMEM((2, size, width), jnp.bfloat16),
        dma((dp,)),
        dma((dp,)),
        dma((2,)),
        dma((2,)),
        dma((2, 2)),
        dma((2, 2)),
    ]


def plane_sum(dp, product, total_ref, scratch):
    side, got, relay, far, side_send, side_got, relay_send, relay_got, far_send, far_got = scratch
    f32, bf16 = jnp.float32, jnp.bfloat16
    _, _, core, peer, twin = team_places()
    size = side.shape[1]
    half = size // 2

    def rows(part):
        return pl.ds(part * half, half)

    def side_copy(k):
        return send(side.at[k], got.at[k], side_send.at[k], side_got.at[k], twin)

    def relay_copy(part):
        return send(
            got.at[3, rows(part)],
            relay.at[part],
            relay_send.at[part],
            relay_got.at[part],
            peer(1 + part),
        )

    def far_copy(which, part):
        return send(
            got.at[1 + which, rows(part)],
            far.at[which, rows(part)],
            far_send.at[which, part],
            far_got.at[which, part],
            peer(1 + which),
        )

    def one(step, carry):
        k = dp - 1 - step
        side[k] = product(k, 1 - core, 0).astype(bf16)
        side_copy(k).start()
        total = product(k, core, 1)
        side_copy(k).wait_recv()
        total = total + got[k].astype(f32)

        @pl.when(k == 0)
        def _():
            total_ref[...] = total

        @pl.when(k > 0)
        def _():
            got[k] = total.astype(bf16)

        @pl.when(k == 3)
        def _():
            relay_copy(0).start()
            relay_copy(1).start()

        @pl.when(k == 2)
        def _():
            far_copy(1, 1).start()

        @pl.when(k == 1)
        def _():
            far_copy(0, 0).start()

        return carry

    lax.fori_loop(0, dp, one, 0)
    for part in range(2):
        which = 1 - part
        relay_copy(part).wait_recv()
        total = got[1 + which, rows(part)].astype(f32) + relay[part].astype(f32)
        got[1 + which, rows(part)] = total.astype(bf16)
        far_copy(which, part).start()

    def complete():
        for which, part in ((0, 0), (1, 1), (0, 1), (1, 0)):
            far_copy(which, part).wait_recv()
            total_ref[rows(part)] += far[which, rows(part)].astype(f32)
        for part in range(2):
            relay_copy(part).wait_send()
            for which in range(2):
                far_copy(which, part).wait_send()
        for k in range(dp):
            side_copy(k).wait_send()

    return complete


def mlp_forward_kernel(dp, depth, x_hbm, wide_hbm, *refs):
    cot_hbms = refs[:dp]
    tokens_hbm, cots_hbm, hidden_hbm, slope_hbm, active_hbm, down_grad_hbm = refs[dp : dp + 6]
    (
        tokens,
        cots,
        wides,
        hidden_t,
        chunk,
        tile_out,
        load_sem,
        cots_sem,
        near_send,
        near_got,
        side_send,
        side_got,
        pass_send,
        pass_got,
        tokens_sem,
        chunk_sem,
        tile_sem,
        twin_send,
        twin_got,
    ) = refs[dp + 6 :]
    bf16 = jnp.bfloat16
    _, _, core, peer, twin = team_places()
    size, width = x_hbm.shape
    half = size // 2
    loads = [pltpu.make_async_copy(x_hbm, tokens.at[0, core], load_sem.at[0])]
    for z in range(depth):
        loads.append(pltpu.make_async_copy(wide_hbm.at[z], wides.at[:, z], load_sem.at[1 + z]))
    cot_loads = []
    for k in range(dp):
        sem = load_sem.at[depth + 1 + k]
        cot_loads.append(pltpu.make_async_copy(cot_hbms[k], cots.at[k, core], sem))
    for load in loads + cot_loads:
        load.start()
    greet([peer(k) for k in range(1, 3)] + [twin])
    loads[0].wait()

    def near_copy(k):
        return send(
            tokens.at[0, core], tokens.at[k, core], near_send.at[k], near_got.at[k], peer(k)
        )

    def pass_copy(part):
        spot = pl.ds(part * half, half)
        return send(
            tokens.at[1 + part, core, spot],
            tokens.at[3, core, spot],
            pass_send.at[part],
            pass_got.at[part],
            peer(2 - part),
        )

    def side_copy(k):
        block = tokens.at[k, core]
        return send(block, block, side_send.at[k], side_got.at[k], twin)

    def side_arrival(k):
        block = tokens.at[k, 1 - core]
        return send(block, block, side_send.at[k], side_got.at[k], twin)

    def twin_copy(k):
        block = cots.at[k, core]
        return send(block, block, twin_send.at[k], twin_got.at[k], twin)

    def twin_arrival(k):
        block = cots.at[k, 1 - core]
        return send(block, block, twin_send.at[k], twin_got.at[k], twin)

    def tokens_out(k, e):
        return pltpu.make_async_copy(tokens.at[k, e], tokens_hbm.at[k, e], tokens_sem.at[k, e])

    def chunk_out(k, e, slot):
        return [
            pltpu.make_async_copy(chunk.at[slot, i], target.at[k, e], chunk_sem.at[slot, i])
            for i, target in enumerate((hidden_hbm, slope_hbm, active_hbm))
        ]

    near_copy(1).start()
    near_copy(2).start()
    side_copy(0).start()
    for load in loads[1:]:
        load.wait()

    def process(k, e, slot, reuse):
        row = tokens[k, e]
        tokens_out(k, e).start()
        both = multiply(row, wides[...].reshape(width, -1))
        inner = both.shape[1] // 2
        gate, up = both[:, :inner], both[:, inner:]
        sigma = 1.0 / (1.0 + jnp.exp(-gate))
        active = gate * sigma
        hidden = (active * up).astype(bf16)
        if reuse:
            for copy in chunk_out(k, e, slot):
                copy.wait()
        chunk[slot, 0] = hidden
        chunk[slot, 1] = (up * sigma * (1.0 + gate * (1.0 - sigma))).astype(bf16)
        chunk[slot, 2] = active.astype(bf16)
        for copy in chunk_out(k, e, slot):
            copy.start()
        spot = pl.ds(pl.multiple_of((k * 2 + e) * size, size), size)
        hidden_t[:, spot] = hidden.T

    process(0, core, 0, False)
    side_arrival(0).wait_recv()
    process(0, 1 - core, 1, False)
    for k in range(dp):
        cot_loads[k].wait()
        twin_copy(k).start()
    for k in range(1, 3):
        near_copy(k).wait_recv()
        pass_copy(k - 1).start()
        side_copy(k).start()
    for k in range(dp):
        twin_arrival(k).wait_recv()
    cots_out = pltpu.make_async_copy(cots, cots_hbm, cots_sem)
    cots_out.start()

    def step(k, carry):
        @pl.when(k == 3)
        def _():
            pass_copy(0).wait_recv()
            pass_copy(1).wait_recv()
            side_copy(3).start()

        process(k, core, 0, True)
        side_arrival(k).wait_recv()
        process(k, 1 - core, 1, True)
        return carry

    lax.fori_loop(1, dp, step, 0)

    def tile_copy(j, slot):
        spot = pl.ds(pl.multiple_of(j * 256, 256), 256)
        return pltpu.make_async_copy(tile_out.at[slot], down_grad_hbm.at[:, spot], tile_sem.at[slot])

    count = width // 256

    def tile(j, carry):
        slot = lax.rem(j, 2)

        @pl.when(j > 1)
        def _():
            tile_copy(j - 2, slot).wait()

        spot = pl.ds(pl.multiple_of(j * 256, 256), 256)
        columns = cots[:, :, :, spot].reshape(-1, 256)
        tile_out[slot] = multiply(hidden_t[...], columns).astype(bf16)
        tile_copy(j, slot).start()
        return carry

    lax.fori_loop(0, count, tile, 0)
    for j in (count - 2, count - 1):
        tile_copy(j, j % 2).wait()
    cots_out.wait()
    for slot, e in ((0, core), (1, 1 - core)):
        for copy in chunk_out(dp - 1, e, slot):
            copy.wait()
    for k in range(dp):
        for e in range(2):
            tokens_out(k, e).wait()
        side_copy(k).wait_send()
        twin_copy(k).wait_send()
    for k in range(1, 3):
        near_copy(k).wait_send()
        pass_copy(k - 1).wait_send()


def mlp_forward(x_own, wide, cots):
    depth, dp = wide.shape[:2]
    size, width = x_own.shape
    inner = wide.shape[-1] // 2
    bf16 = jnp.bfloat16
    hbm = pl.BlockSpec(memory_space=pl.ANY)
    dma = pltpu.SemaphoreType.DMA
    weight = pltpu.VMEM((dp, depth) + wide.shape[2:], bf16)
    whole = jax.ShapeDtypeStruct((dp, 2, size, width), bf16)
    thin = jax.ShapeDtypeStruct((dp, 2, size, inner), bf16)
    return pl.pallas_call(
        functools.partial(mlp_forward_kernel, dp, depth),
        out_shape=(whole, whole, thin, thin, thin, jax.ShapeDtypeStruct((inner, width), bf16)),
        in_specs=[hbm] * (2 + dp),
        out_specs=(hbm,) * 6,
        scratch_shapes=[
            pltpu.VMEM((dp, 2, size, width), bf16),
            pltpu.VMEM((dp, 2, size, width), bf16),
            weight,
            pltpu.VMEM((inner, 2 * dp * size), bf16),
            pltpu.VMEM((2, 3, size, inner), bf16),
            pltpu.VMEM((2, inner, 256), bf16),
            dma((2 * depth + 1 + dp,)),
            dma,
            dma((dp,)),
            dma((dp,)),
            dma((dp,)),
            dma((dp,)),
            dma((2,)),
            dma((2,)),
            dma((dp, 2)),
            dma((2, 3)),
            dma((2,)),
            dma((dp,)),
            dma((dp,)),
        ],
        compiler_params=pltpu.CompilerParams(
            collective_id=1, has_side_effects=True, vmem_limit_bytes=VMEM_LIMIT
        ),
        cost_estimate=LIGHT,
        name="mlp_forward",
    )(x_own, wide, *cots)


def mlp_backward_kernel(
    dp,
    depth,
    tokens_hbm,
    cots_hbm,
    hidden_hbm,
    slope_hbm,
    active_hbm,
    wide_hbm,
    down_hbm,
    grad_ref,
    part_hbm,
    wide_grad_hbm,
    tokens,
    wides,
    downs,
    gate_t,
    up_t,
    cot_slots,
    chunk,
    part_out,
    part_side,
    tile_out,
    load_sem,
    slot_sem,
    part_sem,
    part_send,
    part_got,
    tile_sem,
    *sum_refs,
):
    bf16 = jnp.bfloat16
    _, _, core, peer, twin = team_places()
    size, width = grad_ref.shape
    loads = [pltpu.make_async_copy(down_hbm, downs, load_sem.at[0])]
    for z in range(depth):
        loads.append(pltpu.make_async_copy(wide_hbm.at[z], wides.at[:, z], load_sem.at[1 + z]))
    tokens_load = pltpu.make_async_copy(tokens_hbm, tokens, load_sem.at[depth + 1])

    def slot_loads(k, e, slot):
        copies = [pltpu.make_async_copy(cots_hbm.at[k, e], cot_slots.at[slot], slot_sem.at[slot, 3])]
        for i, source in enumerate((hidden_hbm, slope_hbm, active_hbm)):
            copies.append(
                pltpu.make_async_copy(source.at[k, e], chunk.at[slot, i], slot_sem.at[slot, i])
            )
        return copies

    for copy in slot_loads(dp - 1, 1 - core, 0):
        copy.start()
    for load in loads:
        load.start()
    greet([peer(k) for k in range(1, 3)] + [twin])
    for load in loads:
        load.wait()
    tokens_load.start()

    def part_copy(k):
        return pltpu.make_async_copy(part_out.at[1], part_hbm.at[k], part_sem)

    def part_side_copy(k):
        return send(part_out.at[0], part_side.at[k], part_send.at[k], part_got.at[k], twin)

    def product(k, e, turn):
        slot = turn
        for copy in slot_loads(k, e, slot):
            copy.wait()
        if turn == 0:
            for copy in slot_loads(k, core, 1):
                copy.start()
        else:

            @pl.when(k > 0)
            def _():
                for copy in slot_loads(k - 1, 1 - core, 0):
                    copy.start()

        grad_hid = contract_last(cot_slots[slot], downs[...])
        grad_gate = (grad_hid * chunk[slot, 1].astype(jnp.float32)).astype(bf16)
        grad_up = (grad_hid * chunk[slot, 2].astype(jnp.float32)).astype(bf16)
        spot = pl.ds(pl.multiple_of((k * 2 + e) * size, size), size)
        gate_t[:, spot] = grad_gate.T
        up_t[:, spot] = grad_up.T
        terms = multiply(chunk[slot, 0], downs[...])
        if turn == 0:

            @pl.when(k < dp - 1)
            def _():
                part_side_copy(k + 1).wait_send()

            part_out[0] = terms.astype(bf16)
            part_side_copy(k).start()
        else:

            @pl.when(k < dp - 1)
            def _():
                part_copy(k + 1).wait()

            part_side_copy(k).wait_recv()
            part_out[1] = (terms + part_side[k].astype(jnp.float32)).astype(bf16)
            part_copy(k).start()
        both = jnp.concatenate([grad_gate, grad_up], axis=1)
        return contract_last(both, wides[...].reshape(width, -1))

    complete = plane_sum(dp, product, grad_ref, sum_refs)
    tokens_load.wait()
    block = 256
    count = width // block

    def tile_copies(which, j, slot):
        per = depth * 128 // block
        return [
            pltpu.make_async_copy(
                tile_out.at[slot, :, pl.ds(i * 128, 128)],
                wide_grad_hbm.at[lax.rem(j, per) * (block // 128) + i, which, j // per],
                tile_sem.at[slot, i],
            )
            for i in range(block // 128)
        ]

    for which, left in ((0, gate_t), (1, up_t)):

        def tile(j, carry, which=which, left=left):
            slot = lax.rem(j, 2)

            @pl.when(j > 1)
            def _():
                for copy in tile_copies(which, j - 2, slot):
                    copy.wait()

            spot = pl.ds(pl.multiple_of(j * block, block), block)
            columns = tokens[:, :, :, spot].reshape(-1, block)
            tile_out[slot] = multiply(left[...], columns).astype(bf16)
            for copy in tile_copies(which, j, slot):
                copy.start()
            return carry

        lax.fori_loop(0, count, tile, 0)
        for j in (count - 2, count - 1):
            for copy in tile_copies(which, j, j % 2):
                copy.wait()
    complete()
    part_side_copy(0).wait_send()
    part_copy(0).wait()


def mlp_backward(tokens, cots, hidden, slope, active, wide, down):
    depth, dp = wide.shape[:2]
    size, width = tokens.shape[2:]
    inner = wide.shape[-1] // 2
    f32, bf16 = jnp.float32, jnp.bfloat16
    hbm = pl.BlockSpec(memory_space=pl.ANY)
    dma = pltpu.SemaphoreType.DMA
    weight = pltpu.VMEM((dp, depth) + wide.shape[2:], bf16)
    turned = pltpu.VMEM((inner, 2 * dp * size), bf16)
    return pl.pallas_call(
        functools.partial(mlp_backward_kernel, dp, depth),
        out_shape=(
            jax.ShapeDtypeStruct((size, width), f32),
            jax.ShapeDtypeStruct((dp, size, width), bf16),
            jax.ShapeDtypeStruct((depth, 2, dp, inner, width // (depth * dp)), bf16),
        ),
        in_specs=[hbm] * 7,
        out_specs=(pl.BlockSpec(memory_space=pltpu.VMEM), hbm, hbm),
        scratch_shapes=[
            pltpu.VMEM((dp, 2, size, width), bf16),
            weight,
            pltpu.VMEM((inner, width), bf16),
            turned,
            turned,
            pltpu.VMEM((2, size, width), bf16),
            pltpu.VMEM((2, 3, size, inner), bf16),
            pltpu.VMEM((2, size, width), bf16),
            pltpu.VMEM((dp, size, width), bf16),
            pltpu.VMEM((2, inner, 256), bf16),
            dma((2 * depth + 2,)),
            dma((2, 4)),
            dma,
            dma((dp,)),
            dma((dp,)),
            dma((2, 2)),
        ]
        + sum_scratch(dp, size, width),
        compiler_params=pltpu.CompilerParams(
            collective_id=6, has_side_effects=True, vmem_limit_bytes=60 * 1024 * 1024
        ),
        cost_estimate=LIGHT,
        name="mlp_backward",
    )(tokens, cots, hidden, slope, active, wide, down)


def attend_sum_kernel(
    dp, rows, context_ref, weight_ref, own_ref, gain_ref, middle_ref, normed_ref, *scratch
):
    _, _, _, peer, twin = team_places()
    length = own_ref.shape[1]
    size, width = middle_ref.shape
    greet([peer(k) for k in range(1, 3)] + [twin])

    def product(k, e, turn):
        spot = pl.ds(pl.multiple_of(e * length, length), length)
        block = context_ref[pl.ds(k * rows, rows), spot].reshape(size, -1)
        return multiply(block, weight_ref[...])

    plane_sum(dp, product, middle_ref, scratch)()
    middle = middle_ref[...] + own_ref[...].reshape(size, width).astype(jnp.float32)
    middle_ref[...] = middle
    factor = lax.rsqrt(jnp.mean(middle * middle, axis=-1, keepdims=True) + EPSILON)
    normed_ref[...] = (middle * factor * gain_ref[1:2].astype(jnp.float32)).astype(jnp.bfloat16)


def attend_sum(dp, context, weight, own, gain):
    rows, length, width = own.shape
    size = rows * length
    vmem = pl.BlockSpec(memory_space=pltpu.VMEM)
    return pl.pallas_call(
        functools.partial(attend_sum_kernel, dp, rows),
        out_shape=(
            jax.ShapeDtypeStruct((size, width), jnp.float32),
            jax.ShapeDtypeStruct((size, width), jnp.bfloat16),
        ),
        in_specs=[vmem] * 4,
        out_specs=(vmem, vmem),
        scratch_shapes=sum_scratch(dp, size, width),
        compiler_params=pltpu.CompilerParams(
            collective_id=4, has_side_effects=True, vmem_limit_bytes=VMEM_LIMIT
        ),
        cost_estimate=LIGHT,
        name="attend_sum",
    )(context, weight, own, gain)


def middle_back_kernel(
    dp,
    rows,
    grad_ref,
    middle_ref,
    cot_ref,
    gain_ref,
    context_ref,
    weight_ref,
    grad_middle_ref,
    grad_context_ref,
    weight_grad_ref,
    tokens,
    context_t,
    near_send,
    near_got,
    side_send,
    side_got,
    pass_send,
    pass_got,
):
    f32, bf16 = jnp.float32, jnp.bfloat16
    _, _, core, peer, twin = team_places()
    size, width = grad_ref.shape
    length = size // rows
    half = size // 2
    greet([peer(k) for k in range(1, 3)] + [twin])
    middle = middle_ref[...]
    factor = lax.rsqrt(jnp.mean(middle * middle, axis=-1, keepdims=True) + EPSILON)
    inner = grad_ref[...] * gain_ref[1:2].astype(f32)
    mean = jnp.mean(inner * middle, axis=-1, keepdims=True)
    total = cot_ref[...].astype(f32) + factor * inner - factor * factor * factor * middle * mean
    grad_middle_ref[...] = total
    tokens[0, core] = total.astype(bf16)

    def near_copy(k):
        return send(
            tokens.at[0, core], tokens.at[k, core], near_send.at[k], near_got.at[k], peer(k)
        )

    def pass_copy(part):
        spot = pl.ds(part * half, half)
        return send(
            tokens.at[1 + part, core, spot],
            tokens.at[3, core, spot],
            pass_send.at[part],
            pass_got.at[part],
            peer(2 - part),
        )

    def side_copy(k):
        block = tokens.at[k, core]
        return send(block, block, side_send.at[k], side_got.at[k], twin)

    def side_arrival(k):
        block = tokens.at[k, 1 - core]
        return send(block, block, side_send.at[k], side_got.at[k], twin)

    near_copy(1).start()
    near_copy(2).start()
    side_copy(0).start()
    for k in range(dp):
        for e in range(2):
            for r in range(rows):
                block = context_ref[k * rows + r, e * length : (e + 1) * length]
                spot = pl.ds(((k * 2 + e) * rows + r) * length, length)
                context_t[:, spot] = block.T

    def process(k, e):
        block = contract_last(tokens[k, e], weight_ref[...]).astype(bf16)
        spot = pl.ds(pl.multiple_of(e * length, length), length)
        grad_context_ref[pl.ds(k * rows, rows), spot] = block.reshape(rows, length, -1)

    process(0, core)
    side_arrival(0).wait_recv()
    process(0, 1 - core)
    for k in range(1, 3):
        near_copy(k).wait_recv()
        pass_copy(k - 1).start()
        side_copy(k).start()

    def step(k, carry):
        @pl.when(k == 3)
        def _():
            pass_copy(0).wait_recv()
            pass_copy(1).wait_recv()
            side_copy(3).start()

        process(k, core)
        side_arrival(k).wait_recv()
        process(k, 1 - core)
        return carry

    lax.fori_loop(1, dp, step, 0)

    def tile(j, carry):
        spot = pl.ds(pl.multiple_of(j * 256, 256), 256)
        columns = tokens[:, :, :, spot].reshape(-1, 256)
        weight_grad_ref[:, spot] = multiply(context_t[...], columns).astype(bf16)
        return carry

    lax.fori_loop(0, width // 256, tile, 0)
    for k in range(1, 3):
        near_copy(k).wait_send()
        pass_copy(k - 1).wait_send()
    for k in range(dp):
        side_copy(k).wait_send()


def middle_back(dp, rows, grad, middle, cot, gain, context, weight):
    f32, bf16 = jnp.float32, jnp.bfloat16
    size, width = grad.shape
    vmem = pl.BlockSpec(memory_space=pltpu.VMEM)
    dma = pltpu.SemaphoreType.DMA
    return pl.pallas_call(
        functools.partial(middle_back_kernel, dp, rows),
        out_shape=(
            jax.ShapeDtypeStruct((size, width), f32),
            jax.ShapeDtypeStruct(context.shape, bf16),
            jax.ShapeDtypeStruct(weight.shape, bf16),
        ),
        in_specs=[vmem] * 6,
        out_specs=(vmem, vmem, vmem),
        scratch_shapes=[
            pltpu.VMEM((dp, 2, size, width), bf16),
            pltpu.VMEM((weight.shape[0], 2 * dp * size), bf16),
            dma((dp,)),
            dma((dp,)),
            dma((dp,)),
            dma((dp,)),
            dma((2,)),
            dma((2,)),
        ],
        compiler_params=pltpu.CompilerParams(
            collective_id=5, has_side_effects=True, vmem_limit_bytes=VMEM_LIMIT
        ),
        cost_estimate=LIGHT,
        name="middle_back",
    )(grad, middle, cot, gain, context, weight)


def open_kernel(
    dp,
    depth,
    query_ref,
    key_ref,
    value_ref,
    attn_gain_ref,
    mlp_gain_ref,
    places_ref,
    own_ref,
    out_ref,
    attn_hbm,
    places_hbm,
    near_hbm,
    out_hbm,
    attn_blocks,
    local_sem,
    attn_send,
    attn_got,
    places_send,
    places_got,
    line_send,
    line_got,
    near_send,
    near_got,
    pass_send,
    pass_got,
    out_send,
    out_got,
):
    data, place, core, peer, twin = team_places()
    part = query_ref.shape[0]
    half = HD // 2
    side = depth * half
    middle = own_ref.shape[0] // 2
    attn_blocks[...] = jnp.zeros_like(attn_blocks)
    for d in range(dp):
        for c in range(2):
            team = 2 * d + c
            for z in range(depth):
                owner = (d * depth + z) * 2 + c
                for h in range(2):
                    spot = owner * HD + h * half
                    attn_blocks[team, :, h * side + z * half : h * side + (z + 1) * half] = (
                        query_ref[:, spot : spot + half]
                    )
            pair = key_ref if c == 0 else value_ref
            last = 2 * side + HD
            attn_blocks[team, :, 2 * side : last] = pair[:, d * HD : (d + 1) * HD]
            attn_blocks[team, 0:1, last : last + part] = attn_gain_ref[...]
            attn_blocks[team, 1:2, last : last + part] = mlp_gain_ref[...]

    def device(k, other):
        return (peer(k)[0], place, 1 - core if other else core)

    def number(k, other):
        return 2 * peer(k)[0] + (1 - core if other else core)

    pairs = [(k, other) for k in range(dp) for other in range(2) if k or other]
    greet([device(k, other) for k, other in pairs] + line_neighbours(depth))

    def attn_copy(k, other):
        return send(
            attn_blocks.at[number(k, other)],
            attn_hbm.at[place, data, core],
            attn_send.at[k, other],
            attn_got.at[k, other],
            device(k, other),
        )

    def places_copy(k, other):
        return send(
            places_ref,
            places_hbm.at[k, core],
            places_send.at[k, other],
            places_got.at[k, other],
            device(k, other),
        )

    def arrival(target, send_sem, got_sem):
        return send(target, target, send_sem, got_sem, twin)

    def near_copy(k):
        return send(own_ref, near_hbm.at[k], near_send.at[k], near_got.at[k], peer(k))

    def pass_copy(which):
        spot = pl.ds(which * middle, middle)
        return send(
            near_hbm.at[1 + which, spot],
            near_hbm.at[3, spot],
            pass_send.at[which],
            pass_got.at[which],
            peer(2 - which),
        )

    start, relay, complete = line_gather(depth, lambda z: attn_hbm.at[z], line_send, line_got)
    out_start, out_relay, out_complete = line_gather(
        depth, lambda z: out_hbm.at[z], out_send, out_got
    )
    for k, other in pairs:
        attn_copy(k, other).start()
    for k, other in pairs:
        places_copy(k, other).start()
    near_copy(1).start()
    near_copy(2).start()
    locals_ = [
        pltpu.make_async_copy(
            attn_blocks.at[2 * data + core], attn_hbm.at[place, data, core], local_sem.at[0]
        ),
        pltpu.make_async_copy(places_ref, places_hbm.at[0, core], local_sem.at[1]),
        pltpu.make_async_copy(own_ref, near_hbm.at[0], local_sem.at[2]),
        pltpu.make_async_copy(out_ref, out_hbm.at[place], local_sem.at[3]),
    ]
    for copy in locals_:
        copy.start()
    locals_[0].wait()
    for k, other in pairs:
        target = attn_hbm.at[place, peer(k)[0], 1 - core if other else core]
        arrival(target, attn_send.at[k, other], attn_got.at[k, other]).wait_recv()
    start()
    for copy in locals_[1:]:
        copy.wait()
    out_start()
    relay(1)
    for which in range(2):
        near_copy(1 + which).wait_recv()
        pass_copy(which).start()
    for distance in range(2, depth):
        relay(distance)
        out_relay(distance - 1)
    out_relay(depth - 1)
    for k, other in pairs:
        target = places_hbm.at[k, 1 - core if other else core]
        arrival(target, places_send.at[k, other], places_got.at[k, other]).wait_recv()
    for which in range(2):
        pass_copy(which).wait_recv()
        pass_copy(which).wait_send()
        near_copy(1 + which).wait_send()
    complete()
    out_complete()
    for k, other in pairs:
        attn_copy(k, other).wait_send()
        places_copy(k, other).wait_send()


def open_layer(dp, depth, query, key, value, attn_gain, mlp_gain, places, own, out_weight):
    part = query.shape[0]
    columns = depth * HD + HD + part
    bf16 = jnp.bfloat16
    hbm = pl.BlockSpec(memory_space=pl.ANY)
    vmem = pl.BlockSpec(memory_space=pltpu.VMEM)
    dma = pltpu.SemaphoreType.DMA
    return pl.pallas_call(
        functools.partial(open_kernel, dp, depth),
        out_shape=(
            jax.ShapeDtypeStruct((depth, dp, 2, part, columns), bf16),
            jax.ShapeDtypeStruct((dp, 2) + places.shape, places.dtype),
            jax.ShapeDtypeStruct((dp,) + own.shape, bf16),
            jax.ShapeDtypeStruct((depth,) + out_weight.shape, bf16),
        ),
        in_specs=[vmem] * 8,
        out_specs=(hbm,) * 4,
        scratch_shapes=[
            pltpu.VMEM((2 * dp, part, columns), bf16),
            dma((4,)),
            dma((dp, 2)),
            dma((dp, 2)),
            dma((dp, 2)),
            dma((dp, 2)),
            dma((depth, 2)),
            dma((depth,)),
            dma((dp,)),
            dma((dp,)),
            dma((2,)),
            dma((2,)),
            dma((depth, 2)),
            dma((depth,)),
        ],
        compiler_params=pltpu.CompilerParams(
            collective_id=7, has_side_effects=True, vmem_limit_bytes=VMEM_LIMIT
        ),
        cost_estimate=LIGHT,
        name="open_layer",
    )(query, key, value, attn_gain[None], mlp_gain[None], places, own, out_weight)


def project_kernel(
    dp,
    depth,
    rows,
    *refs,
):
    pieces, places_ref, freq_ref, freq_pair_ref, gate_ref, up_ref, weight_hbm = refs[:7]
    query_ref, normed_ref, cosine_ref, sine_ref, cosine_pair_ref, sine_pair_ref = refs[7:13]
    offset_ref, gain_ref, pair_weight_ref, line_hbm, wide_hbm = refs[13:18]
    (
        weight,
        pair,
        far_pieces,
        load_sem,
        own_sem,
        line_send,
        line_got,
        side_send,
        side_got,
        twin_send,
        twin_got,
        wide_blocks,
        wide_send,
        wide_got,
        wide_sem,
    ) = refs[18:]
    f32, bf16 = jnp.float32, jnp.bfloat16
    data, place, core, peer, twin = team_places()
    length, width = pieces.shape[2:]
    part = weight.shape[3]
    columns = query_ref.shape[2]
    loads = [
        pltpu.make_async_copy(
            weight_hbm.at[z], weight.at[:, z], load_sem.at[z]
        )
        for z in range(depth)
    ]
    for load in loads:
        load.start()

    def device(k, other):
        return (peer(k)[0], place, 1 - core if other else core)

    def number(k, other):
        return 2 * peer(k)[0] + (1 - core if other else core)

    pairs = [(k, other) for k in range(dp) for other in range(2) if k or other]
    greet(line_neighbours(depth) + [device(k, other) for k, other in pairs])

    def wide_copy(k, other):
        return send(
            wide_blocks.at[number(k, other)],
            wide_hbm.at[data, core],
            wide_send.at[k, other],
            wide_got.at[k, other],
            device(k, other),
        )


    def twin_copy(k):
        return send(pieces.at[k], far_pieces.at[k], twin_send.at[k], twin_got.at[k], twin)

    for k in range(dp):
        twin_copy(k).start()
    count = wide_blocks.shape[2] // (2 * depth)
    for d in range(dp):
        for c in range(2):
            for z in range(depth):
                owner = (d * depth + z) * 2 + c
                for which, source in ((0, gate_ref), (1, up_ref)):
                    spot = (which * depth + z) * count
                    wide_blocks[2 * d + c, :, spot : spot + count] = source[
                        :, owner * count : (owner + 1) * count
                    ]
    wide_local = pltpu.make_async_copy(
        wide_blocks.at[2 * data + core], wide_hbm.at[data, core], wide_sem
    )
    wide_local.start()
    for k, other in pairs:
        wide_copy(k, other).start()
    for load in loads:
        load.wait()
    for d in range(dp):
        for z in range(depth):
            for c in range(2):
                spot = ((d * depth + z) * 2 + c) * part
                gain_ref[:, spot : spot + part] = weight[d, z, c, 0:2, columns + HD :]
    pair_weight_ref[...] = weight[...].reshape(width, -1)[:, columns : columns + HD].T
    gain = gain_ref[0:1].astype(f32)
    turning = (1 - core).astype(f32)

    def block_of(which, z, k):
        return line_hbm.at[which, z, pl.ds(k * rows, rows)]

    def pair_of(k):
        return pair.at[pl.ds(k * rows, rows)]

    def own_copy(k):
        return pltpu.make_async_copy(pair_of(k), block_of(core, place, k), own_sem.at[k])

    def own_side_copy(k):
        return send(
            pair_of(k),
            block_of(core, place, k),
            side_send.at[place, k],
            side_got.at[place, k],
            twin,
        )

    def line_copy(z, k):
        block = block_of(core, place if z is None else z, k)
        return send(
            pair_of(k) if z is None else block,
            block,
            line_send.at[place if z is None else z, k],
            line_got.at[place if z is None else z, k],
            (data, lax.rem(place + 1, depth), core),
        )

    def line_arrival(z, k):
        block = block_of(core, z, k)
        return send(block, block, line_send.at[z, k], line_got.at[z, k], twin)

    def side_copy(z, k):
        block = block_of(core, z, k)
        return send(block, block, side_send.at[z, k], side_got.at[z, k], twin)

    def side_arrival(z, k):
        block = block_of(1 - core, z, k)
        return send(block, block, side_send.at[z, k], side_got.at[z, k], twin)

    for k in range(dp):
        for far in range(2):
            e = core if far == 0 else 1 - core
            if far:
                twin_copy(k).wait_recv()
            source = far_pieces.at[k] if far else pieces.at[k]
            values = source[...].reshape(rows * length, width).astype(f32)
            factor = lax.rsqrt(jnp.mean(values * values, axis=-1, keepdims=True) + EPSILON)
            normed = (values * factor * gain).astype(bf16)
            normed_ref[k, e] = normed
            result = multiply(normed, weight[...].reshape(width, -1))
            spot = pl.ds(pl.multiple_of(e * length, length), length)
            for r in range(rows):
                row = k * rows + r
                block = result[r * length : (r + 1) * length]
                offsets = places_ref[k, e][r : r + 1].astype(f32)
                column = jnp.broadcast_to(offsets, (length, length)).T
                offset_ref[row, spot] = column.astype(jnp.int32)
                angles = column * freq_ref[...]
                cosine, sine = jnp.cos(angles), jnp.sin(angles)
                cosine_ref[row, spot] = cosine
                sine_ref[row, spot] = sine
                first, second = block[:, : columns // 2], block[:, columns // 2 : columns]
                turned = (first * cosine - second * sine).astype(bf16)
                query_ref[row, spot, : columns // 2] = turned * bf16(HD ** (-0.5))
                turned = (second * cosine + first * sine).astype(bf16)
                query_ref[row, spot, columns // 2 :] = turned * bf16(HD ** (-0.5))
                keys = block[:, columns : columns + HD].T
                angles = offsets * freq_pair_ref[...] * turning
                cosine, sine = jnp.cos(angles), jnp.sin(angles)
                cosine_pair_ref[row, :, spot] = cosine
                sine_pair_ref[row, :, spot] = sine
                first, second = keys[: HD // 2], keys[HD // 2 :]
                pair[row, : HD // 2, spot] = (first * cosine - second * sine).astype(bf16)
                pair[row, HD // 2 :, spot] = (second * cosine + first * sine).astype(bf16)
        own_copy(k).start()
        own_side_copy(k).start()

        @pl.when(place < depth - 1)
        def _(k=k):
            line_copy(None, k).start()

    for z in reversed(range(depth)):
        for k in range(dp):

            @pl.when(z < place)
            def _(z=z, k=k):
                line_arrival(z, k).wait_recv()
                side_copy(z, k).start()

            @pl.when((z < place) & (place < depth - 1))
            def _(z=z, k=k):
                line_copy(z, k).start()

    wide_local.wait()
    for k, other in pairs:
        block = wide_hbm.at[peer(k)[0], 1 - core if other else core]
        send(block, block, wide_send.at[k, other], wide_got.at[k, other], twin).wait_recv()
        wide_copy(k, other).wait_send()
    for k in range(dp):
        twin_copy(k).wait_send()
        own_copy(k).wait()
        own_side_copy(k).wait_send()
        for z in range(depth):

            @pl.when(z <= place)
            def _(z=z, k=k):
                side_arrival(z, k).wait_recv()

            @pl.when(z < place)
            def _(z=z, k=k):
                side_copy(z, k).wait_send()

            @pl.when((z <= place) & (place < depth - 1))
            def _(z=z, k=k):
                line_copy(z, k).wait_send()


def project(near, places, freqs, gate, up, weight):
    f32, bf16 = jnp.float32, jnp.bfloat16
    dp, rows, length, width = near.shape
    depth = weight.shape[0]
    heads = depth
    row_count, size = dp * rows, 2 * length
    columns = heads * HD
    part = width // (2 * dp * depth)
    hbm = pl.BlockSpec(memory_space=pl.ANY)
    vmem = pl.BlockSpec(memory_space=pltpu.VMEM)
    dma = pltpu.SemaphoreType.DMA
    turned = jax.ShapeDtypeStruct((row_count, size, columns // 2), f32)
    turned_pair = jax.ShapeDtypeStruct((row_count, HD // 2, size), f32)
    return pl.pallas_call(
        functools.partial(project_kernel, dp, depth, rows),
        out_shape=(
            jax.ShapeDtypeStruct((row_count, size, columns), bf16),
            jax.ShapeDtypeStruct((dp, 2, rows * length, width), bf16),
            turned,
            turned,
            turned_pair,
            turned_pair,
            jax.ShapeDtypeStruct((row_count, size, length), jnp.int32),
            jax.ShapeDtypeStruct((2, width), bf16),
            jax.ShapeDtypeStruct((HD, width), bf16),
            jax.ShapeDtypeStruct((2, depth, row_count, HD, size), bf16),
            jax.ShapeDtypeStruct((dp, 2, part, gate.shape[1] // dp), bf16),
        ),
        in_specs=[vmem] * 6 + [hbm],
        out_specs=(vmem,) * 9 + (hbm,) * 2,
        scratch_shapes=[
            pltpu.VMEM((dp, depth) + weight.shape[2:], bf16),
            pltpu.VMEM((row_count, HD, size), bf16),
            pltpu.VMEM((dp, rows, length, width), bf16),
            dma((2 * depth,)),
            dma((dp,)),
            dma((depth, dp)),
            dma((depth, dp)),
            dma((depth, dp)),
            dma((depth, dp)),
            dma((dp,)),
            dma((dp,)),
            pltpu.VMEM((2 * dp, part, gate.shape[1] // dp), bf16),
            dma((dp, 2)),
            dma((dp, 2)),
            dma,
        ],
        compiler_params=pltpu.CompilerParams(
            collective_id=2, has_side_effects=True, vmem_limit_bytes=VMEM_LIMIT
        ),
        cost_estimate=LIGHT,
        name="project",
    )(near, places, jnp.tile(freqs, heads)[None], freqs[:, None], gate, up, weight)


def finish_kernel(
    dp,
    depth,
    rows,
    query_ref,
    cosine_ref,
    sine_ref,
    wide_ref,
    own_ref,
    grad_middle_ref,
    gain_ref,
    query_weight_ref,
    key_weight_ref,
    value_weight_ref,
    gate_weight_ref,
    up_weight_ref,
    grad_k_hbm,
    grad_v_hbm,
    normed_hbm,
    weight_hbm,
    *refs,
):
    pair_hbms, refs = refs[:dp], refs[dp:]
    finish_body(
        dp, depth, rows, query_ref, cosine_ref, sine_ref, wide_ref, own_ref,
        grad_middle_ref, gain_ref, query_weight_ref, key_weight_ref, value_weight_ref,
        gate_weight_ref, up_weight_ref, grad_k_hbm, grad_v_hbm, normed_hbm, weight_hbm, pair_hbms,
        *refs,
    )


def finish_body(
    dp,
    depth,
    rows,
    query_ref,
    cosine_ref,
    sine_ref,
    wide_ref,
    own_ref,
    grad_middle_ref,
    gain_ref,
    query_weight_ref,
    key_weight_ref,
    value_weight_ref,
    gate_weight_ref,
    up_weight_ref,
    grad_k_hbm,
    grad_v_hbm,
    normed_hbm,
    weight_hbm,
    pair_hbms,
    grad_ref,
    query_grad_ref,
    key_grad_ref,
    value_grad_ref,
    gate_grad_ref,
    up_grad_ref,
    attn_gain_ref,
    mlp_gain_ref,
    normed,
    weight,
    kept,
    given,
    arrived,
    line_block,
    line_got_block,
    terms,
    terms_t,
    held,
    line_grads,
    line_grads_got,
    team_block,
    team_got_block,
    wide_block,
    wide_got_block,
    load_sem,
    swap_send,
    swap_got,
    line_send,
    line_got,
    grads_send,
    grads_got,
    team_send,
    team_got,
    wide_send,
    wide_got,
    pair_weight,
    pair_out,
    pair_in,
    pair_load_sem,
    pair_twin_send,
    pair_twin_got,
    pair_send,
    pair_got,
    *sum_refs,
):
    f32, bf16 = jnp.float32, jnp.bfloat16
    data, place, core, peer, twin = team_places()
    columns = query_ref.shape[2]
    size = query_ref.shape[1]
    length = size // 2
    width = grad_ref.shape[1]
    part = weight.shape[3]
    features = columns + HD
    half = HD // 2
    loads = [
        pltpu.make_async_copy(
            weight_hbm.at[z, :, :, :, pl.ds(0, columns)],
            weight.at[:, z],
            load_sem.at[z],
        )
        for z in range(depth)
    ]
    pair_loads = [
        pltpu.make_async_copy(pair_hbms[k], pair_weight.at[k, core], pair_load_sem.at[k])
        for k in range(dp)
    ]
    loads.append(pltpu.make_async_copy(normed_hbm, normed, load_sem.at[depth]))

    @pl.when(core == 0)
    def _():
        pltpu.make_async_copy(grad_k_hbm, kept, load_sem.at[depth + 1]).start()
        pltpu.make_async_copy(grad_v_hbm, given, load_sem.at[depth + 2]).start()

    @pl.when(core == 1)
    def _():
        pltpu.make_async_copy(grad_v_hbm, kept, load_sem.at[depth + 1]).start()
        pltpu.make_async_copy(grad_k_hbm, given, load_sem.at[depth + 2]).start()

    for load in loads + pair_loads:
        load.start()
    others = [(data, lax.rem(place + step, depth), core) for step in range(1, depth)]

    def device(k, other):
        return (peer(k)[0], place, 1 - core if other else core)

    pairs = [(k, other) for k in range(dp) for other in range(2) if k or other]
    greet(others + [device(k, other) for k, other in pairs])
    pltpu.make_async_copy(grad_v_hbm, given, load_sem.at[depth + 2]).wait()
    swap_copy = send(given, arrived, swap_send, swap_got, twin)
    swap_copy.start()

    def pair_twin(k):
        block = pair_weight.at[k, core]
        return send(block, block, pair_twin_send.at[k], pair_twin_got.at[k], twin)

    def pair_twin_arrival(k):
        block = pair_weight.at[k, 1 - core]
        return send(block, block, pair_twin_send.at[k], pair_twin_got.at[k], twin)

    def pair_copy(k, other):
        e = 1 - core if other else core
        return send(
            pair_out.at[k, e],
            pair_in.at[k, core],
            pair_send.at[k, other],
            pair_got.at[k, other],
            device(k, other),
        )

    def pair_arrival(k, other):
        block = pair_in.at[k, 1 - core if other else core]
        return send(block, block, pair_send.at[k, other], pair_got.at[k, other], twin)

    def wide_copy(k, other):
        spot = (peer(k)[0], 1 - core if other else core)
        return send(
            wide_block.at[spot],
            wide_got_block.at[data, core],
            wide_send.at[k, other],
            wide_got.at[k, other],
            device(k, other),
        )

    def wide_arrival(k, other):
        block = wide_got_block.at[peer(k)[0], 1 - core if other else core]
        return send(block, block, wide_send.at[k, other], wide_got.at[k, other], twin)

    def line_copy(z):
        return send(
            line_block.at[z],
            line_got_block.at[place],
            line_send.at[z],
            line_got.at[place],
            (data, z, core),
        )

    def line_arrival(z):
        block = line_got_block.at[z]
        return send(block, block, line_send.at[z], line_got.at[z], twin)

    pltpu.make_async_copy(grad_k_hbm, kept, load_sem.at[depth + 1]).wait()
    swap_copy.wait_recv()
    for z in range(depth):

        @pl.when(z < place)
        def _(z=z):
            total = kept[z].astype(f32) + arrived[z].astype(f32)
            line_block[z] = total.astype(bf16)
            line_copy(z).start()

    for load in loads:
        load.wait()
    for k in range(dp):
        for e in range(2):
            for r in range(rows):
                block = query_ref[k * rows + r, e * length : (e + 1) * length]
                terms[k, e, r * length : (r + 1) * length] = block
                spot = pl.ds(((k * 2 + e) * rows + r) * length, length)
                terms_t[:columns, spot] = block.T

    def tile_rows(first, count):
        def tile(j, carry):
            spot = pl.ds(pl.multiple_of(j * 256, 256), 256)
            block = multiply(
                terms_t[first : first + count], normed[:, :, :, spot].reshape(-1, 256)
            ).astype(bf16)
            for i in range(2):
                group = 2 * j + i
                line_grads[lax.rem(group, depth), group // depth, first : first + count] = block[
                    :, i * 128 : (i + 1) * 128
                ]
            return carry

        lax.fori_loop(0, width // 256, tile, 0)

    def grads_copy(z, piece):
        spot = pl.ds(piece * columns, HD if piece else columns)
        return send(
            line_grads.at[z, :, spot],
            line_grads_got.at[place, :, spot],
            grads_send.at[z, piece],
            grads_got.at[place, piece],
            (data, z, core),
        )

    def grads_arrival(z, piece):
        spot = pl.ds(piece * columns, HD if piece else columns)
        block = line_grads_got.at[z, :, spot]
        return send(block, block, grads_send.at[z, piece], grads_got.at[z, piece], twin)

    def product(k, e, turn):
        return contract_last(terms[k, e], weight[...].reshape(width, columns))

    complete = plane_sum(dp, product, grad_ref, sum_refs)
    for k in range(dp):
        pair_loads[k].wait()
        pair_twin(k).start()
    for which in range(2):
        for d in range(dp):
            block = wide_ref[which, d].T
            wide_block[d, 0, which] = block[:part]
            wide_block[d, 1, which] = block[part:]
    for k, other in pairs:
        wide_copy(k, other).start()
    wide_got_block[data, core] = wide_block[data, core]
    tile_rows(0, columns)
    for z in range(depth):

        @pl.when(z > place)
        def _(z=z):
            grads_copy(z, 0).start()

    for z in range(depth):

        @pl.when(z == place)
        def _(z=z):
            held[...] = kept[z].astype(f32) + arrived[z].astype(f32)

    for z in range(depth):

        @pl.when(z > place)
        def _(z=z):
            line_arrival(z).wait_recv()
            held[...] += line_got_block[z].astype(f32)

    for z in range(depth):

        @pl.when(z < place)
        def _(z=z):
            grads_copy(z, 0).start()

    for k in range(dp):
        for r in range(rows):
            row = k * rows + r
            first, second = held[row, :half], held[row, half:]
            cosine, sine = cosine_ref[row], sine_ref[row]
            turned = jnp.concatenate(
                [first * cosine + second * sine, second * cosine - first * sine], axis=0
            ).astype(bf16)
            for e in range(2):
                block = turned[:, e * length : (e + 1) * length]
                spot = pl.ds(((k * 2 + e) * rows + r) * length, length)
                terms_t[columns:, spot] = block
                pair_out[k, e, :, r * length : (r + 1) * length] = block
    for k, other in pairs:
        pair_copy(k, other).start()
    pair_in[0, core] = pair_out[0, core]

    tile_rows(columns, HD)
    for z in range(depth):

        @pl.when(z != place)
        def _(z=z):
            grads_copy(z, 1).start()

    for k, other in pairs:
        wide_arrival(k, other).wait_recv()
    count = wide_block.shape[4] // depth
    for d in range(dp):
        for c in range(2):
            for which, target in ((0, gate_grad_ref), (1, up_grad_ref)):
                block = wide_got_block[d, c, which].astype(f32)
                for z in range(depth):
                    spot = ((d * depth + z) * 2 + c) * count
                    target[:, spot : spot + count] = block[:, z * count : (z + 1) * count]
    products = gate_weight_ref[...].astype(f32) * gate_grad_ref[...]
    products = products + up_weight_ref[...].astype(f32) * up_grad_ref[...]
    mlp_gain_ref[...] = jnp.sum(products, axis=-1, keepdims=True)

    def team_copy(k, other, piece):
        spot = (peer(k)[0], 1 - core if other else core)
        return send(
            team_block.at[spot + (piece,)],
            team_got_block.at[data, core, piece],
            team_send.at[k, other, piece],
            team_got.at[k, other, piece],
            device(k, other),
        )

    def team_arrival(k, other, piece):
        block = team_got_block.at[peer(k)[0], 1 - core if other else core, piece]
        send_sem, got_sem = team_send.at[k, other, piece], team_got.at[k, other, piece]
        return send(block, block, send_sem, got_sem, twin)

    line_grads_got[place] = line_grads[place]

    def team_piece(piece, first, last):
        for z in range(depth):

            @pl.when(z != place)
            def _(z=z):
                grads_arrival(z, piece).wait_recv()

        for d in range(dp):
            total = line_grads_got[0, d, first:last].astype(f32)
            for z in range(1, depth):
                total = total + line_grads_got[z, d, first:last].astype(f32)
            total = total.T.astype(bf16)
            team_block[d, 0, piece, :, : last - first] = total[:part]
            team_block[d, 1, piece, :, : last - first] = total[part:]
        for k, other in pairs:
            team_copy(k, other, piece).start()
        team_got_block[data, core, piece] = team_block[data, core, piece]

    team_block[...] = jnp.zeros_like(team_block)
    team_piece(0, 0, columns)
    complete()
    for k, other in pairs:
        pair_arrival(k, other).wait_recv()
    for k in range(dp):
        pair_twin_arrival(k).wait_recv()
    grad_ref[...] += multiply(
        pair_in[...].reshape(2 * dp * HD, -1).T, pair_weight[...].reshape(2 * dp * HD, width)
    )
    own = own_ref[...].reshape(grad_ref.shape).astype(f32)
    factor = lax.rsqrt(jnp.mean(own * own, axis=-1, keepdims=True) + EPSILON)
    inner = grad_ref[...] * gain_ref[0:1].astype(f32)
    mean = jnp.mean(inner * own, axis=-1, keepdims=True)
    grad_ref[...] = grad_middle_ref[...] + factor * inner - factor * factor * factor * own * mean
    team_piece(1, columns, features)
    for k, other in pairs:
        team_arrival(k, other, 0).wait_recv()
    side = depth * half
    for d in range(dp):
        for c in range(2):
            block = team_got_block[d, c, 0].astype(f32)
            for z in range(depth):
                for h in range(2):
                    spot = ((d * depth + z) * 2 + c) * HD + h * half
                    start = h * side + z * half
                    query_grad_ref[:, spot : spot + half] = block[:, start : start + half]
    for k, other in pairs:
        team_arrival(k, other, 1).wait_recv()
    for d in range(dp):
        for c in range(2):
            target = key_grad_ref if c == 0 else value_grad_ref
            target[:, d * HD : (d + 1) * HD] = team_got_block[d, c, 1, :, :HD].astype(f32)
    attn_gain_ref[...] = sum(
        jnp.sum(before[...].astype(f32) * after[...], axis=-1, keepdims=True)
        for before, after in (
            (query_weight_ref, query_grad_ref),
            (key_weight_ref, key_grad_ref),
            (value_weight_ref, value_grad_ref),
        )
    )
    swap_copy.wait_send()
    for k in range(dp):
        pair_twin(k).wait_send()
    for k, other in pairs:
        team_copy(k, other, 0).wait_send()
        team_copy(k, other, 1).wait_send()
        pair_copy(k, other).wait_send()
        wide_copy(k, other).wait_send()
    for z in range(depth):

        @pl.when(z < place)
        def _(z=z):
            line_copy(z).wait_send()

        @pl.when(z != place)
        def _(z=z):
            grads_copy(z, 0).wait_send()
            grads_copy(z, 1).wait_send()


def finish(grad_queries, cosine_pair, sine_pair, wide_sum, own, grad_middle, gain, weights, grad_keys, grad_values, normed, weight, pair_weights):
    f32, bf16 = jnp.float32, jnp.bfloat16
    dp, _, size, width = normed.shape
    rows = own.shape[0]
    depth, row_count, features, line_size = grad_keys.shape
    columns = grad_queries.shape[2]
    part = width // (2 * dp * depth)
    inner = wide_sum.shape[2]
    total = columns + features
    hbm = pl.BlockSpec(memory_space=pl.ANY)
    vmem = pl.BlockSpec(memory_space=pltpu.VMEM)
    dma = pltpu.SemaphoreType.DMA
    line = pltpu.VMEM((depth, row_count, features, line_size), bf16)
    grads = pltpu.VMEM((depth, dp, total, 2 * part), bf16)
    team = pltpu.VMEM((dp, 2, 2, part, columns), bf16)
    wide = pltpu.VMEM((dp, 2, 2, part, inner), bf16)
    query_weight, key_weight, value_weight, gate_weight, up_weight = weights
    return pl.pallas_call(
        functools.partial(finish_kernel, dp, depth, rows),
        out_shape=(
            jax.ShapeDtypeStruct((size, width), f32),
            jax.ShapeDtypeStruct(query_weight.shape, f32),
            jax.ShapeDtypeStruct(key_weight.shape, f32),
            jax.ShapeDtypeStruct(value_weight.shape, f32),
            jax.ShapeDtypeStruct(gate_weight.shape, f32),
            jax.ShapeDtypeStruct(up_weight.shape, f32),
            jax.ShapeDtypeStruct((part, 1), f32),
            jax.ShapeDtypeStruct((part, 1), f32),
        ),
        in_specs=[vmem] * 12 + [hbm] * (4 + dp),
        out_specs=(vmem,) * 8,
        scratch_shapes=[
            pltpu.VMEM((dp, 2, size, width), bf16),
            pltpu.VMEM((dp, depth, 2, part, columns), bf16),
            line,
            line,
            line,
            line,
            line,
            pltpu.VMEM((dp, 2, size, columns), bf16),
            pltpu.VMEM((total, 2 * dp * size), bf16),
            pltpu.VMEM((row_count, features, line_size), f32),
            grads,
            grads,
            team,
            team,
            wide,
            wide,
            dma((depth + 3,)),
            dma,
            dma,
            dma((depth,)),
            dma((depth,)),
            dma((depth, 2)),
            dma((depth, 2)),
            dma((dp, 2, 2)),
            dma((dp, 2, 2)),
            dma((dp, 2)),
            dma((dp, 2)),
            pltpu.VMEM((dp, 2, features, width), bf16),
            pltpu.VMEM((dp, 2, features, size), bf16),
            pltpu.VMEM((dp, 2, features, size), bf16),
            dma((dp,)),
            dma((dp,)),
            dma((dp,)),
            dma((dp, 2)),
            dma((dp, 2)),
        ]
        + sum_scratch(dp, size, width),
        compiler_params=pltpu.CompilerParams(
            collective_id=3, has_side_effects=True, vmem_limit_bytes=60 * 1024 * 1024
        ),
        cost_estimate=pl.CostEstimate(flops=10**11, bytes_accessed=1024, transcendentals=0),
        name="finish",
    )(
        grad_queries,
        cosine_pair,
        sine_pair,
        wide_sum,
        own,
        grad_middle,
        gain,
        *weights,
        grad_keys,
        grad_values,
        normed,
        weight,
        *pair_weights,
    )


def split_layer(dp, depth):
    def layer(
        hidden_in,
        segment_ids,
        positions,
        attn_gain,
        query_weight,
        key_weight,
        value_weight,
        out_weight,
        mlp_gain,
        gate_weight,
        up_weight,
        down_weight,
        cotangent,
    ):
        f32, bf16 = jnp.float32, jnp.bfloat16
        rows, length, width = hidden_in.shape
        own = rows * length
        team = 2 * dp
        tokens = team * own
        part = query_weight.shape[0]
        hidden_rows = down_weight.shape[0]
        inner = depth * hidden_rows
        heads = depth
        row_count, size = dp * rows, 2 * length
        core = lax.axis_index("core")
        place = lax.axis_index("z")

        def dot(left, right):
            return jnp.dot(left, right, preferred_element_type=f32)

        weight_attn, places, near, weight_out = open_layer(
            dp, depth, query_weight, key_weight, value_weight, attn_gain, mlp_gain, positions,
            hidden_in, out_weight,
        )
        weight_out = weight_out.reshape(heads * HD, width)
        weight_down = lax.all_gather(down_weight, "z", axis=0, tiled=True)

        x_own = hidden_in.reshape(own, width)
        cot_own = cotangent.reshape(own, width)
        freqs = 10000.0 ** (-jnp.arange(0, HD // 2, dtype=f32) * 2.0 / HD)
        queries, normed1, cosine, sine, cosine_pair, sine_pair, offsets, gains, pair_weight, lines, wide_mine = (
            project(near, places, freqs, gate_weight, up_weight, weight_attn)
        )
        wide_got = lax.all_gather(wide_mine, "z", axis=0)
        cotangent, queries = lax.optimization_barrier((cotangent, queries))
        cots = plane_pieces(cotangent, dp)
        cots = [piece.reshape(own, width) for piece in cots]
        low_block = (place * size - places[:, 0, :, 0].reshape(row_count)) // size
        low_block = jnp.maximum(low_block, 0).astype(jnp.int32)
        place_one = place.astype(jnp.int32).reshape(1)
        context, logs = attend(
            low_block, place_one, offsets, queries, lines
        )

        context, cots = lax.optimization_barrier((context, cots))
        middle, normed2 = attend_sum(dp, context, weight_out, hidden_in, gains)
        pair_weight, normed2 = lax.optimization_barrier((pair_weight, normed2))
        pair_weights = plane_pieces(pair_weight, dp)
        normed2, pair_weights = lax.optimization_barrier((normed2, pair_weights))
        all_normed2, all_cots, hidden, slope, active, grad_down = mlp_forward(
            normed2, wide_got, cots
        )
        grad_normed2, mlp_parts, grad_wide = mlp_backward(
            all_normed2, all_cots, hidden, slope, active, wide_got, weight_down
        )
        def line_sum(array):
            return lax.psum_scatter(array.astype(bf16), "z", scatter_dimension=0, tiled=True)

        down_sum = line_sum(grad_down)
        grad_wide, down_sum = lax.optimization_barrier((grad_wide, down_sum))
        wide_sum = line_sum(grad_wide)[0]
        grad_normed2, down_sum = lax.optimization_barrier((grad_normed2, down_sum))
        grad_middle, grad_context, grad_wout = middle_back(
            dp, rows, grad_normed2, middle, cot_own, gains, context, weight_out
        )
        grad_down = down_sum.astype(f32)
        mlp_parts, grad_context = lax.optimization_barrier((mlp_parts, grad_context))
        mlp_got = [swap(mlp_parts[k], "dp", dp, k) for k in range(1, dp)]
        grad_queries, grad_keys, grad_values = attend_back(
            low_block,
            place_one,
            offsets,
            queries,
            lines,
            context,
            logs,
            grad_context,
            cosine,
            sine,
        )
        out_hidden = middle + mlp_parts[0].astype(f32)
        for got in mlp_got:
            out_hidden = out_hidden + got.astype(f32)
        out_hidden = out_hidden.astype(bf16)
        grad_queries, out_hidden, grad_wout = lax.optimization_barrier(
            (grad_queries, out_hidden, grad_wout)
        )
        out_sum = line_sum(grad_wout)
        (
            grad_in,
            grad_wquery,
            grad_wkey,
            grad_wvalue,
            grad_wgate,
            grad_wup,
            attn_rows,
            mlp_rows,
        ) = finish(
            grad_queries,
            cosine_pair,
            sine_pair,
            wide_sum,
            hidden_in,
            grad_middle,
            gains,
            (query_weight, key_weight, value_weight, gate_weight, up_weight),
            grad_keys,
            grad_values,
            normed1,
            weight_attn,
            pair_weights,
        )
        out_sum, grad_in = lax.optimization_barrier((out_sum, grad_in))
        grad_wout = out_sum.astype(f32)
        grad_gain_one = attn_rows[:, 0] / attn_gain.astype(f32)
        grad_gain_two = mlp_rows[:, 0] / mlp_gain.astype(f32)
        return (
            out_hidden.reshape(rows, length, width),
            grad_in.reshape(rows, length, width),
            grad_gain_one,
            grad_wquery,
            grad_wkey,
            grad_wvalue,
            grad_wout,
            grad_gain_two,
            grad_wgate,
            grad_wup,
            grad_down,
        )

    return layer


def solution(mesh):
    dp, seq = mesh.shape["dp"], mesh.shape["seq"]
    if dp != KVH or seq % 2 or HQ != dp * seq:
        return gathered_weights(mesh)
    depth = seq // 2
    mesh = Mesh(mesh.devices.reshape(dp, depth, 2), ("dp", "z", "core"))
    every = ("dp", "z", "core")
    tokens = P("dp", ("z", "core"), None)
    matrix = P(every, None)
    return jax.shard_map(
        split_layer(dp, depth),
        mesh=mesh,
        in_specs=(
            tokens,
            P("dp", ("z", "core")),
            P("dp", ("z", "core")),
            P(every),
            matrix,
            matrix,
            matrix,
            matrix,
            P(every),
            matrix,
            matrix,
            matrix,
            tokens,
        ),
        out_specs=(
            tokens,
            tokens,
            P(every),
            matrix,
            matrix,
            matrix,
            matrix,
            P(every),
            matrix,
            matrix,
            matrix,
        ),
        check_vma=False,
    )
```

```python
import functools

import jax
import jax.numpy as jnp
from jax import lax
from jax.experimental import pallas as pl
from jax.experimental.pallas import tpu as pltpu
from jax.sharding import Mesh
from jax.sharding import PartitionSpec as P

HQ = 32
HD = 64
KVH = 4


EPSILON = 1e-05


def fetch_attention(attn_gain, query_weight, key_weight, value_weight, out_weight):
    return (
        lax.all_gather(attn_gain, ("dp", "seq"), axis=0, tiled=True),
        lax.all_gather(query_weight, ("dp", "seq"), axis=0, tiled=True),
        lax.all_gather(key_weight, ("dp", "seq"), axis=0, tiled=True),
        lax.all_gather(value_weight, ("dp", "seq"), axis=0, tiled=True),
        lax.all_gather(out_weight, ("dp", "seq"), axis=0, tiled=True),
    )


def fetch_mlp(mlp_gain, gate_weight, up_weight, down_weight):
    return (
        lax.all_gather(mlp_gain, ("dp", "seq"), axis=0, tiled=True),
        lax.all_gather(gate_weight, ("dp", "seq"), axis=0, tiled=True),
        lax.all_gather(up_weight, ("dp", "seq"), axis=0, tiled=True),
        lax.all_gather(down_weight, ("dp", "seq"), axis=0, tiled=True),
    )


def angles_of(positions):
    freqs = 10000.0 ** (-jnp.arange(0, HD // 2, dtype=jnp.float32) * 2.0 / HD)
    return positions.astype(jnp.float32)[:, None] * freqs[None, :]


def rotate(vectors, cosine, sine):
    half = vectors.shape[-1] // 2
    first = vectors[..., :half]
    second = vectors[..., half:]
    cosine = cosine[:, None, :]
    sine = sine[:, None, :]
    return jnp.concatenate(
        [first * cosine - second * sine, second * cosine + first * sine], axis=-1
    )


def norm_forward(values, gain):
    factor = lax.rsqrt(jnp.mean(values * values, axis=-1, keepdims=True) + EPSILON)
    return (values * factor * gain.astype(jnp.float32), factor)


def norm_backward(values, factor, gain, grad_normed):
    inner = grad_normed * gain.astype(jnp.float32)
    grad_gain = jnp.sum(grad_normed * values * factor, axis=0)
    grad_values = factor * inner - factor * factor * factor * values * jnp.mean(
        inner * values, axis=-1, keepdims=True
    )
    return (grad_values, grad_gain)


def masked_scores(queries_rot, keys_heads, query_pos, query_seg, seg_all):
    scores = jnp.einsum(
        "cgjd,kgd->gjck", queries_rot, keys_heads, preferred_element_type=jnp.float32
    ) * HD ** (-0.5)
    key_pos = jnp.arange(keys_heads.shape[0])
    allowed = (key_pos[None, :] <= query_pos[:, None]) & (seg_all[None, :] == query_seg[:, None])
    return jnp.where(allowed, scores, -1e30)


def add_up(total, extra):
    if total is None:
        return extra
    return jax.tree.map(jnp.add, total, extra)


def gathered_weights_layer(
    hidden_in,
    segment_ids,
    positions,
    attn_gain,
    query_weight,
    key_weight,
    value_weight,
    out_weight,
    mlp_gain,
    gate_weight,
    up_weight,
    down_weight,
    cotangent,
):
    batches, local_len, width = hidden_in.shape
    group = HQ // KVH
    query_pos = lax.axis_index("seq") * local_len + jnp.arange(local_len)
    outputs = []
    grads_in = []
    attn_total = None
    mlp_total = None
    for microbatch in range(batches):
        rows_in = hidden_in[microbatch].astype(jnp.float32)
        seg_own = segment_ids[microbatch]
        angles = angles_of(positions[microbatch])
        cosine = jnp.cos(angles)
        sine = jnp.sin(angles)
        attn_set = fetch_attention(attn_gain, query_weight, key_weight, value_weight, out_weight)
        gain_one, weight_query, weight_key, weight_value, weight_out = attn_set
        normed1, factor1 = norm_forward(rows_in, gain_one)
        normed1_low = normed1.astype(jnp.bfloat16)
        queries = jnp.dot(normed1_low, weight_query, preferred_element_type=jnp.float32).reshape(
            local_len, HQ, HD
        )
        keys_own = jnp.dot(normed1_low, weight_key, preferred_element_type=jnp.float32).reshape(
            local_len, KVH, HD
        )
        values_own = jnp.dot(normed1_low, weight_value, preferred_element_type=jnp.float32).astype(
            jnp.bfloat16
        )
        queries_rot = (
            rotate(queries, cosine, sine).astype(jnp.bfloat16).reshape(local_len, KVH, group, HD)
        )
        keys_rot = rotate(keys_own, cosine, sine).astype(jnp.bfloat16).reshape(local_len, KVH * HD)
        keys_all, values_all, seg_all = (
            lax.all_gather(keys_rot, "seq", axis=0, tiled=True),
            lax.all_gather(values_own, "seq", axis=0, tiled=True),
            lax.all_gather(seg_own, "seq", axis=0, tiled=True),
        )
        keys_heads = keys_all.reshape(-1, KVH, HD)
        values_heads = values_all.reshape(-1, KVH, HD)
        scores = masked_scores(queries_rot, keys_heads, query_pos, seg_own, seg_all)
        highest = jnp.max(scores, axis=-1, keepdims=True)
        powers = jnp.exp(scores - highest)
        totals = jnp.sum(powers, axis=-1, keepdims=True)
        logsum = highest + jnp.log(totals)
        probs_low = (powers / totals).astype(jnp.bfloat16)
        context = jnp.einsum(
            "gjck,kgd->cgjd", probs_low, values_heads, preferred_element_type=jnp.float32
        )
        context_low = context.reshape(local_len, HQ * HD).astype(jnp.bfloat16)
        middle = rows_in + jnp.dot(context_low, weight_out, preferred_element_type=jnp.float32)
        mlp_set = fetch_mlp(mlp_gain, gate_weight, up_weight, down_weight)
        gain_two, weight_gate, weight_up, weight_down = mlp_set
        normed2, factor2 = norm_forward(middle, gain_two)
        normed2_low = normed2.astype(jnp.bfloat16)
        gate = jnp.dot(normed2_low, weight_gate, preferred_element_type=jnp.float32)
        up = jnp.dot(normed2_low, weight_up, preferred_element_type=jnp.float32)
        sigma = jax.nn.sigmoid(gate)
        activation = gate * sigma
        hidden = (activation * up).astype(jnp.bfloat16)
        mlp_out = jnp.dot(hidden, weight_down, preferred_element_type=jnp.float32)
        outputs.append((middle + mlp_out).astype(jnp.bfloat16))
        grad_low = cotangent[microbatch]
        grad_out = grad_low.astype(jnp.float32)
        mlp_back = fetch_mlp(mlp_gain, gate_weight, up_weight, down_weight)
        gain_two, weight_gate, weight_up, weight_down = mlp_back
        grad_down = jnp.dot(hidden.T, grad_low, preferred_element_type=jnp.float32)
        grad_hid = jnp.dot(grad_low, weight_down.T, preferred_element_type=jnp.float32)
        grad_gate = (grad_hid * up * sigma * (1.0 + gate * (1.0 - sigma))).astype(jnp.bfloat16)
        grad_up = (grad_hid * activation).astype(jnp.bfloat16)
        grad_wgate = jnp.dot(normed2_low.T, grad_gate, preferred_element_type=jnp.float32)
        grad_wup = jnp.dot(normed2_low.T, grad_up, preferred_element_type=jnp.float32)
        grad_normed2 = jnp.dot(
            grad_gate, weight_gate.T, preferred_element_type=jnp.float32
        ) + jnp.dot(grad_up, weight_up.T, preferred_element_type=jnp.float32)
        grad_mid_norm, grad_gain_two = norm_backward(middle, factor2, gain_two, grad_normed2)
        grad_middle = grad_out + grad_mid_norm
        attn_back = fetch_attention(attn_gain, query_weight, key_weight, value_weight, out_weight)
        gain_one, weight_query, weight_key, weight_value, weight_out = attn_back
        grad_attn = grad_middle.astype(jnp.bfloat16)
        grad_wout = jnp.dot(context_low.T, grad_attn, preferred_element_type=jnp.float32)
        grad_context = (
            jnp.dot(grad_attn, weight_out.T, preferred_element_type=jnp.float32)
            .astype(jnp.bfloat16)
            .reshape(local_len, KVH, group, HD)
        )
        probs = jnp.exp(
            masked_scores(queries_rot, keys_heads, query_pos, seg_own, seg_all) - logsum
        )
        grad_probs = jnp.einsum(
            "cgjd,kgd->gjck", grad_context, values_heads, preferred_element_type=jnp.float32
        )
        inner = jnp.sum(probs * grad_probs, axis=-1, keepdims=True)
        grad_scores = (probs * (grad_probs - inner)).astype(jnp.bfloat16)
        grad_qrot = jnp.einsum(
            "gjck,kgd->cgjd", grad_scores, keys_heads, preferred_element_type=jnp.float32
        ) * HD ** (-0.5)
        grad_krot_all = jnp.einsum(
            "gjck,cgjd->kgd", grad_scores, queries_rot, preferred_element_type=jnp.float32
        ) * HD ** (-0.5)
        grad_vall = jnp.einsum(
            "gjck,cgjd->kgd", probs_low, grad_context, preferred_element_type=jnp.float32
        )
        row_len = keys_heads.shape[0]
        grad_key_own, grad_value_own = (
            lax.psum_scatter(
                grad_krot_all.reshape(row_len, KVH * HD).astype(jnp.bfloat16),
                "seq",
                scatter_dimension=0,
                tiled=True,
            ).astype(jnp.float32),
            lax.psum_scatter(
                grad_vall.reshape(row_len, KVH * HD).astype(jnp.bfloat16),
                "seq",
                scatter_dimension=0,
                tiled=True,
            ).astype(jnp.float32),
        )
        grad_keys = (
            rotate(grad_key_own.reshape(local_len, KVH, HD), cosine, -sine)
            .astype(jnp.bfloat16)
            .reshape(local_len, KVH * HD)
        )
        grad_values = grad_value_own.astype(jnp.bfloat16)
        grad_queries = (
            rotate(grad_qrot.reshape(local_len, HQ, HD), cosine, -sine)
            .astype(jnp.bfloat16)
            .reshape(local_len, HQ * HD)
        )
        grad_wquery = jnp.dot(normed1_low.T, grad_queries, preferred_element_type=jnp.float32)
        grad_wkey = jnp.dot(normed1_low.T, grad_keys, preferred_element_type=jnp.float32)
        grad_wvalue = jnp.dot(normed1_low.T, grad_values, preferred_element_type=jnp.float32)
        grad_normed1 = jnp.dot(grad_queries, weight_query.T, preferred_element_type=jnp.float32)
        grad_normed1 = grad_normed1 + jnp.dot(
            grad_keys, weight_key.T, preferred_element_type=jnp.float32
        )
        grad_normed1 = grad_normed1 + jnp.dot(
            grad_values, weight_value.T, preferred_element_type=jnp.float32
        )
        grad_rows_norm, grad_gain_one = norm_backward(rows_in, factor1, gain_one, grad_normed1)
        grads_in.append(grad_middle + grad_rows_norm)
        attn_terms = (grad_gain_one, grad_wquery, grad_wkey, grad_wvalue, grad_wout)
        mlp_terms = (grad_gain_two, grad_wgate, grad_wup, grad_down)
        attn_shares = (
            lax.psum_scatter(attn_terms[0], ("dp", "seq"), scatter_dimension=0, tiled=True),
            lax.psum_scatter(attn_terms[1], ("dp", "seq"), scatter_dimension=0, tiled=True),
            lax.psum_scatter(attn_terms[2], ("dp", "seq"), scatter_dimension=0, tiled=True),
            lax.psum_scatter(attn_terms[3], ("dp", "seq"), scatter_dimension=0, tiled=True),
            lax.psum_scatter(attn_terms[4], ("dp", "seq"), scatter_dimension=0, tiled=True),
        )
        mlp_shares = (
            lax.psum_scatter(mlp_terms[0], ("dp", "seq"), scatter_dimension=0, tiled=True),
            lax.psum_scatter(mlp_terms[1], ("dp", "seq"), scatter_dimension=0, tiled=True),
            lax.psum_scatter(mlp_terms[2], ("dp", "seq"), scatter_dimension=0, tiled=True),
            lax.psum_scatter(mlp_terms[3], ("dp", "seq"), scatter_dimension=0, tiled=True),
        )
        attn_total = add_up(attn_total, attn_shares)
        mlp_total = add_up(mlp_total, mlp_shares)
    return (
        jnp.stack(outputs),
        jnp.stack(grads_in),
        attn_total[0],
        attn_total[1],
        attn_total[2],
        attn_total[3],
        attn_total[4],
        mlp_total[0],
        mlp_total[1],
        mlp_total[2],
        mlp_total[3],
    )


def gathered_weights(mesh):
    return jax.shard_map(
        gathered_weights_layer,
        mesh=mesh,
        in_specs=(
            P("dp", "seq", None),
            P("dp", "seq"),
            P("dp", "seq"),
            P(("dp", "seq")),
            P(("dp", "seq"), None),
            P(("dp", "seq"), None),
            P(("dp", "seq"), None),
            P(("dp", "seq"), None),
            P(("dp", "seq")),
            P(("dp", "seq"), None),
            P(("dp", "seq"), None),
            P(("dp", "seq"), None),
            P("dp", "seq", None),
        ),
        out_specs=(
            P("dp", "seq", None),
            P("dp", "seq", None),
            P(("dp", "seq")),
            P(("dp", "seq"), None),
            P(("dp", "seq"), None),
            P(("dp", "seq"), None),
            P(("dp", "seq"), None),
            P(("dp", "seq")),
            P(("dp", "seq"), None),
            P(("dp", "seq"), None),
            P(("dp", "seq"), None),
        ),
        check_vma=False,
    )


def swap(values, axis_name, size, step):
    return lax.ppermute(values, axis_name, [(i, i ^ step) for i in range(size)])


def plane_pieces(values, dp):
    return [values] + [swap(values, "dp", dp, k) for k in range(1, dp)]


NEGATIVE = -1e30
VMEM_LIMIT = 56 * 1024 * 1024
MESH = pl.DeviceIdType.MESH
LIGHT = pl.CostEstimate(flops=0, bytes_accessed=1024, transcendentals=0)


def contract_last(left, right):
    return lax.dot_general(
        left, right, (((1,), (1,)), ((), ())), preferred_element_type=jnp.float32
    )


def multiply(left, right):
    return jnp.dot(left, right, preferred_element_type=jnp.float32)


def spread_keys(block, heads):
    half = block.shape[0] // 2
    return jnp.concatenate([block[:half]] * heads + [block[half:]] * heads, axis=0)


def fold_keys(block, heads):
    half = block.shape[0] // (2 * heads)
    first = sum(block[h * half : (h + 1) * half] for h in range(heads))
    rest = range(heads, 2 * heads)
    return jnp.concatenate([first, sum(block[h * half : (h + 1) * half] for h in rest)], axis=0)


def fold_values(block, heads):
    size = block.shape[0] // heads
    return sum(block[h * size : (h + 1) * size] for h in range(heads))


def turned_head(shape, dim, heads):
    index = lax.broadcasted_iota(jnp.int32, shape, dim)
    return lax.rem(index, shape[dim] // 2) // (shape[dim] // 2 // heads)


def plain_head(shape, dim, heads):
    index = lax.broadcasted_iota(jnp.int32, shape, dim)
    return index // (shape[dim] // heads)


def per_head(values, owner, heads, axis):
    zero = jnp.zeros_like(values)
    return jnp.concatenate([jnp.where(owner == h, values, zero) for h in range(heads)], axis=axis)


def join_heads(stacked, owner, heads):
    size = stacked.shape[0] // heads
    return sum(
        jnp.where(owner == h, stacked[h * size : (h + 1) * size], 0.0) for h in range(heads)
    )


def masked(scores, block, start, order_q, heads):
    size = order_q.shape[0]
    order_k = block * size + lax.broadcasted_iota(jnp.int32, (size, size), 1)
    allowed = (order_k >= start) & (order_k <= order_q)
    split = scores.reshape(heads, size, size)
    return jnp.where(allowed[None], split, NEGATIVE).reshape(scores.shape)


def attend_kernel(heads, low_ref, place_ref, offset_ref, q_ref, k_ref, v_ref, out_ref, log_ref, held):
    row = pl.program_id(0)
    place = place_ref[0]
    queries = q_ref[0]
    size = queries.shape[0]
    stacked = per_head(queries, turned_head(queries.shape, 1, heads), heads, 0)
    order_q = place * size + lax.broadcasted_iota(jnp.int32, (size, 1), 0)
    start = order_q - offset_ref[0][:, :1]

    def score(block, highest):
        scores = multiply(stacked, spread_keys(k_ref[block, 0], heads))
        scores = masked(scores, block, start, order_q, heads)
        held[block] = scores
        return jnp.maximum(highest, jnp.max(scores, axis=1, keepdims=True))

    highest = lax.fori_loop(
        low_ref[row], place + 1, score, jnp.full((heads * size, 1), NEGATIVE, jnp.float32)
    )

    def mix(block, carry):
        total, context = carry
        powers = jnp.exp(held[block] - highest)
        total = total + jnp.sum(powers, axis=1, keepdims=True)
        spread = jnp.concatenate([v_ref[block, 0]] * heads, axis=0)
        return total, context + contract_last(powers.astype(jnp.bfloat16), spread)

    total, context = lax.fori_loop(
        low_ref[row],
        place + 1,
        mix,
        (
            jnp.zeros((heads * size, 1), jnp.float32),
            jnp.zeros((heads * size, queries.shape[1]), jnp.float32),
        ),
    )
    owner = plain_head(queries.shape, 1, heads)
    out_ref[0] = join_heads(context / total, owner, heads).astype(jnp.bfloat16)
    log_ref[0] = highest + jnp.log(total)


def attend_back_kernel(
    heads,
    low_ref,
    place_ref,
    offset_ref,
    q_ref,
    k_ref,
    v_ref,
    context_ref,
    log_ref,
    grad_ref,
    cosine_ref,
    sine_ref,
    grad_q_ref,
    grad_k_ref,
    grad_v_ref,
):
    row = pl.program_id(0)
    place = place_ref[0]
    queries = q_ref[0]
    grads = grad_ref[0]
    size = queries.shape[0]
    turned = turned_head(queries.shape, 1, heads)
    plain = plain_head(queries.shape, 1, heads)
    stacked = per_head(queries, turned, heads, 0)
    stacked_grad = per_head(grads, plain, heads, 0)
    flipped = per_head(queries.T, turned_head(queries.shape, 0, heads), heads, 1)
    flipped_grad = per_head(grads.T, plain_head(queries.shape, 0, heads), heads, 1)
    product = grads.astype(jnp.float32) * context_ref[0].astype(jnp.float32)
    inner = jnp.sum(per_head(product, plain, heads, 0), axis=1, keepdims=True)
    logs = log_ref[0]
    order_q = place * size + lax.broadcasted_iota(jnp.int32, (size, 1), 0)
    start = order_q - offset_ref[0][:, :1]
    grad_k_ref[...] = jnp.zeros_like(grad_k_ref)
    grad_v_ref[...] = jnp.zeros_like(grad_v_ref)

    def step(block, grad_q):
        keys = spread_keys(k_ref[block, 0], heads)
        spread = jnp.concatenate([v_ref[block, 0]] * heads, axis=0)
        scores = masked(multiply(stacked, keys), block, start, order_q, heads)
        probs = jnp.exp(scores - logs)
        grad_probs = multiply(stacked_grad, spread)
        grad_scores = (probs * (grad_probs - inner)).astype(jnp.bfloat16)
        grad_k = fold_keys(multiply(flipped, grad_scores), heads)
        grad_v = fold_values(multiply(flipped_grad, probs.astype(jnp.bfloat16)), heads)
        grad_k_ref[block, 0] = grad_k.astype(jnp.bfloat16)
        grad_v_ref[block, 0] = grad_v.astype(jnp.bfloat16)
        return grad_q + contract_last(grad_scores, keys)

    grad_q = lax.fori_loop(
        low_ref[row],
        place + 1,
        step,
        jnp.zeros((heads * size, queries.shape[1]), jnp.float32),
    )
    grad_q = join_heads(grad_q, turned, heads) * HD ** (-0.5)
    half = grad_q.shape[1] // 2
    first, second = grad_q[:, :half], grad_q[:, half:]
    cosine, sine = cosine_ref[0], sine_ref[0]
    grad_q_ref[0, :, :half] = (first * cosine + second * sine).astype(jnp.bfloat16)
    grad_q_ref[0, :, half:] = (second * cosine - first * sine).astype(jnp.bfloat16)


def row_spec(*shape):
    return pl.BlockSpec((1,) + shape, lambda row, low, place: (row,) + (0,) * len(shape))


def line_spec(depth, *shape):
    return pl.BlockSpec((depth, 1) + shape, lambda row, low, place: (0, row) + (0,) * len(shape))


def pair_spec(which, depth, *shape):
    return pl.BlockSpec(
        (None, depth, 1) + shape, lambda row, low, place: (which, 0, row) + (0,) * len(shape)
    )


def attend(low, place, offsets, queries, lines):
    rows, size, width = queries.shape
    depth, features = lines.shape[1], lines.shape[3]
    heads = width // features
    return pl.pallas_call(
        functools.partial(attend_kernel, heads),
        out_shape=(
            jax.ShapeDtypeStruct((rows, size, width), jnp.bfloat16),
            jax.ShapeDtypeStruct((rows, heads * size, 1), jnp.float32),
        ),
        grid_spec=pltpu.PrefetchScalarGridSpec(
            num_scalar_prefetch=2,
            grid=(rows,),
            in_specs=[
                row_spec(size, offsets.shape[2]),
                row_spec(size, width),
                pair_spec(0, depth, features, size),
                pair_spec(1, depth, features, size),
            ],
            out_specs=[row_spec(size, width), row_spec(heads * size, 1)],
            scratch_shapes=[pltpu.VMEM((depth, heads * size, size), jnp.float32)],
        ),
        compiler_params=pltpu.CompilerParams(vmem_limit_bytes=VMEM_LIMIT),
        cost_estimate=LIGHT,
        name="attend",
    )(low, place, offsets, queries, lines, lines)


def attend_back(low, place, offsets, queries, lines, context, logs, grads, cosine, sine):
    rows, size, width = queries.shape
    depth, features = lines.shape[1], lines.shape[3]
    heads = width // features
    line = line_spec(depth, features, size)
    whole = row_spec(size, width)
    half = row_spec(size, width // 2)
    return pl.pallas_call(
        functools.partial(attend_back_kernel, heads),
        out_shape=(
            jax.ShapeDtypeStruct((rows, size, width), jnp.bfloat16),
            jax.ShapeDtypeStruct(lines.shape[1:], jnp.bfloat16),
            jax.ShapeDtypeStruct(lines.shape[1:], jnp.bfloat16),
        ),
        grid_spec=pltpu.PrefetchScalarGridSpec(
            num_scalar_prefetch=2,
            grid=(rows,),
            in_specs=[
                row_spec(size, offsets.shape[2]),
                whole,
                pair_spec(0, depth, features, size),
                pair_spec(1, depth, features, size),
                whole,
                row_spec(heads * size, 1),
                whole,
                half,
                half,
            ],
            out_specs=[whole, line, line],
        ),
        compiler_params=pltpu.CompilerParams(vmem_limit_bytes=VMEM_LIMIT),
        cost_estimate=LIGHT,
        name="attend_back",
    )(low, place, offsets, queries, lines, lines, context, logs, grads, cosine, sine)


def team_places():
    data = lax.axis_index("dp")
    place = lax.axis_index("z")
    core = lax.axis_index("core")

    def peer(k):
        high = lax.rem(data // 2 + k // 2, 2)
        low = lax.rem(lax.rem(data, 2) + lax.rem(k, 2), 2)
        return (high * 2 + low, place, core)

    return data, place, core, peer, (data, place, 1 - core)


def line_neighbours(depth):
    data, place, core, _, _ = team_places()
    return [(data, lax.rem(place + step, depth), core) for step in (1, depth - 1)]


def greet(targets):
    barrier = pltpu.get_barrier_semaphore()
    for target in targets:
        pl.semaphore_signal(barrier, inc=1, device_id=target, device_id_type=MESH)
    pl.semaphore_wait(barrier, len(targets))


def send(source, target, send_sem, got_sem, device):
    return pltpu.make_async_remote_copy(
        src_ref=source,
        dst_ref=target,
        send_sem=send_sem,
        recv_sem=got_sem,
        device_id=device,
        device_id_type=MESH,
    )


def line_gather(depth, block_of, send_sem, got_sem):
    data, place, core, _, twin = team_places()

    def copy(z, step):
        device = (data, lax.rem(place + depth + step, depth), core)
        block = block_of(z)
        return send(block, block, send_sem.at[z, (1 - step) // 2], got_sem.at[z], device)

    def arrival(z):
        block = block_of(z)
        return send(block, block, send_sem.at[z, 0], got_sem.at[z], twin)

    def start():
        @pl.when(place < depth - 1)
        def _():
            copy(place, 1).start()

        @pl.when(place > 0)
        def _():
            copy(place, -1).start()

    def relay(distance):
        @pl.when(place >= distance)
        def _():
            arrival(place - distance).wait_recv()

            @pl.when(place < depth - 1)
            def _():
                copy(place - distance, 1).start()

        @pl.when(place + distance < depth)
        def _():
            arrival(place + distance).wait_recv()

            @pl.when(place > 0)
            def _():
                copy(place + distance, -1).start()

    def finish():
        for z in range(depth):

            @pl.when((z <= place) & (place < depth - 1))
            def _(z=z):
                copy(z, 1).wait_send()

            @pl.when((z >= place) & (place > 0))
            def _(z=z):
                copy(z, -1).wait_send()

    return start, relay, finish


def sum_scratch(dp, size, width):
    dma = pltpu.SemaphoreType.DMA
    block = pltpu.VMEM((dp, size, width), jnp.bfloat16)
    return [
        block,
        block,
        pltpu.VMEM((2, size // 2, width), jnp.bfloat16),
        pltpu.VMEM((2, size, width), jnp.bfloat16),
        dma((dp,)),
        dma((dp,)),
        dma((2,)),
        dma((2,)),
        dma((2, 2)),
        dma((2, 2)),
    ]


def plane_sum(dp, product, total_ref, scratch):
    side, got, relay, far, side_send, side_got, relay_send, relay_got, far_send, far_got = scratch
    f32, bf16 = jnp.float32, jnp.bfloat16
    _, _, core, peer, twin = team_places()
    size = side.shape[1]
    half = size // 2

    def rows(part):
        return pl.ds(part * half, half)

    def side_copy(k):
        return send(side.at[k], got.at[k], side_send.at[k], side_got.at[k], twin)

    def relay_copy(part):
        return send(
            got.at[3, rows(part)],
            relay.at[part],
            relay_send.at[part],
            relay_got.at[part],
            peer(1 + part),
        )

    def far_copy(which, part):
        return send(
            got.at[1 + which, rows(part)],
            far.at[which, rows(part)],
            far_send.at[which, part],
            far_got.at[which, part],
            peer(1 + which),
        )

    def one(step, carry):
        k = dp - 1 - step
        side[k] = product(k, 1 - core, 0).astype(bf16)
        side_copy(k).start()
        total = product(k, core, 1)
        side_copy(k).wait_recv()
        total = total + got[k].astype(f32)

        @pl.when(k == 0)
        def _():
            total_ref[...] = total

        @pl.when(k > 0)
        def _():
            got[k] = total.astype(bf16)

        @pl.when(k == 3)
        def _():
            relay_copy(0).start()
            relay_copy(1).start()

        @pl.when(k == 2)
        def _():
            far_copy(1, 1).start()

        @pl.when(k == 1)
        def _():
            far_copy(0, 0).start()

        return carry

    lax.fori_loop(0, dp, one, 0)
    for part in range(2):
        which = 1 - part
        relay_copy(part).wait_recv()
        total = got[1 + which, rows(part)].astype(f32) + relay[part].astype(f32)
        got[1 + which, rows(part)] = total.astype(bf16)
        far_copy(which, part).start()

    def complete():
        for which, part in ((0, 0), (1, 1), (0, 1), (1, 0)):
            far_copy(which, part).wait_recv()
            total_ref[rows(part)] += far[which, rows(part)].astype(f32)
        for part in range(2):
            relay_copy(part).wait_send()
            for which in range(2):
                far_copy(which, part).wait_send()
        for k in range(dp):
            side_copy(k).wait_send()

    return complete


def mlp_forward_kernel(dp, depth, x_hbm, wide_hbm, *refs):
    cot_hbms = refs[:dp]
    tokens_hbm, cots_hbm, hidden_hbm, slope_hbm, active_hbm, down_grad_hbm = refs[dp : dp + 6]
    (
        tokens,
        cots,
        wides,
        hidden_t,
        chunk,
        tile_out,
        load_sem,
        cots_sem,
        near_send,
        near_got,
        side_send,
        side_got,
        pass_send,
        pass_got,
        tokens_sem,
        chunk_sem,
        tile_sem,
        twin_send,
        twin_got,
    ) = refs[dp + 6 :]
    bf16 = jnp.bfloat16
    _, _, core, peer, twin = team_places()
    size, width = x_hbm.shape
    half = size // 2
    loads = [pltpu.make_async_copy(x_hbm, tokens.at[0, core], load_sem.at[0])]
    for z in range(depth):
        loads.append(pltpu.make_async_copy(wide_hbm.at[z], wides.at[:, z], load_sem.at[1 + z]))
    cot_loads = []
    for k in range(dp):
        sem = load_sem.at[depth + 1 + k]
        cot_loads.append(pltpu.make_async_copy(cot_hbms[k], cots.at[k, core], sem))
    for load in loads + cot_loads:
        load.start()
    greet([peer(k) for k in range(1, 3)] + [twin])
    loads[0].wait()

    def near_copy(k):
        return send(
            tokens.at[0, core], tokens.at[k, core], near_send.at[k], near_got.at[k], peer(k)
        )

    def pass_copy(part):
        spot = pl.ds(part * half, half)
        return send(
            tokens.at[1 + part, core, spot],
            tokens.at[3, core, spot],
            pass_send.at[part],
            pass_got.at[part],
            peer(2 - part),
        )

    def side_copy(k):
        block = tokens.at[k, core]
        return send(block, block, side_send.at[k], side_got.at[k], twin)

    def side_arrival(k):
        block = tokens.at[k, 1 - core]
        return send(block, block, side_send.at[k], side_got.at[k], twin)

    def twin_copy(k):
        block = cots.at[k, core]
        return send(block, block, twin_send.at[k], twin_got.at[k], twin)

    def twin_arrival(k):
        block = cots.at[k, 1 - core]
        return send(block, block, twin_send.at[k], twin_got.at[k], twin)

    def tokens_out(k, e):
        return pltpu.make_async_copy(tokens.at[k, e], tokens_hbm.at[k, e], tokens_sem.at[k, e])

    def chunk_out(k, e, slot):
        return [
            pltpu.make_async_copy(chunk.at[slot, i], target.at[k, e], chunk_sem.at[slot, i])
            for i, target in enumerate((hidden_hbm, slope_hbm, active_hbm))
        ]

    near_copy(1).start()
    near_copy(2).start()
    side_copy(0).start()
    for load in loads[1:]:
        load.wait()

    def process(k, e, slot, reuse):
        row = tokens[k, e]
        tokens_out(k, e).start()
        both = multiply(row, wides[...].reshape(width, -1))
        inner = both.shape[1] // 2
        gate, up = both[:, :inner], both[:, inner:]
        sigma = 1.0 / (1.0 + jnp.exp(-gate))
        active = gate * sigma
        hidden = (active * up).astype(bf16)
        if reuse:
            for copy in chunk_out(k, e, slot):
                copy.wait()
        chunk[slot, 0] = hidden
        chunk[slot, 1] = (up * sigma * (1.0 + gate * (1.0 - sigma))).astype(bf16)
        chunk[slot, 2] = active.astype(bf16)
        for copy in chunk_out(k, e, slot):
            copy.start()
        spot = pl.ds(pl.multiple_of((k * 2 + e) * size, size), size)
        hidden_t[:, spot] = hidden.T

    process(0, core, 0, False)
    side_arrival(0).wait_recv()
    process(0, 1 - core, 1, False)
    for k in range(dp):
        cot_loads[k].wait()
        twin_copy(k).start()
    for k in range(1, 3):
        near_copy(k).wait_recv()
        pass_copy(k - 1).start()
        side_copy(k).start()
    for k in range(dp):
        twin_arrival(k).wait_recv()
    cots_out = pltpu.make_async_copy(cots, cots_hbm, cots_sem)
    cots_out.start()

    def step(k, carry):
        @pl.when(k == 3)
        def _():
            pass_copy(0).wait_recv()
            pass_copy(1).wait_recv()
            side_copy(3).start()

        process(k, core, 0, True)
        side_arrival(k).wait_recv()
        process(k, 1 - core, 1, True)
        return carry

    lax.fori_loop(1, dp, step, 0)

    def tile_copy(j, slot):
        spot = pl.ds(pl.multiple_of(j * 256, 256), 256)
        return pltpu.make_async_copy(tile_out.at[slot], down_grad_hbm.at[:, spot], tile_sem.at[slot])

    count = width // 256

    def tile(j, carry):
        slot = lax.rem(j, 2)

        @pl.when(j > 1)
        def _():
            tile_copy(j - 2, slot).wait()

        spot = pl.ds(pl.multiple_of(j * 256, 256), 256)
        columns = cots[:, :, :, spot].reshape(-1, 256)
        tile_out[slot] = multiply(hidden_t[...], columns).astype(bf16)
        tile_copy(j, slot).start()
        return carry

    lax.fori_loop(0, count, tile, 0)
    for j in (count - 2, count - 1):
        tile_copy(j, j % 2).wait()
    cots_out.wait()
    for slot, e in ((0, core), (1, 1 - core)):
        for copy in chunk_out(dp - 1, e, slot):
            copy.wait()
    for k in range(dp):
        for e in range(2):
            tokens_out(k, e).wait()
        side_copy(k).wait_send()
        twin_copy(k).wait_send()
    for k in range(1, 3):
        near_copy(k).wait_send()
        pass_copy(k - 1).wait_send()


def mlp_forward(x_own, wide, cots):
    depth, dp = wide.shape[:2]
    size, width = x_own.shape
    inner = wide.shape[-1] // 2
    bf16 = jnp.bfloat16
    hbm = pl.BlockSpec(memory_space=pl.ANY)
    dma = pltpu.SemaphoreType.DMA
    weight = pltpu.VMEM((dp, depth) + wide.shape[2:], bf16)
    whole = jax.ShapeDtypeStruct((dp, 2, size, width), bf16)
    thin = jax.ShapeDtypeStruct((dp, 2, size, inner), bf16)
    return pl.pallas_call(
        functools.partial(mlp_forward_kernel, dp, depth),
        out_shape=(whole, whole, thin, thin, thin, jax.ShapeDtypeStruct((inner, width), bf16)),
        in_specs=[hbm] * (2 + dp),
        out_specs=(hbm,) * 6,
        scratch_shapes=[
            pltpu.VMEM((dp, 2, size, width), bf16),
            pltpu.VMEM((dp, 2, size, width), bf16),
            weight,
            pltpu.VMEM((inner, 2 * dp * size), bf16),
            pltpu.VMEM((2, 3, size, inner), bf16),
            pltpu.VMEM((2, inner, 256), bf16),
            dma((2 * depth + 1 + dp,)),
            dma,
            dma((dp,)),
            dma((dp,)),
            dma((dp,)),
            dma((dp,)),
            dma((2,)),
            dma((2,)),
            dma((dp, 2)),
            dma((2, 3)),
            dma((2,)),
            dma((dp,)),
            dma((dp,)),
        ],
        compiler_params=pltpu.CompilerParams(
            collective_id=1, has_side_effects=True, vmem_limit_bytes=VMEM_LIMIT
        ),
        cost_estimate=LIGHT,
        name="mlp_forward",
    )(x_own, wide, *cots)


def mlp_backward_kernel(
    dp,
    depth,
    tokens_hbm,
    cots_hbm,
    hidden_hbm,
    slope_hbm,
    active_hbm,
    wide_hbm,
    down_hbm,
    pair_hbm,
    grad_ref,
    part_hbm,
    wide_grad_hbm,
    pairs_hbm,
    tokens,
    wides,
    downs,
    gate_t,
    up_t,
    cot_slots,
    chunk,
    part_out,
    part_side,
    tile_out,
    load_sem,
    slot_sem,
    part_sem,
    part_send,
    part_got,
    tile_sem,
    pair_send,
    pair_got,
    pair_sem,
    *sum_refs,
):
    bf16 = jnp.bfloat16
    _, _, core, peer, twin = team_places()
    size, width = grad_ref.shape
    loads = [pltpu.make_async_copy(down_hbm, downs, load_sem.at[0])]
    for z in range(depth):
        loads.append(pltpu.make_async_copy(wide_hbm.at[z], wides.at[:, z], load_sem.at[1 + z]))
    tokens_load = pltpu.make_async_copy(tokens_hbm, tokens, load_sem.at[depth + 1])

    def slot_loads(k, e, slot):
        copies = [pltpu.make_async_copy(cots_hbm.at[k, e], cot_slots.at[slot], slot_sem.at[slot, 3])]
        for i, source in enumerate((hidden_hbm, slope_hbm, active_hbm)):
            copies.append(
                pltpu.make_async_copy(source.at[k, e], chunk.at[slot, i], slot_sem.at[slot, i])
            )
        return copies

    for copy in slot_loads(dp - 1, 1 - core, 0):
        copy.start()
    for load in loads:
        load.start()
    pair_local = pltpu.make_async_copy(pair_hbm, pairs_hbm.at[0], pair_sem)
    pair_local.start()
    greet([peer(k) for k in range(1, dp)] + [twin])

    def pair_copy(k):
        return send(pair_hbm, pairs_hbm.at[k], pair_send.at[k], pair_got.at[k], peer(k))

    for k in range(1, dp):
        pair_copy(k).start()
    for load in loads:
        load.wait()
    tokens_load.start()

    def part_copy(k):
        return pltpu.make_async_copy(part_out.at[1], part_hbm.at[k], part_sem)

    def part_side_copy(k):
        return send(part_out.at[0], part_side.at[k], part_send.at[k], part_got.at[k], twin)

    def product(k, e, turn):
        slot = turn
        for copy in slot_loads(k, e, slot):
            copy.wait()
        if turn == 0:
            for copy in slot_loads(k, core, 1):
                copy.start()
        else:

            @pl.when(k > 0)
            def _():
                for copy in slot_loads(k - 1, 1 - core, 0):
                    copy.start()

        grad_hid = contract_last(cot_slots[slot], downs[...])
        grad_gate = (grad_hid * chunk[slot, 1].astype(jnp.float32)).astype(bf16)
        grad_up = (grad_hid * chunk[slot, 2].astype(jnp.float32)).astype(bf16)
        spot = pl.ds(pl.multiple_of((k * 2 + e) * size, size), size)
        gate_t[:, spot] = grad_gate.T
        up_t[:, spot] = grad_up.T
        terms = multiply(chunk[slot, 0], downs[...])
        if turn == 0:

            @pl.when(k < dp - 1)
            def _():
                part_side_copy(k + 1).wait_send()

            part_out[0] = terms.astype(bf16)
            part_side_copy(k).start()
        else:

            @pl.when(k < dp - 1)
            def _():
                part_copy(k + 1).wait()

            part_side_copy(k).wait_recv()
            part_out[1] = (terms + part_side[k].astype(jnp.float32)).astype(bf16)
            part_copy(k).start()
        both = jnp.concatenate([grad_gate, grad_up], axis=1)
        return contract_last(both, wides[...].reshape(width, -1))

    complete = plane_sum(dp, product, grad_ref, sum_refs)
    tokens_load.wait()
    block = 256
    count = width // block

    def tile_copies(which, j, slot):
        per = depth * 128 // block
        return [
            pltpu.make_async_copy(
                tile_out.at[slot, :, pl.ds(i * 128, 128)],
                wide_grad_hbm.at[lax.rem(j, per) * (block // 128) + i, which, j // per],
                tile_sem.at[slot, i],
            )
            for i in range(block // 128)
        ]

    for which, left in ((0, gate_t), (1, up_t)):

        def tile(j, carry, which=which, left=left):
            slot = lax.rem(j, 2)

            @pl.when(j > 1)
            def _():
                for copy in tile_copies(which, j - 2, slot):
                    copy.wait()

            spot = pl.ds(pl.multiple_of(j * block, block), block)
            columns = tokens[:, :, :, spot].reshape(-1, block)
            tile_out[slot] = multiply(left[...], columns).astype(bf16)
            for copy in tile_copies(which, j, slot):
                copy.start()
            return carry

        lax.fori_loop(0, count, tile, 0)
        for j in (count - 2, count - 1):
            for copy in tile_copies(which, j, j % 2):
                copy.wait()
    complete()
    pair_local.wait()
    for k in range(1, dp):
        pair_copy(k).wait_recv()
        pair_copy(k).wait_send()
    part_side_copy(0).wait_send()
    part_copy(0).wait()


def mlp_backward(tokens, cots, hidden, slope, active, wide, down, pair):
    depth, dp = wide.shape[:2]
    size, width = tokens.shape[2:]
    inner = wide.shape[-1] // 2
    f32, bf16 = jnp.float32, jnp.bfloat16
    hbm = pl.BlockSpec(memory_space=pl.ANY)
    dma = pltpu.SemaphoreType.DMA
    weight = pltpu.VMEM((dp, depth) + wide.shape[2:], bf16)
    turned = pltpu.VMEM((inner, 2 * dp * size), bf16)
    return pl.pallas_call(
        functools.partial(mlp_backward_kernel, dp, depth),
        out_shape=(
            jax.ShapeDtypeStruct((size, width), f32),
            jax.ShapeDtypeStruct((dp, size, width), bf16),
            jax.ShapeDtypeStruct((depth, 2, dp, inner, width // (depth * dp)), bf16),
            jax.ShapeDtypeStruct((dp,) + pair.shape, bf16),
        ),
        in_specs=[hbm] * 8,
        out_specs=(pl.BlockSpec(memory_space=pltpu.VMEM), hbm, hbm, hbm),
        scratch_shapes=[
            pltpu.VMEM((dp, 2, size, width), bf16),
            weight,
            pltpu.VMEM((inner, width), bf16),
            turned,
            turned,
            pltpu.VMEM((2, size, width), bf16),
            pltpu.VMEM((2, 3, size, inner), bf16),
            pltpu.VMEM((2, size, width), bf16),
            pltpu.VMEM((dp, size, width), bf16),
            pltpu.VMEM((2, inner, 256), bf16),
            dma((2 * depth + 2,)),
            dma((2, 4)),
            dma,
            dma((dp,)),
            dma((dp,)),
            dma((2, 2)),
            dma((dp,)),
            dma((dp,)),
            dma,
        ]
        + sum_scratch(dp, size, width),
        compiler_params=pltpu.CompilerParams(
            collective_id=6, has_side_effects=True, vmem_limit_bytes=60 * 1024 * 1024
        ),
        cost_estimate=LIGHT,
        name="mlp_backward",
    )(tokens, cots, hidden, slope, active, wide, down, pair)


def attend_sum_kernel(
    dp, rows, context_ref, weight_ref, own_ref, gain_ref, middle_ref, normed_ref, *scratch
):
    _, _, _, peer, twin = team_places()
    length = own_ref.shape[1]
    size, width = middle_ref.shape
    greet([peer(k) for k in range(1, 3)] + [twin])

    def product(k, e, turn):
        spot = pl.ds(pl.multiple_of(e * length, length), length)
        block = context_ref[pl.ds(k * rows, rows), spot].reshape(size, -1)
        return multiply(block, weight_ref[...])

    plane_sum(dp, product, middle_ref, scratch)()
    middle = middle_ref[...] + own_ref[...].reshape(size, width).astype(jnp.float32)
    middle_ref[...] = middle
    factor = lax.rsqrt(jnp.mean(middle * middle, axis=-1, keepdims=True) + EPSILON)
    normed_ref[...] = (middle * factor * gain_ref[1:2].astype(jnp.float32)).astype(jnp.bfloat16)


def attend_sum(dp, context, weight, own, gain):
    rows, length, width = own.shape
    size = rows * length
    vmem = pl.BlockSpec(memory_space=pltpu.VMEM)
    return pl.pallas_call(
        functools.partial(attend_sum_kernel, dp, rows),
        out_shape=(
            jax.ShapeDtypeStruct((size, width), jnp.float32),
            jax.ShapeDtypeStruct((size, width), jnp.bfloat16),
        ),
        in_specs=[vmem] * 4,
        out_specs=(vmem, vmem),
        scratch_shapes=sum_scratch(dp, size, width),
        compiler_params=pltpu.CompilerParams(
            collective_id=4, has_side_effects=True, vmem_limit_bytes=VMEM_LIMIT
        ),
        cost_estimate=LIGHT,
        name="attend_sum",
    )(context, weight, own, gain)


def middle_back_kernel(
    dp,
    rows,
    grad_ref,
    middle_ref,
    cot_ref,
    gain_ref,
    context_ref,
    weight_ref,
    grad_middle_ref,
    grad_context_ref,
    weight_grad_ref,
    tokens,
    context_t,
    near_send,
    near_got,
    side_send,
    side_got,
    pass_send,
    pass_got,
):
    f32, bf16 = jnp.float32, jnp.bfloat16
    _, _, core, peer, twin = team_places()
    size, width = grad_ref.shape
    length = size // rows
    half = size // 2
    greet([peer(k) for k in range(1, 3)] + [twin])
    middle = middle_ref[...]
    factor = lax.rsqrt(jnp.mean(middle * middle, axis=-1, keepdims=True) + EPSILON)
    inner = grad_ref[...] * gain_ref[1:2].astype(f32)
    mean = jnp.mean(inner * middle, axis=-1, keepdims=True)
    total = cot_ref[...].astype(f32) + factor * inner - factor * factor * factor * middle * mean
    grad_middle_ref[...] = total
    tokens[0, core] = total.astype(bf16)

    def near_copy(k):
        return send(
            tokens.at[0, core], tokens.at[k, core], near_send.at[k], near_got.at[k], peer(k)
        )

    def pass_copy(part):
        spot = pl.ds(part * half, half)
        return send(
            tokens.at[1 + part, core, spot],
            tokens.at[3, core, spot],
            pass_send.at[part],
            pass_got.at[part],
            peer(2 - part),
        )

    def side_copy(k):
        block = tokens.at[k, core]
        return send(block, block, side_send.at[k], side_got.at[k], twin)

    def side_arrival(k):
        block = tokens.at[k, 1 - core]
        return send(block, block, side_send.at[k], side_got.at[k], twin)

    near_copy(1).start()
    near_copy(2).start()
    side_copy(0).start()
    for k in range(dp):
        for e in range(2):
            for r in range(rows):
                block = context_ref[k * rows + r, e * length : (e + 1) * length]
                spot = pl.ds(((k * 2 + e) * rows + r) * length, length)
                context_t[:, spot] = block.T

    def process(k, e):
        block = contract_last(tokens[k, e], weight_ref[...]).astype(bf16)
        spot = pl.ds(pl.multiple_of(e * length, length), length)
        grad_context_ref[pl.ds(k * rows, rows), spot] = block.reshape(rows, length, -1)

    process(0, core)
    side_arrival(0).wait_recv()
    process(0, 1 - core)
    for k in range(1, 3):
        near_copy(k).wait_recv()
        pass_copy(k - 1).start()
        side_copy(k).start()

    def step(k, carry):
        @pl.when(k == 3)
        def _():
            pass_copy(0).wait_recv()
            pass_copy(1).wait_recv()
            side_copy(3).start()

        process(k, core)
        side_arrival(k).wait_recv()
        process(k, 1 - core)
        return carry

    lax.fori_loop(1, dp, step, 0)

    def tile(j, carry):
        spot = pl.ds(pl.multiple_of(j * 256, 256), 256)
        columns = tokens[:, :, :, spot].reshape(-1, 256)
        weight_grad_ref[:, spot] = multiply(context_t[...], columns).astype(bf16)
        return carry

    lax.fori_loop(0, width // 256, tile, 0)
    for k in range(1, 3):
        near_copy(k).wait_send()
        pass_copy(k - 1).wait_send()
    for k in range(dp):
        side_copy(k).wait_send()


def middle_back(dp, rows, grad, middle, cot, gain, context, weight):
    f32, bf16 = jnp.float32, jnp.bfloat16
    size, width = grad.shape
    vmem = pl.BlockSpec(memory_space=pltpu.VMEM)
    dma = pltpu.SemaphoreType.DMA
    return pl.pallas_call(
        functools.partial(middle_back_kernel, dp, rows),
        out_shape=(
            jax.ShapeDtypeStruct((size, width), f32),
            jax.ShapeDtypeStruct(context.shape, bf16),
            jax.ShapeDtypeStruct(weight.shape, bf16),
        ),
        in_specs=[vmem] * 6,
        out_specs=(vmem, vmem, vmem),
        scratch_shapes=[
            pltpu.VMEM((dp, 2, size, width), bf16),
            pltpu.VMEM((weight.shape[0], 2 * dp * size), bf16),
            dma((dp,)),
            dma((dp,)),
            dma((dp,)),
            dma((dp,)),
            dma((2,)),
            dma((2,)),
        ],
        compiler_params=pltpu.CompilerParams(
            collective_id=5, has_side_effects=True, vmem_limit_bytes=VMEM_LIMIT
        ),
        cost_estimate=LIGHT,
        name="middle_back",
    )(grad, middle, cot, gain, context, weight)


def open_kernel(
    dp,
    depth,
    query_ref,
    key_ref,
    value_ref,
    attn_gain_ref,
    mlp_gain_ref,
    places_ref,
    own_ref,
    out_ref,
    attn_hbm,
    places_hbm,
    near_hbm,
    out_hbm,
    attn_blocks,
    local_sem,
    attn_send,
    attn_got,
    places_send,
    places_got,
    line_send,
    line_got,
    near_send,
    near_got,
    pass_send,
    pass_got,
    out_send,
    out_got,
):
    data, place, core, peer, twin = team_places()
    part = query_ref.shape[0]
    half = HD // 2
    side = depth * half
    middle = own_ref.shape[0] // 2
    attn_blocks[...] = jnp.zeros_like(attn_blocks)
    for d in range(dp):
        for c in range(2):
            team = 2 * d + c
            for z in range(depth):
                owner = (d * depth + z) * 2 + c
                for h in range(2):
                    spot = owner * HD + h * half
                    attn_blocks[team, :, h * side + z * half : h * side + (z + 1) * half] = (
                        query_ref[:, spot : spot + half]
                    )
            pair = key_ref if c == 0 else value_ref
            last = 2 * side + HD
            attn_blocks[team, :, 2 * side : last] = pair[:, d * HD : (d + 1) * HD]
            attn_blocks[team, 0:1, last : last + part] = attn_gain_ref[...]
            attn_blocks[team, 1:2, last : last + part] = mlp_gain_ref[...]

    def device(k, other):
        return (peer(k)[0], place, 1 - core if other else core)

    def number(k, other):
        return 2 * peer(k)[0] + (1 - core if other else core)

    pairs = [(k, other) for k in range(dp) for other in range(2) if k or other]
    greet([device(k, other) for k, other in pairs] + line_neighbours(depth))

    def attn_copy(k, other):
        return send(
            attn_blocks.at[number(k, other)],
            attn_hbm.at[place, data, core],
            attn_send.at[k, other],
            attn_got.at[k, other],
            device(k, other),
        )

    def places_copy(k, other):
        return send(
            places_ref,
            places_hbm.at[k, core],
            places_send.at[k, other],
            places_got.at[k, other],
            device(k, other),
        )

    def arrival(target, send_sem, got_sem):
        return send(target, target, send_sem, got_sem, twin)

    def near_copy(k):
        return send(own_ref, near_hbm.at[k], near_send.at[k], near_got.at[k], peer(k))

    def pass_copy(which):
        spot = pl.ds(which * middle, middle)
        return send(
            near_hbm.at[1 + which, spot],
            near_hbm.at[3, spot],
            pass_send.at[which],
            pass_got.at[which],
            peer(2 - which),
        )

    start, relay, complete = line_gather(depth, lambda z: attn_hbm.at[z], line_send, line_got)
    out_start, out_relay, out_complete = line_gather(
        depth, lambda z: out_hbm.at[z], out_send, out_got
    )
    for k, other in pairs:
        attn_copy(k, other).start()
    for k, other in pairs:
        places_copy(k, other).start()
    near_copy(1).start()
    near_copy(2).start()
    locals_ = [
        pltpu.make_async_copy(
            attn_blocks.at[2 * data + core], attn_hbm.at[place, data, core], local_sem.at[0]
        ),
        pltpu.make_async_copy(places_ref, places_hbm.at[0, core], local_sem.at[1]),
        pltpu.make_async_copy(own_ref, near_hbm.at[0], local_sem.at[2]),
        pltpu.make_async_copy(out_ref, out_hbm.at[place], local_sem.at[3]),
    ]
    for copy in locals_:
        copy.start()
    locals_[0].wait()
    for k, other in pairs:
        target = attn_hbm.at[place, peer(k)[0], 1 - core if other else core]
        arrival(target, attn_send.at[k, other], attn_got.at[k, other]).wait_recv()
    start()
    for copy in locals_[1:]:
        copy.wait()
    out_start()
    relay(1)
    for which in range(2):
        near_copy(1 + which).wait_recv()
        pass_copy(which).start()
    for distance in range(2, depth):
        relay(distance)
        out_relay(distance - 1)
    out_relay(depth - 1)
    for k, other in pairs:
        target = places_hbm.at[k, 1 - core if other else core]
        arrival(target, places_send.at[k, other], places_got.at[k, other]).wait_recv()
    for which in range(2):
        pass_copy(which).wait_recv()
        pass_copy(which).wait_send()
        near_copy(1 + which).wait_send()
    complete()
    out_complete()
    for k, other in pairs:
        attn_copy(k, other).wait_send()
        places_copy(k, other).wait_send()


def open_layer(dp, depth, query, key, value, attn_gain, mlp_gain, places, own, out_weight):
    part = query.shape[0]
    columns = depth * HD + HD + part
    bf16 = jnp.bfloat16
    hbm = pl.BlockSpec(memory_space=pl.ANY)
    vmem = pl.BlockSpec(memory_space=pltpu.VMEM)
    dma = pltpu.SemaphoreType.DMA
    return pl.pallas_call(
        functools.partial(open_kernel, dp, depth),
        out_shape=(
            jax.ShapeDtypeStruct((depth, dp, 2, part, columns), bf16),
            jax.ShapeDtypeStruct((dp, 2) + places.shape, places.dtype),
            jax.ShapeDtypeStruct((dp,) + own.shape, bf16),
            jax.ShapeDtypeStruct((depth,) + out_weight.shape, bf16),
        ),
        in_specs=[vmem] * 8,
        out_specs=(hbm,) * 4,
        scratch_shapes=[
            pltpu.VMEM((2 * dp, part, columns), bf16),
            dma((4,)),
            dma((dp, 2)),
            dma((dp, 2)),
            dma((dp, 2)),
            dma((dp, 2)),
            dma((depth, 2)),
            dma((depth,)),
            dma((dp,)),
            dma((dp,)),
            dma((2,)),
            dma((2,)),
            dma((depth, 2)),
            dma((depth,)),
        ],
        compiler_params=pltpu.CompilerParams(
            collective_id=7, has_side_effects=True, vmem_limit_bytes=VMEM_LIMIT
        ),
        cost_estimate=LIGHT,
        name="open_layer",
    )(query, key, value, attn_gain[None], mlp_gain[None], places, own, out_weight)


def project_kernel(
    dp,
    depth,
    rows,
    *refs,
):
    pieces, places_ref, freq_ref, freq_pair_ref, gate_ref, up_ref, weight_hbm = refs[:7]
    query_ref, normed_hbm, cosine_ref, sine_ref, cosine_pair_ref, sine_pair_ref = refs[7:13]
    offset_ref, gain_ref, pair_weight_ref, line_hbm, wide_hbm = refs[13:18]
    (
        weight,
        pair,
        far_pieces,
        load_sem,
        own_sem,
        line_send,
        line_got,
        side_send,
        side_got,
        twin_send,
        twin_got,
        wide_blocks,
        wide_send,
        wide_got,
        wide_sem,
        normed,
        normed_sem,
    ) = refs[18:]
    f32, bf16 = jnp.float32, jnp.bfloat16
    data, place, core, peer, twin = team_places()
    length, width = pieces.shape[2:]
    part = weight.shape[3]
    columns = query_ref.shape[2]
    loads = [
        pltpu.make_async_copy(
            weight_hbm.at[z], weight.at[:, z], load_sem.at[z]
        )
        for z in range(depth)
    ]
    for load in loads:
        load.start()

    def device(k, other):
        return (peer(k)[0], place, 1 - core if other else core)

    def number(k, other):
        return 2 * peer(k)[0] + (1 - core if other else core)

    pairs = [(k, other) for k in range(dp) for other in range(2) if k or other]
    others = [(data, lax.rem(place + step, depth), core) for step in range(1, depth)]
    greet(others + [device(k, other) for k, other in pairs])

    def wide_copy(k, other):
        return send(
            wide_blocks.at[number(k, other)],
            wide_hbm.at[data, core],
            wide_send.at[k, other],
            wide_got.at[k, other],
            device(k, other),
        )


    def twin_copy(k):
        return send(pieces.at[k], far_pieces.at[k], twin_send.at[k], twin_got.at[k], twin)

    for k in range(dp):
        twin_copy(k).start()
    count = wide_blocks.shape[2] // (2 * depth)
    for d in range(dp):
        for c in range(2):
            for z in range(depth):
                owner = (d * depth + z) * 2 + c
                for which, source in ((0, gate_ref), (1, up_ref)):
                    spot = (which * depth + z) * count
                    wide_blocks[2 * d + c, :, spot : spot + count] = source[
                        :, owner * count : (owner + 1) * count
                    ]
    wide_local = pltpu.make_async_copy(
        wide_blocks.at[2 * data + core], wide_hbm.at[data, core], wide_sem
    )
    wide_local.start()
    for k, other in pairs:
        wide_copy(k, other).start()
    for load in loads:
        load.wait()
    for d in range(dp):
        for z in range(depth):
            for c in range(2):
                spot = ((d * depth + z) * 2 + c) * part
                gain_ref[:, spot : spot + part] = weight[d, z, c, 0:2, columns + HD :]
    pair_weight_ref[...] = weight[...].reshape(width, -1)[:, columns : columns + HD].T
    gain = gain_ref[0:1].astype(f32)
    turning = (1 - core).astype(f32)

    def block_of(which, z, k):
        return line_hbm.at[which, z, pl.ds(k * rows, rows)]

    def pair_of(k):
        return pair.at[pl.ds(k * rows, rows)]

    def own_copy(k):
        return pltpu.make_async_copy(pair_of(k), block_of(core, place, k), own_sem.at[k])

    def own_side_copy(k):
        return send(
            pair_of(k),
            block_of(core, place, k),
            side_send.at[place, k],
            side_got.at[place, k],
            twin,
        )

    def line_copy(z, k):
        return send(
            pair_of(k),
            block_of(core, place, k),
            line_send.at[z, k],
            line_got.at[place, k],
            (data, z, core),
        )

    def line_arrival(z, k):
        block = block_of(core, z, k)
        return send(block, block, line_send.at[z, k], line_got.at[z, k], twin)

    def side_copy(z, k):
        block = block_of(core, z, k)
        return send(block, block, side_send.at[z, k], side_got.at[z, k], twin)

    def side_arrival(z, k):
        block = block_of(1 - core, z, k)
        return send(block, block, side_send.at[z, k], side_got.at[z, k], twin)

    def normed_copy(k, e):
        return pltpu.make_async_copy(normed.at[k, e], normed_hbm.at[k, e], normed_sem.at[k, e])

    for k in range(dp):
        for far in range(2):
            e = core if far == 0 else 1 - core
            if far:
                twin_copy(k).wait_recv()
            source = far_pieces.at[k] if far else pieces.at[k]
            values = source[...].reshape(rows * length, width).astype(f32)
            factor = lax.rsqrt(jnp.mean(values * values, axis=-1, keepdims=True) + EPSILON)
            tokens = (values * factor * gain).astype(bf16)
            normed[k, e] = tokens
            normed_copy(k, e).start()
            result = multiply(tokens, weight[...].reshape(width, -1)[:, columns:])
            spot = pl.ds(pl.multiple_of(e * length, length), length)
            for r in range(rows):
                row = k * rows + r
                offsets = places_ref[k, e][r : r + 1].astype(f32)
                keys = result[r * length : (r + 1) * length, :HD].T
                angles = offsets * freq_pair_ref[...] * turning
                cosine, sine = jnp.cos(angles), jnp.sin(angles)
                cosine_pair_ref[row, :, spot] = cosine
                sine_pair_ref[row, :, spot] = sine
                first, second = keys[: HD // 2], keys[HD // 2 :]
                pair[row, : HD // 2, spot] = (first * cosine - second * sine).astype(bf16)
                pair[row, HD // 2 :, spot] = (second * cosine + first * sine).astype(bf16)
        own_copy(k).start()
        own_side_copy(k).start()
        for z in range(depth):

            @pl.when(z > place)
            def _(z=z, k=k):
                line_copy(z, k).start()

    def turn_queries(k, carry):
        for e in range(2):
            result = multiply(normed[k, e], weight[...].reshape(width, -1)[:, :columns])
            spot = pl.ds(e * length, length)
            for r in range(rows):
                row = k * rows + r
                block = result[r * length : (r + 1) * length]
                offsets = places_ref[k, e][r : r + 1].astype(f32)
                column = jnp.broadcast_to(offsets, (length, length)).T
                offset_ref[row, spot] = column.astype(jnp.int32)
                angles = column * freq_ref[...]
                cosine, sine = jnp.cos(angles), jnp.sin(angles)
                cosine_ref[row, spot] = cosine
                sine_ref[row, spot] = sine
                first, second = block[:, : columns // 2], block[:, columns // 2 :]
                turned = (first * cosine - second * sine).astype(bf16)
                query_ref[row, spot, : columns // 2] = turned * bf16(HD ** (-0.5))
                turned = (second * cosine + first * sine).astype(bf16)
                query_ref[row, spot, columns // 2 :] = turned * bf16(HD ** (-0.5))
        return carry

    lax.fori_loop(0, dp, turn_queries, 0)
    for k in range(dp):
        for z in reversed(range(depth)):

            @pl.when(z < place)
            def _(z=z, k=k):
                line_arrival(z, k).wait_recv()
                side_copy(z, k).start()

    for k in range(dp):
        for e in range(2):
            normed_copy(k, e).wait()
    wide_local.wait()
    for k, other in pairs:
        block = wide_hbm.at[peer(k)[0], 1 - core if other else core]
        send(block, block, wide_send.at[k, other], wide_got.at[k, other], twin).wait_recv()
        wide_copy(k, other).wait_send()
    for k in range(dp):
        twin_copy(k).wait_send()
        own_copy(k).wait()
        own_side_copy(k).wait_send()
        for z in range(depth):

            @pl.when(z <= place)
            def _(z=z, k=k):
                side_arrival(z, k).wait_recv()

            @pl.when(z < place)
            def _(z=z, k=k):
                side_copy(z, k).wait_send()

            @pl.when(z > place)
            def _(z=z, k=k):
                line_copy(z, k).wait_send()


def project(near, places, freqs, gate, up, weight):
    f32, bf16 = jnp.float32, jnp.bfloat16
    dp, rows, length, width = near.shape
    depth = weight.shape[0]
    heads = depth
    row_count, size = dp * rows, 2 * length
    columns = heads * HD
    part = width // (2 * dp * depth)
    hbm = pl.BlockSpec(memory_space=pl.ANY)
    vmem = pl.BlockSpec(memory_space=pltpu.VMEM)
    dma = pltpu.SemaphoreType.DMA
    turned = jax.ShapeDtypeStruct((row_count, size, columns // 2), f32)
    turned_pair = jax.ShapeDtypeStruct((row_count, HD // 2, size), f32)
    return pl.pallas_call(
        functools.partial(project_kernel, dp, depth, rows),
        out_shape=(
            jax.ShapeDtypeStruct((row_count, size, columns), bf16),
            jax.ShapeDtypeStruct((dp, 2, rows * length, width), bf16),
            turned,
            turned,
            turned_pair,
            turned_pair,
            jax.ShapeDtypeStruct((row_count, size, length), jnp.int32),
            jax.ShapeDtypeStruct((2, width), bf16),
            jax.ShapeDtypeStruct((HD, width), bf16),
            jax.ShapeDtypeStruct((2, depth, row_count, HD, size), bf16),
            jax.ShapeDtypeStruct((dp, 2, part, gate.shape[1] // dp), bf16),
        ),
        in_specs=[vmem] * 6 + [hbm],
        out_specs=(vmem, hbm) + (vmem,) * 7 + (hbm,) * 2,
        scratch_shapes=[
            pltpu.VMEM((dp, depth) + weight.shape[2:], bf16),
            pltpu.VMEM((row_count, HD, size), bf16),
            pltpu.VMEM((dp, rows, length, width), bf16),
            dma((2 * depth,)),
            dma((dp,)),
            dma((depth, dp)),
            dma((depth, dp)),
            dma((depth, dp)),
            dma((depth, dp)),
            dma((dp,)),
            dma((dp,)),
            pltpu.VMEM((2 * dp, part, gate.shape[1] // dp), bf16),
            dma((dp, 2)),
            dma((dp, 2)),
            dma,
            pltpu.VMEM((dp, 2, rows * length, width), bf16),
            dma((dp, 2)),
        ],
        compiler_params=pltpu.CompilerParams(
            collective_id=2, has_side_effects=True, vmem_limit_bytes=VMEM_LIMIT
        ),
        cost_estimate=LIGHT,
        name="project",
    )(near, places, jnp.tile(freqs, heads)[None], freqs[:, None], gate, up, weight)


def finish_kernel(
    dp,
    depth,
    rows,
    query_ref,
    cosine_ref,
    sine_ref,
    wide_ref,
    own_ref,
    grad_middle_ref,
    gain_ref,
    query_weight_ref,
    key_weight_ref,
    value_weight_ref,
    gate_weight_ref,
    up_weight_ref,
    grad_k_hbm,
    grad_v_hbm,
    normed_hbm,
    weight_hbm,
    *refs,
):
    pairs_hbm, *refs = refs
    finish_body(
        dp, depth, rows, query_ref, cosine_ref, sine_ref, wide_ref, own_ref,
        grad_middle_ref, gain_ref, query_weight_ref, key_weight_ref, value_weight_ref,
        gate_weight_ref, up_weight_ref, grad_k_hbm, grad_v_hbm, normed_hbm, weight_hbm, pairs_hbm,
        *refs,
    )


def finish_body(
    dp,
    depth,
    rows,
    query_ref,
    cosine_ref,
    sine_ref,
    wide_ref,
    own_ref,
    grad_middle_ref,
    gain_ref,
    query_weight_ref,
    key_weight_ref,
    value_weight_ref,
    gate_weight_ref,
    up_weight_ref,
    grad_k_hbm,
    grad_v_hbm,
    normed_hbm,
    weight_hbm,
    pairs_hbm,
    grad_ref,
    query_grad_ref,
    key_grad_ref,
    value_grad_ref,
    gate_grad_ref,
    up_grad_ref,
    attn_gain_ref,
    mlp_gain_ref,
    normed,
    weight,
    kept,
    given,
    arrived,
    line_block,
    line_got_block,
    terms,
    terms_t,
    held,
    line_grads,
    line_grads_got,
    team_block,
    team_got_block,
    wide_block,
    wide_got_block,
    load_sem,
    swap_send,
    swap_got,
    line_send,
    line_got,
    grads_send,
    grads_got,
    team_send,
    team_got,
    wide_send,
    wide_got,
    pair_weight,
    pair_out,
    pair_in,
    pair_load_sem,
    pair_twin_send,
    pair_twin_got,
    pair_send,
    pair_got,
    *sum_refs,
):
    f32, bf16 = jnp.float32, jnp.bfloat16
    data, place, core, peer, twin = team_places()
    columns = query_ref.shape[2]
    size = query_ref.shape[1]
    length = size // 2
    width = grad_ref.shape[1]
    part = weight.shape[3]
    features = columns + HD
    half = HD // 2
    loads = [
        pltpu.make_async_copy(
            weight_hbm.at[z, :, :, :, pl.ds(0, columns)],
            weight.at[:, z],
            load_sem.at[z],
        )
        for z in range(depth)
    ]
    pair_loads = [
        pltpu.make_async_copy(pairs_hbm.at[k], pair_weight.at[k, core], pair_load_sem.at[k])
        for k in range(dp)
    ]
    loads.append(pltpu.make_async_copy(normed_hbm, normed, load_sem.at[depth]))

    @pl.when(core == 0)
    def _():
        pltpu.make_async_copy(grad_k_hbm, kept, load_sem.at[depth + 1]).start()
        pltpu.make_async_copy(grad_v_hbm, given, load_sem.at[depth + 2]).start()

    @pl.when(core == 1)
    def _():
        pltpu.make_async_copy(grad_v_hbm, kept, load_sem.at[depth + 1]).start()
        pltpu.make_async_copy(grad_k_hbm, given, load_sem.at[depth + 2]).start()

    for load in loads + pair_loads:
        load.start()
    others = [(data, lax.rem(place + step, depth), core) for step in range(1, depth)]

    def device(k, other):
        return (peer(k)[0], place, 1 - core if other else core)

    pairs = [(k, other) for k in range(dp) for other in range(2) if k or other]
    greet(others + [device(k, other) for k, other in pairs])
    pltpu.make_async_copy(grad_v_hbm, given, load_sem.at[depth + 2]).wait()
    swap_copy = send(given, arrived, swap_send, swap_got, twin)
    swap_copy.start()

    def pair_twin(k):
        block = pair_weight.at[k, core]
        return send(block, block, pair_twin_send.at[k], pair_twin_got.at[k], twin)

    def pair_twin_arrival(k):
        block = pair_weight.at[k, 1 - core]
        return send(block, block, pair_twin_send.at[k], pair_twin_got.at[k], twin)

    def pair_copy(k, other):
        e = 1 - core if other else core
        return send(
            pair_out.at[k, e],
            pair_in.at[k, core],
            pair_send.at[k, other],
            pair_got.at[k, other],
            device(k, other),
        )

    def pair_arrival(k, other):
        block = pair_in.at[k, 1 - core if other else core]
        return send(block, block, pair_send.at[k, other], pair_got.at[k, other], twin)

    def wide_copy(k, other):
        spot = (peer(k)[0], 1 - core if other else core)
        return send(
            wide_block.at[spot],
            wide_got_block.at[data, core],
            wide_send.at[k, other],
            wide_got.at[k, other],
            device(k, other),
        )

    def wide_arrival(k, other):
        block = wide_got_block.at[peer(k)[0], 1 - core if other else core]
        return send(block, block, wide_send.at[k, other], wide_got.at[k, other], twin)

    def line_copy(z):
        return send(
            line_block.at[z],
            line_got_block.at[place],
            line_send.at[z],
            line_got.at[place],
            (data, z, core),
        )

    def line_arrival(z):
        block = line_got_block.at[z]
        return send(block, block, line_send.at[z], line_got.at[z], twin)

    pltpu.make_async_copy(grad_k_hbm, kept, load_sem.at[depth + 1]).wait()
    swap_copy.wait_recv()
    for z in range(depth):

        @pl.when(z < place)
        def _(z=z):
            total = kept[z].astype(f32) + arrived[z].astype(f32)
            line_block[z] = total.astype(bf16)
            line_copy(z).start()

    for load in loads:
        load.wait()
    for k in range(dp):
        for e in range(2):
            for r in range(rows):
                block = query_ref[k * rows + r, e * length : (e + 1) * length]
                terms[k, e, r * length : (r + 1) * length] = block
                spot = pl.ds(((k * 2 + e) * rows + r) * length, length)
                terms_t[:columns, spot] = block.T

    def tile_rows(first, count):
        def tile(j, carry):
            spot = pl.ds(pl.multiple_of(j * 256, 256), 256)
            block = multiply(
                terms_t[first : first + count], normed[:, :, :, spot].reshape(-1, 256)
            ).astype(bf16)
            for i in range(2):
                group = 2 * j + i
                line_grads[lax.rem(group, depth), group // depth, first : first + count] = block[
                    :, i * 128 : (i + 1) * 128
                ]
            return carry

        lax.fori_loop(0, width // 256, tile, 0)

    def grads_copy(z, piece):
        spot = pl.ds(piece * columns, HD if piece else columns)
        return send(
            line_grads.at[z, :, spot],
            line_grads_got.at[place, :, spot],
            grads_send.at[z, piece],
            grads_got.at[place, piece],
            (data, z, core),
        )

    def grads_arrival(z, piece):
        spot = pl.ds(piece * columns, HD if piece else columns)
        block = line_grads_got.at[z, :, spot]
        return send(block, block, grads_send.at[z, piece], grads_got.at[z, piece], twin)

    def product(k, e, turn):
        return contract_last(terms[k, e], weight[...].reshape(width, columns))

    complete = plane_sum(dp, product, grad_ref, sum_refs)
    for k in range(dp):
        pair_loads[k].wait()
        pair_twin(k).start()
    for which in range(2):
        for d in range(dp):
            block = wide_ref[which, d].T
            wide_block[d, 0, which] = block[:part]
            wide_block[d, 1, which] = block[part:]
    for k, other in pairs:
        wide_copy(k, other).start()
    wide_got_block[data, core] = wide_block[data, core]
    tile_rows(0, columns)
    for z in range(depth):

        @pl.when(z > place)
        def _(z=z):
            grads_copy(z, 0).start()

    for z in range(depth):

        @pl.when(z == place)
        def _(z=z):
            held[...] = kept[z].astype(f32) + arrived[z].astype(f32)

    for z in range(depth):

        @pl.when(z > place)
        def _(z=z):
            line_arrival(z).wait_recv()
            held[...] += line_got_block[z].astype(f32)

    for z in range(depth):

        @pl.when(z < place)
        def _(z=z):
            grads_copy(z, 0).start()

    for k in range(dp):
        for r in range(rows):
            row = k * rows + r
            first, second = held[row, :half], held[row, half:]
            cosine, sine = cosine_ref[row], sine_ref[row]
            turned = jnp.concatenate(
                [first * cosine + second * sine, second * cosine - first * sine], axis=0
            ).astype(bf16)
            for e in range(2):
                block = turned[:, e * length : (e + 1) * length]
                spot = pl.ds(((k * 2 + e) * rows + r) * length, length)
                terms_t[columns:, spot] = block
                pair_out[k, e, :, r * length : (r + 1) * length] = block
    for k, other in pairs:
        pair_copy(k, other).start()
    pair_in[0, core] = pair_out[0, core]

    tile_rows(columns, HD)
    for z in range(depth):

        @pl.when(z != place)
        def _(z=z):
            grads_copy(z, 1).start()

    for k, other in pairs:
        wide_arrival(k, other).wait_recv()
    count = wide_block.shape[4] // depth
    for d in range(dp):
        for c in range(2):
            for which, target in ((0, gate_grad_ref), (1, up_grad_ref)):
                block = wide_got_block[d, c, which].astype(f32)
                for z in range(depth):
                    spot = ((d * depth + z) * 2 + c) * count
                    target[:, spot : spot + count] = block[:, z * count : (z + 1) * count]
    products = gate_weight_ref[...].astype(f32) * gate_grad_ref[...]
    products = products + up_weight_ref[...].astype(f32) * up_grad_ref[...]
    mlp_gain_ref[...] = jnp.sum(products, axis=-1, keepdims=True)

    def team_copy(k, other, piece):
        spot = (peer(k)[0], 1 - core if other else core)
        return send(
            team_block.at[spot + (piece,)],
            team_got_block.at[data, core, piece],
            team_send.at[k, other, piece],
            team_got.at[k, other, piece],
            device(k, other),
        )

    def team_arrival(k, other, piece):
        block = team_got_block.at[peer(k)[0], 1 - core if other else core, piece]
        send_sem, got_sem = team_send.at[k, other, piece], team_got.at[k, other, piece]
        return send(block, block, send_sem, got_sem, twin)

    line_grads_got[place] = line_grads[place]

    def team_piece(piece, first, last):
        for z in range(depth):

            @pl.when(z != place)
            def _(z=z):
                grads_arrival(z, piece).wait_recv()

        for d in range(dp):
            total = line_grads_got[0, d, first:last].astype(f32)
            for z in range(1, depth):
                total = total + line_grads_got[z, d, first:last].astype(f32)
            total = total.T.astype(bf16)
            team_block[d, 0, piece, :, : last - first] = total[:part]
            team_block[d, 1, piece, :, : last - first] = total[part:]
        for k, other in pairs:
            team_copy(k, other, piece).start()
        team_got_block[data, core, piece] = team_block[data, core, piece]

    team_block[...] = jnp.zeros_like(team_block)
    team_piece(0, 0, columns)
    complete()
    for k, other in pairs:
        pair_arrival(k, other).wait_recv()
    for k in range(dp):
        pair_twin_arrival(k).wait_recv()
    grad_ref[...] += multiply(
        pair_in[...].reshape(2 * dp * HD, -1).T, pair_weight[...].reshape(2 * dp * HD, width)
    )
    own = own_ref[...].reshape(grad_ref.shape).astype(f32)
    factor = lax.rsqrt(jnp.mean(own * own, axis=-1, keepdims=True) + EPSILON)
    inner = grad_ref[...] * gain_ref[0:1].astype(f32)
    mean = jnp.mean(inner * own, axis=-1, keepdims=True)
    grad_ref[...] = grad_middle_ref[...] + factor * inner - factor * factor * factor * own * mean
    team_piece(1, columns, features)
    for k, other in pairs:
        team_arrival(k, other, 0).wait_recv()
    side = depth * half
    for d in range(dp):
        for c in range(2):
            block = team_got_block[d, c, 0].astype(f32)
            for z in range(depth):
                for h in range(2):
                    spot = ((d * depth + z) * 2 + c) * HD + h * half
                    start = h * side + z * half
                    query_grad_ref[:, spot : spot + half] = block[:, start : start + half]
    for k, other in pairs:
        team_arrival(k, other, 1).wait_recv()
    for d in range(dp):
        for c in range(2):
            target = key_grad_ref if c == 0 else value_grad_ref
            target[:, d * HD : (d + 1) * HD] = team_got_block[d, c, 1, :, :HD].astype(f32)
    attn_gain_ref[...] = sum(
        jnp.sum(before[...].astype(f32) * after[...], axis=-1, keepdims=True)
        for before, after in (
            (query_weight_ref, query_grad_ref),
            (key_weight_ref, key_grad_ref),
            (value_weight_ref, value_grad_ref),
        )
    )
    swap_copy.wait_send()
    for k in range(dp):
        pair_twin(k).wait_send()
    for k, other in pairs:
        team_copy(k, other, 0).wait_send()
        team_copy(k, other, 1).wait_send()
        pair_copy(k, other).wait_send()
        wide_copy(k, other).wait_send()
    for z in range(depth):

        @pl.when(z < place)
        def _(z=z):
            line_copy(z).wait_send()

        @pl.when(z != place)
        def _(z=z):
            grads_copy(z, 0).wait_send()
            grads_copy(z, 1).wait_send()


def finish(grad_queries, cosine_pair, sine_pair, wide_sum, own, grad_middle, gain, weights, grad_keys, grad_values, normed, weight, pair_weights):
    f32, bf16 = jnp.float32, jnp.bfloat16
    dp, _, size, width = normed.shape
    rows = own.shape[0]
    depth, row_count, features, line_size = grad_keys.shape
    columns = grad_queries.shape[2]
    part = width // (2 * dp * depth)
    inner = wide_sum.shape[2]
    total = columns + features
    hbm = pl.BlockSpec(memory_space=pl.ANY)
    vmem = pl.BlockSpec(memory_space=pltpu.VMEM)
    dma = pltpu.SemaphoreType.DMA
    line = pltpu.VMEM((depth, row_count, features, line_size), bf16)
    grads = pltpu.VMEM((depth, dp, total, 2 * part), bf16)
    team = pltpu.VMEM((dp, 2, 2, part, columns), bf16)
    wide = pltpu.VMEM((dp, 2, 2, part, inner), bf16)
    query_weight, key_weight, value_weight, gate_weight, up_weight = weights
    return pl.pallas_call(
        functools.partial(finish_kernel, dp, depth, rows),
        out_shape=(
            jax.ShapeDtypeStruct((size, width), f32),
            jax.ShapeDtypeStruct(query_weight.shape, f32),
            jax.ShapeDtypeStruct(key_weight.shape, f32),
            jax.ShapeDtypeStruct(value_weight.shape, f32),
            jax.ShapeDtypeStruct(gate_weight.shape, f32),
            jax.ShapeDtypeStruct(up_weight.shape, f32),
            jax.ShapeDtypeStruct((part, 1), f32),
            jax.ShapeDtypeStruct((part, 1), f32),
        ),
        in_specs=[vmem] * 12 + [hbm] * 5,
        out_specs=(vmem,) * 8,
        scratch_shapes=[
            pltpu.VMEM((dp, 2, size, width), bf16),
            pltpu.VMEM((dp, depth, 2, part, columns), bf16),
            line,
            line,
            line,
            line,
            line,
            pltpu.VMEM((dp, 2, size, columns), bf16),
            pltpu.VMEM((total, 2 * dp * size), bf16),
            pltpu.VMEM((row_count, features, line_size), f32),
            grads,
            grads,
            team,
            team,
            wide,
            wide,
            dma((depth + 3,)),
            dma,
            dma,
            dma((depth,)),
            dma((depth,)),
            dma((depth, 2)),
            dma((depth, 2)),
            dma((dp, 2, 2)),
            dma((dp, 2, 2)),
            dma((dp, 2)),
            dma((dp, 2)),
            pltpu.VMEM((dp, 2, features, width), bf16),
            pltpu.VMEM((dp, 2, features, size), bf16),
            pltpu.VMEM((dp, 2, features, size), bf16),
            dma((dp,)),
            dma((dp,)),
            dma((dp,)),
            dma((dp, 2)),
            dma((dp, 2)),
        ]
        + sum_scratch(dp, size, width),
        compiler_params=pltpu.CompilerParams(
            collective_id=3, has_side_effects=True, vmem_limit_bytes=60 * 1024 * 1024
        ),
        cost_estimate=pl.CostEstimate(flops=10**11, bytes_accessed=1024, transcendentals=0),
        name="finish",
    )(
        grad_queries,
        cosine_pair,
        sine_pair,
        wide_sum,
        own,
        grad_middle,
        gain,
        *weights,
        grad_keys,
        grad_values,
        normed,
        weight,
        pair_weights,
    )


def split_layer(dp, depth):
    def layer(
        hidden_in,
        segment_ids,
        positions,
        attn_gain,
        query_weight,
        key_weight,
        value_weight,
        out_weight,
        mlp_gain,
        gate_weight,
        up_weight,
        down_weight,
        cotangent,
    ):
        f32, bf16 = jnp.float32, jnp.bfloat16
        rows, length, width = hidden_in.shape
        own = rows * length
        team = 2 * dp
        tokens = team * own
        part = query_weight.shape[0]
        hidden_rows = down_weight.shape[0]
        inner = depth * hidden_rows
        heads = depth
        row_count, size = dp * rows, 2 * length
        core = lax.axis_index("core")
        place = lax.axis_index("z")

        def dot(left, right):
            return jnp.dot(left, right, preferred_element_type=f32)

        weight_attn, places, near, weight_out = open_layer(
            dp, depth, query_weight, key_weight, value_weight, attn_gain, mlp_gain, positions,
            hidden_in, out_weight,
        )
        weight_out = weight_out.reshape(heads * HD, width)
        weight_down = lax.all_gather(down_weight, "z", axis=0, tiled=True)

        x_own = hidden_in.reshape(own, width)
        cot_own = cotangent.reshape(own, width)
        freqs = 10000.0 ** (-jnp.arange(0, HD // 2, dtype=f32) * 2.0 / HD)
        queries, normed1, cosine, sine, cosine_pair, sine_pair, offsets, gains, pair_weight, lines, wide_mine = (
            project(near, places, freqs, gate_weight, up_weight, weight_attn)
        )
        wide_got = lax.all_gather(wide_mine, "z", axis=0)
        cotangent, queries = lax.optimization_barrier((cotangent, queries))
        cots = plane_pieces(cotangent, dp)
        cots = [piece.reshape(own, width) for piece in cots]
        low_block = (place * size - places[:, 0, :, 0].reshape(row_count)) // size
        low_block = jnp.maximum(low_block, 0).astype(jnp.int32)
        place_one = place.astype(jnp.int32).reshape(1)
        context, logs = attend(
            low_block, place_one, offsets, queries, lines
        )

        context, cots = lax.optimization_barrier((context, cots))
        middle, normed2 = attend_sum(dp, context, weight_out, hidden_in, gains)
        all_normed2, all_cots, hidden, slope, active, grad_down = mlp_forward(
            normed2, wide_got, cots
        )
        grad_normed2, mlp_parts, grad_wide, pair_weights = mlp_backward(
            all_normed2, all_cots, hidden, slope, active, wide_got, weight_down, pair_weight
        )
        def line_sum(array):
            return lax.psum_scatter(array.astype(bf16), "z", scatter_dimension=0, tiled=True)

        down_sum = line_sum(grad_down)
        grad_wide, down_sum = lax.optimization_barrier((grad_wide, down_sum))
        wide_sum = line_sum(grad_wide)[0]
        grad_normed2, down_sum = lax.optimization_barrier((grad_normed2, down_sum))
        grad_middle, grad_context, grad_wout = middle_back(
            dp, rows, grad_normed2, middle, cot_own, gains, context, weight_out
        )
        grad_down = down_sum.astype(f32)
        mlp_parts, grad_context = lax.optimization_barrier((mlp_parts, grad_context))
        mlp_got = [swap(mlp_parts[k], "dp", dp, k) for k in range(1, dp)]
        grad_queries, grad_keys, grad_values = attend_back(
            low_block,
            place_one,
            offsets,
            queries,
            lines,
            context,
            logs,
            grad_context,
            cosine,
            sine,
        )
        out_hidden = middle + mlp_parts[0].astype(f32)
        for got in mlp_got:
            out_hidden = out_hidden + got.astype(f32)
        out_hidden = out_hidden.astype(bf16)
        grad_queries, out_hidden, grad_wout = lax.optimization_barrier(
            (grad_queries, out_hidden, grad_wout)
        )
        out_sum = line_sum(grad_wout)
        (
            grad_in,
            grad_wquery,
            grad_wkey,
            grad_wvalue,
            grad_wgate,
            grad_wup,
            attn_rows,
            mlp_rows,
        ) = finish(
            grad_queries,
            cosine_pair,
            sine_pair,
            wide_sum,
            hidden_in,
            grad_middle,
            gains,
            (query_weight, key_weight, value_weight, gate_weight, up_weight),
            grad_keys,
            grad_values,
            normed1,
            weight_attn,
            pair_weights,
        )
        out_sum, grad_in = lax.optimization_barrier((out_sum, grad_in))
        grad_wout = out_sum.astype(f32)
        grad_gain_one = attn_rows[:, 0] / attn_gain.astype(f32)
        grad_gain_two = mlp_rows[:, 0] / mlp_gain.astype(f32)
        return (
            out_hidden.reshape(rows, length, width),
            grad_in.reshape(rows, length, width),
            grad_gain_one,
            grad_wquery,
            grad_wkey,
            grad_wvalue,
            grad_wout,
            grad_gain_two,
            grad_wgate,
            grad_wup,
            grad_down,
        )

    return layer


def solution(mesh):
    dp, seq = mesh.shape["dp"], mesh.shape["seq"]
    if dp != KVH or seq % 2 or HQ != dp * seq:
        return gathered_weights(mesh)
    depth = seq // 2
    mesh = Mesh(mesh.devices.reshape(dp, depth, 2), ("dp", "z", "core"))
    every = ("dp", "z", "core")
    tokens = P("dp", ("z", "core"), None)
    matrix = P(every, None)
    return jax.shard_map(
        split_layer(dp, depth),
        mesh=mesh,
        in_specs=(
            tokens,
            P("dp", ("z", "core")),
            P("dp", ("z", "core")),
            P(every),
            matrix,
            matrix,
            matrix,
            matrix,
            P(every),
            matrix,
            matrix,
            matrix,
            tokens,
        ),
        out_specs=(
            tokens,
            tokens,
            P(every),
            matrix,
            matrix,
            matrix,
            matrix,
            P(every),
            matrix,
            matrix,
            matrix,
        ),
        check_vma=False,
    )
```

```python
import functools

import jax
import jax.numpy as jnp
from jax import lax
from jax.experimental import pallas as pl
from jax.experimental.pallas import tpu as pltpu
from jax.sharding import Mesh
from jax.sharding import PartitionSpec as P

HQ = 32
HD = 64
KVH = 4


EPSILON = 1e-05


def fetch_attention(attn_gain, query_weight, key_weight, value_weight, out_weight):
    return (
        lax.all_gather(attn_gain, ("dp", "seq"), axis=0, tiled=True),
        lax.all_gather(query_weight, ("dp", "seq"), axis=0, tiled=True),
        lax.all_gather(key_weight, ("dp", "seq"), axis=0, tiled=True),
        lax.all_gather(value_weight, ("dp", "seq"), axis=0, tiled=True),
        lax.all_gather(out_weight, ("dp", "seq"), axis=0, tiled=True),
    )


def fetch_mlp(mlp_gain, gate_weight, up_weight, down_weight):
    return (
        lax.all_gather(mlp_gain, ("dp", "seq"), axis=0, tiled=True),
        lax.all_gather(gate_weight, ("dp", "seq"), axis=0, tiled=True),
        lax.all_gather(up_weight, ("dp", "seq"), axis=0, tiled=True),
        lax.all_gather(down_weight, ("dp", "seq"), axis=0, tiled=True),
    )


def angles_of(positions):
    freqs = 10000.0 ** (-jnp.arange(0, HD // 2, dtype=jnp.float32) * 2.0 / HD)
    return positions.astype(jnp.float32)[:, None] * freqs[None, :]


def rotate(vectors, cosine, sine):
    half = vectors.shape[-1] // 2
    first = vectors[..., :half]
    second = vectors[..., half:]
    cosine = cosine[:, None, :]
    sine = sine[:, None, :]
    return jnp.concatenate(
        [first * cosine - second * sine, second * cosine + first * sine], axis=-1
    )


def norm_forward(values, gain):
    factor = lax.rsqrt(jnp.mean(values * values, axis=-1, keepdims=True) + EPSILON)
    return (values * factor * gain.astype(jnp.float32), factor)


def norm_backward(values, factor, gain, grad_normed):
    inner = grad_normed * gain.astype(jnp.float32)
    grad_gain = jnp.sum(grad_normed * values * factor, axis=0)
    grad_values = factor * inner - factor * factor * factor * values * jnp.mean(
        inner * values, axis=-1, keepdims=True
    )
    return (grad_values, grad_gain)


def masked_scores(queries_rot, keys_heads, query_pos, query_seg, seg_all):
    scores = jnp.einsum(
        "cgjd,kgd->gjck", queries_rot, keys_heads, preferred_element_type=jnp.float32
    ) * HD ** (-0.5)
    key_pos = jnp.arange(keys_heads.shape[0])
    allowed = (key_pos[None, :] <= query_pos[:, None]) & (seg_all[None, :] == query_seg[:, None])
    return jnp.where(allowed, scores, -1e30)


def add_up(total, extra):
    if total is None:
        return extra
    return jax.tree.map(jnp.add, total, extra)


def gathered_weights_layer(
    hidden_in,
    segment_ids,
    positions,
    attn_gain,
    query_weight,
    key_weight,
    value_weight,
    out_weight,
    mlp_gain,
    gate_weight,
    up_weight,
    down_weight,
    cotangent,
):
    batches, local_len, width = hidden_in.shape
    group = HQ // KVH
    query_pos = lax.axis_index("seq") * local_len + jnp.arange(local_len)
    outputs = []
    grads_in = []
    attn_total = None
    mlp_total = None
    for microbatch in range(batches):
        rows_in = hidden_in[microbatch].astype(jnp.float32)
        seg_own = segment_ids[microbatch]
        angles = angles_of(positions[microbatch])
        cosine = jnp.cos(angles)
        sine = jnp.sin(angles)
        attn_set = fetch_attention(attn_gain, query_weight, key_weight, value_weight, out_weight)
        gain_one, weight_query, weight_key, weight_value, weight_out = attn_set
        normed1, factor1 = norm_forward(rows_in, gain_one)
        normed1_low = normed1.astype(jnp.bfloat16)
        queries = jnp.dot(normed1_low, weight_query, preferred_element_type=jnp.float32).reshape(
            local_len, HQ, HD
        )
        keys_own = jnp.dot(normed1_low, weight_key, preferred_element_type=jnp.float32).reshape(
            local_len, KVH, HD
        )
        values_own = jnp.dot(normed1_low, weight_value, preferred_element_type=jnp.float32).astype(
            jnp.bfloat16
        )
        queries_rot = (
            rotate(queries, cosine, sine).astype(jnp.bfloat16).reshape(local_len, KVH, group, HD)
        )
        keys_rot = rotate(keys_own, cosine, sine).astype(jnp.bfloat16).reshape(local_len, KVH * HD)
        keys_all, values_all, seg_all = (
            lax.all_gather(keys_rot, "seq", axis=0, tiled=True),
            lax.all_gather(values_own, "seq", axis=0, tiled=True),
            lax.all_gather(seg_own, "seq", axis=0, tiled=True),
        )
        keys_heads = keys_all.reshape(-1, KVH, HD)
        values_heads = values_all.reshape(-1, KVH, HD)
        scores = masked_scores(queries_rot, keys_heads, query_pos, seg_own, seg_all)
        highest = jnp.max(scores, axis=-1, keepdims=True)
        powers = jnp.exp(scores - highest)
        totals = jnp.sum(powers, axis=-1, keepdims=True)
        logsum = highest + jnp.log(totals)
        probs_low = (powers / totals).astype(jnp.bfloat16)
        context = jnp.einsum(
            "gjck,kgd->cgjd", probs_low, values_heads, preferred_element_type=jnp.float32
        )
        context_low = context.reshape(local_len, HQ * HD).astype(jnp.bfloat16)
        middle = rows_in + jnp.dot(context_low, weight_out, preferred_element_type=jnp.float32)
        mlp_set = fetch_mlp(mlp_gain, gate_weight, up_weight, down_weight)
        gain_two, weight_gate, weight_up, weight_down = mlp_set
        normed2, factor2 = norm_forward(middle, gain_two)
        normed2_low = normed2.astype(jnp.bfloat16)
        gate = jnp.dot(normed2_low, weight_gate, preferred_element_type=jnp.float32)
        up = jnp.dot(normed2_low, weight_up, preferred_element_type=jnp.float32)
        sigma = jax.nn.sigmoid(gate)
        activation = gate * sigma
        hidden = (activation * up).astype(jnp.bfloat16)
        mlp_out = jnp.dot(hidden, weight_down, preferred_element_type=jnp.float32)
        outputs.append((middle + mlp_out).astype(jnp.bfloat16))
        grad_low = cotangent[microbatch]
        grad_out = grad_low.astype(jnp.float32)
        mlp_back = fetch_mlp(mlp_gain, gate_weight, up_weight, down_weight)
        gain_two, weight_gate, weight_up, weight_down = mlp_back
        grad_down = jnp.dot(hidden.T, grad_low, preferred_element_type=jnp.float32)
        grad_hid = jnp.dot(grad_low, weight_down.T, preferred_element_type=jnp.float32)
        grad_gate = (grad_hid * up * sigma * (1.0 + gate * (1.0 - sigma))).astype(jnp.bfloat16)
        grad_up = (grad_hid * activation).astype(jnp.bfloat16)
        grad_wgate = jnp.dot(normed2_low.T, grad_gate, preferred_element_type=jnp.float32)
        grad_wup = jnp.dot(normed2_low.T, grad_up, preferred_element_type=jnp.float32)
        grad_normed2 = jnp.dot(
            grad_gate, weight_gate.T, preferred_element_type=jnp.float32
        ) + jnp.dot(grad_up, weight_up.T, preferred_element_type=jnp.float32)
        grad_mid_norm, grad_gain_two = norm_backward(middle, factor2, gain_two, grad_normed2)
        grad_middle = grad_out + grad_mid_norm
        attn_back = fetch_attention(attn_gain, query_weight, key_weight, value_weight, out_weight)
        gain_one, weight_query, weight_key, weight_value, weight_out = attn_back
        grad_attn = grad_middle.astype(jnp.bfloat16)
        grad_wout = jnp.dot(context_low.T, grad_attn, preferred_element_type=jnp.float32)
        grad_context = (
            jnp.dot(grad_attn, weight_out.T, preferred_element_type=jnp.float32)
            .astype(jnp.bfloat16)
            .reshape(local_len, KVH, group, HD)
        )
        probs = jnp.exp(
            masked_scores(queries_rot, keys_heads, query_pos, seg_own, seg_all) - logsum
        )
        grad_probs = jnp.einsum(
            "cgjd,kgd->gjck", grad_context, values_heads, preferred_element_type=jnp.float32
        )
        inner = jnp.sum(probs * grad_probs, axis=-1, keepdims=True)
        grad_scores = (probs * (grad_probs - inner)).astype(jnp.bfloat16)
        grad_qrot = jnp.einsum(
            "gjck,kgd->cgjd", grad_scores, keys_heads, preferred_element_type=jnp.float32
        ) * HD ** (-0.5)
        grad_krot_all = jnp.einsum(
            "gjck,cgjd->kgd", grad_scores, queries_rot, preferred_element_type=jnp.float32
        ) * HD ** (-0.5)
        grad_vall = jnp.einsum(
            "gjck,cgjd->kgd", probs_low, grad_context, preferred_element_type=jnp.float32
        )
        row_len = keys_heads.shape[0]
        grad_key_own, grad_value_own = (
            lax.psum_scatter(
                grad_krot_all.reshape(row_len, KVH * HD).astype(jnp.bfloat16),
                "seq",
                scatter_dimension=0,
                tiled=True,
            ).astype(jnp.float32),
            lax.psum_scatter(
                grad_vall.reshape(row_len, KVH * HD).astype(jnp.bfloat16),
                "seq",
                scatter_dimension=0,
                tiled=True,
            ).astype(jnp.float32),
        )
        grad_keys = (
            rotate(grad_key_own.reshape(local_len, KVH, HD), cosine, -sine)
            .astype(jnp.bfloat16)
            .reshape(local_len, KVH * HD)
        )
        grad_values = grad_value_own.astype(jnp.bfloat16)
        grad_queries = (
            rotate(grad_qrot.reshape(local_len, HQ, HD), cosine, -sine)
            .astype(jnp.bfloat16)
            .reshape(local_len, HQ * HD)
        )
        grad_wquery = jnp.dot(normed1_low.T, grad_queries, preferred_element_type=jnp.float32)
        grad_wkey = jnp.dot(normed1_low.T, grad_keys, preferred_element_type=jnp.float32)
        grad_wvalue = jnp.dot(normed1_low.T, grad_values, preferred_element_type=jnp.float32)
        grad_normed1 = jnp.dot(grad_queries, weight_query.T, preferred_element_type=jnp.float32)
        grad_normed1 = grad_normed1 + jnp.dot(
            grad_keys, weight_key.T, preferred_element_type=jnp.float32
        )
        grad_normed1 = grad_normed1 + jnp.dot(
            grad_values, weight_value.T, preferred_element_type=jnp.float32
        )
        grad_rows_norm, grad_gain_one = norm_backward(rows_in, factor1, gain_one, grad_normed1)
        grads_in.append(grad_middle + grad_rows_norm)
        attn_terms = (grad_gain_one, grad_wquery, grad_wkey, grad_wvalue, grad_wout)
        mlp_terms = (grad_gain_two, grad_wgate, grad_wup, grad_down)
        attn_shares = (
            lax.psum_scatter(attn_terms[0], ("dp", "seq"), scatter_dimension=0, tiled=True),
            lax.psum_scatter(attn_terms[1], ("dp", "seq"), scatter_dimension=0, tiled=True),
            lax.psum_scatter(attn_terms[2], ("dp", "seq"), scatter_dimension=0, tiled=True),
            lax.psum_scatter(attn_terms[3], ("dp", "seq"), scatter_dimension=0, tiled=True),
            lax.psum_scatter(attn_terms[4], ("dp", "seq"), scatter_dimension=0, tiled=True),
        )
        mlp_shares = (
            lax.psum_scatter(mlp_terms[0], ("dp", "seq"), scatter_dimension=0, tiled=True),
            lax.psum_scatter(mlp_terms[1], ("dp", "seq"), scatter_dimension=0, tiled=True),
            lax.psum_scatter(mlp_terms[2], ("dp", "seq"), scatter_dimension=0, tiled=True),
            lax.psum_scatter(mlp_terms[3], ("dp", "seq"), scatter_dimension=0, tiled=True),
        )
        attn_total = add_up(attn_total, attn_shares)
        mlp_total = add_up(mlp_total, mlp_shares)
    return (
        jnp.stack(outputs),
        jnp.stack(grads_in),
        attn_total[0],
        attn_total[1],
        attn_total[2],
        attn_total[3],
        attn_total[4],
        mlp_total[0],
        mlp_total[1],
        mlp_total[2],
        mlp_total[3],
    )


def gathered_weights(mesh):
    return jax.shard_map(
        gathered_weights_layer,
        mesh=mesh,
        in_specs=(
            P("dp", "seq", None),
            P("dp", "seq"),
            P("dp", "seq"),
            P(("dp", "seq")),
            P(("dp", "seq"), None),
            P(("dp", "seq"), None),
            P(("dp", "seq"), None),
            P(("dp", "seq"), None),
            P(("dp", "seq")),
            P(("dp", "seq"), None),
            P(("dp", "seq"), None),
            P(("dp", "seq"), None),
            P("dp", "seq", None),
        ),
        out_specs=(
            P("dp", "seq", None),
            P("dp", "seq", None),
            P(("dp", "seq")),
            P(("dp", "seq"), None),
            P(("dp", "seq"), None),
            P(("dp", "seq"), None),
            P(("dp", "seq"), None),
            P(("dp", "seq")),
            P(("dp", "seq"), None),
            P(("dp", "seq"), None),
            P(("dp", "seq"), None),
        ),
        check_vma=False,
    )


def swap(values, axis_name, size, step):
    return lax.ppermute(values, axis_name, [(i, i ^ step) for i in range(size)])


def plane_pieces(values, dp):
    return [values] + [swap(values, "dp", dp, k) for k in range(1, dp)]


NEGATIVE = -1e30
VMEM_LIMIT = 56 * 1024 * 1024
MESH = pl.DeviceIdType.MESH
LIGHT = pl.CostEstimate(flops=0, bytes_accessed=1024, transcendentals=0)


def contract_last(left, right):
    return lax.dot_general(
        left, right, (((1,), (1,)), ((), ())), preferred_element_type=jnp.float32
    )


def multiply(left, right):
    return jnp.dot(left, right, preferred_element_type=jnp.float32)


def spread_keys(block, heads):
    half = block.shape[0] // 2
    return jnp.concatenate([block[:half]] * heads + [block[half:]] * heads, axis=0)


def fold_keys(block, heads):
    half = block.shape[0] // (2 * heads)
    first = sum(block[h * half : (h + 1) * half] for h in range(heads))
    rest = range(heads, 2 * heads)
    return jnp.concatenate([first, sum(block[h * half : (h + 1) * half] for h in rest)], axis=0)


def fold_values(block, heads):
    size = block.shape[0] // heads
    return sum(block[h * size : (h + 1) * size] for h in range(heads))


def turned_head(shape, dim, heads):
    index = lax.broadcasted_iota(jnp.int32, shape, dim)
    return lax.rem(index, shape[dim] // 2) // (shape[dim] // 2 // heads)


def plain_head(shape, dim, heads):
    index = lax.broadcasted_iota(jnp.int32, shape, dim)
    return index // (shape[dim] // heads)


def per_head(values, owner, heads, axis):
    zero = jnp.zeros_like(values)
    return jnp.concatenate([jnp.where(owner == h, values, zero) for h in range(heads)], axis=axis)


def join_heads(stacked, owner, heads):
    size = stacked.shape[0] // heads
    return sum(
        jnp.where(owner == h, stacked[h * size : (h + 1) * size], 0.0) for h in range(heads)
    )


def masked(scores, block, start, order_q, heads):
    size = order_q.shape[0]
    order_k = block * size + lax.broadcasted_iota(jnp.int32, (size, size), 1)
    allowed = (order_k >= start) & (order_k <= order_q)
    split = scores.reshape(heads, size, size)
    return jnp.where(allowed[None], split, NEGATIVE).reshape(scores.shape)


def attend_kernel(heads, low_ref, place_ref, offset_ref, q_ref, k_ref, v_ref, out_ref, log_ref, held):
    row = pl.program_id(0)
    place = place_ref[0]
    queries = q_ref[0]
    size = queries.shape[0]
    stacked = per_head(queries, turned_head(queries.shape, 1, heads), heads, 0)
    order_q = place * size + lax.broadcasted_iota(jnp.int32, (size, 1), 0)
    start = order_q - offset_ref[0][:, :1]

    def score(block, highest):
        scores = multiply(stacked, spread_keys(k_ref[block, 0], heads))
        scores = masked(scores, block, start, order_q, heads)
        held[block] = scores
        return jnp.maximum(highest, jnp.max(scores, axis=1, keepdims=True))

    highest = lax.fori_loop(
        low_ref[row], place + 1, score, jnp.full((heads * size, 1), NEGATIVE, jnp.float32)
    )

    def mix(block, carry):
        total, context = carry
        powers = jnp.exp(held[block] - highest)
        total = total + jnp.sum(powers, axis=1, keepdims=True)
        spread = jnp.concatenate([v_ref[block, 0]] * heads, axis=0)
        return total, context + contract_last(powers.astype(jnp.bfloat16), spread)

    total, context = lax.fori_loop(
        low_ref[row],
        place + 1,
        mix,
        (
            jnp.zeros((heads * size, 1), jnp.float32),
            jnp.zeros((heads * size, queries.shape[1]), jnp.float32),
        ),
    )
    owner = plain_head(queries.shape, 1, heads)
    out_ref[0] = join_heads(context / total, owner, heads).astype(jnp.bfloat16)
    log_ref[0] = highest + jnp.log(total)


def attend_back_kernel(
    heads,
    low_ref,
    place_ref,
    offset_ref,
    q_ref,
    k_ref,
    v_ref,
    context_ref,
    log_ref,
    grad_ref,
    cosine_ref,
    sine_ref,
    grad_q_ref,
    grad_k_ref,
    grad_v_ref,
):
    row = pl.program_id(0)
    place = place_ref[0]
    queries = q_ref[0]
    grads = grad_ref[0]
    size = queries.shape[0]
    turned = turned_head(queries.shape, 1, heads)
    plain = plain_head(queries.shape, 1, heads)
    stacked = per_head(queries, turned, heads, 0)
    stacked_grad = per_head(grads, plain, heads, 0)
    flipped = per_head(queries.T, turned_head(queries.shape, 0, heads), heads, 1)
    flipped_grad = per_head(grads.T, plain_head(queries.shape, 0, heads), heads, 1)
    product = grads.astype(jnp.float32) * context_ref[0].astype(jnp.float32)
    inner = jnp.sum(per_head(product, plain, heads, 0), axis=1, keepdims=True)
    logs = log_ref[0]
    order_q = place * size + lax.broadcasted_iota(jnp.int32, (size, 1), 0)
    start = order_q - offset_ref[0][:, :1]
    grad_k_ref[...] = jnp.zeros_like(grad_k_ref)
    grad_v_ref[...] = jnp.zeros_like(grad_v_ref)

    def step(block, grad_q):
        keys = spread_keys(k_ref[block, 0], heads)
        spread = jnp.concatenate([v_ref[block, 0]] * heads, axis=0)
        scores = masked(multiply(stacked, keys), block, start, order_q, heads)
        probs = jnp.exp(scores - logs)
        grad_probs = multiply(stacked_grad, spread)
        grad_scores = (probs * (grad_probs - inner)).astype(jnp.bfloat16)
        grad_k = fold_keys(multiply(flipped, grad_scores), heads)
        grad_v = fold_values(multiply(flipped_grad, probs.astype(jnp.bfloat16)), heads)
        grad_k_ref[block, 0] = grad_k.astype(jnp.bfloat16)
        grad_v_ref[block, 0] = grad_v.astype(jnp.bfloat16)
        return grad_q + contract_last(grad_scores, keys)

    grad_q = lax.fori_loop(
        low_ref[row],
        place + 1,
        step,
        jnp.zeros((heads * size, queries.shape[1]), jnp.float32),
    )
    grad_q = join_heads(grad_q, turned, heads) * HD ** (-0.5)
    half = grad_q.shape[1] // 2
    first, second = grad_q[:, :half], grad_q[:, half:]
    cosine, sine = cosine_ref[0], sine_ref[0]
    grad_q_ref[0, :, :half] = (first * cosine + second * sine).astype(jnp.bfloat16)
    grad_q_ref[0, :, half:] = (second * cosine - first * sine).astype(jnp.bfloat16)


def row_spec(*shape):
    return pl.BlockSpec((1,) + shape, lambda row, low, place: (row,) + (0,) * len(shape))


def line_spec(depth, *shape):
    return pl.BlockSpec((depth, 1) + shape, lambda row, low, place: (0, row) + (0,) * len(shape))


def pair_spec(which, depth, *shape):
    return pl.BlockSpec(
        (None, depth, 1) + shape, lambda row, low, place: (which, 0, row) + (0,) * len(shape)
    )


def attend(low, place, offsets, queries, lines):
    rows, size, width = queries.shape
    depth, features = lines.shape[1], lines.shape[3]
    heads = width // features
    return pl.pallas_call(
        functools.partial(attend_kernel, heads),
        out_shape=(
            jax.ShapeDtypeStruct((rows, size, width), jnp.bfloat16),
            jax.ShapeDtypeStruct((rows, heads * size, 1), jnp.float32),
        ),
        grid_spec=pltpu.PrefetchScalarGridSpec(
            num_scalar_prefetch=2,
            grid=(rows,),
            in_specs=[
                row_spec(size, offsets.shape[2]),
                row_spec(size, width),
                pair_spec(0, depth, features, size),
                pair_spec(1, depth, features, size),
            ],
            out_specs=[row_spec(size, width), row_spec(heads * size, 1)],
            scratch_shapes=[pltpu.VMEM((depth, heads * size, size), jnp.float32)],
        ),
        compiler_params=pltpu.CompilerParams(vmem_limit_bytes=VMEM_LIMIT),
        cost_estimate=LIGHT,
        name="attend",
    )(low, place, offsets, queries, lines, lines)


def attend_back(low, place, offsets, queries, lines, context, logs, grads, cosine, sine):
    rows, size, width = queries.shape
    depth, features = lines.shape[1], lines.shape[3]
    heads = width // features
    line = line_spec(depth, features, size)
    whole = row_spec(size, width)
    half = row_spec(size, width // 2)
    return pl.pallas_call(
        functools.partial(attend_back_kernel, heads),
        out_shape=(
            jax.ShapeDtypeStruct((rows, size, width), jnp.bfloat16),
            jax.ShapeDtypeStruct(lines.shape[1:], jnp.bfloat16),
            jax.ShapeDtypeStruct(lines.shape[1:], jnp.bfloat16),
        ),
        grid_spec=pltpu.PrefetchScalarGridSpec(
            num_scalar_prefetch=2,
            grid=(rows,),
            in_specs=[
                row_spec(size, offsets.shape[2]),
                whole,
                pair_spec(0, depth, features, size),
                pair_spec(1, depth, features, size),
                whole,
                row_spec(heads * size, 1),
                whole,
                half,
                half,
            ],
            out_specs=[whole, line, line],
        ),
        compiler_params=pltpu.CompilerParams(vmem_limit_bytes=VMEM_LIMIT),
        cost_estimate=LIGHT,
        name="attend_back",
    )(low, place, offsets, queries, lines, lines, context, logs, grads, cosine, sine)


def team_places():
    data = lax.axis_index("dp")
    place = lax.axis_index("z")
    core = lax.axis_index("core")

    def peer(k):
        high = lax.rem(data // 2 + k // 2, 2)
        low = lax.rem(lax.rem(data, 2) + lax.rem(k, 2), 2)
        return (high * 2 + low, place, core)

    return data, place, core, peer, (data, place, 1 - core)


def line_neighbours(depth):
    data, place, core, _, _ = team_places()
    return [(data, lax.rem(place + step, depth), core) for step in (1, depth - 1)]


def greet(targets):
    barrier = pltpu.get_barrier_semaphore()
    for target in targets:
        pl.semaphore_signal(barrier, inc=1, device_id=target, device_id_type=MESH)
    pl.semaphore_wait(barrier, len(targets))


def send(source, target, send_sem, got_sem, device):
    return pltpu.make_async_remote_copy(
        src_ref=source,
        dst_ref=target,
        send_sem=send_sem,
        recv_sem=got_sem,
        device_id=device,
        device_id_type=MESH,
    )


def line_gather(depth, block_of, send_sem, got_sem):
    data, place, core, _, twin = team_places()

    def copy(z, step):
        device = (data, lax.rem(place + depth + step, depth), core)
        block = block_of(z)
        return send(block, block, send_sem.at[z, (1 - step) // 2], got_sem.at[z], device)

    def arrival(z):
        block = block_of(z)
        return send(block, block, send_sem.at[z, 0], got_sem.at[z], twin)

    def start():
        @pl.when(place < depth - 1)
        def _():
            copy(place, 1).start()

        @pl.when(place > 0)
        def _():
            copy(place, -1).start()

    def relay(distance):
        @pl.when(place >= distance)
        def _():
            arrival(place - distance).wait_recv()

            @pl.when(place < depth - 1)
            def _():
                copy(place - distance, 1).start()

        @pl.when(place + distance < depth)
        def _():
            arrival(place + distance).wait_recv()

            @pl.when(place > 0)
            def _():
                copy(place + distance, -1).start()

    def finish():
        for z in range(depth):

            @pl.when((z <= place) & (place < depth - 1))
            def _(z=z):
                copy(z, 1).wait_send()

            @pl.when((z >= place) & (place > 0))
            def _(z=z):
                copy(z, -1).wait_send()

    return start, relay, finish


def sum_scratch(dp, size, width):
    dma = pltpu.SemaphoreType.DMA
    block = pltpu.VMEM((dp, size, width), jnp.bfloat16)
    return [
        block,
        block,
        pltpu.VMEM((2, size // 2, width), jnp.bfloat16),
        pltpu.VMEM((2, size, width), jnp.bfloat16),
        dma((dp,)),
        dma((dp,)),
        dma((2,)),
        dma((2,)),
        dma((2, 2)),
        dma((2, 2)),
    ]


def plane_sum(dp, product, total_ref, scratch):
    side, got, relay, far, side_send, side_got, relay_send, relay_got, far_send, far_got = scratch
    f32, bf16 = jnp.float32, jnp.bfloat16
    _, _, core, peer, twin = team_places()
    size = side.shape[1]
    half = size // 2

    def rows(part):
        return pl.ds(part * half, half)

    def side_copy(k):
        return send(side.at[k], got.at[k], side_send.at[k], side_got.at[k], twin)

    def relay_copy(part):
        return send(
            got.at[3, rows(part)],
            relay.at[part],
            relay_send.at[part],
            relay_got.at[part],
            peer(1 + part),
        )

    def far_copy(which, part):
        return send(
            got.at[1 + which, rows(part)],
            far.at[which, rows(part)],
            far_send.at[which, part],
            far_got.at[which, part],
            peer(1 + which),
        )

    def one(step, carry):
        k = dp - 1 - step
        side[k] = product(k, 1 - core, 0).astype(bf16)
        side_copy(k).start()
        total = product(k, core, 1)
        side_copy(k).wait_recv()
        total = total + got[k].astype(f32)

        @pl.when(k == 0)
        def _():
            total_ref[...] = total

        @pl.when(k > 0)
        def _():
            got[k] = total.astype(bf16)

        @pl.when(k == 3)
        def _():
            relay_copy(0).start()
            relay_copy(1).start()

        @pl.when(k == 2)
        def _():
            far_copy(1, 1).start()

        @pl.when(k == 1)
        def _():
            far_copy(0, 0).start()

        return carry

    lax.fori_loop(0, dp, one, 0)
    for part in range(2):
        which = 1 - part
        relay_copy(part).wait_recv()
        total = got[1 + which, rows(part)].astype(f32) + relay[part].astype(f32)
        got[1 + which, rows(part)] = total.astype(bf16)
        far_copy(which, part).start()

    def complete():
        for which, part in ((0, 0), (1, 1), (0, 1), (1, 0)):
            far_copy(which, part).wait_recv()
            total_ref[rows(part)] += far[which, rows(part)].astype(f32)
        for part in range(2):
            relay_copy(part).wait_send()
            for which in range(2):
                far_copy(which, part).wait_send()
        for k in range(dp):
            side_copy(k).wait_send()

    return complete


def mlp_forward_kernel(dp, depth, x_hbm, wide_hbm, *refs):
    cot_hbms = refs[:dp]
    tokens_hbm, cots_hbm, hidden_hbm, slope_hbm, active_hbm, down_grad_hbm = refs[dp : dp + 6]
    (
        tokens,
        cots,
        wides,
        hidden_t,
        chunk,
        tile_out,
        load_sem,
        cots_sem,
        near_send,
        near_got,
        side_send,
        side_got,
        pass_send,
        pass_got,
        tokens_sem,
        chunk_sem,
        tile_sem,
        twin_send,
        twin_got,
    ) = refs[dp + 6 :]
    bf16 = jnp.bfloat16
    _, _, core, peer, twin = team_places()
    size, width = x_hbm.shape
    half = size // 2
    loads = [pltpu.make_async_copy(x_hbm, tokens.at[0, core], load_sem.at[0])]
    for z in range(depth):
        loads.append(pltpu.make_async_copy(wide_hbm.at[z], wides.at[:, z], load_sem.at[1 + z]))
    cot_loads = []
    for k in range(dp):
        sem = load_sem.at[depth + 1 + k]
        cot_loads.append(pltpu.make_async_copy(cot_hbms[k], cots.at[k, core], sem))
    for load in loads + cot_loads:
        load.start()
    greet([peer(k) for k in range(1, 3)] + [twin])
    loads[0].wait()

    def near_copy(k):
        return send(
            tokens.at[0, core], tokens.at[k, core], near_send.at[k], near_got.at[k], peer(k)
        )

    def pass_copy(part):
        spot = pl.ds(part * half, half)
        return send(
            tokens.at[1 + part, core, spot],
            tokens.at[3, core, spot],
            pass_send.at[part],
            pass_got.at[part],
            peer(2 - part),
        )

    def side_copy(k):
        block = tokens.at[k, core]
        return send(block, block, side_send.at[k], side_got.at[k], twin)

    def side_arrival(k):
        block = tokens.at[k, 1 - core]
        return send(block, block, side_send.at[k], side_got.at[k], twin)

    def twin_copy(k):
        block = cots.at[k, core]
        return send(block, block, twin_send.at[k], twin_got.at[k], twin)

    def twin_arrival(k):
        block = cots.at[k, 1 - core]
        return send(block, block, twin_send.at[k], twin_got.at[k], twin)

    def tokens_out(k, e):
        return pltpu.make_async_copy(tokens.at[k, e], tokens_hbm.at[k, e], tokens_sem.at[k, e])

    def chunk_out(k, e, slot):
        return [
            pltpu.make_async_copy(chunk.at[slot, i], target.at[k, e], chunk_sem.at[slot, i])
            for i, target in enumerate((hidden_hbm, slope_hbm, active_hbm))
        ]

    near_copy(1).start()
    near_copy(2).start()
    side_copy(0).start()
    for load in loads[1:]:
        load.wait()

    def process(k, e, slot, reuse):
        row = tokens[k, e]
        tokens_out(k, e).start()
        both = multiply(row, wides[...].reshape(width, -1))
        inner = both.shape[1] // 2
        gate, up = both[:, :inner], both[:, inner:]
        sigma = 1.0 / (1.0 + jnp.exp(-gate))
        active = gate * sigma
        hidden = (active * up).astype(bf16)
        if reuse:
            for copy in chunk_out(k, e, slot):
                copy.wait()
        chunk[slot, 0] = hidden
        chunk[slot, 1] = (up * sigma * (1.0 + gate * (1.0 - sigma))).astype(bf16)
        chunk[slot, 2] = active.astype(bf16)
        for copy in chunk_out(k, e, slot):
            copy.start()
        spot = pl.ds(pl.multiple_of((k * 2 + e) * size, size), size)
        hidden_t[:, spot] = hidden.T

    process(0, core, 0, False)
    side_arrival(0).wait_recv()
    process(0, 1 - core, 1, False)
    for k in range(dp):
        cot_loads[k].wait()
        twin_copy(k).start()
    for k in range(1, 3):
        near_copy(k).wait_recv()
        pass_copy(k - 1).start()
        side_copy(k).start()
    for k in range(dp):
        twin_arrival(k).wait_recv()
    cots_out = pltpu.make_async_copy(cots, cots_hbm, cots_sem)
    cots_out.start()

    def step(k, carry):
        @pl.when(k == 3)
        def _():
            pass_copy(0).wait_recv()
            pass_copy(1).wait_recv()
            side_copy(3).start()

        process(k, core, 0, True)
        side_arrival(k).wait_recv()
        process(k, 1 - core, 1, True)
        return carry

    lax.fori_loop(1, dp, step, 0)

    def tile_copy(j, slot):
        spot = pl.ds(pl.multiple_of(j * 256, 256), 256)
        return pltpu.make_async_copy(tile_out.at[slot], down_grad_hbm.at[:, spot], tile_sem.at[slot])

    count = width // 256

    def tile(j, carry):
        slot = lax.rem(j, 2)

        @pl.when(j > 1)
        def _():
            tile_copy(j - 2, slot).wait()

        spot = pl.ds(pl.multiple_of(j * 256, 256), 256)
        columns = cots[:, :, :, spot].reshape(-1, 256)
        tile_out[slot] = multiply(hidden_t[...], columns).astype(bf16)
        tile_copy(j, slot).start()
        return carry

    lax.fori_loop(0, count, tile, 0)
    for j in (count - 2, count - 1):
        tile_copy(j, j % 2).wait()
    cots_out.wait()
    for slot, e in ((0, core), (1, 1 - core)):
        for copy in chunk_out(dp - 1, e, slot):
            copy.wait()
    for k in range(dp):
        for e in range(2):
            tokens_out(k, e).wait()
        side_copy(k).wait_send()
        twin_copy(k).wait_send()
    for k in range(1, 3):
        near_copy(k).wait_send()
        pass_copy(k - 1).wait_send()


def mlp_forward(x_own, wide, cots):
    depth, dp = wide.shape[:2]
    size, width = x_own.shape
    inner = wide.shape[-1] // 2
    bf16 = jnp.bfloat16
    hbm = pl.BlockSpec(memory_space=pl.ANY)
    dma = pltpu.SemaphoreType.DMA
    weight = pltpu.VMEM((dp, depth) + wide.shape[2:], bf16)
    whole = jax.ShapeDtypeStruct((dp, 2, size, width), bf16)
    thin = jax.ShapeDtypeStruct((dp, 2, size, inner), bf16)
    return pl.pallas_call(
        functools.partial(mlp_forward_kernel, dp, depth),
        out_shape=(whole, whole, thin, thin, thin, jax.ShapeDtypeStruct((inner, width), bf16)),
        in_specs=[hbm] * (2 + dp),
        out_specs=(hbm,) * 6,
        scratch_shapes=[
            pltpu.VMEM((dp, 2, size, width), bf16),
            pltpu.VMEM((dp, 2, size, width), bf16),
            weight,
            pltpu.VMEM((inner, 2 * dp * size), bf16),
            pltpu.VMEM((2, 3, size, inner), bf16),
            pltpu.VMEM((2, inner, 256), bf16),
            dma((2 * depth + 1 + dp,)),
            dma,
            dma((dp,)),
            dma((dp,)),
            dma((dp,)),
            dma((dp,)),
            dma((2,)),
            dma((2,)),
            dma((dp, 2)),
            dma((2, 3)),
            dma((2,)),
            dma((dp,)),
            dma((dp,)),
        ],
        compiler_params=pltpu.CompilerParams(
            collective_id=1, has_side_effects=True, vmem_limit_bytes=VMEM_LIMIT
        ),
        cost_estimate=LIGHT,
        name="mlp_forward",
    )(x_own, wide, *cots)


def mlp_backward_kernel(
    dp,
    depth,
    tokens_hbm,
    cots_hbm,
    hidden_hbm,
    slope_hbm,
    active_hbm,
    wide_hbm,
    down_hbm,
    pair_hbm,
    grad_ref,
    part_hbm,
    wide_grad_hbm,
    pairs_hbm,
    tokens,
    wides,
    downs,
    wide_t,
    cot_slots,
    chunk,
    part_out,
    part_side,
    tile_out,
    load_sem,
    slot_sem,
    part_sem,
    part_send,
    part_got,
    tile_sem,
    pair_send,
    pair_got,
    pair_sem,
    *sum_refs,
):
    bf16 = jnp.bfloat16
    _, _, core, peer, twin = team_places()
    size, width = grad_ref.shape
    loads = [pltpu.make_async_copy(down_hbm, downs, load_sem.at[0])]
    for z in range(depth):
        loads.append(pltpu.make_async_copy(wide_hbm.at[z], wides.at[:, z], load_sem.at[1 + z]))
    tokens_load = pltpu.make_async_copy(tokens_hbm, tokens, load_sem.at[depth + 1])

    def slot_loads(k, e, slot):
        copies = [pltpu.make_async_copy(cots_hbm.at[k, e], cot_slots.at[slot], slot_sem.at[slot, 3])]
        for i, source in enumerate((hidden_hbm, slope_hbm, active_hbm)):
            copies.append(
                pltpu.make_async_copy(source.at[k, e], chunk.at[slot, i], slot_sem.at[slot, i])
            )
        return copies

    for copy in slot_loads(dp - 1, 1 - core, 0):
        copy.start()
    for load in loads:
        load.start()
    pair_local = pltpu.make_async_copy(pair_hbm, pairs_hbm.at[0], pair_sem)
    pair_local.start()
    greet([peer(k) for k in range(1, dp)] + [twin])

    def pair_copy(k):
        return send(pair_hbm, pairs_hbm.at[k], pair_send.at[k], pair_got.at[k], peer(k))

    for k in range(1, dp):
        pair_copy(k).start()
    for load in loads:
        load.wait()
    tokens_load.start()

    def part_copy(k):
        return pltpu.make_async_copy(part_out.at[1], part_hbm.at[k], part_sem)

    def part_side_copy(k):
        return send(part_out.at[0], part_side.at[k], part_send.at[k], part_got.at[k], twin)

    def product(k, e, turn):
        slot = turn
        for copy in slot_loads(k, e, slot):
            copy.wait()
        if turn == 0:
            for copy in slot_loads(k, core, 1):
                copy.start()
        else:

            @pl.when(k > 0)
            def _():
                for copy in slot_loads(k - 1, 1 - core, 0):
                    copy.start()

        grad_hid = contract_last(cot_slots[slot], downs[...])
        grad_gate = (grad_hid * chunk[slot, 1].astype(jnp.float32)).astype(bf16)
        grad_up = (grad_hid * chunk[slot, 2].astype(jnp.float32)).astype(bf16)
        spot = pl.ds(pl.multiple_of((k * 2 + e) * size, size), size)
        inner = grad_gate.shape[1]
        wide_t[:inner, spot] = grad_gate.T
        wide_t[inner:, spot] = grad_up.T
        terms = multiply(chunk[slot, 0], downs[...])
        if turn == 0:

            @pl.when(k < dp - 1)
            def _():
                part_side_copy(k + 1).wait_send()

            part_out[0] = terms.astype(bf16)
            part_side_copy(k).start()
        else:

            @pl.when(k < dp - 1)
            def _():
                part_copy(k + 1).wait()

            part_side_copy(k).wait_recv()
            part_out[1] = (terms + part_side[k].astype(jnp.float32)).astype(bf16)
            part_copy(k).start()
        both = jnp.concatenate([grad_gate, grad_up], axis=1)
        return contract_last(both, wides[...].reshape(width, -1))

    complete = plane_sum(dp, product, grad_ref, sum_refs)
    tokens_load.wait()
    block = 256
    count = width // block

    inner = wide_t.shape[0] // 2
    per = depth * 128 // block

    def tile_copies(j, slot):
        return [
            pltpu.make_async_copy(
                tile_out.at[slot, pl.ds(which * inner, inner), pl.ds(i * 128, 128)],
                wide_grad_hbm.at[lax.rem(j, per) * (block // 128) + i, which, j // per],
                tile_sem.at[slot, which, i],
            )
            for which in range(2)
            for i in range(block // 128)
        ]

    def tile(j, carry):
        slot = lax.rem(j, 2)

        @pl.when(j > 1)
        def _():
            for copy in tile_copies(j - 2, slot):
                copy.wait()

        spot = pl.ds(pl.multiple_of(j * block, block), block)
        columns = tokens[:, :, :, spot].reshape(-1, block)
        tile_out[slot] = multiply(wide_t[...], columns).astype(bf16)
        for copy in tile_copies(j, slot):
            copy.start()
        return carry

    lax.fori_loop(0, count, tile, 0)
    for j in (count - 2, count - 1):
        for copy in tile_copies(j, j % 2):
            copy.wait()
    complete()
    pair_local.wait()
    for k in range(1, dp):
        pair_copy(k).wait_recv()
        pair_copy(k).wait_send()
    part_side_copy(0).wait_send()
    part_copy(0).wait()


def mlp_backward(tokens, cots, hidden, slope, active, wide, down, pair):
    depth, dp = wide.shape[:2]
    size, width = tokens.shape[2:]
    inner = wide.shape[-1] // 2
    f32, bf16 = jnp.float32, jnp.bfloat16
    hbm = pl.BlockSpec(memory_space=pl.ANY)
    dma = pltpu.SemaphoreType.DMA
    weight = pltpu.VMEM((dp, depth) + wide.shape[2:], bf16)
    turned = pltpu.VMEM((2 * inner, 2 * dp * size), bf16)
    return pl.pallas_call(
        functools.partial(mlp_backward_kernel, dp, depth),
        out_shape=(
            jax.ShapeDtypeStruct((size, width), f32),
            jax.ShapeDtypeStruct((dp, size, width), bf16),
            jax.ShapeDtypeStruct((depth, 2, dp, inner, width // (depth * dp)), bf16),
            jax.ShapeDtypeStruct((dp,) + pair.shape, bf16),
        ),
        in_specs=[hbm] * 8,
        out_specs=(pl.BlockSpec(memory_space=pltpu.VMEM), hbm, hbm, hbm),
        scratch_shapes=[
            pltpu.VMEM((dp, 2, size, width), bf16),
            weight,
            pltpu.VMEM((inner, width), bf16),
            turned,
            pltpu.VMEM((2, size, width), bf16),
            pltpu.VMEM((2, 3, size, inner), bf16),
            pltpu.VMEM((2, size, width), bf16),
            pltpu.VMEM((dp, size, width), bf16),
            pltpu.VMEM((2, 2 * inner, 256), bf16),
            dma((2 * depth + 2,)),
            dma((2, 4)),
            dma,
            dma((dp,)),
            dma((dp,)),
            dma((2, 2, 2)),
            dma((dp,)),
            dma((dp,)),
            dma,
        ]
        + sum_scratch(dp, size, width),
        compiler_params=pltpu.CompilerParams(
            collective_id=6, has_side_effects=True, vmem_limit_bytes=60 * 1024 * 1024
        ),
        cost_estimate=LIGHT,
        name="mlp_backward",
    )(tokens, cots, hidden, slope, active, wide, down, pair)


def attend_sum_kernel(
    dp, rows, context_ref, weight_ref, own_ref, gain_ref, middle_ref, normed_ref, *scratch
):
    _, _, _, peer, twin = team_places()
    length = own_ref.shape[1]
    size, width = middle_ref.shape
    greet([peer(k) for k in range(1, 3)] + [twin])

    def product(k, e, turn):
        spot = pl.ds(pl.multiple_of(e * length, length), length)
        block = context_ref[pl.ds(k * rows, rows), spot].reshape(size, -1)
        return multiply(block, weight_ref[...])

    plane_sum(dp, product, middle_ref, scratch)()
    middle = middle_ref[...] + own_ref[...].reshape(size, width).astype(jnp.float32)
    middle_ref[...] = middle
    factor = lax.rsqrt(jnp.mean(middle * middle, axis=-1, keepdims=True) + EPSILON)
    normed_ref[...] = (middle * factor * gain_ref[1:2].astype(jnp.float32)).astype(jnp.bfloat16)


def attend_sum(dp, context, weight, own, gain):
    rows, length, width = own.shape
    size = rows * length
    vmem = pl.BlockSpec(memory_space=pltpu.VMEM)
    return pl.pallas_call(
        functools.partial(attend_sum_kernel, dp, rows),
        out_shape=(
            jax.ShapeDtypeStruct((size, width), jnp.float32),
            jax.ShapeDtypeStruct((size, width), jnp.bfloat16),
        ),
        in_specs=[vmem] * 4,
        out_specs=(vmem, vmem),
        scratch_shapes=sum_scratch(dp, size, width),
        compiler_params=pltpu.CompilerParams(
            collective_id=4, has_side_effects=True, vmem_limit_bytes=VMEM_LIMIT
        ),
        cost_estimate=LIGHT,
        name="attend_sum",
    )(context, weight, own, gain)


def middle_back_kernel(
    dp,
    rows,
    grad_ref,
    middle_ref,
    cot_ref,
    gain_ref,
    context_ref,
    weight_ref,
    grad_middle_ref,
    grad_context_ref,
    weight_grad_ref,
    tokens,
    context_t,
    near_send,
    near_got,
    side_send,
    side_got,
    pass_send,
    pass_got,
):
    f32, bf16 = jnp.float32, jnp.bfloat16
    _, _, core, peer, twin = team_places()
    size, width = grad_ref.shape
    length = size // rows
    half = size // 2
    greet([peer(k) for k in range(1, 3)] + [twin])
    middle = middle_ref[...]
    factor = lax.rsqrt(jnp.mean(middle * middle, axis=-1, keepdims=True) + EPSILON)
    inner = grad_ref[...] * gain_ref[1:2].astype(f32)
    mean = jnp.mean(inner * middle, axis=-1, keepdims=True)
    total = cot_ref[...].astype(f32) + factor * inner - factor * factor * factor * middle * mean
    grad_middle_ref[...] = total
    tokens[0, core] = total.astype(bf16)

    def near_copy(k):
        return send(
            tokens.at[0, core], tokens.at[k, core], near_send.at[k], near_got.at[k], peer(k)
        )

    def pass_copy(part):
        spot = pl.ds(part * half, half)
        return send(
            tokens.at[1 + part, core, spot],
            tokens.at[3, core, spot],
            pass_send.at[part],
            pass_got.at[part],
            peer(2 - part),
        )

    def side_copy(k):
        block = tokens.at[k, core]
        return send(block, block, side_send.at[k], side_got.at[k], twin)

    def side_arrival(k):
        block = tokens.at[k, 1 - core]
        return send(block, block, side_send.at[k], side_got.at[k], twin)

    near_copy(1).start()
    near_copy(2).start()
    side_copy(0).start()
    for k in range(dp):
        for e in range(2):
            for r in range(rows):
                block = context_ref[k * rows + r, e * length : (e + 1) * length]
                spot = pl.ds(((k * 2 + e) * rows + r) * length, length)
                context_t[:, spot] = block.T

    def process(k, e):
        block = contract_last(tokens[k, e], weight_ref[...]).astype(bf16)
        spot = pl.ds(pl.multiple_of(e * length, length), length)
        grad_context_ref[pl.ds(k * rows, rows), spot] = block.reshape(rows, length, -1)

    process(0, core)
    side_arrival(0).wait_recv()
    process(0, 1 - core)
    for k in range(1, 3):
        near_copy(k).wait_recv()
        pass_copy(k - 1).start()
        side_copy(k).start()

    def step(k, carry):
        @pl.when(k == 3)
        def _():
            pass_copy(0).wait_recv()
            pass_copy(1).wait_recv()
            side_copy(3).start()

        process(k, core)
        side_arrival(k).wait_recv()
        process(k, 1 - core)
        return carry

    lax.fori_loop(1, dp, step, 0)

    def tile(j, carry):
        spot = pl.ds(pl.multiple_of(j * 256, 256), 256)
        columns = tokens[:, :, :, spot].reshape(-1, 256)
        weight_grad_ref[:, spot] = multiply(context_t[...], columns).astype(bf16)
        return carry

    lax.fori_loop(0, width // 256, tile, 0)
    for k in range(1, 3):
        near_copy(k).wait_send()
        pass_copy(k - 1).wait_send()
    for k in range(dp):
        side_copy(k).wait_send()


def middle_back(dp, rows, grad, middle, cot, gain, context, weight):
    f32, bf16 = jnp.float32, jnp.bfloat16
    size, width = grad.shape
    vmem = pl.BlockSpec(memory_space=pltpu.VMEM)
    dma = pltpu.SemaphoreType.DMA
    return pl.pallas_call(
        functools.partial(middle_back_kernel, dp, rows),
        out_shape=(
            jax.ShapeDtypeStruct((size, width), f32),
            jax.ShapeDtypeStruct(context.shape, bf16),
            jax.ShapeDtypeStruct(weight.shape, bf16),
        ),
        in_specs=[vmem] * 6,
        out_specs=(vmem, vmem, vmem),
        scratch_shapes=[
            pltpu.VMEM((dp, 2, size, width), bf16),
            pltpu.VMEM((weight.shape[0], 2 * dp * size), bf16),
            dma((dp,)),
            dma((dp,)),
            dma((dp,)),
            dma((dp,)),
            dma((2,)),
            dma((2,)),
        ],
        compiler_params=pltpu.CompilerParams(
            collective_id=5, has_side_effects=True, vmem_limit_bytes=VMEM_LIMIT
        ),
        cost_estimate=LIGHT,
        name="middle_back",
    )(grad, middle, cot, gain, context, weight)


def open_kernel(
    dp,
    depth,
    query_ref,
    key_ref,
    value_ref,
    attn_gain_ref,
    mlp_gain_ref,
    places_ref,
    own_ref,
    out_ref,
    attn_hbm,
    places_hbm,
    near_hbm,
    out_hbm,
    attn_blocks,
    local_sem,
    attn_send,
    attn_got,
    places_send,
    places_got,
    line_send,
    line_got,
    near_send,
    near_got,
    pass_send,
    pass_got,
    out_send,
    out_got,
):
    data, place, core, peer, twin = team_places()
    part = query_ref.shape[0]
    half = HD // 2
    side = depth * half
    middle = own_ref.shape[0] // 2
    attn_blocks[...] = jnp.zeros_like(attn_blocks)
    for d in range(dp):
        for c in range(2):
            team = 2 * d + c
            for z in range(depth):
                owner = (d * depth + z) * 2 + c
                for h in range(2):
                    spot = owner * HD + h * half
                    attn_blocks[team, :, h * side + z * half : h * side + (z + 1) * half] = (
                        query_ref[:, spot : spot + half]
                    )
            pair = key_ref if c == 0 else value_ref
            last = 2 * side + HD
            attn_blocks[team, :, 2 * side : last] = pair[:, d * HD : (d + 1) * HD]
            attn_blocks[team, 0:1, last : last + part] = attn_gain_ref[...]
            attn_blocks[team, 1:2, last : last + part] = mlp_gain_ref[...]

    def device(k, other):
        return (peer(k)[0], place, 1 - core if other else core)

    def number(k, other):
        return 2 * peer(k)[0] + (1 - core if other else core)

    pairs = [(k, other) for k in range(dp) for other in range(2) if k or other]
    greet([device(k, other) for k, other in pairs] + line_neighbours(depth))

    def attn_copy(k, other):
        return send(
            attn_blocks.at[number(k, other)],
            attn_hbm.at[place, data, core],
            attn_send.at[k, other],
            attn_got.at[k, other],
            device(k, other),
        )

    def places_copy(k, other):
        return send(
            places_ref,
            places_hbm.at[k, core],
            places_send.at[k, other],
            places_got.at[k, other],
            device(k, other),
        )

    def arrival(target, send_sem, got_sem):
        return send(target, target, send_sem, got_sem, twin)

    def near_copy(k):
        return send(own_ref, near_hbm.at[k], near_send.at[k], near_got.at[k], peer(k))

    def pass_copy(which):
        spot = pl.ds(which * middle, middle)
        return send(
            near_hbm.at[1 + which, spot],
            near_hbm.at[3, spot],
            pass_send.at[which],
            pass_got.at[which],
            peer(2 - which),
        )

    start, relay, complete = line_gather(depth, lambda z: attn_hbm.at[z], line_send, line_got)
    out_start, out_relay, out_complete = line_gather(
        depth, lambda z: out_hbm.at[z], out_send, out_got
    )
    for k, other in pairs:
        attn_copy(k, other).start()
    for k, other in pairs:
        places_copy(k, other).start()
    near_copy(1).start()
    near_copy(2).start()
    locals_ = [
        pltpu.make_async_copy(
            attn_blocks.at[2 * data + core], attn_hbm.at[place, data, core], local_sem.at[0]
        ),
        pltpu.make_async_copy(places_ref, places_hbm.at[0, core], local_sem.at[1]),
        pltpu.make_async_copy(own_ref, near_hbm.at[0], local_sem.at[2]),
        pltpu.make_async_copy(out_ref, out_hbm.at[place], local_sem.at[3]),
    ]
    for copy in locals_:
        copy.start()
    locals_[0].wait()
    for k, other in pairs:
        target = attn_hbm.at[place, peer(k)[0], 1 - core if other else core]
        arrival(target, attn_send.at[k, other], attn_got.at[k, other]).wait_recv()
    start()
    for copy in locals_[1:]:
        copy.wait()
    out_start()
    relay(1)
    for which in range(2):
        near_copy(1 + which).wait_recv()
        pass_copy(which).start()
    for distance in range(2, depth):
        relay(distance)
        out_relay(distance - 1)
    out_relay(depth - 1)
    for k, other in pairs:
        target = places_hbm.at[k, 1 - core if other else core]
        arrival(target, places_send.at[k, other], places_got.at[k, other]).wait_recv()
    for which in range(2):
        pass_copy(which).wait_recv()
        pass_copy(which).wait_send()
        near_copy(1 + which).wait_send()
    complete()
    out_complete()
    for k, other in pairs:
        attn_copy(k, other).wait_send()
        places_copy(k, other).wait_send()


def open_layer(dp, depth, query, key, value, attn_gain, mlp_gain, places, own, out_weight):
    part = query.shape[0]
    columns = depth * HD + HD + part
    bf16 = jnp.bfloat16
    hbm = pl.BlockSpec(memory_space=pl.ANY)
    vmem = pl.BlockSpec(memory_space=pltpu.VMEM)
    dma = pltpu.SemaphoreType.DMA
    return pl.pallas_call(
        functools.partial(open_kernel, dp, depth),
        out_shape=(
            jax.ShapeDtypeStruct((depth, dp, 2, part, columns), bf16),
            jax.ShapeDtypeStruct((dp, 2) + places.shape, places.dtype),
            jax.ShapeDtypeStruct((dp,) + own.shape, bf16),
            jax.ShapeDtypeStruct((depth,) + out_weight.shape, bf16),
        ),
        in_specs=[vmem] * 8,
        out_specs=(hbm,) * 4,
        scratch_shapes=[
            pltpu.VMEM((2 * dp, part, columns), bf16),
            dma((4,)),
            dma((dp, 2)),
            dma((dp, 2)),
            dma((dp, 2)),
            dma((dp, 2)),
            dma((depth, 2)),
            dma((depth,)),
            dma((dp,)),
            dma((dp,)),
            dma((2,)),
            dma((2,)),
            dma((depth, 2)),
            dma((depth,)),
        ],
        compiler_params=pltpu.CompilerParams(
            collective_id=7, has_side_effects=True, vmem_limit_bytes=VMEM_LIMIT
        ),
        cost_estimate=LIGHT,
        name="open_layer",
    )(query, key, value, attn_gain[None], mlp_gain[None], places, own, out_weight)


def project_kernel(
    dp,
    depth,
    rows,
    *refs,
):
    pieces, places_ref, freq_ref, freq_pair_ref, gate_ref, up_ref, weight_hbm = refs[:7]
    query_ref, normed_hbm, cosine_ref, sine_ref, cosine_pair_ref, sine_pair_ref = refs[7:13]
    offset_ref, gain_ref, pair_weight_ref, line_hbm, wide_hbm = refs[13:18]
    (
        weight,
        pair,
        far_pieces,
        load_sem,
        own_sem,
        line_send,
        line_got,
        side_send,
        side_got,
        twin_send,
        twin_got,
        wide_blocks,
        wide_send,
        wide_got,
        wide_sem,
        normed,
        normed_sem,
    ) = refs[18:]
    f32, bf16 = jnp.float32, jnp.bfloat16
    data, place, core, peer, twin = team_places()
    length, width = pieces.shape[2:]
    part = weight.shape[3]
    columns = query_ref.shape[2]
    loads = [
        pltpu.make_async_copy(
            weight_hbm.at[z], weight.at[:, z], load_sem.at[z]
        )
        for z in range(depth)
    ]
    for load in loads:
        load.start()

    def device(k, other):
        return (peer(k)[0], place, 1 - core if other else core)

    def number(k, other):
        return 2 * peer(k)[0] + (1 - core if other else core)

    pairs = [(k, other) for k in range(dp) for other in range(2) if k or other]
    others = [(data, lax.rem(place + step, depth), core) for step in range(1, depth)]
    greet(others + [device(k, other) for k, other in pairs])

    def wide_copy(k, other):
        return send(
            wide_blocks.at[number(k, other)],
            wide_hbm.at[data, core],
            wide_send.at[k, other],
            wide_got.at[k, other],
            device(k, other),
        )


    def twin_copy(k):
        return send(pieces.at[k], far_pieces.at[k], twin_send.at[k], twin_got.at[k], twin)

    for k in range(dp):
        twin_copy(k).start()
    count = wide_blocks.shape[2] // (2 * depth)
    for d in range(dp):
        for c in range(2):
            for z in range(depth):
                owner = (d * depth + z) * 2 + c
                for which, source in ((0, gate_ref), (1, up_ref)):
                    spot = (which * depth + z) * count
                    wide_blocks[2 * d + c, :, spot : spot + count] = source[
                        :, owner * count : (owner + 1) * count
                    ]
    wide_local = pltpu.make_async_copy(
        wide_blocks.at[2 * data + core], wide_hbm.at[data, core], wide_sem
    )
    wide_local.start()
    for k, other in pairs:
        wide_copy(k, other).start()
    for load in loads:
        load.wait()
    for d in range(dp):
        for z in range(depth):
            for c in range(2):
                spot = ((d * depth + z) * 2 + c) * part
                gain_ref[:, spot : spot + part] = weight[d, z, c, 0:2, columns + HD :]
    pair_weight_ref[...] = weight[...].reshape(width, -1)[:, columns : columns + HD].T
    gain = gain_ref[0:1].astype(f32)
    turning = (1 - core).astype(f32)

    def block_of(which, z, k):
        return line_hbm.at[which, z, pl.ds(k * rows, rows)]

    def pair_of(k):
        return pair.at[pl.ds(k * rows, rows)]

    def own_copy(k):
        return pltpu.make_async_copy(pair_of(k), block_of(core, place, k), own_sem.at[k])

    def own_side_copy(k):
        return send(
            pair_of(k),
            block_of(core, place, k),
            side_send.at[place, k],
            side_got.at[place, k],
            twin,
        )

    def line_copy(z, k):
        return send(
            pair_of(k),
            block_of(core, place, k),
            line_send.at[z, k],
            line_got.at[place, k],
            (data, z, core),
        )

    def line_arrival(z, k):
        block = block_of(core, z, k)
        return send(block, block, line_send.at[z, k], line_got.at[z, k], twin)

    def side_copy(z, k):
        block = block_of(core, z, k)
        return send(block, block, side_send.at[z, k], side_got.at[z, k], twin)

    def side_arrival(z, k):
        block = block_of(1 - core, z, k)
        return send(block, block, side_send.at[z, k], side_got.at[z, k], twin)

    def normed_copy(k, e):
        return pltpu.make_async_copy(normed.at[k, e], normed_hbm.at[k, e], normed_sem.at[k, e])

    for k in range(dp):
        for far in range(2):
            e = core if far == 0 else 1 - core
            if far:
                twin_copy(k).wait_recv()
            source = far_pieces.at[k] if far else pieces.at[k]
            values = source[...].reshape(rows * length, width).astype(f32)
            factor = lax.rsqrt(jnp.mean(values * values, axis=-1, keepdims=True) + EPSILON)
            tokens = (values * factor * gain).astype(bf16)
            normed[k, e] = tokens
            normed_copy(k, e).start()
            result = multiply(tokens, weight[...].reshape(width, -1)[:, columns:])
            spot = pl.ds(pl.multiple_of(e * length, length), length)
            for r in range(rows):
                row = k * rows + r
                offsets = places_ref[k, e][r : r + 1].astype(f32)
                keys = result[r * length : (r + 1) * length, :HD].T
                angles = offsets * freq_pair_ref[...] * turning
                cosine, sine = jnp.cos(angles), jnp.sin(angles)
                cosine_pair_ref[row, :, spot] = cosine
                sine_pair_ref[row, :, spot] = sine
                first, second = keys[: HD // 2], keys[HD // 2 :]
                pair[row, : HD // 2, spot] = (first * cosine - second * sine).astype(bf16)
                pair[row, HD // 2 :, spot] = (second * cosine + first * sine).astype(bf16)
        own_copy(k).start()
        own_side_copy(k).start()
        for z in range(depth):

            @pl.when(z > place)
            def _(z=z, k=k):
                line_copy(z, k).start()

    def turn_queries(k, carry):
        for e in range(2):
            result = multiply(normed[k, e], weight[...].reshape(width, -1)[:, :columns])
            spot = pl.ds(e * length, length)
            for r in range(rows):
                row = k * rows + r
                block = result[r * length : (r + 1) * length]
                offsets = places_ref[k, e][r : r + 1].astype(f32)
                column = jnp.broadcast_to(offsets, (length, length)).T
                offset_ref[row, spot] = column.astype(jnp.int32)
                angles = column * freq_ref[...]
                cosine, sine = jnp.cos(angles), jnp.sin(angles)
                cosine_ref[row, spot] = cosine
                sine_ref[row, spot] = sine
                first, second = block[:, : columns // 2], block[:, columns // 2 :]
                turned = (first * cosine - second * sine).astype(bf16)
                query_ref[row, spot, : columns // 2] = turned * bf16(HD ** (-0.5))
                turned = (second * cosine + first * sine).astype(bf16)
                query_ref[row, spot, columns // 2 :] = turned * bf16(HD ** (-0.5))
        return carry

    lax.fori_loop(0, dp, turn_queries, 0)
    for k in range(dp):
        for z in reversed(range(depth)):

            @pl.when(z < place)
            def _(z=z, k=k):
                line_arrival(z, k).wait_recv()
                side_copy(z, k).start()

    for k in range(dp):
        for e in range(2):
            normed_copy(k, e).wait()
    wide_local.wait()
    for k, other in pairs:
        block = wide_hbm.at[peer(k)[0], 1 - core if other else core]
        send(block, block, wide_send.at[k, other], wide_got.at[k, other], twin).wait_recv()
        wide_copy(k, other).wait_send()
    for k in range(dp):
        twin_copy(k).wait_send()
        own_copy(k).wait()
        own_side_copy(k).wait_send()
        for z in range(depth):

            @pl.when(z <= place)
            def _(z=z, k=k):
                side_arrival(z, k).wait_recv()

            @pl.when(z < place)
            def _(z=z, k=k):
                side_copy(z, k).wait_send()

            @pl.when(z > place)
            def _(z=z, k=k):
                line_copy(z, k).wait_send()


def project(near, places, freqs, gate, up, weight):
    f32, bf16 = jnp.float32, jnp.bfloat16
    dp, rows, length, width = near.shape
    depth = weight.shape[0]
    heads = depth
    row_count, size = dp * rows, 2 * length
    columns = heads * HD
    part = width // (2 * dp * depth)
    hbm = pl.BlockSpec(memory_space=pl.ANY)
    vmem = pl.BlockSpec(memory_space=pltpu.VMEM)
    dma = pltpu.SemaphoreType.DMA
    turned = jax.ShapeDtypeStruct((row_count, size, columns // 2), f32)
    turned_pair = jax.ShapeDtypeStruct((row_count, HD // 2, size), f32)
    return pl.pallas_call(
        functools.partial(project_kernel, dp, depth, rows),
        out_shape=(
            jax.ShapeDtypeStruct((row_count, size, columns), bf16),
            jax.ShapeDtypeStruct((dp, 2, rows * length, width), bf16),
            turned,
            turned,
            turned_pair,
            turned_pair,
            jax.ShapeDtypeStruct((row_count, size, length), jnp.int32),
            jax.ShapeDtypeStruct((2, width), bf16),
            jax.ShapeDtypeStruct((HD, width), bf16),
            jax.ShapeDtypeStruct((2, depth, row_count, HD, size), bf16),
            jax.ShapeDtypeStruct((dp, 2, part, gate.shape[1] // dp), bf16),
        ),
        in_specs=[vmem] * 6 + [hbm],
        out_specs=(vmem, hbm) + (vmem,) * 7 + (hbm,) * 2,
        scratch_shapes=[
            pltpu.VMEM((dp, depth) + weight.shape[2:], bf16),
            pltpu.VMEM((row_count, HD, size), bf16),
            pltpu.VMEM((dp, rows, length, width), bf16),
            dma((2 * depth,)),
            dma((dp,)),
            dma((depth, dp)),
            dma((depth, dp)),
            dma((depth, dp)),
            dma((depth, dp)),
            dma((dp,)),
            dma((dp,)),
            pltpu.VMEM((2 * dp, part, gate.shape[1] // dp), bf16),
            dma((dp, 2)),
            dma((dp, 2)),
            dma,
            pltpu.VMEM((dp, 2, rows * length, width), bf16),
            dma((dp, 2)),
        ],
        compiler_params=pltpu.CompilerParams(
            collective_id=2, has_side_effects=True, vmem_limit_bytes=VMEM_LIMIT
        ),
        cost_estimate=LIGHT,
        name="project",
    )(near, places, jnp.tile(freqs, heads)[None], freqs[:, None], gate, up, weight)


def as_row(column):
    return jnp.broadcast_to(column, (column.shape[0], 128)).T[0:1]


def finish_kernel(
    dp,
    depth,
    rows,
    query_ref,
    cosine_ref,
    sine_ref,
    wide_ref,
    own_ref,
    grad_middle_ref,
    gain_ref,
    query_weight_ref,
    key_weight_ref,
    value_weight_ref,
    gate_weight_ref,
    up_weight_ref,
    grad_k_hbm,
    grad_v_hbm,
    normed_hbm,
    weight_hbm,
    *refs,
):
    pairs_hbm, *refs = refs
    finish_body(
        dp, depth, rows, query_ref, cosine_ref, sine_ref, wide_ref, own_ref,
        grad_middle_ref, gain_ref, query_weight_ref, key_weight_ref, value_weight_ref,
        gate_weight_ref, up_weight_ref, grad_k_hbm, grad_v_hbm, normed_hbm, weight_hbm, pairs_hbm,
        *refs,
    )


def finish_body(
    dp,
    depth,
    rows,
    query_ref,
    cosine_ref,
    sine_ref,
    wide_ref,
    own_ref,
    grad_middle_ref,
    gain_ref,
    query_weight_ref,
    key_weight_ref,
    value_weight_ref,
    gate_weight_ref,
    up_weight_ref,
    grad_k_hbm,
    grad_v_hbm,
    normed_hbm,
    weight_hbm,
    pairs_hbm,
    grad_ref,
    query_grad_ref,
    key_grad_ref,
    value_grad_ref,
    gate_grad_ref,
    up_grad_ref,
    attn_gain_ref,
    mlp_gain_ref,
    normed,
    weight,
    kept,
    given,
    arrived,
    line_block,
    line_got_block,
    terms,
    terms_t,
    held,
    line_grads,
    line_grads_got,
    team_block,
    team_got_block,
    wide_block,
    wide_got_block,
    load_sem,
    swap_send,
    swap_got,
    line_send,
    line_got,
    grads_send,
    grads_got,
    team_send,
    team_got,
    wide_send,
    wide_got,
    pair_weight,
    pair_out,
    pair_in,
    pair_load_sem,
    pair_twin_send,
    pair_twin_got,
    pair_send,
    pair_got,
    *sum_refs,
):
    f32, bf16 = jnp.float32, jnp.bfloat16
    data, place, core, peer, twin = team_places()
    columns = query_ref.shape[2]
    size = query_ref.shape[1]
    length = size // 2
    width = grad_ref.shape[1]
    part = weight.shape[3]
    features = columns + HD
    half = HD // 2
    loads = [
        pltpu.make_async_copy(
            weight_hbm.at[z, :, :, :, pl.ds(0, columns)],
            weight.at[:, z],
            load_sem.at[z],
        )
        for z in range(depth)
    ]
    pair_loads = [
        pltpu.make_async_copy(pairs_hbm.at[k], pair_weight.at[k, core], pair_load_sem.at[k])
        for k in range(dp)
    ]
    loads.append(pltpu.make_async_copy(normed_hbm, normed, load_sem.at[depth]))

    @pl.when(core == 0)
    def _():
        pltpu.make_async_copy(grad_k_hbm, kept, load_sem.at[depth + 1]).start()
        pltpu.make_async_copy(grad_v_hbm, given, load_sem.at[depth + 2]).start()

    @pl.when(core == 1)
    def _():
        pltpu.make_async_copy(grad_v_hbm, kept, load_sem.at[depth + 1]).start()
        pltpu.make_async_copy(grad_k_hbm, given, load_sem.at[depth + 2]).start()

    for load in loads + pair_loads:
        load.start()
    others = [(data, lax.rem(place + step, depth), core) for step in range(1, depth)]

    def device(k, other):
        return (peer(k)[0], place, 1 - core if other else core)

    pairs = [(k, other) for k in range(dp) for other in range(2) if k or other]
    greet(others + [device(k, other) for k, other in pairs])
    pltpu.make_async_copy(grad_v_hbm, given, load_sem.at[depth + 2]).wait()
    swap_copy = send(given, arrived, swap_send, swap_got, twin)
    swap_copy.start()

    def pair_twin(k):
        block = pair_weight.at[k, core]
        return send(block, block, pair_twin_send.at[k], pair_twin_got.at[k], twin)

    def pair_twin_arrival(k):
        block = pair_weight.at[k, 1 - core]
        return send(block, block, pair_twin_send.at[k], pair_twin_got.at[k], twin)

    def pair_copy(k, other):
        e = 1 - core if other else core
        return send(
            pair_out.at[k, e],
            pair_in.at[k, core],
            pair_send.at[k, other],
            pair_got.at[k, other],
            device(k, other),
        )

    def pair_arrival(k, other):
        block = pair_in.at[k, 1 - core if other else core]
        return send(block, block, pair_send.at[k, other], pair_got.at[k, other], twin)

    def wide_copy(k, other):
        spot = (peer(k)[0], 1 - core if other else core)
        return send(
            wide_block.at[spot],
            wide_got_block.at[data, core],
            wide_send.at[k, other],
            wide_got.at[k, other],
            device(k, other),
        )

    def wide_arrival(k, other):
        block = wide_got_block.at[peer(k)[0], 1 - core if other else core]
        return send(block, block, wide_send.at[k, other], wide_got.at[k, other], twin)

    def line_copy(z):
        return send(
            line_block.at[z],
            line_got_block.at[place],
            line_send.at[z],
            line_got.at[place],
            (data, z, core),
        )

    def line_arrival(z):
        block = line_got_block.at[z]
        return send(block, block, line_send.at[z], line_got.at[z], twin)

    pltpu.make_async_copy(grad_k_hbm, kept, load_sem.at[depth + 1]).wait()
    swap_copy.wait_recv()
    for z in range(depth):

        @pl.when(z < place)
        def _(z=z):
            total = kept[z].astype(f32) + arrived[z].astype(f32)
            line_block[z] = total.astype(bf16)
            line_copy(z).start()

    for load in loads:
        load.wait()
    for k in range(dp):
        for e in range(2):
            for r in range(rows):
                block = query_ref[k * rows + r, e * length : (e + 1) * length]
                terms[k, e, r * length : (r + 1) * length] = block
                spot = pl.ds(((k * 2 + e) * rows + r) * length, length)
                terms_t[:columns, spot] = block.T

    def tile_rows(first, count):
        def tile(j, carry):
            spot = pl.ds(pl.multiple_of(j * 256, 256), 256)
            block = multiply(
                terms_t[first : first + count], normed[:, :, :, spot].reshape(-1, 256)
            ).astype(bf16)
            for i in range(2):
                group = 2 * j + i
                line_grads[lax.rem(group, depth), group // depth, first : first + count] = block[
                    :, i * 128 : (i + 1) * 128
                ]
            return carry

        lax.fori_loop(0, width // 256, tile, 0)

    def grads_copy(z, piece):
        spot = pl.ds(piece * columns, HD if piece else columns)
        return send(
            line_grads.at[z, :, spot],
            line_grads_got.at[place, :, spot],
            grads_send.at[z, piece],
            grads_got.at[place, piece],
            (data, z, core),
        )

    def grads_arrival(z, piece):
        spot = pl.ds(piece * columns, HD if piece else columns)
        block = line_grads_got.at[z, :, spot]
        return send(block, block, grads_send.at[z, piece], grads_got.at[z, piece], twin)

    def product(k, e, turn):
        return contract_last(terms[k, e], weight[...].reshape(width, columns))

    complete = plane_sum(dp, product, grad_ref, sum_refs)
    for k in range(dp):
        pair_loads[k].wait()
        pair_twin(k).start()
    for which in range(2):
        for d in range(dp):
            block = wide_ref[which, d].T
            wide_block[d, 0, which] = block[:part]
            wide_block[d, 1, which] = block[part:]
    for k, other in pairs:
        wide_copy(k, other).start()
    wide_got_block[data, core] = wide_block[data, core]
    tile_rows(0, columns)
    for z in range(depth):

        @pl.when(z > place)
        def _(z=z):
            grads_copy(z, 0).start()

    for z in range(depth):

        @pl.when(z == place)
        def _(z=z):
            held[...] = kept[z].astype(f32) + arrived[z].astype(f32)

    for z in range(depth):

        @pl.when(z > place)
        def _(z=z):
            line_arrival(z).wait_recv()
            held[...] += line_got_block[z].astype(f32)

    for z in range(depth):

        @pl.when(z < place)
        def _(z=z):
            grads_copy(z, 0).start()

    for k in range(dp):
        for r in range(rows):
            row = k * rows + r
            first, second = held[row, :half], held[row, half:]
            cosine, sine = cosine_ref[row], sine_ref[row]
            turned = jnp.concatenate(
                [first * cosine + second * sine, second * cosine - first * sine], axis=0
            ).astype(bf16)
            for e in range(2):
                block = turned[:, e * length : (e + 1) * length]
                spot = pl.ds(((k * 2 + e) * rows + r) * length, length)
                terms_t[columns:, spot] = block
                pair_out[k, e, :, r * length : (r + 1) * length] = block
    for k, other in pairs:
        pair_copy(k, other).start()
    pair_in[0, core] = pair_out[0, core]

    tile_rows(columns, HD)
    for z in range(depth):

        @pl.when(z != place)
        def _(z=z):
            grads_copy(z, 1).start()

    for k, other in pairs:
        wide_arrival(k, other).wait_recv()
    count = wide_block.shape[4] // depth
    for d in range(dp):
        for c in range(2):
            for which, target in ((0, gate_grad_ref), (1, up_grad_ref)):
                block = wide_got_block[d, c, which].astype(f32)
                for z in range(depth):
                    spot = ((d * depth + z) * 2 + c) * count
                    target[:, spot : spot + count] = block[:, z * count : (z + 1) * count]
    products = gate_weight_ref[...].astype(f32) * gate_grad_ref[...]
    products = products + up_weight_ref[...].astype(f32) * up_grad_ref[...]
    mlp_gain_ref[...] = as_row(jnp.sum(products, axis=-1, keepdims=True))

    def team_copy(k, other, piece):
        spot = (peer(k)[0], 1 - core if other else core)
        return send(
            team_block.at[spot + (piece,)],
            team_got_block.at[data, core, piece],
            team_send.at[k, other, piece],
            team_got.at[k, other, piece],
            device(k, other),
        )

    def team_arrival(k, other, piece):
        block = team_got_block.at[peer(k)[0], 1 - core if other else core, piece]
        send_sem, got_sem = team_send.at[k, other, piece], team_got.at[k, other, piece]
        return send(block, block, send_sem, got_sem, twin)

    line_grads_got[place] = line_grads[place]

    def team_piece(piece, first, last):
        for z in range(depth):

            @pl.when(z != place)
            def _(z=z):
                grads_arrival(z, piece).wait_recv()

        for d in range(dp):
            total = line_grads_got[0, d, first:last].astype(f32)
            for z in range(1, depth):
                total = total + line_grads_got[z, d, first:last].astype(f32)
            total = total.T.astype(bf16)
            team_block[d, 0, piece, :, : last - first] = total[:part]
            team_block[d, 1, piece, :, : last - first] = total[part:]
        for k, other in pairs:
            team_copy(k, other, piece).start()
        team_got_block[data, core, piece] = team_block[data, core, piece]

    team_block[...] = jnp.zeros_like(team_block)
    team_piece(0, 0, columns)
    complete()
    for k, other in pairs:
        pair_arrival(k, other).wait_recv()
    for k in range(dp):
        pair_twin_arrival(k).wait_recv()
    grad_ref[...] += multiply(
        pair_in[...].reshape(2 * dp * HD, -1).T, pair_weight[...].reshape(2 * dp * HD, width)
    )
    own = own_ref[...].reshape(grad_ref.shape).astype(f32)
    factor = lax.rsqrt(jnp.mean(own * own, axis=-1, keepdims=True) + EPSILON)
    inner = grad_ref[...] * gain_ref[0:1].astype(f32)
    mean = jnp.mean(inner * own, axis=-1, keepdims=True)
    grad_ref[...] = grad_middle_ref[...] + factor * inner - factor * factor * factor * own * mean
    team_piece(1, columns, features)
    for k, other in pairs:
        team_arrival(k, other, 0).wait_recv()
    side = depth * half
    for d in range(dp):
        for c in range(2):
            block = team_got_block[d, c, 0].astype(f32)
            for z in range(depth):
                for h in range(2):
                    spot = ((d * depth + z) * 2 + c) * HD + h * half
                    start = h * side + z * half
                    query_grad_ref[:, spot : spot + half] = block[:, start : start + half]
    for k, other in pairs:
        team_arrival(k, other, 1).wait_recv()
    for d in range(dp):
        for c in range(2):
            target = key_grad_ref if c == 0 else value_grad_ref
            target[:, d * HD : (d + 1) * HD] = team_got_block[d, c, 1, :, :HD].astype(f32)
    total = sum(
        jnp.sum(before[...].astype(f32) * after[...], axis=-1, keepdims=True)
        for before, after in (
            (query_weight_ref, query_grad_ref),
            (key_weight_ref, key_grad_ref),
            (value_weight_ref, value_grad_ref),
        )
    )
    attn_gain_ref[...] = as_row(total)
    swap_copy.wait_send()
    for k in range(dp):
        pair_twin(k).wait_send()
    for k, other in pairs:
        team_copy(k, other, 0).wait_send()
        team_copy(k, other, 1).wait_send()
        pair_copy(k, other).wait_send()
        wide_copy(k, other).wait_send()
    for z in range(depth):

        @pl.when(z < place)
        def _(z=z):
            line_copy(z).wait_send()

        @pl.when(z != place)
        def _(z=z):
            grads_copy(z, 0).wait_send()
            grads_copy(z, 1).wait_send()


def finish(grad_queries, cosine_pair, sine_pair, wide_sum, own, grad_middle, gain, weights, grad_keys, grad_values, normed, weight, pair_weights):
    f32, bf16 = jnp.float32, jnp.bfloat16
    dp, _, size, width = normed.shape
    rows = own.shape[0]
    depth, row_count, features, line_size = grad_keys.shape
    columns = grad_queries.shape[2]
    part = width // (2 * dp * depth)
    inner = wide_sum.shape[2]
    total = columns + features
    hbm = pl.BlockSpec(memory_space=pl.ANY)
    vmem = pl.BlockSpec(memory_space=pltpu.VMEM)
    dma = pltpu.SemaphoreType.DMA
    line = pltpu.VMEM((depth, row_count, features, line_size), bf16)
    grads = pltpu.VMEM((depth, dp, total, 2 * part), bf16)
    team = pltpu.VMEM((dp, 2, 2, part, columns), bf16)
    wide = pltpu.VMEM((dp, 2, 2, part, inner), bf16)
    query_weight, key_weight, value_weight, gate_weight, up_weight = weights
    return pl.pallas_call(
        functools.partial(finish_kernel, dp, depth, rows),
        out_shape=(
            jax.ShapeDtypeStruct((size, width), f32),
            jax.ShapeDtypeStruct(query_weight.shape, f32),
            jax.ShapeDtypeStruct(key_weight.shape, f32),
            jax.ShapeDtypeStruct(value_weight.shape, f32),
            jax.ShapeDtypeStruct(gate_weight.shape, f32),
            jax.ShapeDtypeStruct(up_weight.shape, f32),
            jax.ShapeDtypeStruct((1, part), f32),
            jax.ShapeDtypeStruct((1, part), f32),
        ),
        in_specs=[vmem] * 12 + [hbm] * 5,
        out_specs=(vmem,) * 8,
        scratch_shapes=[
            pltpu.VMEM((dp, 2, size, width), bf16),
            pltpu.VMEM((dp, depth, 2, part, columns), bf16),
            line,
            line,
            line,
            line,
            line,
            pltpu.VMEM((dp, 2, size, columns), bf16),
            pltpu.VMEM((total, 2 * dp * size), bf16),
            pltpu.VMEM((row_count, features, line_size), f32),
            grads,
            grads,
            team,
            team,
            wide,
            wide,
            dma((depth + 3,)),
            dma,
            dma,
            dma((depth,)),
            dma((depth,)),
            dma((depth, 2)),
            dma((depth, 2)),
            dma((dp, 2, 2)),
            dma((dp, 2, 2)),
            dma((dp, 2)),
            dma((dp, 2)),
            pltpu.VMEM((dp, 2, features, width), bf16),
            pltpu.VMEM((dp, 2, features, size), bf16),
            pltpu.VMEM((dp, 2, features, size), bf16),
            dma((dp,)),
            dma((dp,)),
            dma((dp,)),
            dma((dp, 2)),
            dma((dp, 2)),
        ]
        + sum_scratch(dp, size, width),
        compiler_params=pltpu.CompilerParams(
            collective_id=3, has_side_effects=True, vmem_limit_bytes=60 * 1024 * 1024
        ),
        cost_estimate=pl.CostEstimate(flops=10**11, bytes_accessed=1024, transcendentals=0),
        name="finish",
    )(
        grad_queries,
        cosine_pair,
        sine_pair,
        wide_sum,
        own,
        grad_middle,
        gain,
        *weights,
        grad_keys,
        grad_values,
        normed,
        weight,
        pair_weights,
    )


def split_layer(dp, depth):
    def layer(
        hidden_in,
        segment_ids,
        positions,
        attn_gain,
        query_weight,
        key_weight,
        value_weight,
        out_weight,
        mlp_gain,
        gate_weight,
        up_weight,
        down_weight,
        cotangent,
    ):
        f32, bf16 = jnp.float32, jnp.bfloat16
        rows, length, width = hidden_in.shape
        own = rows * length
        team = 2 * dp
        tokens = team * own
        part = query_weight.shape[0]
        hidden_rows = down_weight.shape[0]
        inner = depth * hidden_rows
        heads = depth
        row_count, size = dp * rows, 2 * length
        core = lax.axis_index("core")
        place = lax.axis_index("z")

        def dot(left, right):
            return jnp.dot(left, right, preferred_element_type=f32)

        weight_attn, places, near, weight_out = open_layer(
            dp, depth, query_weight, key_weight, value_weight, attn_gain, mlp_gain, positions,
            hidden_in, out_weight,
        )
        weight_out = weight_out.reshape(heads * HD, width)
        weight_down = lax.all_gather(down_weight, "z", axis=0, tiled=True)

        x_own = hidden_in.reshape(own, width)
        cot_own = cotangent.reshape(own, width)
        freqs = 10000.0 ** (-jnp.arange(0, HD // 2, dtype=f32) * 2.0 / HD)
        queries, normed1, cosine, sine, cosine_pair, sine_pair, offsets, gains, pair_weight, lines, wide_mine = (
            project(near, places, freqs, gate_weight, up_weight, weight_attn)
        )
        wide_got = lax.all_gather(wide_mine, "z", axis=0)
        cotangent, queries = lax.optimization_barrier((cotangent, queries))
        cots = plane_pieces(cotangent, dp)
        cots = [piece.reshape(own, width) for piece in cots]
        low_block = (place * size - places[:, 0, :, 0].reshape(row_count)) // size
        low_block = jnp.maximum(low_block, 0).astype(jnp.int32)
        place_one = place.astype(jnp.int32).reshape(1)
        context, logs = attend(
            low_block, place_one, offsets, queries, lines
        )

        context, cots = lax.optimization_barrier((context, cots))
        middle, normed2 = attend_sum(dp, context, weight_out, hidden_in, gains)
        all_normed2, all_cots, hidden, slope, active, grad_down = mlp_forward(
            normed2, wide_got, cots
        )
        grad_normed2, mlp_parts, grad_wide, pair_weights = mlp_backward(
            all_normed2, all_cots, hidden, slope, active, wide_got, weight_down, pair_weight
        )
        def line_sum(array):
            return lax.psum_scatter(array.astype(bf16), "z", scatter_dimension=0, tiled=True)

        down_sum = line_sum(grad_down)
        grad_wide, down_sum = lax.optimization_barrier((grad_wide, down_sum))
        wide_sum = line_sum(grad_wide)[0]
        grad_normed2, down_sum = lax.optimization_barrier((grad_normed2, down_sum))
        grad_middle, grad_context, grad_wout = middle_back(
            dp, rows, grad_normed2, middle, cot_own, gains, context, weight_out
        )
        grad_down = down_sum.astype(f32)
        mlp_parts, grad_context = lax.optimization_barrier((mlp_parts, grad_context))
        mlp_got = [swap(mlp_parts[k], "dp", dp, k) for k in range(1, dp)]
        grad_queries, grad_keys, grad_values = attend_back(
            low_block,
            place_one,
            offsets,
            queries,
            lines,
            context,
            logs,
            grad_context,
            cosine,
            sine,
        )
        out_hidden = middle + mlp_parts[0].astype(f32)
        for got in mlp_got:
            out_hidden = out_hidden + got.astype(f32)
        out_hidden = out_hidden.astype(bf16)
        grad_queries, out_hidden, grad_wout = lax.optimization_barrier(
            (grad_queries, out_hidden, grad_wout)
        )
        out_sum = line_sum(grad_wout)
        (
            grad_in,
            grad_wquery,
            grad_wkey,
            grad_wvalue,
            grad_wgate,
            grad_wup,
            attn_rows,
            mlp_rows,
        ) = finish(
            grad_queries,
            cosine_pair,
            sine_pair,
            wide_sum,
            hidden_in,
            grad_middle,
            gains,
            (query_weight, key_weight, value_weight, gate_weight, up_weight),
            grad_keys,
            grad_values,
            normed1,
            weight_attn,
            pair_weights,
        )
        out_sum, grad_in = lax.optimization_barrier((out_sum, grad_in))
        grad_wout = out_sum.astype(f32)
        grad_gain_one = attn_rows[0] / attn_gain.astype(f32)
        grad_gain_two = mlp_rows[0] / mlp_gain.astype(f32)
        return (
            out_hidden.reshape(rows, length, width),
            grad_in.reshape(rows, length, width),
            grad_gain_one,
            grad_wquery,
            grad_wkey,
            grad_wvalue,
            grad_wout,
            grad_gain_two,
            grad_wgate,
            grad_wup,
            grad_down,
        )

    return layer


def solution(mesh):
    dp, seq = mesh.shape["dp"], mesh.shape["seq"]
    if dp != KVH or seq % 2 or HQ != dp * seq:
        return gathered_weights(mesh)
    depth = seq // 2
    mesh = Mesh(mesh.devices.reshape(dp, depth, 2), ("dp", "z", "core"))
    every = ("dp", "z", "core")
    tokens = P("dp", ("z", "core"), None)
    matrix = P(every, None)
    return jax.shard_map(
        split_layer(dp, depth),
        mesh=mesh,
        in_specs=(
            tokens,
            P("dp", ("z", "core")),
            P("dp", ("z", "core")),
            P(every),
            matrix,
            matrix,
            matrix,
            matrix,
            P(every),
            matrix,
            matrix,
            matrix,
            tokens,
        ),
        out_specs=(
            tokens,
            tokens,
            P(every),
            matrix,
            matrix,
            matrix,
            matrix,
            P(every),
            matrix,
            matrix,
            matrix,
        ),
        check_vma=False,
    )
```

```python
import functools

import jax
import jax.numpy as jnp
from jax import lax
from jax.experimental import pallas as pl
from jax.experimental.pallas import tpu as pltpu
from jax.sharding import Mesh
from jax.sharding import PartitionSpec as P

HQ = 32
HD = 64
KVH = 4


EPSILON = 1e-05


def fetch_attention(attn_gain, query_weight, key_weight, value_weight, out_weight):
    return (
        lax.all_gather(attn_gain, ("dp", "seq"), axis=0, tiled=True),
        lax.all_gather(query_weight, ("dp", "seq"), axis=0, tiled=True),
        lax.all_gather(key_weight, ("dp", "seq"), axis=0, tiled=True),
        lax.all_gather(value_weight, ("dp", "seq"), axis=0, tiled=True),
        lax.all_gather(out_weight, ("dp", "seq"), axis=0, tiled=True),
    )


def fetch_mlp(mlp_gain, gate_weight, up_weight, down_weight):
    return (
        lax.all_gather(mlp_gain, ("dp", "seq"), axis=0, tiled=True),
        lax.all_gather(gate_weight, ("dp", "seq"), axis=0, tiled=True),
        lax.all_gather(up_weight, ("dp", "seq"), axis=0, tiled=True),
        lax.all_gather(down_weight, ("dp", "seq"), axis=0, tiled=True),
    )


def angles_of(positions):
    freqs = 10000.0 ** (-jnp.arange(0, HD // 2, dtype=jnp.float32) * 2.0 / HD)
    return positions.astype(jnp.float32)[:, None] * freqs[None, :]


def rotate(vectors, cosine, sine):
    half = vectors.shape[-1] // 2
    first = vectors[..., :half]
    second = vectors[..., half:]
    cosine = cosine[:, None, :]
    sine = sine[:, None, :]
    return jnp.concatenate(
        [first * cosine - second * sine, second * cosine + first * sine], axis=-1
    )


def norm_forward(values, gain):
    factor = lax.rsqrt(jnp.mean(values * values, axis=-1, keepdims=True) + EPSILON)
    return (values * factor * gain.astype(jnp.float32), factor)


def norm_backward(values, factor, gain, grad_normed):
    inner = grad_normed * gain.astype(jnp.float32)
    grad_gain = jnp.sum(grad_normed * values * factor, axis=0)
    grad_values = factor * inner - factor * factor * factor * values * jnp.mean(
        inner * values, axis=-1, keepdims=True
    )
    return (grad_values, grad_gain)


def masked_scores(queries_rot, keys_heads, query_pos, query_seg, seg_all):
    scores = jnp.einsum(
        "cgjd,kgd->gjck", queries_rot, keys_heads, preferred_element_type=jnp.float32
    ) * HD ** (-0.5)
    key_pos = jnp.arange(keys_heads.shape[0])
    allowed = (key_pos[None, :] <= query_pos[:, None]) & (seg_all[None, :] == query_seg[:, None])
    return jnp.where(allowed, scores, -1e30)


def add_up(total, extra):
    if total is None:
        return extra
    return jax.tree.map(jnp.add, total, extra)


def gathered_weights_layer(
    hidden_in,
    segment_ids,
    positions,
    attn_gain,
    query_weight,
    key_weight,
    value_weight,
    out_weight,
    mlp_gain,
    gate_weight,
    up_weight,
    down_weight,
    cotangent,
):
    batches, local_len, width = hidden_in.shape
    group = HQ // KVH
    query_pos = lax.axis_index("seq") * local_len + jnp.arange(local_len)
    outputs = []
    grads_in = []
    attn_total = None
    mlp_total = None
    for microbatch in range(batches):
        rows_in = hidden_in[microbatch].astype(jnp.float32)
        seg_own = segment_ids[microbatch]
        angles = angles_of(positions[microbatch])
        cosine = jnp.cos(angles)
        sine = jnp.sin(angles)
        attn_set = fetch_attention(attn_gain, query_weight, key_weight, value_weight, out_weight)
        gain_one, weight_query, weight_key, weight_value, weight_out = attn_set
        normed1, factor1 = norm_forward(rows_in, gain_one)
        normed1_low = normed1.astype(jnp.bfloat16)
        queries = jnp.dot(normed1_low, weight_query, preferred_element_type=jnp.float32).reshape(
            local_len, HQ, HD
        )
        keys_own = jnp.dot(normed1_low, weight_key, preferred_element_type=jnp.float32).reshape(
            local_len, KVH, HD
        )
        values_own = jnp.dot(normed1_low, weight_value, preferred_element_type=jnp.float32).astype(
            jnp.bfloat16
        )
        queries_rot = (
            rotate(queries, cosine, sine).astype(jnp.bfloat16).reshape(local_len, KVH, group, HD)
        )
        keys_rot = rotate(keys_own, cosine, sine).astype(jnp.bfloat16).reshape(local_len, KVH * HD)
        keys_all, values_all, seg_all = (
            lax.all_gather(keys_rot, "seq", axis=0, tiled=True),
            lax.all_gather(values_own, "seq", axis=0, tiled=True),
            lax.all_gather(seg_own, "seq", axis=0, tiled=True),
        )
        keys_heads = keys_all.reshape(-1, KVH, HD)
        values_heads = values_all.reshape(-1, KVH, HD)
        scores = masked_scores(queries_rot, keys_heads, query_pos, seg_own, seg_all)
        highest = jnp.max(scores, axis=-1, keepdims=True)
        powers = jnp.exp(scores - highest)
        totals = jnp.sum(powers, axis=-1, keepdims=True)
        logsum = highest + jnp.log(totals)
        probs_low = (powers / totals).astype(jnp.bfloat16)
        context = jnp.einsum(
            "gjck,kgd->cgjd", probs_low, values_heads, preferred_element_type=jnp.float32
        )
        context_low = context.reshape(local_len, HQ * HD).astype(jnp.bfloat16)
        middle = rows_in + jnp.dot(context_low, weight_out, preferred_element_type=jnp.float32)
        mlp_set = fetch_mlp(mlp_gain, gate_weight, up_weight, down_weight)
        gain_two, weight_gate, weight_up, weight_down = mlp_set
        normed2, factor2 = norm_forward(middle, gain_two)
        normed2_low = normed2.astype(jnp.bfloat16)
        gate = jnp.dot(normed2_low, weight_gate, preferred_element_type=jnp.float32)
        up = jnp.dot(normed2_low, weight_up, preferred_element_type=jnp.float32)
        sigma = jax.nn.sigmoid(gate)
        activation = gate * sigma
        hidden = (activation * up).astype(jnp.bfloat16)
        mlp_out = jnp.dot(hidden, weight_down, preferred_element_type=jnp.float32)
        outputs.append((middle + mlp_out).astype(jnp.bfloat16))
        grad_low = cotangent[microbatch]
        grad_out = grad_low.astype(jnp.float32)
        mlp_back = fetch_mlp(mlp_gain, gate_weight, up_weight, down_weight)
        gain_two, weight_gate, weight_up, weight_down = mlp_back
        grad_down = jnp.dot(hidden.T, grad_low, preferred_element_type=jnp.float32)
        grad_hid = jnp.dot(grad_low, weight_down.T, preferred_element_type=jnp.float32)
        grad_gate = (grad_hid * up * sigma * (1.0 + gate * (1.0 - sigma))).astype(jnp.bfloat16)
        grad_up = (grad_hid * activation).astype(jnp.bfloat16)
        grad_wgate = jnp.dot(normed2_low.T, grad_gate, preferred_element_type=jnp.float32)
        grad_wup = jnp.dot(normed2_low.T, grad_up, preferred_element_type=jnp.float32)
        grad_normed2 = jnp.dot(
            grad_gate, weight_gate.T, preferred_element_type=jnp.float32
        ) + jnp.dot(grad_up, weight_up.T, preferred_element_type=jnp.float32)
        grad_mid_norm, grad_gain_two = norm_backward(middle, factor2, gain_two, grad_normed2)
        grad_middle = grad_out + grad_mid_norm
        attn_back = fetch_attention(attn_gain, query_weight, key_weight, value_weight, out_weight)
        gain_one, weight_query, weight_key, weight_value, weight_out = attn_back
        grad_attn = grad_middle.astype(jnp.bfloat16)
        grad_wout = jnp.dot(context_low.T, grad_attn, preferred_element_type=jnp.float32)
        grad_context = (
            jnp.dot(grad_attn, weight_out.T, preferred_element_type=jnp.float32)
            .astype(jnp.bfloat16)
            .reshape(local_len, KVH, group, HD)
        )
        probs = jnp.exp(
            masked_scores(queries_rot, keys_heads, query_pos, seg_own, seg_all) - logsum
        )
        grad_probs = jnp.einsum(
            "cgjd,kgd->gjck", grad_context, values_heads, preferred_element_type=jnp.float32
        )
        inner = jnp.sum(probs * grad_probs, axis=-1, keepdims=True)
        grad_scores = (probs * (grad_probs - inner)).astype(jnp.bfloat16)
        grad_qrot = jnp.einsum(
            "gjck,kgd->cgjd", grad_scores, keys_heads, preferred_element_type=jnp.float32
        ) * HD ** (-0.5)
        grad_krot_all = jnp.einsum(
            "gjck,cgjd->kgd", grad_scores, queries_rot, preferred_element_type=jnp.float32
        ) * HD ** (-0.5)
        grad_vall = jnp.einsum(
            "gjck,cgjd->kgd", probs_low, grad_context, preferred_element_type=jnp.float32
        )
        row_len = keys_heads.shape[0]
        grad_key_own, grad_value_own = (
            lax.psum_scatter(
                grad_krot_all.reshape(row_len, KVH * HD).astype(jnp.bfloat16),
                "seq",
                scatter_dimension=0,
                tiled=True,
            ).astype(jnp.float32),
            lax.psum_scatter(
                grad_vall.reshape(row_len, KVH * HD).astype(jnp.bfloat16),
                "seq",
                scatter_dimension=0,
                tiled=True,
            ).astype(jnp.float32),
        )
        grad_keys = (
            rotate(grad_key_own.reshape(local_len, KVH, HD), cosine, -sine)
            .astype(jnp.bfloat16)
            .reshape(local_len, KVH * HD)
        )
        grad_values = grad_value_own.astype(jnp.bfloat16)
        grad_queries = (
            rotate(grad_qrot.reshape(local_len, HQ, HD), cosine, -sine)
            .astype(jnp.bfloat16)
            .reshape(local_len, HQ * HD)
        )
        grad_wquery = jnp.dot(normed1_low.T, grad_queries, preferred_element_type=jnp.float32)
        grad_wkey = jnp.dot(normed1_low.T, grad_keys, preferred_element_type=jnp.float32)
        grad_wvalue = jnp.dot(normed1_low.T, grad_values, preferred_element_type=jnp.float32)
        grad_normed1 = jnp.dot(grad_queries, weight_query.T, preferred_element_type=jnp.float32)
        grad_normed1 = grad_normed1 + jnp.dot(
            grad_keys, weight_key.T, preferred_element_type=jnp.float32
        )
        grad_normed1 = grad_normed1 + jnp.dot(
            grad_values, weight_value.T, preferred_element_type=jnp.float32
        )
        grad_rows_norm, grad_gain_one = norm_backward(rows_in, factor1, gain_one, grad_normed1)
        grads_in.append(grad_middle + grad_rows_norm)
        attn_terms = (grad_gain_one, grad_wquery, grad_wkey, grad_wvalue, grad_wout)
        mlp_terms = (grad_gain_two, grad_wgate, grad_wup, grad_down)
        attn_shares = (
            lax.psum_scatter(attn_terms[0], ("dp", "seq"), scatter_dimension=0, tiled=True),
            lax.psum_scatter(attn_terms[1], ("dp", "seq"), scatter_dimension=0, tiled=True),
            lax.psum_scatter(attn_terms[2], ("dp", "seq"), scatter_dimension=0, tiled=True),
            lax.psum_scatter(attn_terms[3], ("dp", "seq"), scatter_dimension=0, tiled=True),
            lax.psum_scatter(attn_terms[4], ("dp", "seq"), scatter_dimension=0, tiled=True),
        )
        mlp_shares = (
            lax.psum_scatter(mlp_terms[0], ("dp", "seq"), scatter_dimension=0, tiled=True),
            lax.psum_scatter(mlp_terms[1], ("dp", "seq"), scatter_dimension=0, tiled=True),
            lax.psum_scatter(mlp_terms[2], ("dp", "seq"), scatter_dimension=0, tiled=True),
            lax.psum_scatter(mlp_terms[3], ("dp", "seq"), scatter_dimension=0, tiled=True),
        )
        attn_total = add_up(attn_total, attn_shares)
        mlp_total = add_up(mlp_total, mlp_shares)
    return (
        jnp.stack(outputs),
        jnp.stack(grads_in),
        attn_total[0],
        attn_total[1],
        attn_total[2],
        attn_total[3],
        attn_total[4],
        mlp_total[0],
        mlp_total[1],
        mlp_total[2],
        mlp_total[3],
    )


def gathered_weights(mesh):
    return jax.shard_map(
        gathered_weights_layer,
        mesh=mesh,
        in_specs=(
            P("dp", "seq", None),
            P("dp", "seq"),
            P("dp", "seq"),
            P(("dp", "seq")),
            P(("dp", "seq"), None),
            P(("dp", "seq"), None),
            P(("dp", "seq"), None),
            P(("dp", "seq"), None),
            P(("dp", "seq")),
            P(("dp", "seq"), None),
            P(("dp", "seq"), None),
            P(("dp", "seq"), None),
            P("dp", "seq", None),
        ),
        out_specs=(
            P("dp", "seq", None),
            P("dp", "seq", None),
            P(("dp", "seq")),
            P(("dp", "seq"), None),
            P(("dp", "seq"), None),
            P(("dp", "seq"), None),
            P(("dp", "seq"), None),
            P(("dp", "seq")),
            P(("dp", "seq"), None),
            P(("dp", "seq"), None),
            P(("dp", "seq"), None),
        ),
        check_vma=False,
    )


def swap(values, axis_name, size, step):
    return lax.ppermute(values, axis_name, [(i, i ^ step) for i in range(size)])


def plane_pieces(values, dp):
    return [values] + [swap(values, "dp", dp, k) for k in range(1, dp)]


NEGATIVE = -1e30
VMEM_LIMIT = 56 * 1024 * 1024
MESH = pl.DeviceIdType.MESH
LIGHT = pl.CostEstimate(flops=0, bytes_accessed=1024, transcendentals=0)


def contract_last(left, right):
    return lax.dot_general(
        left, right, (((1,), (1,)), ((), ())), preferred_element_type=jnp.float32
    )


def multiply(left, right):
    return jnp.dot(left, right, preferred_element_type=jnp.float32)


def spread_keys(block, heads):
    half = block.shape[0] // 2
    return jnp.concatenate([block[:half]] * heads + [block[half:]] * heads, axis=0)


def fold_keys(block, heads):
    half = block.shape[0] // (2 * heads)
    first = sum(block[h * half : (h + 1) * half] for h in range(heads))
    rest = range(heads, 2 * heads)
    return jnp.concatenate([first, sum(block[h * half : (h + 1) * half] for h in rest)], axis=0)


def fold_values(block, heads):
    size = block.shape[0] // heads
    return sum(block[h * size : (h + 1) * size] for h in range(heads))


def turned_head(shape, dim, heads):
    index = lax.broadcasted_iota(jnp.int32, shape, dim)
    return lax.rem(index, shape[dim] // 2) // (shape[dim] // 2 // heads)


def plain_head(shape, dim, heads):
    index = lax.broadcasted_iota(jnp.int32, shape, dim)
    return index // (shape[dim] // heads)


def per_head(values, owner, heads, axis):
    zero = jnp.zeros_like(values)
    return jnp.concatenate([jnp.where(owner == h, values, zero) for h in range(heads)], axis=axis)


def join_heads(stacked, owner, heads):
    size = stacked.shape[0] // heads
    return sum(
        jnp.where(owner == h, stacked[h * size : (h + 1) * size], 0.0) for h in range(heads)
    )


def masked(scores, block, start, order_q, heads):
    size = order_q.shape[0]
    order_k = block * size + lax.broadcasted_iota(jnp.int32, (size, size), 1)
    allowed = (order_k >= start) & (order_k <= order_q)
    split = scores.reshape(heads, size, size)
    return jnp.where(allowed[None], split, NEGATIVE).reshape(scores.shape)


def attend_kernel(heads, low_ref, place_ref, offset_ref, q_ref, k_ref, v_ref, out_ref, log_ref, held):
    row = pl.program_id(0)
    place = place_ref[0]
    queries = q_ref[0]
    size = queries.shape[0]
    stacked = per_head(queries, turned_head(queries.shape, 1, heads), heads, 0)
    order_q = place * size + lax.broadcasted_iota(jnp.int32, (size, 1), 0)
    start = order_q - offset_ref[0][:, :1]

    def score(block, highest):
        scores = multiply(stacked, spread_keys(k_ref[block, 0], heads))
        scores = masked(scores, block, start, order_q, heads)
        held[block] = scores
        return jnp.maximum(highest, jnp.max(scores, axis=1, keepdims=True))

    highest = lax.fori_loop(
        low_ref[row], place + 1, score, jnp.full((heads * size, 1), NEGATIVE, jnp.float32)
    )

    def mix(block, carry):
        total, context = carry
        powers = jnp.exp(held[block] - highest)
        total = total + jnp.sum(powers, axis=1, keepdims=True)
        spread = jnp.concatenate([v_ref[block, 0]] * heads, axis=0)
        return total, context + contract_last(powers.astype(jnp.bfloat16), spread)

    total, context = lax.fori_loop(
        low_ref[row],
        place + 1,
        mix,
        (
            jnp.zeros((heads * size, 1), jnp.float32),
            jnp.zeros((heads * size, queries.shape[1]), jnp.float32),
        ),
    )
    owner = plain_head(queries.shape, 1, heads)
    out_ref[0] = join_heads(context / total, owner, heads).astype(jnp.bfloat16)
    log_ref[0] = highest + jnp.log(total)


def attend_back_kernel(
    heads,
    low_ref,
    place_ref,
    offset_ref,
    q_ref,
    k_ref,
    v_ref,
    context_ref,
    log_ref,
    grad_ref,
    cosine_ref,
    sine_ref,
    grad_q_ref,
    grad_k_ref,
    grad_v_ref,
):
    row = pl.program_id(0)
    place = place_ref[0]
    queries = q_ref[0]
    grads = grad_ref[0]
    size = queries.shape[0]
    turned = turned_head(queries.shape, 1, heads)
    plain = plain_head(queries.shape, 1, heads)
    stacked = per_head(queries, turned, heads, 0)
    stacked_grad = per_head(grads, plain, heads, 0)
    flipped = per_head(queries.T, turned_head(queries.shape, 0, heads), heads, 1)
    flipped_grad = per_head(grads.T, plain_head(queries.shape, 0, heads), heads, 1)
    product = grads.astype(jnp.float32) * context_ref[0].astype(jnp.float32)
    inner = jnp.sum(per_head(product, plain, heads, 0), axis=1, keepdims=True)
    logs = log_ref[0]
    order_q = place * size + lax.broadcasted_iota(jnp.int32, (size, 1), 0)
    start = order_q - offset_ref[0][:, :1]
    grad_k_ref[...] = jnp.zeros_like(grad_k_ref)
    grad_v_ref[...] = jnp.zeros_like(grad_v_ref)

    def step(block, grad_q):
        keys = spread_keys(k_ref[block, 0], heads)
        spread = jnp.concatenate([v_ref[block, 0]] * heads, axis=0)
        scores = masked(multiply(stacked, keys), block, start, order_q, heads)
        probs = jnp.exp(scores - logs)
        grad_probs = multiply(stacked_grad, spread)
        grad_scores = (probs * (grad_probs - inner)).astype(jnp.bfloat16)
        grad_k = fold_keys(multiply(flipped, grad_scores), heads)
        grad_v = fold_values(multiply(flipped_grad, probs.astype(jnp.bfloat16)), heads)
        grad_k_ref[block, 0] = grad_k.astype(jnp.bfloat16)
        grad_v_ref[block, 0] = grad_v.astype(jnp.bfloat16)
        return grad_q + contract_last(grad_scores, keys)

    grad_q = lax.fori_loop(
        low_ref[row],
        place + 1,
        step,
        jnp.zeros((heads * size, queries.shape[1]), jnp.float32),
    )
    grad_q = join_heads(grad_q, turned, heads) * HD ** (-0.5)
    half = grad_q.shape[1] // 2
    first, second = grad_q[:, :half], grad_q[:, half:]
    cosine, sine = cosine_ref[0], sine_ref[0]
    grad_q_ref[0, :, :half] = (first * cosine + second * sine).astype(jnp.bfloat16)
    grad_q_ref[0, :, half:] = (second * cosine - first * sine).astype(jnp.bfloat16)


def row_spec(*shape):
    return pl.BlockSpec((1,) + shape, lambda row, low, place: (row,) + (0,) * len(shape))


def line_spec(depth, *shape):
    return pl.BlockSpec((depth, 1) + shape, lambda row, low, place: (0, row) + (0,) * len(shape))


def pair_spec(which, depth, *shape):
    return pl.BlockSpec(
        (None, depth, 1) + shape, lambda row, low, place: (which, 0, row) + (0,) * len(shape)
    )


def attend(low, place, offsets, queries, lines):
    rows, size, width = queries.shape
    depth, features = lines.shape[1], lines.shape[3]
    heads = width // features
    return pl.pallas_call(
        functools.partial(attend_kernel, heads),
        out_shape=(
            jax.ShapeDtypeStruct((rows, size, width), jnp.bfloat16),
            jax.ShapeDtypeStruct((rows, heads * size, 1), jnp.float32),
        ),
        grid_spec=pltpu.PrefetchScalarGridSpec(
            num_scalar_prefetch=2,
            grid=(rows,),
            in_specs=[
                row_spec(size, offsets.shape[2]),
                row_spec(size, width),
                pair_spec(0, depth, features, size),
                pair_spec(1, depth, features, size),
            ],
            out_specs=[row_spec(size, width), row_spec(heads * size, 1)],
            scratch_shapes=[pltpu.VMEM((depth, heads * size, size), jnp.float32)],
        ),
        compiler_params=pltpu.CompilerParams(vmem_limit_bytes=VMEM_LIMIT),
        cost_estimate=LIGHT,
        name="attend",
    )(low, place, offsets, queries, lines, lines)


def attend_back(low, place, offsets, queries, lines, context, logs, grads, cosine, sine):
    rows, size, width = queries.shape
    depth, features = lines.shape[1], lines.shape[3]
    heads = width // features
    line = line_spec(depth, features, size)
    whole = row_spec(size, width)
    half = row_spec(size, width // 2)
    return pl.pallas_call(
        functools.partial(attend_back_kernel, heads),
        out_shape=(
            jax.ShapeDtypeStruct((rows, size, width), jnp.bfloat16),
            jax.ShapeDtypeStruct(lines.shape[1:], jnp.bfloat16),
            jax.ShapeDtypeStruct(lines.shape[1:], jnp.bfloat16),
        ),
        grid_spec=pltpu.PrefetchScalarGridSpec(
            num_scalar_prefetch=2,
            grid=(rows,),
            in_specs=[
                row_spec(size, offsets.shape[2]),
                whole,
                pair_spec(0, depth, features, size),
                pair_spec(1, depth, features, size),
                whole,
                row_spec(heads * size, 1),
                whole,
                half,
                half,
            ],
            out_specs=[whole, line, line],
        ),
        compiler_params=pltpu.CompilerParams(vmem_limit_bytes=VMEM_LIMIT),
        cost_estimate=LIGHT,
        name="attend_back",
    )(low, place, offsets, queries, lines, lines, context, logs, grads, cosine, sine)


def team_places():
    data = lax.axis_index("dp")
    place = lax.axis_index("z")
    core = lax.axis_index("core")

    def peer(k):
        high = lax.rem(data // 2 + k // 2, 2)
        low = lax.rem(lax.rem(data, 2) + lax.rem(k, 2), 2)
        return (high * 2 + low, place, core)

    return data, place, core, peer, (data, place, 1 - core)


def line_neighbours(depth):
    data, place, core, _, _ = team_places()
    return [(data, lax.rem(place + step, depth), core) for step in (1, depth - 1)]


def greet(targets):
    barrier = pltpu.get_barrier_semaphore()
    for target in targets:
        pl.semaphore_signal(barrier, inc=1, device_id=target, device_id_type=MESH)
    pl.semaphore_wait(barrier, len(targets))


def send(source, target, send_sem, got_sem, device):
    return pltpu.make_async_remote_copy(
        src_ref=source,
        dst_ref=target,
        send_sem=send_sem,
        recv_sem=got_sem,
        device_id=device,
        device_id_type=MESH,
    )


def line_gather(depth, block_of, send_sem, got_sem):
    data, place, core, _, twin = team_places()

    def copy(z, step):
        device = (data, lax.rem(place + depth + step, depth), core)
        block = block_of(z)
        return send(block, block, send_sem.at[z, (1 - step) // 2], got_sem.at[z], device)

    def arrival(z):
        block = block_of(z)
        return send(block, block, send_sem.at[z, 0], got_sem.at[z], twin)

    def start():
        @pl.when(place < depth - 1)
        def _():
            copy(place, 1).start()

        @pl.when(place > 0)
        def _():
            copy(place, -1).start()

    def relay(distance):
        @pl.when(place >= distance)
        def _():
            arrival(place - distance).wait_recv()

            @pl.when(place < depth - 1)
            def _():
                copy(place - distance, 1).start()

        @pl.when(place + distance < depth)
        def _():
            arrival(place + distance).wait_recv()

            @pl.when(place > 0)
            def _():
                copy(place + distance, -1).start()

    def finish():
        for z in range(depth):

            @pl.when((z <= place) & (place < depth - 1))
            def _(z=z):
                copy(z, 1).wait_send()

            @pl.when((z >= place) & (place > 0))
            def _(z=z):
                copy(z, -1).wait_send()

    return start, relay, finish


def sum_scratch(dp, size, width):
    dma = pltpu.SemaphoreType.DMA
    block = pltpu.VMEM((dp, size, width), jnp.bfloat16)
    return [
        block,
        block,
        pltpu.VMEM((2, size // 2, width), jnp.bfloat16),
        pltpu.VMEM((2, size, width), jnp.bfloat16),
        dma((dp,)),
        dma((dp,)),
        dma((2,)),
        dma((2,)),
        dma((2, 2)),
        dma((2, 2)),
    ]


def plane_sum(dp, product, total_ref, scratch):
    side, got, relay, far, side_send, side_got, relay_send, relay_got, far_send, far_got = scratch
    f32, bf16 = jnp.float32, jnp.bfloat16
    _, _, core, peer, twin = team_places()
    size = side.shape[1]
    half = size // 2

    def rows(part):
        return pl.ds(part * half, half)

    def side_copy(k):
        return send(side.at[k], got.at[k], side_send.at[k], side_got.at[k], twin)

    def relay_copy(part):
        return send(
            got.at[3, rows(part)],
            relay.at[part],
            relay_send.at[part],
            relay_got.at[part],
            peer(1 + part),
        )

    def far_copy(which, part):
        return send(
            got.at[1 + which, rows(part)],
            far.at[which, rows(part)],
            far_send.at[which, part],
            far_got.at[which, part],
            peer(1 + which),
        )

    def one(step, carry):
        k = dp - 1 - step
        side[k] = product(k, 1 - core, 0).astype(bf16)
        side_copy(k).start()
        total = product(k, core, 1)
        side_copy(k).wait_recv()
        total = total + got[k].astype(f32)

        @pl.when(k == 0)
        def _():
            total_ref[...] = total

        @pl.when(k > 0)
        def _():
            got[k] = total.astype(bf16)

        @pl.when(k == 3)
        def _():
            relay_copy(0).start()
            relay_copy(1).start()

        @pl.when(k == 2)
        def _():
            far_copy(1, 1).start()

        @pl.when(k == 1)
        def _():
            far_copy(0, 0).start()

        return carry

    lax.fori_loop(0, dp, one, 0)
    for part in range(2):
        which = 1 - part
        relay_copy(part).wait_recv()
        total = got[1 + which, rows(part)].astype(f32) + relay[part].astype(f32)
        got[1 + which, rows(part)] = total.astype(bf16)
        far_copy(which, part).start()

    def complete():
        for which, part in ((0, 0), (1, 1), (0, 1), (1, 0)):
            far_copy(which, part).wait_recv()
            total_ref[rows(part)] += far[which, rows(part)].astype(f32)
        for part in range(2):
            relay_copy(part).wait_send()
            for which in range(2):
                far_copy(which, part).wait_send()
        for k in range(dp):
            side_copy(k).wait_send()

    return complete


def mlp_forward_kernel(dp, depth, x_hbm, wide_hbm, *refs):
    cot_hbms = refs[:dp]
    tokens_hbm, cots_hbm, hidden_hbm, slope_hbm, active_hbm, down_grad_hbm = refs[dp : dp + 6]
    (
        tokens,
        cots,
        wides,
        hidden_t,
        chunk,
        tile_out,
        load_sem,
        cots_sem,
        near_send,
        near_got,
        side_send,
        side_got,
        pass_send,
        pass_got,
        tokens_sem,
        chunk_sem,
        tile_sem,
        twin_send,
        twin_got,
    ) = refs[dp + 6 :]
    bf16 = jnp.bfloat16
    _, _, core, peer, twin = team_places()
    size, width = x_hbm.shape
    half = size // 2
    loads = [pltpu.make_async_copy(x_hbm, tokens.at[0, core], load_sem.at[0])]
    for z in range(depth):
        loads.append(pltpu.make_async_copy(wide_hbm.at[z], wides.at[:, z], load_sem.at[1 + z]))
    cot_loads = []
    for k in range(dp):
        sem = load_sem.at[depth + 1 + k]
        cot_loads.append(pltpu.make_async_copy(cot_hbms[k], cots.at[k, core], sem))
    for load in loads + cot_loads:
        load.start()
    greet([peer(k) for k in range(1, 3)] + [twin])
    loads[0].wait()

    def near_copy(k):
        return send(
            tokens.at[0, core], tokens.at[k, core], near_send.at[k], near_got.at[k], peer(k)
        )

    def pass_copy(part):
        spot = pl.ds(part * half, half)
        return send(
            tokens.at[1 + part, core, spot],
            tokens.at[3, core, spot],
            pass_send.at[part],
            pass_got.at[part],
            peer(2 - part),
        )

    def side_copy(k):
        block = tokens.at[k, core]
        return send(block, block, side_send.at[k], side_got.at[k], twin)

    def side_arrival(k):
        block = tokens.at[k, 1 - core]
        return send(block, block, side_send.at[k], side_got.at[k], twin)

    def twin_copy(k):
        block = cots.at[k, core]
        return send(block, block, twin_send.at[k], twin_got.at[k], twin)

    def twin_arrival(k):
        block = cots.at[k, 1 - core]
        return send(block, block, twin_send.at[k], twin_got.at[k], twin)

    def tokens_out(k, e):
        return pltpu.make_async_copy(tokens.at[k, e], tokens_hbm.at[k, e], tokens_sem.at[k, e])

    def chunk_out(k, e, slot):
        return [
            pltpu.make_async_copy(chunk.at[slot, i], target.at[k, e], chunk_sem.at[slot, i])
            for i, target in enumerate((hidden_hbm, slope_hbm, active_hbm))
        ]

    near_copy(1).start()
    near_copy(2).start()
    side_copy(0).start()
    for load in loads[1:]:
        load.wait()

    def process(k, e, slot, reuse):
        row = tokens[k, e]
        tokens_out(k, e).start()
        both = multiply(row, wides[...].reshape(width, -1))
        inner = both.shape[1] // 2
        gate, up = both[:, :inner], both[:, inner:]
        sigma = 1.0 / (1.0 + jnp.exp(-gate))
        active = gate * sigma
        hidden = (active * up).astype(bf16)
        if reuse:
            for copy in chunk_out(k, e, slot):
                copy.wait()
        chunk[slot, 0] = hidden
        chunk[slot, 1] = (up * sigma * (1.0 + gate * (1.0 - sigma))).astype(bf16)
        chunk[slot, 2] = active.astype(bf16)
        for copy in chunk_out(k, e, slot):
            copy.start()
        spot = pl.ds(pl.multiple_of((k * 2 + e) * size, size), size)
        hidden_t[:, spot] = hidden.T

    process(0, core, 0, False)
    side_arrival(0).wait_recv()
    process(0, 1 - core, 1, False)
    for k in range(dp):
        cot_loads[k].wait()
        twin_copy(k).start()
    for k in range(1, 3):
        near_copy(k).wait_recv()
        pass_copy(k - 1).start()
        side_copy(k).start()
    for k in range(dp):
        twin_arrival(k).wait_recv()
    cots_out = pltpu.make_async_copy(cots, cots_hbm, cots_sem)
    cots_out.start()

    def step(k, carry):
        @pl.when(k == 3)
        def _():
            pass_copy(0).wait_recv()
            pass_copy(1).wait_recv()
            side_copy(3).start()

        process(k, core, 0, True)
        side_arrival(k).wait_recv()
        process(k, 1 - core, 1, True)
        return carry

    lax.fori_loop(1, dp, step, 0)

    def tile_copy(j, slot):
        spot = pl.ds(pl.multiple_of(j * 256, 256), 256)
        return pltpu.make_async_copy(tile_out.at[slot], down_grad_hbm.at[:, spot], tile_sem.at[slot])

    count = width // 256

    def tile(j, carry):
        slot = lax.rem(j, 2)

        @pl.when(j > 1)
        def _():
            tile_copy(j - 2, slot).wait()

        spot = pl.ds(pl.multiple_of(j * 256, 256), 256)
        columns = cots[:, :, :, spot].reshape(-1, 256)
        tile_out[slot] = multiply(hidden_t[...], columns).astype(bf16)
        tile_copy(j, slot).start()
        return carry

    lax.fori_loop(0, count, tile, 0)
    for j in (count - 2, count - 1):
        tile_copy(j, j % 2).wait()
    cots_out.wait()
    for slot, e in ((0, core), (1, 1 - core)):
        for copy in chunk_out(dp - 1, e, slot):
            copy.wait()
    for k in range(dp):
        for e in range(2):
            tokens_out(k, e).wait()
        side_copy(k).wait_send()
        twin_copy(k).wait_send()
    for k in range(1, 3):
        near_copy(k).wait_send()
        pass_copy(k - 1).wait_send()


def mlp_forward(x_own, wide, cots):
    depth, dp = wide.shape[:2]
    size, width = x_own.shape
    inner = wide.shape[-1] // 2
    bf16 = jnp.bfloat16
    hbm = pl.BlockSpec(memory_space=pl.ANY)
    dma = pltpu.SemaphoreType.DMA
    weight = pltpu.VMEM((dp, depth) + wide.shape[2:], bf16)
    whole = jax.ShapeDtypeStruct((dp, 2, size, width), bf16)
    thin = jax.ShapeDtypeStruct((dp, 2, size, inner), bf16)
    return pl.pallas_call(
        functools.partial(mlp_forward_kernel, dp, depth),
        out_shape=(whole, whole, thin, thin, thin, jax.ShapeDtypeStruct((inner, width), bf16)),
        in_specs=[hbm] * (2 + dp),
        out_specs=(hbm,) * 6,
        scratch_shapes=[
            pltpu.VMEM((dp, 2, size, width), bf16),
            pltpu.VMEM((dp, 2, size, width), bf16),
            weight,
            pltpu.VMEM((inner, 2 * dp * size), bf16),
            pltpu.VMEM((2, 3, size, inner), bf16),
            pltpu.VMEM((2, inner, 256), bf16),
            dma((2 * depth + 1 + dp,)),
            dma,
            dma((dp,)),
            dma((dp,)),
            dma((dp,)),
            dma((dp,)),
            dma((2,)),
            dma((2,)),
            dma((dp, 2)),
            dma((2, 3)),
            dma((2,)),
            dma((dp,)),
            dma((dp,)),
        ],
        compiler_params=pltpu.CompilerParams(
            collective_id=1, has_side_effects=True, vmem_limit_bytes=VMEM_LIMIT
        ),
        cost_estimate=LIGHT,
        name="mlp_forward",
    )(x_own, wide, *cots)


def mlp_backward_kernel(
    dp,
    depth,
    tokens_hbm,
    cots_hbm,
    hidden_hbm,
    slope_hbm,
    active_hbm,
    wide_hbm,
    down_hbm,
    pair_hbm,
    grad_ref,
    part_hbm,
    wide_grad_hbm,
    pairs_hbm,
    tokens,
    wides,
    downs,
    wide_t,
    cot_slots,
    chunk,
    part_out,
    part_side,
    tile_out,
    load_sem,
    slot_sem,
    part_sem,
    part_send,
    part_got,
    tile_sem,
    pair_send,
    pair_got,
    pair_sem,
    *sum_refs,
):
    bf16 = jnp.bfloat16
    _, _, core, peer, twin = team_places()
    size, width = grad_ref.shape
    loads = [pltpu.make_async_copy(down_hbm, downs, load_sem.at[0])]
    for z in range(depth):
        loads.append(pltpu.make_async_copy(wide_hbm.at[z], wides.at[:, z], load_sem.at[1 + z]))
    tokens_load = pltpu.make_async_copy(tokens_hbm, tokens, load_sem.at[depth + 1])

    def slot_loads(k, e, slot):
        copies = [pltpu.make_async_copy(cots_hbm.at[k, e], cot_slots.at[slot], slot_sem.at[slot, 3])]
        for i, source in enumerate((hidden_hbm, slope_hbm, active_hbm)):
            copies.append(
                pltpu.make_async_copy(source.at[k, e], chunk.at[slot, i], slot_sem.at[slot, i])
            )
        return copies

    for copy in slot_loads(dp - 1, 1 - core, 0):
        copy.start()
    for load in loads:
        load.start()
    pair_local = pltpu.make_async_copy(pair_hbm, pairs_hbm.at[0], pair_sem)
    pair_local.start()
    greet([peer(k) for k in range(1, dp)] + [twin])

    def pair_copy(k):
        return send(pair_hbm, pairs_hbm.at[k], pair_send.at[k], pair_got.at[k], peer(k))

    for k in range(1, dp):
        pair_copy(k).start()
    for load in loads:
        load.wait()
    tokens_load.start()

    def part_copy(k):
        return pltpu.make_async_copy(part_out.at[1], part_hbm.at[k], part_sem)

    def part_side_copy(k):
        return send(part_out.at[0], part_side.at[k], part_send.at[k], part_got.at[k], twin)

    def product(k, e, turn):
        slot = turn
        for copy in slot_loads(k, e, slot):
            copy.wait()
        if turn == 0:
            for copy in slot_loads(k, core, 1):
                copy.start()
        else:

            @pl.when(k > 0)
            def _():
                for copy in slot_loads(k - 1, 1 - core, 0):
                    copy.start()

        grad_hid = contract_last(cot_slots[slot], downs[...])
        grad_gate = (grad_hid * chunk[slot, 1].astype(jnp.float32)).astype(bf16)
        grad_up = (grad_hid * chunk[slot, 2].astype(jnp.float32)).astype(bf16)
        spot = pl.ds(pl.multiple_of((k * 2 + e) * size, size), size)
        inner = grad_gate.shape[1]
        wide_t[:inner, spot] = grad_gate.T
        wide_t[inner:, spot] = grad_up.T
        terms = multiply(chunk[slot, 0], downs[...])
        if turn == 0:

            @pl.when(k < dp - 1)
            def _():
                part_side_copy(k + 1).wait_send()

            part_out[0] = terms.astype(bf16)
            part_side_copy(k).start()
        else:

            @pl.when(k < dp - 1)
            def _():
                part_copy(k + 1).wait()

            part_side_copy(k).wait_recv()
            part_out[1] = (terms + part_side[k].astype(jnp.float32)).astype(bf16)
            part_copy(k).start()
        both = jnp.concatenate([grad_gate, grad_up], axis=1)
        return contract_last(both, wides[...].reshape(width, -1))

    complete = plane_sum(dp, product, grad_ref, sum_refs)
    tokens_load.wait()
    block = 256
    count = width // block

    inner = wide_t.shape[0] // 2
    per = depth * 128 // block

    def tile_copies(j, slot):
        return [
            pltpu.make_async_copy(
                tile_out.at[slot, pl.ds(which * inner, inner), pl.ds(i * 128, 128)],
                wide_grad_hbm.at[lax.rem(j, per) * (block // 128) + i, which, j // per],
                tile_sem.at[slot, which, i],
            )
            for which in range(2)
            for i in range(block // 128)
        ]

    def tile(j, carry):
        slot = lax.rem(j, 2)

        @pl.when(j > 1)
        def _():
            for copy in tile_copies(j - 2, slot):
                copy.wait()

        spot = pl.ds(pl.multiple_of(j * block, block), block)
        columns = tokens[:, :, :, spot].reshape(-1, block)
        tile_out[slot] = multiply(wide_t[...], columns).astype(bf16)
        for copy in tile_copies(j, slot):
            copy.start()
        return carry

    lax.fori_loop(0, count, tile, 0)
    for j in (count - 2, count - 1):
        for copy in tile_copies(j, j % 2):
            copy.wait()
    complete()
    pair_local.wait()
    for k in range(1, dp):
        pair_copy(k).wait_recv()
        pair_copy(k).wait_send()
    part_side_copy(0).wait_send()
    part_copy(0).wait()


def mlp_backward(tokens, cots, hidden, slope, active, wide, down, pair):
    depth, dp = wide.shape[:2]
    size, width = tokens.shape[2:]
    inner = wide.shape[-1] // 2
    f32, bf16 = jnp.float32, jnp.bfloat16
    hbm = pl.BlockSpec(memory_space=pl.ANY)
    dma = pltpu.SemaphoreType.DMA
    weight = pltpu.VMEM((dp, depth) + wide.shape[2:], bf16)
    turned = pltpu.VMEM((2 * inner, 2 * dp * size), bf16)
    return pl.pallas_call(
        functools.partial(mlp_backward_kernel, dp, depth),
        out_shape=(
            jax.ShapeDtypeStruct((size, width), f32),
            jax.ShapeDtypeStruct((dp, size, width), bf16),
            jax.ShapeDtypeStruct((depth, 2, dp, inner, width // (depth * dp)), bf16),
            jax.ShapeDtypeStruct((dp,) + pair.shape, bf16),
        ),
        in_specs=[hbm] * 8,
        out_specs=(pl.BlockSpec(memory_space=pltpu.VMEM), hbm, hbm, hbm),
        scratch_shapes=[
            pltpu.VMEM((dp, 2, size, width), bf16),
            weight,
            pltpu.VMEM((inner, width), bf16),
            turned,
            pltpu.VMEM((2, size, width), bf16),
            pltpu.VMEM((2, 3, size, inner), bf16),
            pltpu.VMEM((2, size, width), bf16),
            pltpu.VMEM((dp, size, width), bf16),
            pltpu.VMEM((2, 2 * inner, 256), bf16),
            dma((2 * depth + 2,)),
            dma((2, 4)),
            dma,
            dma((dp,)),
            dma((dp,)),
            dma((2, 2, 2)),
            dma((dp,)),
            dma((dp,)),
            dma,
        ]
        + sum_scratch(dp, size, width),
        compiler_params=pltpu.CompilerParams(
            collective_id=6, has_side_effects=True, vmem_limit_bytes=60 * 1024 * 1024
        ),
        cost_estimate=LIGHT,
        name="mlp_backward",
    )(tokens, cots, hidden, slope, active, wide, down, pair)


def attend_sum_kernel(
    dp, rows, context_ref, weight_ref, own_ref, gain_ref, middle_ref, normed_ref, *scratch
):
    _, _, _, peer, twin = team_places()
    length = own_ref.shape[1]
    size, width = middle_ref.shape
    greet([peer(k) for k in range(1, 3)] + [twin])

    def product(k, e, turn):
        spot = pl.ds(pl.multiple_of(e * length, length), length)
        block = context_ref[pl.ds(k * rows, rows), spot].reshape(size, -1)
        return multiply(block, weight_ref[...])

    plane_sum(dp, product, middle_ref, scratch)()
    middle = middle_ref[...] + own_ref[...].reshape(size, width).astype(jnp.float32)
    middle_ref[...] = middle
    factor = lax.rsqrt(jnp.mean(middle * middle, axis=-1, keepdims=True) + EPSILON)
    normed_ref[...] = (middle * factor * gain_ref[1:2].astype(jnp.float32)).astype(jnp.bfloat16)


def attend_sum(dp, context, weight, own, gain):
    rows, length, width = own.shape
    size = rows * length
    vmem = pl.BlockSpec(memory_space=pltpu.VMEM)
    return pl.pallas_call(
        functools.partial(attend_sum_kernel, dp, rows),
        out_shape=(
            jax.ShapeDtypeStruct((size, width), jnp.float32),
            jax.ShapeDtypeStruct((size, width), jnp.bfloat16),
        ),
        in_specs=[vmem] * 4,
        out_specs=(vmem, vmem),
        scratch_shapes=sum_scratch(dp, size, width),
        compiler_params=pltpu.CompilerParams(
            collective_id=4, has_side_effects=True, vmem_limit_bytes=VMEM_LIMIT
        ),
        cost_estimate=LIGHT,
        name="attend_sum",
    )(context, weight, own, gain)


def middle_back_kernel(
    dp,
    rows,
    grad_ref,
    middle_ref,
    cot_ref,
    gain_ref,
    context_ref,
    weight_ref,
    grad_middle_ref,
    grad_context_ref,
    weight_grad_ref,
    tokens,
    context_t,
    near_send,
    near_got,
    side_send,
    side_got,
    pass_send,
    pass_got,
):
    f32, bf16 = jnp.float32, jnp.bfloat16
    _, _, core, peer, twin = team_places()
    size, width = grad_ref.shape
    length = size // rows
    half = size // 2
    greet([peer(k) for k in range(1, 3)] + [twin])
    middle = middle_ref[...]
    factor = lax.rsqrt(jnp.mean(middle * middle, axis=-1, keepdims=True) + EPSILON)
    inner = grad_ref[...] * gain_ref[1:2].astype(f32)
    mean = jnp.mean(inner * middle, axis=-1, keepdims=True)
    total = cot_ref[...].astype(f32) + factor * inner - factor * factor * factor * middle * mean
    grad_middle_ref[...] = total
    tokens[0, core] = total.astype(bf16)

    def near_copy(k):
        return send(
            tokens.at[0, core], tokens.at[k, core], near_send.at[k], near_got.at[k], peer(k)
        )

    def pass_copy(part):
        spot = pl.ds(part * half, half)
        return send(
            tokens.at[1 + part, core, spot],
            tokens.at[3, core, spot],
            pass_send.at[part],
            pass_got.at[part],
            peer(2 - part),
        )

    def side_copy(k):
        block = tokens.at[k, core]
        return send(block, block, side_send.at[k], side_got.at[k], twin)

    def side_arrival(k):
        block = tokens.at[k, 1 - core]
        return send(block, block, side_send.at[k], side_got.at[k], twin)

    near_copy(1).start()
    near_copy(2).start()
    side_copy(0).start()
    for k in range(dp):
        for e in range(2):
            for r in range(rows):
                block = context_ref[k * rows + r, e * length : (e + 1) * length]
                spot = pl.ds(((k * 2 + e) * rows + r) * length, length)
                context_t[:, spot] = block.T

    def process(k, e):
        block = contract_last(tokens[k, e], weight_ref[...]).astype(bf16)
        spot = pl.ds(pl.multiple_of(e * length, length), length)
        grad_context_ref[pl.ds(k * rows, rows), spot] = block.reshape(rows, length, -1)

    process(0, core)
    side_arrival(0).wait_recv()
    process(0, 1 - core)
    for k in range(1, 3):
        near_copy(k).wait_recv()
        pass_copy(k - 1).start()
        side_copy(k).start()

    def step(k, carry):
        @pl.when(k == 3)
        def _():
            pass_copy(0).wait_recv()
            pass_copy(1).wait_recv()
            side_copy(3).start()

        process(k, core)
        side_arrival(k).wait_recv()
        process(k, 1 - core)
        return carry

    lax.fori_loop(1, dp, step, 0)

    def tile(j, carry):
        spot = pl.ds(pl.multiple_of(j * 256, 256), 256)
        columns = tokens[:, :, :, spot].reshape(-1, 256)
        weight_grad_ref[:, spot] = multiply(context_t[...], columns).astype(bf16)
        return carry

    lax.fori_loop(0, width // 256, tile, 0)
    for k in range(1, 3):
        near_copy(k).wait_send()
        pass_copy(k - 1).wait_send()
    for k in range(dp):
        side_copy(k).wait_send()


def middle_back(dp, rows, grad, middle, cot, gain, context, weight):
    f32, bf16 = jnp.float32, jnp.bfloat16
    size, width = grad.shape
    vmem = pl.BlockSpec(memory_space=pltpu.VMEM)
    dma = pltpu.SemaphoreType.DMA
    return pl.pallas_call(
        functools.partial(middle_back_kernel, dp, rows),
        out_shape=(
            jax.ShapeDtypeStruct((size, width), f32),
            jax.ShapeDtypeStruct(context.shape, bf16),
            jax.ShapeDtypeStruct(weight.shape, bf16),
        ),
        in_specs=[vmem] * 6,
        out_specs=(vmem, vmem, vmem),
        scratch_shapes=[
            pltpu.VMEM((dp, 2, size, width), bf16),
            pltpu.VMEM((weight.shape[0], 2 * dp * size), bf16),
            dma((dp,)),
            dma((dp,)),
            dma((dp,)),
            dma((dp,)),
            dma((2,)),
            dma((2,)),
        ],
        compiler_params=pltpu.CompilerParams(
            collective_id=5, has_side_effects=True, vmem_limit_bytes=VMEM_LIMIT
        ),
        cost_estimate=LIGHT,
        name="middle_back",
    )(grad, middle, cot, gain, context, weight)


def open_kernel(
    dp,
    depth,
    query_ref,
    key_ref,
    value_ref,
    attn_gain_ref,
    mlp_gain_ref,
    places_ref,
    own_ref,
    out_ref,
    attn_hbm,
    places_hbm,
    near_hbm,
    out_hbm,
    attn_blocks,
    local_sem,
    attn_send,
    attn_got,
    places_send,
    places_got,
    line_send,
    line_got,
    near_send,
    near_got,
    pass_send,
    pass_got,
    out_send,
    out_got,
):
    data, place, core, peer, twin = team_places()
    part = query_ref.shape[0]
    half = HD // 2
    side = depth * half
    middle = own_ref.shape[0] // 2
    attn_blocks[...] = jnp.zeros_like(attn_blocks)
    for d in range(dp):
        for c in range(2):
            team = 2 * d + c
            for z in range(depth):
                owner = (d * depth + z) * 2 + c
                for h in range(2):
                    spot = owner * HD + h * half
                    attn_blocks[team, :, h * side + z * half : h * side + (z + 1) * half] = (
                        query_ref[:, spot : spot + half]
                    )
            pair = key_ref if c == 0 else value_ref
            last = 2 * side + HD
            attn_blocks[team, :, 2 * side : last] = pair[:, d * HD : (d + 1) * HD]
            attn_blocks[team, 0:1, last : last + part] = attn_gain_ref[...]
            attn_blocks[team, 1:2, last : last + part] = mlp_gain_ref[...]

    def device(k, other):
        return (peer(k)[0], place, 1 - core if other else core)

    def number(k, other):
        return 2 * peer(k)[0] + (1 - core if other else core)

    pairs = [(k, other) for k in range(dp) for other in range(2) if k or other]
    greet([device(k, other) for k, other in pairs] + line_neighbours(depth))

    def attn_copy(k, other):
        return send(
            attn_blocks.at[number(k, other)],
            attn_hbm.at[place, data, core],
            attn_send.at[k, other],
            attn_got.at[k, other],
            device(k, other),
        )

    def places_copy(k, other):
        return send(
            places_ref,
            places_hbm.at[k, core],
            places_send.at[k, other],
            places_got.at[k, other],
            device(k, other),
        )

    def arrival(target, send_sem, got_sem):
        return send(target, target, send_sem, got_sem, twin)

    def near_copy(k):
        return send(own_ref, near_hbm.at[k], near_send.at[k], near_got.at[k], peer(k))

    def pass_copy(which):
        spot = pl.ds(which * middle, middle)
        return send(
            near_hbm.at[1 + which, spot],
            near_hbm.at[3, spot],
            pass_send.at[which],
            pass_got.at[which],
            peer(2 - which),
        )

    start, relay, complete = line_gather(depth, lambda z: attn_hbm.at[z], line_send, line_got)
    out_start, out_relay, out_complete = line_gather(
        depth, lambda z: out_hbm.at[z], out_send, out_got
    )
    for k, other in pairs:
        attn_copy(k, other).start()
    for k, other in pairs:
        places_copy(k, other).start()
    near_copy(1).start()
    near_copy(2).start()
    locals_ = [
        pltpu.make_async_copy(
            attn_blocks.at[2 * data + core], attn_hbm.at[place, data, core], local_sem.at[0]
        ),
        pltpu.make_async_copy(places_ref, places_hbm.at[0, core], local_sem.at[1]),
        pltpu.make_async_copy(own_ref, near_hbm.at[0], local_sem.at[2]),
        pltpu.make_async_copy(out_ref, out_hbm.at[place], local_sem.at[3]),
    ]
    for copy in locals_:
        copy.start()
    locals_[0].wait()
    for k, other in pairs:
        target = attn_hbm.at[place, peer(k)[0], 1 - core if other else core]
        arrival(target, attn_send.at[k, other], attn_got.at[k, other]).wait_recv()
    start()
    for copy in locals_[1:]:
        copy.wait()
    out_start()
    relay(1)
    for which in range(2):
        near_copy(1 + which).wait_recv()
        pass_copy(which).start()
    for distance in range(2, depth):
        relay(distance)
        out_relay(distance - 1)
    out_relay(depth - 1)
    for k, other in pairs:
        target = places_hbm.at[k, 1 - core if other else core]
        arrival(target, places_send.at[k, other], places_got.at[k, other]).wait_recv()
    for which in range(2):
        pass_copy(which).wait_recv()
        pass_copy(which).wait_send()
        near_copy(1 + which).wait_send()
    complete()
    out_complete()
    for k, other in pairs:
        attn_copy(k, other).wait_send()
        places_copy(k, other).wait_send()


def open_layer(dp, depth, query, key, value, attn_gain, mlp_gain, places, own, out_weight):
    part = query.shape[0]
    columns = depth * HD + HD + part
    bf16 = jnp.bfloat16
    hbm = pl.BlockSpec(memory_space=pl.ANY)
    vmem = pl.BlockSpec(memory_space=pltpu.VMEM)
    dma = pltpu.SemaphoreType.DMA
    return pl.pallas_call(
        functools.partial(open_kernel, dp, depth),
        out_shape=(
            jax.ShapeDtypeStruct((depth, dp, 2, part, columns), bf16),
            jax.ShapeDtypeStruct((dp, 2) + places.shape, places.dtype),
            jax.ShapeDtypeStruct((dp,) + own.shape, bf16),
            jax.ShapeDtypeStruct((depth,) + out_weight.shape, bf16),
        ),
        in_specs=[vmem] * 8,
        out_specs=(hbm,) * 4,
        scratch_shapes=[
            pltpu.VMEM((2 * dp, part, columns), bf16),
            dma((4,)),
            dma((dp, 2)),
            dma((dp, 2)),
            dma((dp, 2)),
            dma((dp, 2)),
            dma((depth, 2)),
            dma((depth,)),
            dma((dp,)),
            dma((dp,)),
            dma((2,)),
            dma((2,)),
            dma((depth, 2)),
            dma((depth,)),
        ],
        compiler_params=pltpu.CompilerParams(
            collective_id=7, has_side_effects=True, vmem_limit_bytes=VMEM_LIMIT
        ),
        cost_estimate=LIGHT,
        name="open_layer",
    )(query, key, value, attn_gain[None], mlp_gain[None], places, own, out_weight)


def project_kernel(
    dp,
    depth,
    rows,
    *refs,
):
    pieces, places_ref, freq_ref, freq_pair_ref, gate_ref, up_ref, weight_hbm = refs[:7]
    query_ref, normed_hbm, cosine_ref, sine_ref, cosine_pair_ref, sine_pair_ref = refs[7:13]
    offset_ref, gain_ref, pair_weight_ref, line_hbm, wide_hbm = refs[13:18]
    (
        weight,
        pair,
        far_pieces,
        load_sem,
        own_sem,
        line_send,
        line_got,
        side_send,
        side_got,
        twin_send,
        twin_got,
        wide_blocks,
        wide_send,
        wide_got,
        wide_sem,
        normed,
        normed_sem,
    ) = refs[18:]
    f32, bf16 = jnp.float32, jnp.bfloat16
    data, place, core, peer, twin = team_places()
    length, width = pieces.shape[2:]
    part = weight.shape[3]
    columns = query_ref.shape[2]
    loads = [
        pltpu.make_async_copy(
            weight_hbm.at[z], weight.at[:, z], load_sem.at[z]
        )
        for z in range(depth)
    ]
    for load in loads:
        load.start()

    def device(k, other):
        return (peer(k)[0], place, 1 - core if other else core)

    def number(k, other):
        return 2 * peer(k)[0] + (1 - core if other else core)

    pairs = [(k, other) for k in range(dp) for other in range(2) if k or other]
    others = [(data, lax.rem(place + step, depth), core) for step in range(1, depth)]
    greet(others + [device(k, other) for k, other in pairs])

    def wide_copy(k, other):
        return send(
            wide_blocks.at[number(k, other)],
            wide_hbm.at[data, core],
            wide_send.at[k, other],
            wide_got.at[k, other],
            device(k, other),
        )


    def twin_copy(k):
        return send(pieces.at[k], far_pieces.at[k], twin_send.at[k], twin_got.at[k], twin)

    for k in range(dp):
        twin_copy(k).start()
    count = wide_blocks.shape[2] // (2 * depth)
    for d in range(dp):
        for c in range(2):
            for z in range(depth):
                owner = (d * depth + z) * 2 + c
                for which, source in ((0, gate_ref), (1, up_ref)):
                    spot = (which * depth + z) * count
                    wide_blocks[2 * d + c, :, spot : spot + count] = source[
                        :, owner * count : (owner + 1) * count
                    ]
    wide_local = pltpu.make_async_copy(
        wide_blocks.at[2 * data + core], wide_hbm.at[data, core], wide_sem
    )
    wide_local.start()
    for k, other in pairs:
        wide_copy(k, other).start()
    for load in loads:
        load.wait()
    for d in range(dp):
        for z in range(depth):
            for c in range(2):
                spot = ((d * depth + z) * 2 + c) * part
                gain_ref[:, spot : spot + part] = weight[d, z, c, 0:2, columns + HD :]
    pair_weight_ref[...] = weight[...].reshape(width, -1)[:, columns : columns + HD].T
    gain = gain_ref[0:1].astype(f32)
    turning = (1 - core).astype(f32)

    def block_of(which, z, k):
        return line_hbm.at[which, z, pl.ds(k * rows, rows)]

    def pair_of(k):
        return pair.at[pl.ds(k * rows, rows)]

    def own_copy(k):
        return pltpu.make_async_copy(pair_of(k), block_of(core, place, k), own_sem.at[k])

    def own_side_copy(k):
        return send(
            pair_of(k),
            block_of(core, place, k),
            side_send.at[place, k],
            side_got.at[place, k],
            twin,
        )

    def line_copy(z, k):
        return send(
            pair_of(k),
            block_of(core, place, k),
            line_send.at[z, k],
            line_got.at[place, k],
            (data, z, core),
        )

    def line_arrival(z, k):
        block = block_of(core, z, k)
        return send(block, block, line_send.at[z, k], line_got.at[z, k], twin)

    def side_copy(z, k):
        block = block_of(core, z, k)
        return send(block, block, side_send.at[z, k], side_got.at[z, k], twin)

    def side_arrival(z, k):
        block = block_of(1 - core, z, k)
        return send(block, block, side_send.at[z, k], side_got.at[z, k], twin)

    def normed_copy(k, e):
        return pltpu.make_async_copy(normed.at[k, e], normed_hbm.at[k, e], normed_sem.at[k, e])

    for k in range(dp):
        for far in range(2):
            e = core if far == 0 else 1 - core
            if far:
                twin_copy(k).wait_recv()
            source = far_pieces.at[k] if far else pieces.at[k]
            values = source[...].reshape(rows * length, width).astype(f32)
            factor = lax.rsqrt(jnp.mean(values * values, axis=-1, keepdims=True) + EPSILON)
            tokens = (values * factor * gain).astype(bf16)
            normed[k, e] = tokens
            normed_copy(k, e).start()
            result = multiply(tokens, weight[...].reshape(width, -1)[:, columns:])
            spot = pl.ds(pl.multiple_of(e * length, length), length)
            for r in range(rows):
                row = k * rows + r
                offsets = places_ref[k, e][r : r + 1].astype(f32)
                keys = result[r * length : (r + 1) * length, :HD].T
                angles = offsets * freq_pair_ref[...] * turning
                cosine, sine = jnp.cos(angles), jnp.sin(angles)
                cosine_pair_ref[row, :, spot] = cosine
                sine_pair_ref[row, :, spot] = sine
                first, second = keys[: HD // 2], keys[HD // 2 :]
                pair[row, : HD // 2, spot] = (first * cosine - second * sine).astype(bf16)
                pair[row, HD // 2 :, spot] = (second * cosine + first * sine).astype(bf16)
        own_copy(k).start()
        own_side_copy(k).start()
        for z in range(depth):

            @pl.when(z > place)
            def _(z=z, k=k):
                line_copy(z, k).start()

    def turn_queries(k, carry):
        for e in range(2):
            result = multiply(normed[k, e], weight[...].reshape(width, -1)[:, :columns])
            spot = pl.ds(e * length, length)
            for r in range(rows):
                row = k * rows + r
                block = result[r * length : (r + 1) * length]
                offsets = places_ref[k, e][r : r + 1].astype(f32)
                column = jnp.broadcast_to(offsets, (length, length)).T
                offset_ref[row, spot] = column.astype(jnp.int32)
                angles = column * freq_ref[...]
                cosine, sine = jnp.cos(angles), jnp.sin(angles)
                cosine_ref[row, spot] = cosine
                sine_ref[row, spot] = sine
                first, second = block[:, : columns // 2], block[:, columns // 2 :]
                turned = (first * cosine - second * sine).astype(bf16)
                query_ref[row, spot, : columns // 2] = turned * bf16(HD ** (-0.5))
                turned = (second * cosine + first * sine).astype(bf16)
                query_ref[row, spot, columns // 2 :] = turned * bf16(HD ** (-0.5))
        return carry

    lax.fori_loop(0, dp, turn_queries, 0)
    for k in range(dp):
        for z in reversed(range(depth)):

            @pl.when(z < place)
            def _(z=z, k=k):
                line_arrival(z, k).wait_recv()
                side_copy(z, k).start()

    for k in range(dp):
        for e in range(2):
            normed_copy(k, e).wait()
    wide_local.wait()
    for k, other in pairs:
        block = wide_hbm.at[peer(k)[0], 1 - core if other else core]
        send(block, block, wide_send.at[k, other], wide_got.at[k, other], twin).wait_recv()
        wide_copy(k, other).wait_send()
    for k in range(dp):
        twin_copy(k).wait_send()
        own_copy(k).wait()
        own_side_copy(k).wait_send()
        for z in range(depth):

            @pl.when(z <= place)
            def _(z=z, k=k):
                side_arrival(z, k).wait_recv()

            @pl.when(z < place)
            def _(z=z, k=k):
                side_copy(z, k).wait_send()

            @pl.when(z > place)
            def _(z=z, k=k):
                line_copy(z, k).wait_send()


def project(near, places, freqs, gate, up, weight):
    f32, bf16 = jnp.float32, jnp.bfloat16
    dp, rows, length, width = near.shape
    depth = weight.shape[0]
    heads = depth
    row_count, size = dp * rows, 2 * length
    columns = heads * HD
    part = width // (2 * dp * depth)
    hbm = pl.BlockSpec(memory_space=pl.ANY)
    vmem = pl.BlockSpec(memory_space=pltpu.VMEM)
    dma = pltpu.SemaphoreType.DMA
    turned = jax.ShapeDtypeStruct((row_count, size, columns // 2), f32)
    turned_pair = jax.ShapeDtypeStruct((row_count, HD // 2, size), f32)
    return pl.pallas_call(
        functools.partial(project_kernel, dp, depth, rows),
        out_shape=(
            jax.ShapeDtypeStruct((row_count, size, columns), bf16),
            jax.ShapeDtypeStruct((dp, 2, rows * length, width), bf16),
            turned,
            turned,
            turned_pair,
            turned_pair,
            jax.ShapeDtypeStruct((row_count, size, length), jnp.int32),
            jax.ShapeDtypeStruct((2, width), bf16),
            jax.ShapeDtypeStruct((HD, width), bf16),
            jax.ShapeDtypeStruct((2, depth, row_count, HD, size), bf16),
            jax.ShapeDtypeStruct((dp, 2, part, gate.shape[1] // dp), bf16),
        ),
        in_specs=[vmem] * 6 + [hbm],
        out_specs=(vmem, hbm) + (vmem,) * 7 + (hbm,) * 2,
        scratch_shapes=[
            pltpu.VMEM((dp, depth) + weight.shape[2:], bf16),
            pltpu.VMEM((row_count, HD, size), bf16),
            pltpu.VMEM((dp, rows, length, width), bf16),
            dma((2 * depth,)),
            dma((dp,)),
            dma((depth, dp)),
            dma((depth, dp)),
            dma((depth, dp)),
            dma((depth, dp)),
            dma((dp,)),
            dma((dp,)),
            pltpu.VMEM((2 * dp, part, gate.shape[1] // dp), bf16),
            dma((dp, 2)),
            dma((dp, 2)),
            dma,
            pltpu.VMEM((dp, 2, rows * length, width), bf16),
            dma((dp, 2)),
        ],
        compiler_params=pltpu.CompilerParams(
            collective_id=2, has_side_effects=True, vmem_limit_bytes=VMEM_LIMIT
        ),
        cost_estimate=LIGHT,
        name="project",
    )(near, places, jnp.tile(freqs, heads)[None], freqs[:, None], gate, up, weight)


def as_row(column):
    return jnp.broadcast_to(column, (column.shape[0], 128)).T[0:1]


def finish_kernel(
    dp,
    depth,
    rows,
    query_ref,
    cosine_ref,
    sine_ref,
    wide_ref,
    own_ref,
    grad_middle_ref,
    gain_ref,
    query_weight_ref,
    key_weight_ref,
    value_weight_ref,
    gate_weight_ref,
    up_weight_ref,
    grad_k_hbm,
    grad_v_hbm,
    normed_hbm,
    weight_hbm,
    *refs,
):
    pairs_hbm, *refs = refs
    finish_body(
        dp, depth, rows, query_ref, cosine_ref, sine_ref, wide_ref, own_ref,
        grad_middle_ref, gain_ref, query_weight_ref, key_weight_ref, value_weight_ref,
        gate_weight_ref, up_weight_ref, grad_k_hbm, grad_v_hbm, normed_hbm, weight_hbm, pairs_hbm,
        *refs,
    )


def finish_body(
    dp,
    depth,
    rows,
    query_ref,
    cosine_ref,
    sine_ref,
    wide_ref,
    own_ref,
    grad_middle_ref,
    gain_ref,
    query_weight_ref,
    key_weight_ref,
    value_weight_ref,
    gate_weight_ref,
    up_weight_ref,
    grad_k_hbm,
    grad_v_hbm,
    normed_hbm,
    weight_hbm,
    pairs_hbm,
    grad_ref,
    query_grad_ref,
    key_grad_ref,
    value_grad_ref,
    gate_grad_ref,
    up_grad_ref,
    attn_gain_ref,
    mlp_gain_ref,
    normed,
    weight,
    kept,
    given,
    arrived,
    line_block,
    line_got_block,
    terms,
    terms_t,
    held,
    line_grads,
    line_grads_got,
    team_block,
    team_got_block,
    wide_block,
    wide_got_block,
    load_sem,
    swap_send,
    swap_got,
    line_send,
    line_got,
    grads_send,
    grads_got,
    team_send,
    team_got,
    wide_send,
    wide_got,
    pair_weight,
    pair_out,
    pair_in,
    pair_load_sem,
    pair_twin_send,
    pair_twin_got,
    pair_send,
    pair_got,
    *sum_refs,
):
    f32, bf16 = jnp.float32, jnp.bfloat16
    data, place, core, peer, twin = team_places()
    columns = query_ref.shape[2]
    size = query_ref.shape[1]
    length = size // 2
    width = grad_ref.shape[1]
    part = weight.shape[3]
    features = columns + HD
    half = HD // 2
    loads = [
        pltpu.make_async_copy(
            weight_hbm.at[z, :, :, :, pl.ds(0, columns)],
            weight.at[:, z],
            load_sem.at[z],
        )
        for z in range(depth)
    ]
    pair_loads = [
        pltpu.make_async_copy(pairs_hbm.at[k], pair_weight.at[k, core], pair_load_sem.at[k])
        for k in range(dp)
    ]
    loads.append(pltpu.make_async_copy(normed_hbm, normed, load_sem.at[depth]))

    @pl.when(core == 0)
    def _():
        pltpu.make_async_copy(grad_k_hbm, kept, load_sem.at[depth + 1]).start()
        pltpu.make_async_copy(grad_v_hbm, given, load_sem.at[depth + 2]).start()

    @pl.when(core == 1)
    def _():
        pltpu.make_async_copy(grad_v_hbm, kept, load_sem.at[depth + 1]).start()
        pltpu.make_async_copy(grad_k_hbm, given, load_sem.at[depth + 2]).start()

    for load in loads + pair_loads:
        load.start()
    others = [(data, lax.rem(place + step, depth), core) for step in range(1, depth)]

    def device(k, other):
        return (peer(k)[0], place, 1 - core if other else core)

    pairs = [(k, other) for k in range(dp) for other in range(2) if k or other]
    greet(others + [device(k, other) for k, other in pairs])
    pltpu.make_async_copy(grad_v_hbm, given, load_sem.at[depth + 2]).wait()
    swap_copy = send(given, arrived, swap_send, swap_got, twin)
    swap_copy.start()

    def pair_twin(k):
        block = pair_weight.at[k, core]
        return send(block, block, pair_twin_send.at[k], pair_twin_got.at[k], twin)

    def pair_twin_arrival(k):
        block = pair_weight.at[k, 1 - core]
        return send(block, block, pair_twin_send.at[k], pair_twin_got.at[k], twin)

    def pair_copy(k, other):
        e = 1 - core if other else core
        return send(
            pair_out.at[k, e],
            pair_in.at[k, core],
            pair_send.at[k, other],
            pair_got.at[k, other],
            device(k, other),
        )

    def pair_arrival(k, other):
        block = pair_in.at[k, 1 - core if other else core]
        return send(block, block, pair_send.at[k, other], pair_got.at[k, other], twin)

    def wide_copy(k, other):
        spot = (peer(k)[0], 1 - core if other else core)
        return send(
            wide_block.at[spot],
            wide_got_block.at[data, core],
            wide_send.at[k, other],
            wide_got.at[k, other],
            device(k, other),
        )

    def wide_arrival(k, other):
        block = wide_got_block.at[peer(k)[0], 1 - core if other else core]
        return send(block, block, wide_send.at[k, other], wide_got.at[k, other], twin)

    def line_copy(z):
        return send(
            line_block.at[z],
            line_got_block.at[place],
            line_send.at[z],
            line_got.at[place],
            (data, z, core),
        )

    def line_arrival(z):
        block = line_got_block.at[z]
        return send(block, block, line_send.at[z], line_got.at[z], twin)

    pltpu.make_async_copy(grad_k_hbm, kept, load_sem.at[depth + 1]).wait()
    swap_copy.wait_recv()
    for z in range(depth):

        @pl.when(z < place)
        def _(z=z):
            total = kept[z].astype(f32) + arrived[z].astype(f32)
            line_block[z] = total.astype(bf16)
            line_copy(z).start()

    for load in loads:
        load.wait()
    for k in range(dp):
        for e in range(2):
            for r in range(rows):
                block = query_ref[k * rows + r, e * length : (e + 1) * length]
                terms[k, e, r * length : (r + 1) * length] = block
                spot = pl.ds(((k * 2 + e) * rows + r) * length, length)
                terms_t[:columns, spot] = block.T

    def tile_rows(first, count):
        def tile(j, carry):
            spot = pl.ds(pl.multiple_of(j * 256, 256), 256)
            block = multiply(
                terms_t[first : first + count], normed[:, :, :, spot].reshape(-1, 256)
            ).astype(bf16)
            for i in range(2):
                group = 2 * j + i
                line_grads[lax.rem(group, depth), group // depth, first : first + count] = block[
                    :, i * 128 : (i + 1) * 128
                ]
            return carry

        lax.fori_loop(0, width // 256, tile, 0)

    def grads_copy(z, piece):
        spot = pl.ds(piece * columns, HD if piece else columns)
        return send(
            line_grads.at[z, :, spot],
            line_grads_got.at[place, :, spot],
            grads_send.at[z, piece],
            grads_got.at[place, piece],
            (data, z, core),
        )

    def grads_arrival(z, piece):
        spot = pl.ds(piece * columns, HD if piece else columns)
        block = line_grads_got.at[z, :, spot]
        return send(block, block, grads_send.at[z, piece], grads_got.at[z, piece], twin)

    def product(k, e, turn):
        return contract_last(terms[k, e], weight[...].reshape(width, columns))

    complete = plane_sum(dp, product, grad_ref, sum_refs)
    for k in range(dp):
        pair_loads[k].wait()
        pair_twin(k).start()
    for which in range(2):
        for d in range(dp):
            block = wide_ref[which, d].T
            wide_block[d, 0, which] = block[:part]
            wide_block[d, 1, which] = block[part:]
    for k, other in pairs:
        wide_copy(k, other).start()
    wide_got_block[data, core] = wide_block[data, core]
    tile_rows(0, columns)
    for z in range(depth):

        @pl.when(z > place)
        def _(z=z):
            grads_copy(z, 0).start()

    for z in range(depth):

        @pl.when(z == place)
        def _(z=z):
            held[...] = kept[z].astype(f32) + arrived[z].astype(f32)

    for z in range(depth):

        @pl.when(z > place)
        def _(z=z):
            line_arrival(z).wait_recv()
            held[...] += line_got_block[z].astype(f32)

    for z in range(depth):

        @pl.when(z < place)
        def _(z=z):
            grads_copy(z, 0).start()

    for k in range(dp):
        for r in range(rows):
            row = k * rows + r
            first, second = held[row, :half], held[row, half:]
            cosine, sine = cosine_ref[row], sine_ref[row]
            turned = jnp.concatenate(
                [first * cosine + second * sine, second * cosine - first * sine], axis=0
            ).astype(bf16)
            for e in range(2):
                block = turned[:, e * length : (e + 1) * length]
                spot = pl.ds(((k * 2 + e) * rows + r) * length, length)
                terms_t[columns:, spot] = block
                pair_out[k, e, :, r * length : (r + 1) * length] = block
    for k, other in pairs:
        pair_copy(k, other).start()
    pair_in[0, core] = pair_out[0, core]

    tile_rows(columns, HD)
    for z in range(depth):

        @pl.when(z != place)
        def _(z=z):
            grads_copy(z, 1).start()

    for k, other in pairs:
        wide_arrival(k, other).wait_recv()
    count = wide_block.shape[4] // depth
    for d in range(dp):
        for c in range(2):
            for which, target in ((0, gate_grad_ref), (1, up_grad_ref)):
                block = wide_got_block[d, c, which]
                for z in range(depth):
                    spot = ((d * depth + z) * 2 + c) * count
                    target[:, spot : spot + count] = block[:, z * count : (z + 1) * count]
    products = gate_weight_ref[...].astype(f32) * gate_grad_ref[...].astype(f32)
    products = products + up_weight_ref[...].astype(f32) * up_grad_ref[...].astype(f32)
    mlp_gain_ref[...] = as_row(jnp.sum(products, axis=-1, keepdims=True))

    def team_copy(k, other, piece):
        spot = (peer(k)[0], 1 - core if other else core)
        return send(
            team_block.at[spot + (piece,)],
            team_got_block.at[data, core, piece],
            team_send.at[k, other, piece],
            team_got.at[k, other, piece],
            device(k, other),
        )

    def team_arrival(k, other, piece):
        block = team_got_block.at[peer(k)[0], 1 - core if other else core, piece]
        send_sem, got_sem = team_send.at[k, other, piece], team_got.at[k, other, piece]
        return send(block, block, send_sem, got_sem, twin)

    line_grads_got[place] = line_grads[place]

    def team_piece(piece, first, last):
        for z in range(depth):

            @pl.when(z != place)
            def _(z=z):
                grads_arrival(z, piece).wait_recv()

        for d in range(dp):
            total = line_grads_got[0, d, first:last].astype(f32)
            for z in range(1, depth):
                total = total + line_grads_got[z, d, first:last].astype(f32)
            total = total.T.astype(bf16)
            team_block[d, 0, piece, :, : last - first] = total[:part]
            team_block[d, 1, piece, :, : last - first] = total[part:]
        for k, other in pairs:
            team_copy(k, other, piece).start()
        team_got_block[data, core, piece] = team_block[data, core, piece]

    team_block[...] = jnp.zeros_like(team_block)
    team_piece(0, 0, columns)
    complete()
    for k, other in pairs:
        pair_arrival(k, other).wait_recv()
    for k in range(dp):
        pair_twin_arrival(k).wait_recv()
    grad_ref[...] += multiply(
        pair_in[...].reshape(2 * dp * HD, -1).T, pair_weight[...].reshape(2 * dp * HD, width)
    )
    own = own_ref[...].reshape(grad_ref.shape).astype(f32)
    factor = lax.rsqrt(jnp.mean(own * own, axis=-1, keepdims=True) + EPSILON)
    inner = grad_ref[...] * gain_ref[0:1].astype(f32)
    mean = jnp.mean(inner * own, axis=-1, keepdims=True)
    grad_ref[...] = grad_middle_ref[...] + factor * inner - factor * factor * factor * own * mean
    team_piece(1, columns, features)
    for k, other in pairs:
        team_arrival(k, other, 0).wait_recv()
    side = depth * half
    for d in range(dp):
        for c in range(2):
            block = team_got_block[d, c, 0]
            for z in range(depth):
                for h in range(2):
                    spot = ((d * depth + z) * 2 + c) * HD + h * half
                    start = h * side + z * half
                    query_grad_ref[:, spot : spot + half] = block[:, start : start + half]
    for k, other in pairs:
        team_arrival(k, other, 1).wait_recv()
    for d in range(dp):
        for c in range(2):
            target = key_grad_ref if c == 0 else value_grad_ref
            target[:, d * HD : (d + 1) * HD] = team_got_block[d, c, 1, :, :HD]
    total = sum(
        jnp.sum(before[...].astype(f32) * after[...].astype(f32), axis=-1, keepdims=True)
        for before, after in (
            (query_weight_ref, query_grad_ref),
            (key_weight_ref, key_grad_ref),
            (value_weight_ref, value_grad_ref),
        )
    )
    attn_gain_ref[...] = as_row(total)
    swap_copy.wait_send()
    for k in range(dp):
        pair_twin(k).wait_send()
    for k, other in pairs:
        team_copy(k, other, 0).wait_send()
        team_copy(k, other, 1).wait_send()
        pair_copy(k, other).wait_send()
        wide_copy(k, other).wait_send()
    for z in range(depth):

        @pl.when(z < place)
        def _(z=z):
            line_copy(z).wait_send()

        @pl.when(z != place)
        def _(z=z):
            grads_copy(z, 0).wait_send()
            grads_copy(z, 1).wait_send()


def finish(grad_queries, cosine_pair, sine_pair, wide_sum, own, grad_middle, gain, weights, grad_keys, grad_values, normed, weight, pair_weights):
    f32, bf16 = jnp.float32, jnp.bfloat16
    dp, _, size, width = normed.shape
    rows = own.shape[0]
    depth, row_count, features, line_size = grad_keys.shape
    columns = grad_queries.shape[2]
    part = width // (2 * dp * depth)
    inner = wide_sum.shape[2]
    total = columns + features
    hbm = pl.BlockSpec(memory_space=pl.ANY)
    vmem = pl.BlockSpec(memory_space=pltpu.VMEM)
    dma = pltpu.SemaphoreType.DMA
    line = pltpu.VMEM((depth, row_count, features, line_size), bf16)
    grads = pltpu.VMEM((depth, dp, total, 2 * part), bf16)
    team = pltpu.VMEM((dp, 2, 2, part, columns), bf16)
    wide = pltpu.VMEM((dp, 2, 2, part, inner), bf16)
    query_weight, key_weight, value_weight, gate_weight, up_weight = weights
    return pl.pallas_call(
        functools.partial(finish_kernel, dp, depth, rows),
        out_shape=(
            jax.ShapeDtypeStruct((size, width), f32),
            jax.ShapeDtypeStruct(query_weight.shape, bf16),
            jax.ShapeDtypeStruct(key_weight.shape, bf16),
            jax.ShapeDtypeStruct(value_weight.shape, bf16),
            jax.ShapeDtypeStruct(gate_weight.shape, bf16),
            jax.ShapeDtypeStruct(up_weight.shape, bf16),
            jax.ShapeDtypeStruct((1, part), f32),
            jax.ShapeDtypeStruct((1, part), f32),
        ),
        in_specs=[vmem] * 12 + [hbm] * 5,
        out_specs=(vmem,) * 8,
        scratch_shapes=[
            pltpu.VMEM((dp, 2, size, width), bf16),
            pltpu.VMEM((dp, depth, 2, part, columns), bf16),
            line,
            line,
            line,
            line,
            line,
            pltpu.VMEM((dp, 2, size, columns), bf16),
            pltpu.VMEM((total, 2 * dp * size), bf16),
            pltpu.VMEM((row_count, features, line_size), f32),
            grads,
            grads,
            team,
            team,
            wide,
            wide,
            dma((depth + 3,)),
            dma,
            dma,
            dma((depth,)),
            dma((depth,)),
            dma((depth, 2)),
            dma((depth, 2)),
            dma((dp, 2, 2)),
            dma((dp, 2, 2)),
            dma((dp, 2)),
            dma((dp, 2)),
            pltpu.VMEM((dp, 2, features, width), bf16),
            pltpu.VMEM((dp, 2, features, size), bf16),
            pltpu.VMEM((dp, 2, features, size), bf16),
            dma((dp,)),
            dma((dp,)),
            dma((dp,)),
            dma((dp, 2)),
            dma((dp, 2)),
        ]
        + sum_scratch(dp, size, width),
        compiler_params=pltpu.CompilerParams(
            collective_id=3, has_side_effects=True, vmem_limit_bytes=60 * 1024 * 1024
        ),
        cost_estimate=pl.CostEstimate(flops=10**11, bytes_accessed=1024, transcendentals=0),
        name="finish",
    )(
        grad_queries,
        cosine_pair,
        sine_pair,
        wide_sum,
        own,
        grad_middle,
        gain,
        *weights,
        grad_keys,
        grad_values,
        normed,
        weight,
        pair_weights,
    )


def split_layer(dp, depth):
    def layer(
        hidden_in,
        segment_ids,
        positions,
        attn_gain,
        query_weight,
        key_weight,
        value_weight,
        out_weight,
        mlp_gain,
        gate_weight,
        up_weight,
        down_weight,
        cotangent,
    ):
        f32, bf16 = jnp.float32, jnp.bfloat16
        rows, length, width = hidden_in.shape
        own = rows * length
        team = 2 * dp
        tokens = team * own
        part = query_weight.shape[0]
        hidden_rows = down_weight.shape[0]
        inner = depth * hidden_rows
        heads = depth
        row_count, size = dp * rows, 2 * length
        core = lax.axis_index("core")
        place = lax.axis_index("z")

        def dot(left, right):
            return jnp.dot(left, right, preferred_element_type=f32)

        weight_attn, places, near, weight_out = open_layer(
            dp, depth, query_weight, key_weight, value_weight, attn_gain, mlp_gain, positions,
            hidden_in, out_weight,
        )
        weight_out = weight_out.reshape(heads * HD, width)
        weight_down = lax.all_gather(down_weight, "z", axis=0, tiled=True)

        x_own = hidden_in.reshape(own, width)
        cot_own = cotangent.reshape(own, width)
        freqs = 10000.0 ** (-jnp.arange(0, HD // 2, dtype=f32) * 2.0 / HD)
        queries, normed1, cosine, sine, cosine_pair, sine_pair, offsets, gains, pair_weight, lines, wide_mine = (
            project(near, places, freqs, gate_weight, up_weight, weight_attn)
        )
        wide_got = lax.all_gather(wide_mine, "z", axis=0)
        cotangent, queries = lax.optimization_barrier((cotangent, queries))
        cots = plane_pieces(cotangent, dp)
        cots = [piece.reshape(own, width) for piece in cots]
        low_block = (place * size - places[:, 0, :, 0].reshape(row_count)) // size
        low_block = jnp.maximum(low_block, 0).astype(jnp.int32)
        place_one = place.astype(jnp.int32).reshape(1)
        context, logs = attend(
            low_block, place_one, offsets, queries, lines
        )

        context, cots = lax.optimization_barrier((context, cots))
        middle, normed2 = attend_sum(dp, context, weight_out, hidden_in, gains)
        all_normed2, all_cots, hidden, slope, active, grad_down = mlp_forward(
            normed2, wide_got, cots
        )
        grad_normed2, mlp_parts, grad_wide, pair_weights = mlp_backward(
            all_normed2, all_cots, hidden, slope, active, wide_got, weight_down, pair_weight
        )
        def line_sum(array):
            return lax.psum_scatter(array.astype(bf16), "z", scatter_dimension=0, tiled=True)

        down_sum = line_sum(grad_down)
        grad_wide, down_sum = lax.optimization_barrier((grad_wide, down_sum))
        wide_sum = line_sum(grad_wide)[0]
        grad_normed2, down_sum = lax.optimization_barrier((grad_normed2, down_sum))
        grad_middle, grad_context, grad_wout = middle_back(
            dp, rows, grad_normed2, middle, cot_own, gains, context, weight_out
        )
        grad_down = down_sum.astype(f32)
        mlp_parts, grad_context = lax.optimization_barrier((mlp_parts, grad_context))
        mlp_got = [swap(mlp_parts[k], "dp", dp, k) for k in range(1, dp)]
        grad_queries, grad_keys, grad_values = attend_back(
            low_block,
            place_one,
            offsets,
            queries,
            lines,
            context,
            logs,
            grad_context,
            cosine,
            sine,
        )
        out_hidden = middle + mlp_parts[0].astype(f32)
        for got in mlp_got:
            out_hidden = out_hidden + got.astype(f32)
        out_hidden = out_hidden.astype(bf16)
        grad_queries, out_hidden, grad_wout = lax.optimization_barrier(
            (grad_queries, out_hidden, grad_wout)
        )
        out_sum = line_sum(grad_wout)
        (
            grad_in,
            grad_wquery,
            grad_wkey,
            grad_wvalue,
            grad_wgate,
            grad_wup,
            attn_rows,
            mlp_rows,
        ) = finish(
            grad_queries,
            cosine_pair,
            sine_pair,
            wide_sum,
            hidden_in,
            grad_middle,
            gains,
            (query_weight, key_weight, value_weight, gate_weight, up_weight),
            grad_keys,
            grad_values,
            normed1,
            weight_attn,
            pair_weights,
        )
        out_sum, grad_in = lax.optimization_barrier((out_sum, grad_in))
        grad_wout = out_sum.astype(f32)
        grad_wquery, grad_wkey, grad_wvalue, grad_wgate, grad_wup = (
            grad.astype(f32) for grad in (grad_wquery, grad_wkey, grad_wvalue, grad_wgate, grad_wup)
        )
        grad_gain_one = attn_rows[0] / attn_gain.astype(f32)
        grad_gain_two = mlp_rows[0] / mlp_gain.astype(f32)
        return (
            out_hidden.reshape(rows, length, width),
            grad_in.reshape(rows, length, width),
            grad_gain_one,
            grad_wquery,
            grad_wkey,
            grad_wvalue,
            grad_wout,
            grad_gain_two,
            grad_wgate,
            grad_wup,
            grad_down,
        )

    return layer


def solution(mesh):
    dp, seq = mesh.shape["dp"], mesh.shape["seq"]
    if dp != KVH or seq % 2 or HQ != dp * seq:
        return gathered_weights(mesh)
    depth = seq // 2
    mesh = Mesh(mesh.devices.reshape(dp, depth, 2), ("dp", "z", "core"))
    every = ("dp", "z", "core")
    tokens = P("dp", ("z", "core"), None)
    matrix = P(every, None)
    return jax.shard_map(
        split_layer(dp, depth),
        mesh=mesh,
        in_specs=(
            tokens,
            P("dp", ("z", "core")),
            P("dp", ("z", "core")),
            P(every),
            matrix,
            matrix,
            matrix,
            matrix,
            P(every),
            matrix,
            matrix,
            matrix,
            tokens,
        ),
        out_specs=(
            tokens,
            tokens,
            P(every),
            matrix,
            matrix,
            matrix,
            matrix,
            P(every),
            matrix,
            matrix,
            matrix,
        ),
        check_vma=False,
    )
```
